32 devices in a mesh: dp: 2 (over core), shard: 16 (over z, y, x).
Axes of the slice: x: 2, y: 2, z: 4, core: 2. Of those that a mesh axis runs over, the one named last changes fastest.
Arguments:
- hidden_in: bfloat16 [4096, 1024], P(('dp', 'shard')), may hold values from -6 to 6
- doc_ids: int32 [32, 128], P(('dp', 'shard')), may hold values from 0 to 3, never falling along the last dimension, each value on 1 to 64 neighbouring positions
- expert_ids: int32 [4096], P(('dp', 'shard')), may hold values from 0 to 1, as said below
- slot_ids: int32 [4096], P(('dp', 'shard')), may hold values from 0 to 73, as said below
- out_grad: bfloat16 [4096, 1024], P(('dp', 'shard')), may hold values from -6 to 6
- ln1_gain: bfloat16 [1024], P(('dp', 'shard')), may hold values from 0.5 to 1.5
- ln1_bias: bfloat16 [1024], P(('dp', 'shard')), may hold values from -1 to 1
- w_query: bfloat16 [1024, 1024], P(('dp', 'shard')), may hold values from -0.1875 to 0.1875
- w_key: bfloat16 [1024, 1024], P(('dp', 'shard')), may hold values from -0.1875 to 0.1875
- w_value: bfloat16 [1024, 1024], P(('dp', 'shard')), may hold values from -0.1875 to 0.1875
- w_out: bfloat16 [1024, 1024], P(('dp', 'shard')), may hold values from -0.5 to 0.5
- ln2_gain: bfloat16 [1024], P(('dp', 'shard')), may hold values from 0.5 to 1.5
- ln2_bias: bfloat16 [1024], P(('dp', 'shard')), may hold values from -1 to 1
- w_up: bfloat16 [1024, 4096], P(('dp', 'shard')), may hold values from -0.1875 to 0.1875
- w_down: bfloat16 [4096, 1024], P(('dp', 'shard')), may hold values from -0.09375 to 0.09375
- w_router: bfloat16 [1024, 2], P(('dp', 'shard')), may hold values from -0.125 to 0.125
- w_mix: bfloat16 [1024, 2], P(('dp', 'shard')), may hold values from -0.1875 to 0.1875
- expert_up: bfloat16 [2, 1024, 4096], P(None, ('dp', 'shard')), may hold values from -0.1875 to 0.1875
- expert_down: bfloat16 [2, 4096, 1024], P(None, ('dp', 'shard')), may hold values from -0.09375 to 0.09375
- load_avg: float32 [2], replicated, may hold values from 0.05 to 0.3
Outputs:
- layer_out: bfloat16 [4096, 1024], P(('dp', 'shard'))
- input_grad: bfloat16 [4096, 1024], P(('dp', 'shard'))
- grad_ln1_gain: float32 [1024], P(('dp', 'shard'))
- grad_ln1_bias: float32 [1024], P(('dp', 'shard'))
- grad_w_query: float32 [1024, 1024], P(('dp', 'shard'))
- grad_w_key: float32 [1024, 1024], P(('dp', 'shard'))
- grad_w_value: float32 [1024, 1024], P(('dp', 'shard'))
- grad_w_out: float32 [1024, 1024], P(('dp', 'shard'))
- grad_ln2_gain: float32 [1024], P(('dp', 'shard'))
- grad_ln2_bias: float32 [1024], P(('dp', 'shard'))
- grad_w_up: float32 [1024, 4096], P(('dp', 'shard'))
- grad_w_down: float32 [4096, 1024], P(('dp', 'shard'))
- grad_w_router: float32 [1024, 2], P(('dp', 'shard'))
- grad_w_mix: float32 [1024, 2], P(('dp', 'shard'))
- grad_expert_up: float32 [2, 1024, 4096], P(None, ('dp', 'shard'))
- grad_expert_down: float32 [2, 4096, 1024], P(None, ('dp', 'shard'))
- expert_counts: int32 [2], replicated
- load_avg_new: float32 [2], replicated
The draws below stay inside these ranges and needn't reach their ends.
Inputs may be any that keep to these rules, and one draw needn't show every extreme that they name: `expert_ids`: of the 128 tokens of one sequence at most 74 go to one expert, and in some sequence exactly 74 do. `slot_ids`: A token's slot is the number of earlier tokens of the same sequence routed to the same expert.
All inputs are finite; a program needn't handle non-finite values.
Results may differ from the reference program's by a relative error of at most 0.012.
The reference program's roundings to bfloat16 on the way count: a program that leaves them out, or rounds other values in their place, can miss the bound.
Values may be sent and summed in bfloat16 or wider, within the bound.
A program may use at most 384 MiB of HBM per device.

```python
import math
import jax
import jax.numpy as jnp
import numpy as np
from jax import lax

D = 1024
HEADS = 16
HEAD_DIM = 64
FF = 4096
EXPERTS = 2
DOCS = 4
TOK_DEV = 128
CAP = 74
SEQS = 32
TOKENS = 4096


def route_pair(key):
    blocks = TOKENS // TOK_DEV
    base = jax.random.fold_in(key, 11)
    key_count, key_side, key_full, key_perm = jax.random.split(base, 4)
    loads = jax.random.randint(key_count, (blocks,), TOK_DEV - CAP, CAP + 1)
    full_block = jax.random.randint(key_full, (), 0, blocks)
    loads = jnp.where(jnp.arange(blocks) == full_block, CAP, loads)
    sides = jax.random.randint(key_side, (blocks,), 0, 2)
    orders = jax.vmap(lambda sub: jax.random.permutation(sub, TOK_DEV))(jax.random.split(key_perm, blocks))
    chosen = jnp.where(orders < loads[:, None], sides[:, None], 1 - sides[:, None]).astype(jnp.int32)
    onehot = (chosen[:, :, None] == jnp.arange(EXPERTS, dtype=jnp.int32)[None, None, :]).astype(jnp.int32)
    ranks = jnp.cumsum(onehot, axis=1) - onehot
    slots = jnp.sum(ranks * onehot, axis=2).astype(jnp.int32)
    return (chosen.reshape(-1), slots.reshape(-1))


def draw_expert_ids(key, part):
    return route_pair(key)[0]


def draw_slot_ids(key, part):
    return route_pair(key)[1]


def block_levels(key, shape, shards, least, largest):
    level = 1.0
    for axis_at, parts in shards:
        heights = jax.random.uniform(jax.random.fold_in(jax.random.fold_in(key, 6), axis_at), (parts,), jnp.float32, least / len(shards), largest / len(shards))
        level = level * jnp.repeat(jnp.exp(heights), shape[axis_at] // parts).reshape((-1,) + (1,) * (len(shape) - 1 - axis_at))
    return level


def split_up(amount, total, most, skew):
    weights = [(1 << 20) // math.isqrt(rank ** skew) + 1 for rank in range(2, amount + 1)]
    spare, given = total - most - (amount - 1), [1] * (amount - 1)
    while spare > 0:
        free = [i for i in range(amount - 1) if given[i] < most]
        mass, budget = sum([weights[i] for i in free]), spare
        for i in free:
            extra = min(most - given[i], max(1, budget * weights[i] // mass), spare)
            given[i] = given[i] + extra
            spare = spare - extra
    return np.array([most] + given)


def ragged_sizes(key, amount, total, bound, lean):
    if amount == 2:
        one = jax.random.randint(key, (), max(1, total - bound), min(bound, total - 1) + 1)
        return jnp.stack([one, total - one])
    lengths = jnp.asarray(split_up(amount, total, bound, lean), jnp.int32)
    pairs = (amount - 1) // 2
    giver, sink = lengths[1:1 + 2 * pairs:2], lengths[2:2 + 2 * pairs:2]
    room = jnp.minimum(giver - 1, bound - sink)
    moved = jax.random.randint(jax.random.fold_in(key, 1), (pairs,), 0, 1 << 20) % (room + 1)
    lengths = lengths.at[1:1 + 2 * pairs:2].set(giver - moved).at[2:2 + 2 * pairs:2].set(sink + moved)
    return lengths[jax.random.permutation(jax.random.fold_in(key, 2), amount)]


def normal_values(own_key, shape, deviation, most, cuts=(), held_as=jnp.bfloat16):
    level = block_levels(own_key, shape, cuts, -0.22, 0.18) if cuts else 1.0
    array = jax.random.normal(own_key, shape, jnp.float32) * deviation * level
    return jnp.minimum(jnp.maximum(array, -most), most).astype(held_as)


def setup_inputs(seed: int = 0) -> dict:
    arg_keys = jax.random.split(jax.random.key(seed), 21)
    hidden_in = normal_values(arg_keys[0], (TOKENS, D), 1.0, 6.0, ((0, 32),))
    doc_ids = jax.vmap(lambda own: jnp.searchsorted(jnp.cumsum(ragged_sizes(own, DOCS, TOK_DEV, TOK_DEV // 2, 1)), jnp.arange(TOK_DEV), side="right"))(jax.random.split(arg_keys[1], SEQS)).reshape((SEQS, TOK_DEV)).astype(jnp.int32)
    expert_ids = draw_expert_ids(jax.random.fold_in(arg_keys[20], 71), 0)
    slot_ids = draw_slot_ids(jax.random.fold_in(arg_keys[20], 71), 0)
    out_grad = normal_values(arg_keys[4], (TOKENS, D), 1.0, 6.0, ((0, 32),))
    ln1_gain = jnp.clip(1.0 + 0.1 * jax.random.normal(arg_keys[5], (D,), jnp.float32), 0.5, 1.5).astype(jnp.bfloat16)
    ln1_bias = normal_values(arg_keys[6], (D,), 0.2, 1.0, ((0, 32),))
    w_query = normal_values(arg_keys[7], (D, D), D ** -0.5, 0.1875, ((0, 32),))
    w_key = normal_values(arg_keys[8], (D, D), D ** -0.5, 0.1875, ((0, 32),))
    w_value = normal_values(arg_keys[9], (D, D), D ** -0.5, 0.1875, ((0, 32),))
    w_out = normal_values(arg_keys[10], (D, D), (D // 8) ** -0.5, 0.5, ((0, 32),))
    ln2_gain = jnp.clip(1.0 + 0.1 * jax.random.normal(arg_keys[11], (D,), jnp.float32), 0.5, 1.5).astype(jnp.bfloat16)
    ln2_bias = normal_values(arg_keys[12], (D,), 0.2, 1.0, ((0, 32),))
    w_up = normal_values(arg_keys[13], (D, FF), D ** -0.5, 0.1875, ((0, 32),))
    w_down = normal_values(arg_keys[14], (FF, D), FF ** -0.5, 0.09375, ((0, 32),))
    w_router = normal_values(arg_keys[15], (D, EXPERTS), (2 * D) ** -0.5, 0.125, ((0, 32),))
    w_mix = normal_values(arg_keys[16], (D, 2), D ** -0.5, 0.1875, ((0, 32),))
    expert_up = normal_values(arg_keys[17], (EXPERTS, D, FF), D ** -0.5, 0.1875, ((1, 32),))
    expert_down = normal_values(arg_keys[18], (EXPERTS, FF, D), FF ** -0.5, 0.09375, ((1, 32),))
    load_avg = jnp.clip(jax.random.uniform(arg_keys[19], (EXPERTS,), jnp.float32, 0.05, 0.3), 0.05, 0.3)
    return {"hidden_in": hidden_in, "doc_ids": doc_ids, "expert_ids": expert_ids, "slot_ids": slot_ids, "out_grad": out_grad, "ln1_gain": ln1_gain, "ln1_bias": ln1_bias, "w_query": w_query, "w_key": w_key, "w_value": w_value, "w_out": w_out, "ln2_gain": ln2_gain, "ln2_bias": ln2_bias, "w_up": w_up, "w_down": w_down, "w_router": w_router, "w_mix": w_mix, "expert_up": expert_up, "expert_down": expert_down, "load_avg": load_avg}


@jax.custom_vjp
def low(v):
    return lax.optimization_barrier(v.astype(jnp.bfloat16)).astype(jnp.float32)

@jax.custom_vjp
def low_back(v):
    return v

def low_keep(v):
    return (low(v), None)

def low_pass(kept, grad):
    return (grad,)

def back_keep(v):
    return (v, None)

def back_low(kept, grad):
    return (low(grad),)
low.defvjp(low_keep, low_pass)
low_back.defvjp(back_keep, back_low)

def both_low(value):
    return low(low_back(value))

def matmul(left, right):
    return jnp.dot(left, right, precision=lax.Precision.HIGHEST)

def norm_layer(values, gain, bias):
    centre = values - lax.optimization_barrier(jnp.mean(values, axis=-1, keepdims=True))
    scale_inv = lax.rsqrt(lax.optimization_barrier(jnp.mean(centre * centre, axis=-1, keepdims=True)) + 1e-05)
    return centre * scale_inv * gain + bias

def gelu_fn(values):
    return jax.nn.gelu(values, approximate=True)

def block_layer(params, hidden_row, doc_row, expert_row, slot_row):
    gain_one, bias_one, w_query, w_key, w_value, w_out, gain_two, bias_two, w_up, w_down, w_router, w_mix, expert_up, expert_down = params
    row_count = hidden_row.shape[0]
    highest = lax.Precision.HIGHEST
    normed_one = norm_layer(hidden_row, gain_one, bias_one)
    low_one = low(normed_one)
    query = both_low(matmul(low_one, w_query) * 0.125).reshape(row_count, HEADS, HEAD_DIM)
    keys = both_low(matmul(low_one, w_key)).reshape(row_count, HEADS, HEAD_DIM)
    values = both_low(matmul(low_one, w_value)).reshape(row_count, HEADS, HEAD_DIM)
    places = jnp.arange(row_count, dtype=jnp.int32)
    allowed = (places[None, :] <= places[:, None]) & (doc_row[:, None] == doc_row[None, :])
    scores = jnp.einsum('ihd,jhd->hij', query, keys, precision=highest)
    scores = low_back(jnp.where(allowed[None], scores, -1e+30))
    probs = low(jax.nn.softmax(scores, axis=-1))
    mixed = jnp.einsum('hij,jhd->ihd', probs, values, precision=highest).reshape(row_count, D)
    mixed = both_low(mixed)
    branch = low_back(matmul(mixed, w_out))
    resid = hidden_row + branch
    normed_two = norm_layer(resid, gain_two, bias_two)
    low_two = low(normed_two)
    up_pre = low_back(matmul(low_two, w_up))
    up_act = low(gelu_fn(up_pre))
    dense_out = low_back(matmul(up_act, w_down))
    router_probs = jax.nn.softmax(matmul(normed_two, w_router), axis=-1)
    onehot = (expert_row[:, None] == jnp.arange(EXPERTS, dtype=jnp.int32)[None, :]).astype(jnp.float32)
    gate_prob = lax.optimization_barrier(jnp.sum(router_probs * onehot, axis=-1))
    mix_coef = jax.nn.softmax(matmul(normed_two, w_mix), axis=-1)
    flat_slot = (expert_row * CAP + slot_row).astype(jnp.int32)
    token_of = jnp.zeros((EXPERTS * CAP,), jnp.int32).at[flat_slot].set(places)
    filled = jnp.zeros((EXPERTS * CAP,), jnp.float32).at[flat_slot].set(1.0)
    packed = (low_two[token_of] * filled[:, None]).reshape(EXPERTS, CAP, D)
    expert_pre = low_back(jnp.einsum('ecd,edf->ecf', packed, expert_up, precision=highest))
    expert_act = low(gelu_fn(expert_pre))
    expert_res = low_back(jnp.einsum('ecf,efd->ecd', expert_act, expert_down, precision=highest))
    routed = expert_res.reshape(EXPERTS * CAP, D)[flat_slot] * gate_prob[:, None]
    return resid + mix_coef[:, 0:1] * routed + mix_coef[:, 1:2] * dense_out

def reference(hidden_in, doc_ids, expert_ids, slot_ids, out_grad, ln1_gain, ln1_bias, w_query, w_key, w_value, w_out, ln2_gain, ln2_bias, w_up, w_down, w_router, w_mix, expert_up, expert_down, load_avg):
    params = tuple((item.astype(jnp.float32) for item in (ln1_gain, ln1_bias, w_query, w_key, w_value, w_out, ln2_gain, ln2_bias, w_up, w_down, w_router, w_mix, expert_up, expert_down)))
    seq_count = hidden_in.shape[0] // TOK_DEV
    inputs = hidden_in.astype(jnp.float32).reshape(seq_count, TOK_DEV, D)
    expert_rows = expert_ids.reshape(seq_count, TOK_DEV)
    slot_rows = slot_ids.reshape(seq_count, TOK_DEV)

    def forward(inputs_all, params_all):

        def one_seq(item):
            return block_layer(params_all, item[0], item[1], item[2], item[3])
        return lax.map(jax.checkpoint(one_seq), (inputs_all, doc_ids, expert_rows, slot_rows))
    outputs, pullback = jax.vjp(forward, inputs, params)
    grad_inputs, grad_params = pullback(out_grad.astype(jnp.float32).reshape(seq_count, TOK_DEV, D))
    layer_out = outputs.reshape(seq_count * TOK_DEV, D).astype(jnp.bfloat16)
    input_grad = grad_inputs.reshape(seq_count * TOK_DEV, D).astype(jnp.bfloat16)
    counts = lax.optimization_barrier(jnp.sum((expert_ids[:, None] == jnp.arange(EXPERTS, dtype=jnp.int32)[None, :]).astype(jnp.int32), axis=0)).astype(jnp.int32)
    load_new = 0.9 * load_avg + 0.1 * counts.astype(jnp.float32) * EXPERTS / TOKENS
    return (layer_out, input_grad, grad_params[0], grad_params[1], grad_params[2], grad_params[3], grad_params[4], grad_params[5], grad_params[6], grad_params[7], grad_params[8], grad_params[9], grad_params[10], grad_params[11], grad_params[12], grad_params[13], counts, load_new)
```

```python
import jax
import jax.numpy as jnp
from jax import lax
from jax.sharding import PartitionSpec as P

HEADS = 16
CAP = 74
BF = jnp.bfloat16
F32 = jnp.float32
BOTH = ("dp", "shard")


def mm(a, b, dims=((1,), (0,))):
    return lax.dot_general(a, b, (dims, ((), ())), preferred_element_type=F32)


def layer_norm(values, gain, bias):
    centre = values - jnp.mean(values, axis=-1, keepdims=True)
    scale_inv = lax.rsqrt(jnp.mean(centre * centre, axis=-1, keepdims=True) + 1e-05)
    normed = centre * scale_inv
    return (normed * gain + bias, normed, scale_inv)


def norm_back(grad_out, normed, scale_inv, gain):
    grad_normed = grad_out * gain
    inner = grad_normed - jnp.mean(grad_normed, axis=-1, keepdims=True)
    inner = inner - normed * jnp.mean(grad_normed * normed, axis=-1, keepdims=True)
    return (scale_inv * inner, jnp.sum(grad_out * normed, axis=0), jnp.sum(grad_out, axis=0))


def gelu_pair(t):
    inner = 0.7978845608 * (t + 0.044715 * t * t * t)
    th = jnp.tanh(inner)
    val = 0.5 * t * (1.0 + th)
    der = 0.5 * (1.0 + th) + 0.5 * t * (1.0 - th * th) * 0.7978845608 * (1.0 + 3.0 * 0.044715 * t * t)
    return val, der


def ag(block):
    return lax.all_gather(block, "shard", axis=0, tiled=False)


def rs(parts):
    return lax.psum_scatter(parts.astype(BF), "shard", scatter_dimension=0, tiled=False).astype(F32)


def body(
    hidden_in, doc_ids, expert_ids, slot_ids, out_grad, ln1_gain, ln1_bias, w_query, w_key, w_value,
    w_out, ln2_gain, ln2_bias, w_up, w_down, w_router, w_mix, expert_up, expert_down, load_avg,
):
    T, D = hidden_in.shape
    H, HD = HEADS, D // HEADS
    S = lax.axis_size("shard")
    C = lax.axis_size("dp")
    WR = w_query.shape[0]
    FF = w_up.shape[1]
    FR = w_down.shape[0]
    F = FR * C
    E = expert_up.shape[0]
    LO, HI = 80, T - 80

    pos = jnp.where(expert_ids == 0, slot_ids, jnp.sum((expert_ids == 0).astype(jnp.int32)) + slot_ids)
    n0 = jnp.sum((expert_ids == 0).astype(jnp.int32))
    place = lax.iota(jnp.int32, T)
    perm = (pos[None, :] == place[:, None]).astype(BF)
    xs = mm(perm, hidden_in)
    dys = mm(perm, out_grad).astype(BF)
    doc = doc_ids[0]
    allowed = (place[None, :] <= place[:, None]) & (doc[:, None] == doc[None, :])
    allowed = mm(mm(perm, allowed.astype(BF)).astype(BF), perm, ((1,), (1,))) > 0.5
    is0 = (place < n0)[:, None]

    small = jnp.stack(
        [ln1_gain, ln1_bias, ln2_gain, ln2_bias, w_router[:, 0], w_router[:, 1], w_mix[:, 0], w_mix[:, 1]]
    ).astype(F32)
    small = lax.all_gather(small, BOTH, axis=1, tiled=True)
    g1, b1, g2, b2 = small[0], small[1], small[2], small[3]
    wr, wm = small[4:6], small[6:8]

    wa = jnp.stack([w_query, w_key, w_value, w_out])
    wa = lax.all_gather(wa, BOTH, axis=1, tiled=True)
    wq, wk, wv, wo = wa[0], wa[1], wa[2], wa[3]

    ups = jnp.stack([w_up, expert_up[0], expert_up[1]])
    ups = ups.reshape(3, WR, C, S, FR).transpose(3, 0, 1, 2, 4).reshape(S, 3, WR, F)
    ups = lax.all_to_all(ups, "shard", 0, 0)
    ups = lax.all_gather(ups, "dp", axis=0)
    ups = ups.transpose(2, 0, 1, 3, 4).reshape(3, D, F)
    downs = jnp.stack([w_down, expert_down[0], expert_down[1]])
    downs = lax.all_gather(downs, "dp", axis=1, tiled=True)

    dy_all = ag(dys)

    n1, u1, i1 = layer_norm(xs, g1, b1)
    h1b = n1.astype(BF)
    q = (mm(h1b, wq) * 0.125).astype(BF).reshape(T, H, HD)
    k = mm(h1b, wk).astype(BF).reshape(T, H, HD)
    v = mm(h1b, wv).astype(BF).reshape(T, H, HD)
    s = jnp.einsum("ihd,jhd->hij", q, k, preferred_element_type=F32)
    s = jnp.where(allowed[None], s, -1e30)
    ex = jnp.exp(s - jnp.max(s, axis=-1, keepdims=True))
    p = ex / jnp.sum(ex, axis=-1, keepdims=True)
    pb = p.astype(BF)
    o = jnp.einsum("hij,jhd->ihd", pb, v, preferred_element_type=F32).reshape(T, D).astype(BF)
    x1 = xs + mm(o, wo)
    h2, u2, i2 = layer_norm(x1, g2, b2)
    h2b = h2.astype(BF)

    def two(w):
        return jnp.stack([jnp.sum(h2 * w[0], axis=-1), jnp.sum(h2 * w[1], axis=-1)], axis=-1)

    r = jax.nn.softmax(two(wr), axis=-1)
    c = jax.nn.softmax(two(wm), axis=-1)
    gate = jnp.where(is0, r[:, 0:1], r[:, 1:2])
    c0, c1 = c[:, 0:1], c[:, 1:2]
    we = c0 * gate
    scal = jnp.concatenate([c1, jnp.where(is0, we, 0.0), jnp.where(is0, 0.0, we)], axis=1)

    h_all = ag(h2b)
    scal_all = ag(scal)

    def cut(a, e):
        return (a[:, :LO] if e == 1 else a[:, HI:]) if e else a

    partial_y = jnp.zeros((S, T, D), F32)
    partial_dh = jnp.zeros((S, T, D), F32)
    score = []
    gup, gdown = [], []
    for e in range(3):
        he = cut(h_all, e)
        dye = cut(dy_all, e).astype(F32)
        se = cut(scal_all, e)[:, :, e : e + 1]
        n = he.shape[1]
        hf = he.reshape(S * n, D)
        pre = mm(hf, ups[e])
        val, der = gelu_pair(pre)
        ub = val.astype(BF)
        m = mm(ub, downs[e]).reshape(S, n, D)
        dm = (dye * se).astype(BF).reshape(S * n, D)
        dg = (mm(dm, downs[e], ((1,), (1,))) * der).astype(BF)
        gdown.append(mm(ub, dm, ((0,), (0,))))
        gup.append(mm(hf, dg, ((0,), (0,))))
        dx = mm(dg, ups[e], ((1,), (1,))).reshape(S, n, D)
        y = m * se
        sc = jnp.sum(dye * m, axis=-1)
        pad = [(0, 0), (0, T - n) if e < 2 else (T - n, 0)]
        live = is0[None, :, 0]
        partial_y += jnp.pad(y, pad + [(0, 0)])
        partial_dh += jnp.pad(dx, pad + [(0, 0)])
        score.append(jnp.pad(sc, pad))
    yfull = rs(partial_y)
    dh2 = rs(partial_dh)
    sc = lax.psum_scatter(jnp.stack(score, axis=1), "shard", scatter_dimension=0, tiled=False)
    sm = sc[0][:, None]
    se = jnp.where(is0, sc[1][:, None], sc[2][:, None])

    dc0, dc1 = gate * se, sm
    tot = c0 * dc0 + c1 * dc1
    dcl0, dcl1 = c0 * (dc0 - tot), c1 * (dc1 - tot)
    dgate = c0 * se
    dr0, dr1 = jnp.where(is0, dgate, 0.0), jnp.where(is0, 0.0, dgate)
    tot = r[:, 0:1] * dr0 + r[:, 1:2] * dr1
    drl0, drl1 = r[:, 0:1] * (dr0 - tot), r[:, 1:2] * (dr1 - tot)
    layer_out = (x1 + yfull).astype(BF)
    dh2 = dh2 + drl0 * wr[0] + drl1 * wr[1] + dcl0 * wm[0] + dcl1 * wm[1]
    gw = [jnp.sum(h2 * t, axis=0) for t in (drl0, drl1, dcl0, dcl1)]
    dx1, gg2, gb2 = norm_back(dh2, u2, i2, g2)
    dx1 = dx1 + dys.astype(F32)
    dab = dx1.astype(BF)
    gwo = mm(o, dab, ((0,), (0,)))
    do = mm(dab, wo, ((1,), (1,))).astype(BF).reshape(T, H, HD)
    dp = jnp.einsum("ihd,jhd->hij", do, v, preferred_element_type=F32)
    ds = (p * (dp - jnp.sum(p * dp, axis=-1, keepdims=True))).astype(BF)
    dq = jnp.einsum("hij,jhd->ihd", ds, k, preferred_element_type=F32).astype(BF)
    dq = (dq * BF(0.125)).reshape(T, D)
    dk = jnp.einsum("hij,ihd->jhd", ds, q, preferred_element_type=F32).astype(BF).reshape(T, D)
    dv = jnp.einsum("hij,ihd->jhd", pb, do, preferred_element_type=F32).astype(BF).reshape(T, D)
    dh1 = mm(dq, wq, ((1,), (1,))) + mm(dk, wk, ((1,), (1,))) + mm(dv, wv, ((1,), (1,)))
    ga = jnp.stack([mm(h1b, dq, ((0,), (0,))), mm(h1b, dk, ((0,), (0,))), mm(h1b, dv, ((0,), (0,))), gwo])
    dxn, gg1, gb1 = norm_back(dh1, u1, i1, g1)
    input_grad = (dx1 + dxn).astype(BF)

    layer_out = mm(perm, layer_out, ((0,), (0,))).astype(BF)
    input_grad = mm(perm, input_grad, ((0,), (0,))).astype(BF)

    smalls = lax.psum(jnp.stack([gg1, gb1, gg2, gb2] + gw), BOTH)
    mine = lax.dynamic_slice_in_dim(smalls, lax.axis_index(BOTH) * WR, WR, 1)
    ga = ga.reshape(4, C, S, WR, D).transpose(1, 2, 0, 3, 4)
    ga = lax.psum_scatter(ga.astype(BF), "dp", scatter_dimension=0, tiled=False)
    ga = lax.psum_scatter(ga, "shard", scatter_dimension=0, tiled=False).astype(F32)
    gdown = lax.psum_scatter(jnp.stack(gdown), "dp", scatter_dimension=1, tiled=True)
    gup = jnp.stack(gup).reshape(3, C, S, WR, F).transpose(1, 2, 0, 3, 4)
    gup = lax.psum_scatter(gup, "dp", scatter_dimension=0, tiled=False).astype(BF)
    gup = lax.all_to_all(gup, "shard", 0, 0).astype(F32)
    gup = gup.reshape(S, 3, WR, C, FR).transpose(1, 2, 3, 0, 4).reshape(3, WR, FF)

    counts = lax.psum(jnp.stack([n0, T - n0]), BOTH)
    load_new = 0.9 * load_avg + 0.1 * counts.astype(F32) * E / (T * C * S)
    return (
        layer_out, input_grad, mine[0], mine[1], ga[0], ga[1], ga[2], ga[3], mine[2], mine[3],
        gup[0], gdown[0], jnp.stack([mine[4], mine[5]], axis=1), jnp.stack([mine[6], mine[7]], axis=1),
        gup[1:], gdown[1:], counts, load_new,
    )


def solution(mesh):
    row, vec = P(BOTH, None), P(BOTH)
    mid = P(None, BOTH, None)
    return jax.shard_map(
        body,
        mesh=mesh,
        in_specs=(row, row, vec, vec, row, vec, vec, row, row, row, row, vec, vec, row, row, row, row, mid, mid, P()),
        out_specs=(row, row, vec, vec, row, row, row, row, vec, vec, row, row, row, row, mid, mid, P(), P()),
        check_vma=False,
    )
```

```python
import jax
import jax.numpy as jnp
from jax import lax
from jax.experimental import pallas as pl
from jax.experimental.pallas import tpu as pltpu
from jax.sharding import PartitionSpec as P

HEADS = 16
CAP = 74
BF = jnp.bfloat16
F32 = jnp.float32
BOTH = ("dp", "shard")
MESH = pl.DeviceIdType.MESH


def mm(a, b, dims=((1,), (0,))):
    return lax.dot_general(a, b, (dims, ((), ())), preferred_element_type=F32)


def layer_norm(values, gain, bias):
    centre = values - jnp.mean(values, axis=-1, keepdims=True)
    scale_inv = lax.rsqrt(jnp.mean(centre * centre, axis=-1, keepdims=True) + 1e-05)
    normed = centre * scale_inv
    return (normed * gain + bias, normed, scale_inv)


def norm_back(grad_out, normed, scale_inv, gain):
    grad_normed = grad_out * gain
    inner = grad_normed - jnp.mean(grad_normed, axis=-1, keepdims=True)
    inner = inner - normed * jnp.mean(grad_normed * normed, axis=-1, keepdims=True)
    return (scale_inv * inner, jnp.sum(grad_out * normed, axis=0), jnp.sum(grad_out, axis=0))


def gelu_pair(t):
    inner = 0.7978845608 * (t + 0.044715 * t * t * t)
    th = jnp.tanh(inner)
    val = 0.5 * t * (1.0 + th)
    der = 0.5 * (1.0 + th) + 0.5 * t * (1.0 - th * th) * 0.7978845608 * (1.0 + 3.0 * 0.044715 * t * t)
    return val, der


def ag(block):
    return lax.all_gather(block, "shard", axis=0, tiled=False)


def rs(parts):
    return lax.psum_scatter(parts.astype(BF), "shard", scatter_dimension=0, tiled=False).astype(F32)


def place_of():
    me = lax.axis_index("shard")
    core = lax.axis_index("dp")
    z, p = me // 4, me % 4
    xq = p + 1 - 2 * (p % 2)
    yq = p + 2 - 4 * (p // 2)
    return me, core, z, p, xq, yq, 3 - p


def greet(shards, core):
    bar = pltpu.get_barrier_semaphore()
    me = lax.axis_index("shard")

    @pl.loop(1, shards)
    def _(i):
        pl.semaphore_signal(bar, inc=1, device_id=(core, (me + i) % shards), device_id_type=MESH)

    pl.semaphore_signal(bar, inc=1, device_id=(1 - core, me), device_id_type=MESH)
    pl.semaphore_wait(bar, shards)


def remote(src, dst, send, recv, dev):
    return pltpu.make_async_remote_copy(
        src_ref=src, dst_ref=dst, send_sem=send, recv_sem=recv, device_id=dev, device_id_type=MESH
    )


def rows_loop(count, step, fn):
    @pl.loop(0, count // step)
    def _(i):
        fn(pl.multiple_of(i * step, step))


def ffn_kernel(
    h_ref, scal_ref, dy_ref, up_ref, dn_ref,
    y_out, dh_out, sc_out, gup_out, gdn0_out, gdn12_out,
    hall, scall, psc, screcv, wcol, scol, part, ra, rbx, rby, rd, final,
    pre, der, ub, dg, dm, m, yacc, dxacc, gdn, gup, sib_dn, sib_up, gsend, grecv,
    ag_s, ag_r, rs_s, rs_r, one_s, one_r, sm_s, sm_r,
):
    S, T, D = hall.shape
    F = up_ref.shape[2]
    L = S // 4
    LO = 80
    HI = T - LO
    me, core, z, p, xq, yq, dq = place_of()
    xn, yn = z * 4 + xq, z * 4 + yq
    sgn = 1 - 2 * (z // (L // 2))
    greet(S, core)

    def lev_of(k):
        return (z + k * sgn + L) % L

    def h_copy(kind, slot, src, idx, dev):
        return remote(src, hall.at[idx], ag_s.at[kind, slot], ag_r.at[kind, slot], (core, dev))

    @pl.loop(1, L)
    def _(k):
        lev = lev_of(k)
        remote(h_ref, hall.at[me], ag_s.at[0, lev], ag_r.at[0, z], (core, lev * 4 + p)).start()

    h_copy(1, z, h_ref, me, xn).start()
    h_copy(2, z, h_ref, me, yn).start()

    @pl.loop(1, S)
    def _(i):
        remote(scal_ref, scall.at[me], sm_s.at[0, i], sm_r.at[0], (core, (me + i) % S)).start()

    hall[me] = h_ref[...]
    scall[me] = scal_ref[...]
    gdn[...] = jnp.zeros_like(gdn)
    gup[...] = jnp.zeros_like(gup)
    remote(scall.at[pl.ds(0, S - 1)], scall.at[pl.ds(0, S - 1)], sm_s.at[0, 0], sm_r.at[0], (core, xn)).wait_recv()

    def stage_a(k):
        lev = lev_of(k)
        idx = lev * 4 + p
        h_copy(0, lev, hall.at[idx], idx, xn).wait_recv()
        h_copy(1, lev, hall.at[idx], idx, xn).start()
        h_copy(2, lev, hall.at[idx], idx, yn).start()

    def stage_b(k):
        lev = lev_of(k)
        odd = k % 2
        h_copy(1, lev, h_ref, lev * 4 + xq, xn).wait_recv()
        h_copy(2, lev, h_ref, lev * 4 + yq, yn).wait_recv()
        idx = lev * 4 + xq + odd * (yq - xq)
        h_copy(3, lev, hall.at[idx], idx, yn + odd * (xn - yn)).start()
        h_copy(3, lev, h_ref, lev * 4 + dq, xn).wait_recv()

    lane = lax.broadcasted_iota(jnp.int32, (16, 128), 1)

    def compute(lev):
        base = lev * 4
        for q in range(4):
            full = jnp.concatenate([scall[base + q], jnp.zeros((120, 128), F32)], axis=0)
            wcol[q] = full.T
        for e in range(3):
            n = LO if e else T
            off = HI if e == 2 else 0
            rows = 4 * n
            hm = hall[pl.ds(base, 4), off : off + n, :].reshape(rows, D)
            pre[0:rows, :] = mm(hm, up_ref[e])

            def act(r):
                val, d = gelu_pair(pre[pl.ds(r, 32), :])
                ub[pl.ds(r, 32), :] = val.astype(BF)
                der[pl.ds(r, 32), :] = d

            rows_loop(rows, 32, act)
            m[0:rows, :] = mm(ub[0:rows, :], dn_ref[e])
            for q in range(4):

                def elem(r):
                    at = pl.multiple_of(r + off, 16)
                    mine = pl.ds(pl.multiple_of(q * n + r, 16), 16)
                    t = pl.ds(pl.multiple_of(q * T + off + r, 16), 16)
                    w = wcol[q, pl.ds(at, 16), :][:, e : e + 1]
                    dyv = dy_ref[base + q, pl.ds(at, 16), :].astype(F32)
                    mv = m[mine, :]
                    s = jnp.sum(dyv * mv, axis=1, keepdims=True)
                    s = jnp.where(lane == e, s, 0.0)
                    dm[mine, :] = (dyv * w).astype(BF)
                    if e:
                        yacc[t, :] = yacc[t, :] + mv * w
                        scol[q, pl.ds(at, 16), :] = scol[q, pl.ds(at, 16), :] + s
                    else:
                        yacc[t, :] = mv * w
                        scol[q, pl.ds(at, 16), :] = s

                rows_loop(n, 16, elem)
            pre[0:rows, :] = mm(dm[0:rows, :], dn_ref[e], ((1,), (1,)))

            def back(r):
                dg[pl.ds(r, 32), :] = (pre[pl.ds(r, 32), :] * der[pl.ds(r, 32), :]).astype(BF)

            rows_loop(rows, 32, back)
            gdn[e] = gdn[e] + mm(ub[0:rows, :], dm[0:rows, :], ((0,), (0,)))
            gup[e] = gup[e] + mm(dg[0:rows, :], hm, ((0,), (0,)))
            if e:
                m[0:rows, :] = mm(dg[0:rows, :], up_ref[e], ((1,), (1,)))
                for q in range(4):

                    def addx(r):
                        t = pl.ds(pl.multiple_of(q * T + off + r, 16), 16)
                        dxacc[t, :] = dxacc[t, :] + m[pl.ds(pl.multiple_of(q * n + r, 16), 16), :]

                    rows_loop(n, 16, addx)
            else:
                dxacc[...] = mm(dg[...], up_ref[0], ((1,), (1,)))
        for q in range(4):
            psc[base + q] = scol[q].T[0:8, :]

            def out(r):
                t = pl.ds(pl.multiple_of(q * T + r, 16), 16)
                part[0, base + q, pl.ds(r, 16), :] = dxacc[t, :].astype(BF)
                part[1, base + q, pl.ds(r, 16), :] = yacc[t, :].astype(BF)

            rows_loop(T, 16, out)

    def r_copy(kind, a, lev, src, dst, dev):
        return remote(src, dst, rs_s.at[kind, a, lev], rs_r.at[kind, a, lev], (core, dev))

    def rs_a(k):
        lev = lev_of(k)
        odd = k % 2
        for a in range(2):
            r_copy(0, a, lev, part.at[a, lev * 4 + dq], ra.at[a, lev], yn + odd * (xn - yn)).start()

    def rs_b(k):
        lev = lev_of(k)
        odd = k % 2
        via = lev * 4 + xq + odd * (yq - xq)
        for a in range(2):
            r_copy(0, a, lev, ra.at[a, lev], ra.at[a, lev], xn).wait_recv()

            def add(r):
                t = pl.ds(r, 16)
                part[a, via, t, :] = (part[a, via, t, :].astype(F32) + ra[a, lev, t, :].astype(F32)).astype(BF)

            rows_loop(T, 16, add)
            r_copy(1, a, lev, part.at[a, lev * 4 + xq], rbx.at[a, lev], xn).start()
            r_copy(2, a, lev, part.at[a, lev * 4 + yq], rby.at[a, lev], yn).start()

    def rs_c(k):
        lev = lev_of(k)
        own = lev * 4 + p
        for a in range(2):
            r_copy(1, a, lev, rbx.at[a, lev], rbx.at[a, lev], xn).wait_recv()
            r_copy(2, a, lev, rby.at[a, lev], rby.at[a, lev], yn).wait_recv()

            def add(r):
                t = pl.ds(r, 16)
                tot = part[a, own, t, :].astype(F32) + rbx[a, lev, t, :].astype(F32) + rby[a, lev, t, :].astype(F32)

                @pl.when(k == 0)
                def _():
                    final[a, t, :] = tot

                @pl.when(k > 0)
                def _():
                    part[a, own, t, :] = tot.astype(BF)

            rows_loop(T, 16, add)

            @pl.when(k > 0)
            def _():
                remote(
                    part.at[a, own], rd.at[a, z], rs_s.at[3, a, lev], rs_r.at[3, a, z], (core, lev * 4 + p)
                ).start()

    stage_a(1)

    @pl.loop(0, L)
    def _(k):
        stage_b(k)

        @pl.when(k < L - 2)
        def _():
            stage_a(k + 2)

        compute(lev_of(k))
        rs_a(k)

        @pl.when(k > 0)
        def _():
            rs_c(k - 1)

        rs_b(k)

    half = D // 2
    other = pl.multiple_of((1 - core) * half, half)
    mine_d = pl.multiple_of(core * half, half)
    FR = F // 2
    other_f = pl.multiple_of((1 - core) * FR, FR)
    mine_f = pl.multiple_of(core * FR, FR)
    sib = (1 - core, me)
    c_up = remote(gup.at[:, :, pl.ds(other, half)], sib_up, one_s.at[0], one_r.at[0], sib)
    c_dn = remote(gdn.at[:, pl.ds(other_f, FR), :], sib_dn, one_s.at[1], one_r.at[1], sib)
    c_up.start()
    c_dn.start()

    @pl.loop(1, S)
    def _(i):
        to = (me + i) % S
        remote(psc.at[to], screcv.at[i], sm_s.at[1, i], sm_r.at[1], (core, to)).start()

    rs_c(L - 1)
    c_up.wait_recv()
    for e in range(3):
        tot = gup[e, :, pl.ds(mine_d, half)] + sib_up[e]
        gsend[e] = tot.T.astype(BF)
    WR = half // S
    screcv[0] = psc[me]

    def g_copy(i, to):
        return remote(
            gsend.at[:, pl.ds(pl.multiple_of(to * WR, WR), WR), :], grecv.at[me], sm_s.at[2, i], sm_r.at[2], (core, to)
        )

    @pl.loop(1, S)
    def _(i):
        g_copy(i, (me + i) % S).start()

    grecv[me] = gsend[:, pl.ds(pl.multiple_of(me * WR, WR), WR), :]
    c_dn.wait_recv()
    gdn0_out[...] = gdn[0, pl.ds(mine_f, FR), :] + sib_dn[0]
    for e in range(1, 3):
        gdn12_out[e - 1] = gdn[e, pl.ds(mine_f, FR), :] + sib_dn[e]

    @pl.loop(1, L)
    def _(k):
        lev = lev_of(k)
        for a in range(2):
            r_copy(3, a, lev, rd.at[a, lev], rd.at[a, lev], xn).wait_recv()

            def add(r):
                t = pl.ds(r, 16)
                final[a, t, :] = final[a, t, :] + rd[a, lev, t, :].astype(F32)

            rows_loop(T, 16, add)

    dh_out[...] = final[0]
    y_out[...] = final[1]
    remote(screcv.at[pl.ds(1, S - 1)], screcv.at[pl.ds(1, S - 1)], sm_s.at[1, 0], sm_r.at[1], (core, xn)).wait_recv()
    sc_out[...] = jnp.sum(screcv[...], axis=0)
    remote(grecv.at[pl.ds(0, S - 1)], grecv.at[pl.ds(0, S - 1)], sm_s.at[2, 0], sm_r.at[2], (core, xn)).wait_recv()
    gup_out[...] = grecv[...]

    c_up.wait_send()
    c_dn.wait_send()

    @pl.loop(1, S)
    def _(i):
        remote(scal_ref, scall.at[0], sm_s.at[0, i], sm_r.at[0], (core, xn)).wait_send()
        remote(psc.at[0], screcv.at[0], sm_s.at[1, i], sm_r.at[1], (core, xn)).wait_send()
        g_copy(i, (me + i) % S).wait_send()

    @pl.loop(0, L)
    def _(k):
        lev = lev_of(k)
        for kind in range(1, 4):
            h_copy(kind, lev, hall.at[0], 0, xn).wait_send()
        for a in range(2):
            for kind in range(3):
                r_copy(kind, a, lev, ra.at[a, 0], ra.at[a, 0], xn).wait_send()

        @pl.when(k > 0)
        def _():
            h_copy(0, lev, hall.at[0], 0, xn).wait_send()
            for a in range(2):
                r_copy(3, a, lev, ra.at[a, 0], ra.at[a, 0], xn).wait_send()


def ffn_call(h2b, scal, dy_all, ups, downs):
    S, T, D = dy_all.shape
    F = ups.shape[2]
    L = S // 4
    WR = D // 2 // S
    vm = pl.BlockSpec(memory_space=pltpu.VMEM)
    V = pltpu.VMEM
    dma = pltpu.SemaphoreType.DMA
    sds = jax.ShapeDtypeStruct
    return pl.pallas_call(
        ffn_kernel,
        out_shape=(
            sds((T, D), F32), sds((T, D), F32), sds((8, 128), F32), sds((S, 3, WR, F), BF),
            sds((F // 2, D), F32), sds((2, F // 2, D), F32),
        ),
        in_specs=[vm] * 5,
        out_specs=(vm,) * 6,
        scratch_shapes=[
            V((S, T, D), BF), V((S, 8, 128), F32), V((S, 8, 128), F32), V((S, 8, 128), F32),
            V((4, T, 128), F32), V((4, T, 128), F32),
            V((2, S, T, D), BF), V((2, L, T, D), BF), V((2, L, T, D), BF), V((2, L, T, D), BF), V((2, L, T, D), BF),
            V((2, T, D), F32),
            V((4 * T, F), F32), V((4 * T, F), F32), V((4 * T, F), BF), V((4 * T, F), BF), V((4 * T, D), BF),
            V((4 * T, D), F32), V((4 * T, D), F32), V((4 * T, D), F32),
            V((3, F, D), F32), V((3, F, D), F32), V((3, F // 2, D), F32), V((3, F, D // 2), F32),
            V((3, D // 2, F), BF), V((S, 3, WR, F), BF),
            dma((4, L)), dma((4, L)), dma((4, 2, L)), dma((4, 2, L)), dma((2,)), dma((2,)), dma((3, S)), dma((3,)),
        ],
        compiler_params=pltpu.CompilerParams(collective_id=2, has_side_effects=True, vmem_limit_bytes=64000000),
        cost_estimate=pl.CostEstimate(flops=15 * 10**9, bytes_accessed=20 * 2**20, transcendentals=2**20),
        name="ffn",
    )(h2b, scal, dy_all, ups, downs)


def body(
    hidden_in, doc_ids, expert_ids, slot_ids, out_grad, ln1_gain, ln1_bias, w_query, w_key, w_value,
    w_out, ln2_gain, ln2_bias, w_up, w_down, w_router, w_mix, expert_up, expert_down, load_avg,
):
    T, D = hidden_in.shape
    H, HD = HEADS, D // HEADS
    S = lax.axis_size("shard")
    C = lax.axis_size("dp")
    WR = w_query.shape[0]
    FF = w_up.shape[1]
    FR = w_down.shape[0]
    F = FR * C
    E = expert_up.shape[0]
    LO, HI = 80, T - 80

    pos = jnp.where(expert_ids == 0, slot_ids, jnp.sum((expert_ids == 0).astype(jnp.int32)) + slot_ids)
    n0 = jnp.sum((expert_ids == 0).astype(jnp.int32))
    place = lax.iota(jnp.int32, T)
    perm = (pos[None, :] == place[:, None]).astype(BF)
    xs = mm(perm, hidden_in)
    dys = mm(perm, out_grad).astype(BF)
    doc = doc_ids[0]
    allowed = (place[None, :] <= place[:, None]) & (doc[:, None] == doc[None, :])
    allowed = mm(mm(perm, allowed.astype(BF)).astype(BF), perm, ((1,), (1,))) > 0.5
    is0 = (place < n0)[:, None]

    small = jnp.stack(
        [ln1_gain, ln1_bias, ln2_gain, ln2_bias, w_router[:, 0], w_router[:, 1], w_mix[:, 0], w_mix[:, 1]]
    ).astype(F32)
    small = lax.all_gather(small, BOTH, axis=1, tiled=True)
    g1, b1, g2, b2 = small[0], small[1], small[2], small[3]
    wr, wm = small[4:6], small[6:8]

    wa = jnp.stack([w_query, w_key, w_value, w_out])
    wa = lax.all_gather(wa, BOTH, axis=1, tiled=True)
    wq, wk, wv, wo = wa[0], wa[1], wa[2], wa[3]

    ups = jnp.stack([w_up, expert_up[0], expert_up[1]])
    ups = ups.reshape(3, WR, C, S, FR).transpose(3, 0, 1, 2, 4).reshape(S, 3, WR, F)
    ups = lax.all_to_all(ups, "shard", 0, 0)
    ups = lax.all_gather(ups, "dp", axis=0)
    ups = ups.transpose(2, 0, 1, 3, 4).reshape(3, D, F)
    downs = jnp.stack([w_down, expert_down[0], expert_down[1]])
    downs = lax.all_gather(downs, "dp", axis=1, tiled=True)

    dy_all = ag(dys)

    n1, u1, i1 = layer_norm(xs, g1, b1)
    h1b = n1.astype(BF)
    q = (mm(h1b, wq) * 0.125).astype(BF).reshape(T, H, HD)
    k = mm(h1b, wk).astype(BF).reshape(T, H, HD)
    v = mm(h1b, wv).astype(BF).reshape(T, H, HD)
    s = jnp.einsum("ihd,jhd->hij", q, k, preferred_element_type=F32)
    s = jnp.where(allowed[None], s, -1e30)
    ex = jnp.exp(s - jnp.max(s, axis=-1, keepdims=True))
    p = ex / jnp.sum(ex, axis=-1, keepdims=True)
    pb = p.astype(BF)
    o = jnp.einsum("hij,jhd->ihd", pb, v, preferred_element_type=F32).reshape(T, D).astype(BF)
    x1 = xs + mm(o, wo)
    h2, u2, i2 = layer_norm(x1, g2, b2)
    h2b = h2.astype(BF)

    def two(w):
        return jnp.stack([jnp.sum(h2 * w[0], axis=-1), jnp.sum(h2 * w[1], axis=-1)], axis=-1)

    r = jax.nn.softmax(two(wr), axis=-1)
    c = jax.nn.softmax(two(wm), axis=-1)
    gate = jnp.where(is0, r[:, 0:1], r[:, 1:2])
    c0, c1 = c[:, 0:1], c[:, 1:2]
    we = c0 * gate
    scal = jnp.concatenate([c1, jnp.where(is0, we, 0.0), jnp.where(is0, 0.0, we)], axis=1)

    fast = C == 2 and S % 4 == 0 and S >= 8 and FR % 128 == 0 and WR % 16 == 0
    if fast:
        scal8 = jnp.pad(scal.T, ((0, 5), (0, 0)))
        yfull, dh2, sc, gup, gdn0, gdn12 = ffn_call(h2b, scal8, dy_all, ups, downs)
    else:
        h_all = ag(h2b)
        scal_all = ag(scal)

        def cut(a, e):
            return (a[:, :LO] if e == 1 else a[:, HI:]) if e else a

        partial_y = jnp.zeros((S, T, D), F32)
        partial_dh = jnp.zeros((S, T, D), F32)
        score = []
        gup, gdown = [], []
        for e in range(3):
            he = cut(h_all, e)
            dye = cut(dy_all, e).astype(F32)
            se = cut(scal_all, e)[:, :, e : e + 1]
            n = he.shape[1]
            hf = he.reshape(S * n, D)
            pre = mm(hf, ups[e])
            val, der = gelu_pair(pre)
            ub = val.astype(BF)
            m = mm(ub, downs[e]).reshape(S, n, D)
            dm = (dye * se).astype(BF).reshape(S * n, D)
            dg = (mm(dm, downs[e], ((1,), (1,))) * der).astype(BF)
            gdown.append(mm(ub, dm, ((0,), (0,))))
            gup.append(mm(hf, dg, ((0,), (0,))))
            dx = mm(dg, ups[e], ((1,), (1,))).reshape(S, n, D)
            y = m * se
            sc = jnp.sum(dye * m, axis=-1)
            pad = [(0, 0), (0, T - n) if e < 2 else (T - n, 0)]
            live = is0[None, :, 0]
            partial_y += jnp.pad(y, pad + [(0, 0)])
            partial_dh += jnp.pad(dx, pad + [(0, 0)])
            score.append(jnp.pad(sc, pad))
        yfull = rs(partial_y)
        dh2 = rs(partial_dh)
        sc = lax.psum_scatter(jnp.stack(score, axis=1), "shard", scatter_dimension=0, tiled=False)

    sm = sc[0][:, None]
    se = jnp.where(is0, sc[1][:, None], sc[2][:, None])
    dc0, dc1 = gate * se, sm
    tot = c0 * dc0 + c1 * dc1
    dcl0, dcl1 = c0 * (dc0 - tot), c1 * (dc1 - tot)
    dgate = c0 * se
    dr0, dr1 = jnp.where(is0, dgate, 0.0), jnp.where(is0, 0.0, dgate)
    tot = r[:, 0:1] * dr0 + r[:, 1:2] * dr1
    drl0, drl1 = r[:, 0:1] * (dr0 - tot), r[:, 1:2] * (dr1 - tot)
    layer_out = (x1 + yfull).astype(BF)
    dh2 = dh2 + drl0 * wr[0] + drl1 * wr[1] + dcl0 * wm[0] + dcl1 * wm[1]
    gw = [jnp.sum(h2 * t, axis=0) for t in (drl0, drl1, dcl0, dcl1)]
    dx1, gg2, gb2 = norm_back(dh2, u2, i2, g2)
    dx1 = dx1 + dys.astype(F32)
    dab = dx1.astype(BF)
    gwo = mm(o, dab, ((0,), (0,)))
    do = mm(dab, wo, ((1,), (1,))).astype(BF).reshape(T, H, HD)
    dp = jnp.einsum("ihd,jhd->hij", do, v, preferred_element_type=F32)
    ds = (p * (dp - jnp.sum(p * dp, axis=-1, keepdims=True))).astype(BF)
    dq = jnp.einsum("hij,jhd->ihd", ds, k, preferred_element_type=F32).astype(BF)
    dq = (dq * BF(0.125)).reshape(T, D)
    dk = jnp.einsum("hij,ihd->jhd", ds, q, preferred_element_type=F32).astype(BF).reshape(T, D)
    dv = jnp.einsum("hij,ihd->jhd", pb, do, preferred_element_type=F32).astype(BF).reshape(T, D)
    dh1 = mm(dq, wq, ((1,), (1,))) + mm(dk, wk, ((1,), (1,))) + mm(dv, wv, ((1,), (1,)))
    ga = jnp.stack([mm(h1b, dq, ((0,), (0,))), mm(h1b, dk, ((0,), (0,))), mm(h1b, dv, ((0,), (0,))), gwo])
    dxn, gg1, gb1 = norm_back(dh1, u1, i1, g1)
    input_grad = (dx1 + dxn).astype(BF)

    layer_out = mm(perm, layer_out, ((0,), (0,))).astype(BF)
    input_grad = mm(perm, input_grad, ((0,), (0,))).astype(BF)

    smalls = lax.psum(jnp.stack([gg1, gb1, gg2, gb2] + gw), BOTH)
    mine = lax.dynamic_slice_in_dim(smalls, lax.axis_index(BOTH) * WR, WR, 1)
    ga = ga.reshape(4, C, S, WR, D).transpose(1, 2, 0, 3, 4)
    ga = lax.psum_scatter(ga.astype(BF), "dp", scatter_dimension=0, tiled=False)
    ga = lax.psum_scatter(ga, "shard", scatter_dimension=0, tiled=False).astype(F32)
    if not fast:
        gdown = lax.psum_scatter(jnp.stack(gdown), "dp", scatter_dimension=1, tiled=True)
        gdn0, gdn12 = gdown[0], gdown[1:]
        gup = jnp.stack(gup).reshape(3, C, S, WR, F)
        gup = gup.transpose(1, 2, 0, 3, 4)
        gup = lax.psum_scatter(gup, "dp", scatter_dimension=0, tiled=False).astype(BF)
        gup = lax.all_to_all(gup, "shard", 0, 0)
    gup = gup.astype(F32)
    gup = gup.reshape(S, 3, WR, C, FR).transpose(1, 2, 3, 0, 4).reshape(3, WR, FF)

    counts = lax.psum(jnp.stack([n0, T - n0]), BOTH)
    load_new = 0.9 * load_avg + 0.1 * counts.astype(F32) * E / (T * C * S)
    return (
        layer_out, input_grad, mine[0], mine[1], ga[0], ga[1], ga[2], ga[3], mine[2], mine[3],
        gup[0], gdn0, jnp.stack([mine[4], mine[5]], axis=1), jnp.stack([mine[6], mine[7]], axis=1),
        gup[1:], gdn12, counts, load_new,
    )


def solution(mesh):
    row, vec = P(BOTH, None), P(BOTH)
    mid = P(None, BOTH, None)
    return jax.shard_map(
        body,
        mesh=mesh,
        in_specs=(row, row, vec, vec, row, vec, vec, row, row, row, row, vec, vec, row, row, row, row, mid, mid, P()),
        out_specs=(row, row, vec, vec, row, row, row, row, vec, vec, row, row, row, row, mid, mid, P(), P()),
        check_vma=False,
    )
```

```python
import jax
import jax.numpy as jnp
from jax import lax
from jax.experimental import pallas as pl
from jax.experimental.pallas import tpu as pltpu
from jax.sharding import PartitionSpec as P

HEADS = 16
CAP = 74
BF = jnp.bfloat16
F32 = jnp.float32
BOTH = ("dp", "shard")
MESH = pl.DeviceIdType.MESH


def mm(a, b, dims=((1,), (0,))):
    return lax.dot_general(a, b, (dims, ((), ())), preferred_element_type=F32)


def layer_norm(values, gain, bias):
    centre = values - jnp.mean(values, axis=-1, keepdims=True)
    scale_inv = lax.rsqrt(jnp.mean(centre * centre, axis=-1, keepdims=True) + 1e-05)
    normed = centre * scale_inv
    return (normed * gain + bias, normed, scale_inv)


def norm_back(grad_out, normed, scale_inv, gain):
    grad_normed = grad_out * gain
    inner = grad_normed - jnp.mean(grad_normed, axis=-1, keepdims=True)
    inner = inner - normed * jnp.mean(grad_normed * normed, axis=-1, keepdims=True)
    return (scale_inv * inner, jnp.sum(grad_out * normed, axis=0), jnp.sum(grad_out, axis=0))


def gelu_pair(t):
    inner = 0.7978845608 * (t + 0.044715 * t * t * t)
    th = jnp.tanh(inner)
    val = 0.5 * t * (1.0 + th)
    der = 0.5 * (1.0 + th) + 0.5 * t * (1.0 - th * th) * 0.7978845608 * (1.0 + 3.0 * 0.044715 * t * t)
    return val, der


def ag(block):
    return lax.all_gather(block, "shard", axis=0, tiled=False)


def rs(parts):
    return lax.psum_scatter(parts.astype(BF), "shard", scatter_dimension=0, tiled=False).astype(F32)


def place_of():
    me = lax.axis_index("shard")
    core = lax.axis_index("dp")
    z, p = me // 4, me % 4
    xq = p + 1 - 2 * (p % 2)
    yq = p + 2 - 4 * (p // 2)
    return me, core, z, p, xq, yq, 3 - p


def greet(shards, core):
    bar = pltpu.get_barrier_semaphore()
    me = lax.axis_index("shard")

    @pl.loop(1, shards)
    def _(i):
        pl.semaphore_signal(bar, inc=1, device_id=(core, (me + i) % shards), device_id_type=MESH)

    pl.semaphore_signal(bar, inc=1, device_id=(1 - core, me), device_id_type=MESH)
    pl.semaphore_wait(bar, shards)


def remote(src, dst, send, recv, dev):
    return pltpu.make_async_remote_copy(
        src_ref=src, dst_ref=dst, send_sem=send, recv_sem=recv, device_id=dev, device_id_type=MESH
    )


def rows_loop(count, step, fn):
    @pl.loop(0, count // step)
    def _(i):
        fn(pl.multiple_of(i * step, step))


def ffn_kernel(
    h_ref, scal_ref, dy_ref, up_ref, dn_ref,
    y_out, dh_out, sc_out, gup_out, gdn0_out, gdn12_out,
    hall, scall, psc, screcv, wcol, scol, part, ra, rbx, rby, rd, final,
    pre, der, ub, dg, dm, m, yacc, dxacc, gdn, gup, sib_dn, sib_up, gsend, grecv,
    ag_s, ag_r, rs_s, rs_r, one_s, one_r, sm_s, sm_r,
):
    S, T, D = hall.shape
    F = up_ref.shape[2]
    L = S // 4
    LO = 80
    HI = T - LO
    me, core, z, p, xq, yq, dq = place_of()
    xn, yn = z * 4 + xq, z * 4 + yq
    sgn = 1 - 2 * (z // (L // 2))
    greet(S, core)

    def lev_of(k):
        return (z + k * sgn + L) % L

    def h_copy(kind, slot, src, idx, dev):
        return remote(src, hall.at[idx], ag_s.at[kind, slot], ag_r.at[kind, slot], (core, dev))

    @pl.loop(1, L)
    def _(k):
        lev = lev_of(k)
        remote(h_ref, hall.at[me], ag_s.at[0, lev], ag_r.at[0, z], (core, lev * 4 + p)).start()

    h_copy(1, z, h_ref, me, xn).start()
    h_copy(2, z, h_ref, me, yn).start()

    @pl.loop(1, S)
    def _(i):
        remote(scal_ref, scall.at[me], sm_s.at[0, i], sm_r.at[0], (core, (me + i) % S)).start()

    hall[me] = h_ref[...]
    scall[me] = scal_ref[...]
    gdn[...] = jnp.zeros_like(gdn)
    gup[...] = jnp.zeros_like(gup)
    remote(scall.at[pl.ds(0, S - 1)], scall.at[pl.ds(0, S - 1)], sm_s.at[0, 0], sm_r.at[0], (core, xn)).wait_recv()

    def stage_a(k):
        lev = lev_of(k)
        idx = lev * 4 + p
        h_copy(0, lev, hall.at[idx], idx, xn).wait_recv()
        h_copy(1, lev, hall.at[idx], idx, xn).start()
        h_copy(2, lev, hall.at[idx], idx, yn).start()

    def stage_b(k):
        lev = lev_of(k)
        odd = k % 2
        h_copy(1, lev, h_ref, lev * 4 + xq, xn).wait_recv()
        h_copy(2, lev, h_ref, lev * 4 + yq, yn).wait_recv()
        idx = lev * 4 + xq + odd * (yq - xq)
        h_copy(3, lev, hall.at[idx], idx, yn + odd * (xn - yn)).start()
        h_copy(3, lev, h_ref, lev * 4 + dq, xn).wait_recv()

    lane = lax.broadcasted_iota(jnp.int32, (16, 128), 1)

    def compute(lev):
        base = lev * 4
        for q in range(4):
            full = jnp.concatenate([scall[base + q], jnp.zeros((120, 128), F32)], axis=0)
            wcol[q] = full.T
        for e in range(3):
            n = LO if e else T
            off = HI if e == 2 else 0
            rows = 4 * n
            hm = hall[pl.ds(base, 4), off : off + n, :].reshape(rows, D)
            pre[0:rows, :] = mm(hm, up_ref[e])

            def act(r):
                val, d = gelu_pair(pre[pl.ds(r, 32), :])
                ub[pl.ds(r, 32), :] = val.astype(BF)
                der[pl.ds(r, 32), :] = d

            rows_loop(rows, 32, act)
            m[0:rows, :] = mm(ub[0:rows, :], dn_ref[e])
            for q in range(4):

                def elem(r):
                    at = pl.multiple_of(r + off, 16)
                    mine = pl.ds(pl.multiple_of(q * n + r, 16), 16)
                    t = pl.ds(pl.multiple_of(q * T + off + r, 16), 16)
                    w = wcol[q, pl.ds(at, 16), :][:, e : e + 1]
                    dyv = dy_ref[base + q, pl.ds(at, 16), :].astype(F32)
                    mv = m[mine, :]
                    s = jnp.sum(dyv * mv, axis=1, keepdims=True)
                    s = jnp.where(lane == e, s, 0.0)
                    dm[mine, :] = (dyv * w).astype(BF)
                    if e:
                        yacc[t, :] = yacc[t, :] + mv * w
                        scol[q, pl.ds(at, 16), :] = scol[q, pl.ds(at, 16), :] + s
                    else:
                        yacc[t, :] = mv * w
                        scol[q, pl.ds(at, 16), :] = s

                rows_loop(n, 16, elem)
            pre[0:rows, :] = mm(dm[0:rows, :], dn_ref[e], ((1,), (1,)))

            def back(r):
                dg[pl.ds(r, 32), :] = (pre[pl.ds(r, 32), :] * der[pl.ds(r, 32), :]).astype(BF)

            rows_loop(rows, 32, back)
            gdn[e] = gdn[e] + mm(ub[0:rows, :], dm[0:rows, :], ((0,), (0,)))
            gup[e] = gup[e] + mm(dg[0:rows, :], hm, ((0,), (0,)))
            if e:
                m[0:rows, :] = mm(dg[0:rows, :], up_ref[e], ((1,), (1,)))
                for q in range(4):

                    def addx(r):
                        t = pl.ds(pl.multiple_of(q * T + off + r, 16), 16)
                        dxacc[t, :] = dxacc[t, :] + m[pl.ds(pl.multiple_of(q * n + r, 16), 16), :]

                    rows_loop(n, 16, addx)
            else:
                dxacc[...] = mm(dg[...], up_ref[0], ((1,), (1,)))
        for q in range(4):
            psc[base + q] = scol[q].T[0:8, :]

            def out(r):
                t = pl.ds(pl.multiple_of(q * T + r, 16), 16)
                part[0, base + q, pl.ds(r, 16), :] = dxacc[t, :].astype(BF)
                part[1, base + q, pl.ds(r, 16), :] = yacc[t, :].astype(BF)

            rows_loop(T, 16, out)

    def r_copy(kind, a, lev, src, dst, dev):
        return remote(src, dst, rs_s.at[kind, a, lev], rs_r.at[kind, a, lev], (core, dev))

    def rs_a(k):
        lev = lev_of(k)
        odd = k % 2
        for a in range(2):
            r_copy(0, a, lev, part.at[a, lev * 4 + dq], ra.at[a, lev], yn + odd * (xn - yn)).start()

    def rs_b(k):
        lev = lev_of(k)
        odd = k % 2
        via = lev * 4 + xq + odd * (yq - xq)
        for a in range(2):
            r_copy(0, a, lev, ra.at[a, lev], ra.at[a, lev], xn).wait_recv()

            def add(r):
                t = pl.ds(r, 16)
                part[a, via, t, :] = (part[a, via, t, :].astype(F32) + ra[a, lev, t, :].astype(F32)).astype(BF)

            rows_loop(T, 16, add)
            r_copy(1, a, lev, part.at[a, lev * 4 + xq], rbx.at[a, lev], xn).start()
            r_copy(2, a, lev, part.at[a, lev * 4 + yq], rby.at[a, lev], yn).start()

    def rs_c(k):
        lev = lev_of(k)
        own = lev * 4 + p
        for a in range(2):
            r_copy(1, a, lev, rbx.at[a, lev], rbx.at[a, lev], xn).wait_recv()
            r_copy(2, a, lev, rby.at[a, lev], rby.at[a, lev], yn).wait_recv()

            def add(r):
                t = pl.ds(r, 16)
                tot = part[a, own, t, :].astype(F32) + rbx[a, lev, t, :].astype(F32) + rby[a, lev, t, :].astype(F32)

                @pl.when(k == 0)
                def _():
                    final[a, t, :] = tot

                @pl.when(k > 0)
                def _():
                    part[a, own, t, :] = tot.astype(BF)

            rows_loop(T, 16, add)

            @pl.when(k > 0)
            def _():
                remote(
                    part.at[a, own], rd.at[a, z], rs_s.at[3, a, lev], rs_r.at[3, a, z], (core, lev * 4 + p)
                ).start()

    stage_a(1)

    @pl.loop(0, L)
    def _(k):
        stage_b(k)

        @pl.when(k < L - 2)
        def _():
            stage_a(k + 2)

        compute(lev_of(k))
        rs_a(k)

        @pl.when(k > 0)
        def _():
            rs_c(k - 1)

        rs_b(k)

    half = D // 2
    other = pl.multiple_of((1 - core) * half, half)
    mine_d = pl.multiple_of(core * half, half)
    FR = F // 2
    other_f = pl.multiple_of((1 - core) * FR, FR)
    mine_f = pl.multiple_of(core * FR, FR)
    sib = (1 - core, me)
    c_up = remote(gup.at[:, :, pl.ds(other, half)], sib_up, one_s.at[0], one_r.at[0], sib)
    c_dn = remote(gdn.at[:, pl.ds(other_f, FR), :], sib_dn, one_s.at[1], one_r.at[1], sib)
    c_up.start()
    c_dn.start()

    @pl.loop(1, S)
    def _(i):
        to = (me + i) % S
        remote(psc.at[to], screcv.at[i], sm_s.at[1, i], sm_r.at[1], (core, to)).start()

    rs_c(L - 1)
    c_up.wait_recv()
    for e in range(3):
        tot = gup[e, :, pl.ds(mine_d, half)] + sib_up[e]
        gsend[e] = tot.T.astype(BF)
    WR = half // S
    screcv[0] = psc[me]

    def g_copy(i, to):
        return remote(
            gsend.at[:, pl.ds(pl.multiple_of(to * WR, WR), WR), :], grecv.at[me], sm_s.at[2, i], sm_r.at[2], (core, to)
        )

    @pl.loop(1, S)
    def _(i):
        g_copy(i, (me + i) % S).start()

    grecv[me] = gsend[:, pl.ds(pl.multiple_of(me * WR, WR), WR), :]
    c_dn.wait_recv()
    gdn0_out[...] = gdn[0, pl.ds(mine_f, FR), :] + sib_dn[0]
    for e in range(1, 3):
        gdn12_out[e - 1] = gdn[e, pl.ds(mine_f, FR), :] + sib_dn[e]

    @pl.loop(1, L)
    def _(k):
        lev = lev_of(k)
        for a in range(2):
            r_copy(3, a, lev, rd.at[a, lev], rd.at[a, lev], xn).wait_recv()

            def add(r):
                t = pl.ds(r, 16)
                final[a, t, :] = final[a, t, :] + rd[a, lev, t, :].astype(F32)

            rows_loop(T, 16, add)

    dh_out[...] = final[0]
    y_out[...] = final[1]
    remote(screcv.at[pl.ds(1, S - 1)], screcv.at[pl.ds(1, S - 1)], sm_s.at[1, 0], sm_r.at[1], (core, xn)).wait_recv()
    sc_out[...] = jnp.sum(screcv[...], axis=0)
    remote(grecv.at[pl.ds(0, S - 1)], grecv.at[pl.ds(0, S - 1)], sm_s.at[2, 0], sm_r.at[2], (core, xn)).wait_recv()
    gup_out[...] = grecv[...]

    c_up.wait_send()
    c_dn.wait_send()

    @pl.loop(1, S)
    def _(i):
        remote(scal_ref, scall.at[0], sm_s.at[0, i], sm_r.at[0], (core, xn)).wait_send()
        remote(psc.at[0], screcv.at[0], sm_s.at[1, i], sm_r.at[1], (core, xn)).wait_send()
        g_copy(i, (me + i) % S).wait_send()

    @pl.loop(0, L)
    def _(k):
        lev = lev_of(k)
        for kind in range(1, 4):
            h_copy(kind, lev, hall.at[0], 0, xn).wait_send()
        for a in range(2):
            for kind in range(3):
                r_copy(kind, a, lev, ra.at[a, 0], ra.at[a, 0], xn).wait_send()

        @pl.when(k > 0)
        def _():
            h_copy(0, lev, hall.at[0], 0, xn).wait_send()
            for a in range(2):
                r_copy(3, a, lev, ra.at[a, 0], ra.at[a, 0], xn).wait_send()


def ffn_call(h2b, scal, dy_all, ups, downs):
    S, T, D = dy_all.shape
    F = ups.shape[2]
    L = S // 4
    WR = D // 2 // S
    vm = pl.BlockSpec(memory_space=pltpu.VMEM)
    V = pltpu.VMEM
    dma = pltpu.SemaphoreType.DMA
    sds = jax.ShapeDtypeStruct
    return pl.pallas_call(
        ffn_kernel,
        out_shape=(
            sds((T, D), F32), sds((T, D), F32), sds((8, 128), F32), sds((S, 3, WR, F), BF),
            sds((F // 2, D), F32), sds((2, F // 2, D), F32),
        ),
        in_specs=[vm] * 5,
        out_specs=(vm,) * 6,
        scratch_shapes=[
            V((S, T, D), BF), V((S, 8, 128), F32), V((S, 8, 128), F32), V((S, 8, 128), F32),
            V((4, T, 128), F32), V((4, T, 128), F32),
            V((2, S, T, D), BF), V((2, L, T, D), BF), V((2, L, T, D), BF), V((2, L, T, D), BF), V((2, L, T, D), BF),
            V((2, T, D), F32),
            V((4 * T, F), F32), V((4 * T, F), F32), V((4 * T, F), BF), V((4 * T, F), BF), V((4 * T, D), BF),
            V((4 * T, D), F32), V((4 * T, D), F32), V((4 * T, D), F32),
            V((3, F, D), F32), V((3, F, D), F32), V((3, F // 2, D), F32), V((3, F, D // 2), F32),
            V((3, D // 2, F), BF), V((S, 3, WR, F), BF),
            dma((4, L)), dma((4, L)), dma((4, 2, L)), dma((4, 2, L)), dma((2,)), dma((2,)), dma((3, S)), dma((3,)),
        ],
        compiler_params=pltpu.CompilerParams(collective_id=2, has_side_effects=True, vmem_limit_bytes=64000000),
        cost_estimate=pl.CostEstimate(flops=15 * 10**9, bytes_accessed=20 * 2**20, transcendentals=2**20),
        name="ffn",
    )(h2b, scal, dy_all, ups, downs)


def tree_gather(at, own, ss, rs, dev, levels):
    core, z, p, xq, yq, dq = dev
    xn, yn = z * 4 + xq, z * 4 + yq
    me = z * 4 + p
    lev_of, L = levels

    def copy(kind, slot, src, idx, to):
        return remote(src, at(idx), ss.at[kind, slot], rs.at[kind, slot], (core, to))

    class Stages:
        @staticmethod
        def start():
            @pl.loop(1, L)
            def _(k):
                lev = lev_of(k)
                remote(own, at(me), ss.at[0, lev], rs.at[0, z], (core, lev * 4 + p)).start()

            copy(1, z, own, me, xn).start()
            copy(2, z, own, me, yn).start()

        @staticmethod
        def a(k):
            lev = lev_of(k)
            idx = lev * 4 + p
            copy(0, lev, own, idx, xn).wait_recv()
            copy(1, lev, at(idx), idx, xn).start()
            copy(2, lev, at(idx), idx, yn).start()

        @staticmethod
        def b(k):
            lev = lev_of(k)
            odd = k % 2
            copy(1, lev, own, lev * 4 + xq, xn).wait_recv()
            copy(2, lev, own, lev * 4 + yq, yn).wait_recv()
            idx = lev * 4 + xq + odd * (yq - xq)
            copy(3, lev, at(idx), idx, yn + odd * (xn - yn)).start()

        @staticmethod
        def c(k):
            lev = lev_of(k)
            copy(3, lev, own, lev * 4 + dq, xn).wait_recv()

        @staticmethod
        def finish():
            @pl.loop(0, L)
            def _(k):
                lev = lev_of(k)
                for kind in range(1, 4):
                    copy(kind, lev, own, me, xn).wait_send()

                @pl.when(k > 0)
                def _():
                    copy(0, lev, own, me, xn).wait_send()

    return Stages


def sort_matrix(ids_e, ids_s, T):
    zero = ids_e == 0
    n0 = jnp.sum(jnp.where(zero, 1.0, 0.0), axis=1, keepdims=True)
    slot = ids_s.astype(F32)
    pos = jnp.where(zero, slot, slot + n0)
    sub = lax.broadcasted_iota(jnp.int32, (T, T), 0).astype(F32)
    return jnp.where(sub == pos, 1.0, 0.0), n0


def attn_kernel(
    x_ref, dy_ref, doc_ref, e_ref, s_ref, small_ref, wq_ref, wk_ref, wv_ref, wo_ref,
    wu_ref, eu_ref, wd_ref, ed_ref,
    h2b_out, stat_out, scal_out, u1_out, u2_out, x1_out, dys_out, q_out, k_out, v_out, p_out, o_out,
    small_out, count_out, w_out, dyall_out, up_out, dn_out,
    wbuf, smallbuf, h1b, bias, xs, tmp,
    ag_s, ag_r, sib_s, sib_r, sm_s, sm_r, loc,
):
    T, D = x_ref.shape
    WR = wq_ref.shape[0]
    FR = wd_ref.shape[0]
    N = wbuf.shape[1]
    S = N // 2
    L = S // 4
    me, core, z, p, xq, yq, dq = place_of()
    xn = z * 4 + xq
    sgn = 1 - 2 * (z // (L // 2))
    my = core * S + me
    sib = (1 - core, me)
    greet(S, core)

    def lev_of(k):
        return (z + k * sgn + L) % L

    dev, levels = (core, z, p, xq, yq, dq), (lev_of, L)

    def w1_at(i):
        return wbuf.at[pl.ds(0, 3), core * S + i]

    def w2_at(i):
        return wbuf.at[3, core * S + i]

    w1 = tree_gather(w1_at, w1_at(me), ag_s.at[0], ag_r.at[0], dev, levels)
    w2 = tree_gather(w2_at, w2_at(me), ag_s.at[1], ag_r.at[1], dev, levels)
    dyg = tree_gather(lambda i: dyall_out.at[i], dys_out, ag_s.at[2], ag_r.at[2], dev, levels)

    for i, w in enumerate((wq_ref, wk_ref, wv_ref, wo_ref)):
        wbuf[i, my] = w[...]
    w1.start()

    perm, n0 = sort_matrix(e_ref[...], s_ref[...], T)
    smallbuf[my, 0:8, :] = small_ref[...]
    lane8 = lax.broadcasted_iota(jnp.int32, (8, 128), 1)
    smallbuf[my, 8:16, :] = jnp.where(lane8 == 0, jnp.broadcast_to(n0, (8, 128)), 0.0)

    @pl.loop(1, S)
    def _(i):
        remote(smallbuf.at[my], smallbuf.at[my], sm_s.at[0, i], sm_r.at[0], (core, (me + i) % S)).start()

    def dn_own(e0, n, src):
        dst = dn_out.at[pl.ds(e0, n), pl.ds(pl.multiple_of(core * FR, FR), FR), :]
        return src, dst

    d0 = dn_own(0, 1, wd_ref)
    d0 = (wd_ref, dn_out.at[0, pl.ds(pl.multiple_of(core * FR, FR), FR), :])
    d1 = dn_own(1, 2, ed_ref)
    dn_copies = []
    for j, (src, dst) in enumerate((d0, d1)):
        r = remote(src, dst, sib_s.at[2, j], sib_r.at[2, j], sib)
        lc = pltpu.make_async_copy(src, dst, loc.at[j])
        r.start()
        lc.start()
        dn_copies.append((r, lc))

    permb = perm.astype(BF)
    xs[...] = mm(permb, x_ref[...])
    dys_out[...] = mm(permb, dy_ref[...]).astype(BF)
    dy_local = pltpu.make_async_copy(dys_out, dyall_out.at[me], loc.at[2])
    dy_local.start()

    docs = (doc_ref[...] == lax.broadcasted_iota(jnp.int32, (16, T), 0)).astype(F32).astype(BF)
    docs = mm(docs, permb, ((1,), (1,))).astype(BF)
    same = mm(docs, docs, ((0,), (0,)))
    place = lax.broadcasted_iota(jnp.int32, (T, T), 1).astype(F32)
    ord_col = jnp.sum(perm * place, axis=1, keepdims=True)
    ord_row = mm(place[0:16, :].astype(BF), permb, ((1,), (1,)))[0:1, :]
    bias[...] = jnp.where((same > 0.5) & (ord_row <= ord_col), 0.0, -1e30)

    lane = lax.broadcasted_iota(jnp.int32, (16, 128), 1)

    def norm1(r):
        t = pl.ds(r, 16)
        v = xs[t, :]
        cen = v - jnp.mean(v, axis=1, keepdims=True)
        inv = lax.rsqrt(jnp.mean(cen * cen, axis=1, keepdims=True) + 1e-05)
        u1_out[t, :] = cen * inv
        stat_out[t, :] = jnp.where(lane == 8, inv, 0.0)

    rows_loop(T, 16, norm1)

    w1.a(1)
    w1.b(0)
    w1.a(2)
    w1.b(1)

    group = 128 // WR
    remote(smallbuf.at[pl.ds(0, S - 1)], smallbuf.at[pl.ds(0, S - 1)], sm_s.at[0, 0], sm_r.at[0], (core, xn)).wait_recv()
    mine_small = smallbuf.at[pl.ds(core * S, S)]
    c_small = remote(mine_small, mine_small, sib_s.at[2, 2], sib_r.at[2, 2], sib)
    c_small.start()

    def w1_sib(lev, who):
        b = wbuf.at[pl.ds(0, 3), pl.ds(who * S + lev * 4, 4)]
        return remote(b, b, sib_s.at[0, lev], sib_r.at[0, lev], sib)

    def w2_sib(lev, who):
        b = wbuf.at[3, pl.ds(who * S + lev * 4, 4)]
        return remote(b, b, sib_s.at[1, lev], sib_r.at[1, lev], sib)

    def c1(k):
        w1.c(k)
        w1_sib(lev_of(k), core).start()

    def c2(k):
        w2.c(k)
        w2_sib(lev_of(k), core).start()

    for k in range(3, L):
        w1.a(k)
    c1(0)
    w2.start()
    for k in range(2, L):
        w1.b(k)
        c1(k - 1)

    def up_copy(e, h, i):
        to = (me + i) % S
        src = wu_ref if e == 0 else eu_ref.at[e - 1]
        return remote(
            src.at[:, pl.ds(pl.multiple_of((h * S + to) * FR, FR), FR)],
            up_out.at[e, pl.ds(pl.multiple_of(my * WR, WR), WR), pl.ds(h * FR, FR)],
            sm_s.at[1, i], sm_r.at[1], (core, to),
        )

    def up_local(e, h):
        src = wu_ref if e == 0 else eu_ref.at[e - 1]
        return pltpu.make_async_copy(
            src.at[:, pl.ds(pl.multiple_of((h * S + me) * FR, FR), FR)],
            up_out.at[e, pl.ds(pl.multiple_of(my * WR, WR), WR), pl.ds(h * FR, FR)],
            loc.at[4 + 2 * e + h],
        )

    @pl.loop(1, S)
    def _(i):
        for e in range(3):
            for h in range(2):
                up_copy(e, h, i).start()

    for e in range(3):
        for h in range(2):
            up_local(e, h).start()

    c_small.wait_recv()
    for g in range(D // 128):
        part = smallbuf[g * group, 0:8, :]
        for j in range(1, group):
            part = part + smallbuf[g * group + j, 0:8, :]
        small_out[:, g * 128 : (g + 1) * 128] = part
    cnt = smallbuf[0, 8:16, :]
    for i in range(1, N):
        cnt = cnt + smallbuf[i, 8:16, :]
    count_out[...] = cnt

    def norm1b(r):
        t = pl.ds(r, 16)
        h1b[t, :] = (u1_out[t, :] * small_out[0:1, :] + small_out[1:2, :]).astype(BF)

    rows_loop(T, 16, norm1b)
    c1(L - 1)
    w2.a(1)
    w2.b(0)
    for k in range(L):
        w1_sib(lev_of(k), 1 - core).wait_recv()

    def full(i):
        return wbuf[i].reshape(D, D)

    tmp[...] = mm(h1b[...], full(0))
    q_out[...] = (tmp[...] * 0.125).astype(BF)
    for k in range(2, L):
        w2.a(k)
    w2.b(1)
    tmp[...] = mm(h1b[...], full(1))
    k_out[...] = tmp[...].astype(BF)
    c2(0)
    dyg.start()
    for k in range(2, L):
        w2.b(k)
        c2(k - 1)
    tmp[...] = mm(h1b[...], full(2))
    v_out[...] = tmp[...].astype(BF)
    c2(L - 1)
    dyg.a(1)
    dyg.b(0)

    low = lax.broadcasted_iota(jnp.int32, (T, 128), 1) < 64
    lowb = low.astype(F32).astype(BF)
    highb = (1.0 - low.astype(F32)).astype(BF)

    def heads(j):
        ln = pl.ds(pl.multiple_of(j * 128, 128), 128)
        qp = q_out[:, ln]
        q2 = jnp.concatenate([qp * lowb, qp * highb], axis=0)
        s = mm(q2, k_out[:, ln], ((1,), (1,)))
        s = s + jnp.concatenate([bias[...], bias[...]], axis=0)
        ex = jnp.exp(s - jnp.max(s, axis=1, keepdims=True))
        pr = ex / jnp.sum(ex, axis=1, keepdims=True)
        p_out[j] = pr
        o2 = mm(pr.astype(BF), v_out[:, ln])
        o_out[:, ln] = jnp.where(low, o2[0:T], o2[T:]).astype(BF)

    half = D // 256

    @pl.loop(0, half)
    def _(j):
        heads(j)

    dyg.a(2)
    dyg.b(1)

    @pl.loop(half, 2 * half)
    def _(j):
        heads(j)

    for k in range(3, L):
        dyg.a(k)
    for k in range(L):
        w2_sib(lev_of(k), 1 - core).wait_recv()
    w_save = pltpu.make_async_copy(wbuf, w_out, loc.at[3])
    w_save.start()
    tmp[...] = mm(o_out[...], full(3))

    def norm2(r):
        t = pl.ds(r, 16)
        v = xs[t, :] + tmp[t, :]
        x1_out[t, :] = v
        cen = v - jnp.mean(v, axis=1, keepdims=True)
        inv = lax.rsqrt(jnp.mean(cen * cen, axis=1, keepdims=True) + 1e-05)
        u = cen * inv
        u2_out[t, :] = u
        h2 = u * small_out[2:3, :] + small_out[3:4, :]
        h2b_out[t, :] = h2.astype(BF)
        lg = [jnp.sum(h2 * small_out[i : i + 1, :], axis=1, keepdims=True) for i in range(4, 8)]

        def soft(a, b):
            mx = jnp.maximum(a, b)
            ea, eb = jnp.exp(a - mx), jnp.exp(b - mx)
            return ea / (ea + eb), eb / (ea + eb)

        r0, r1 = soft(lg[0], lg[1])
        k0, k1 = soft(lg[2], lg[3])
        row = (lax.broadcasted_iota(jnp.int32, (16, 1), 0) + r).astype(F32)
        is0 = row < n0
        gate = jnp.where(is0, r0, r1)
        we = k0 * gate
        cols = (k1, jnp.where(is0, we, 0.0), jnp.where(is0, 0.0, we), k0, gate, r0, r1)
        st = stat_out[t, :] + jnp.where(lane == 9, inv, 0.0)
        for i, col in enumerate(cols):
            st = st + jnp.where(lane == i, col, 0.0)
        stat_out[t, :] = st

    rows_loop(T, 16, norm2)
    scal_out[...] = stat_out[...].T[0:8, :]

    for k in range(2, L):
        dyg.b(k)
    for k in range(L):
        dyg.c(k)

    got = up_out.at[:, pl.ds(0, (S - 1) * WR), :]
    remote(got, got, sm_s.at[1, 0], sm_r.at[1], (core, xn)).wait_recv()
    for e in range(3):
        for h in range(2):
            up_local(e, h).wait()
    mine_up = up_out.at[:, pl.ds(pl.multiple_of(core * S * WR, S * WR), S * WR), :]
    c_up = remote(mine_up, mine_up, sib_s.at[2, 3], sib_r.at[2, 3], sib)
    c_up.start()
    c_up.wait()
    w_save.wait()
    dy_local.wait()
    for r, lc in dn_copies:
        r.wait()
        lc.wait()
    c_small.wait_send()
    w1.finish()
    w2.finish()
    dyg.finish()

    @pl.loop(0, L)
    def _(k):
        w1_sib(k, core).wait_send()
        w2_sib(k, core).wait_send()

    @pl.loop(1, S)
    def _(i):
        remote(smallbuf.at[my], smallbuf.at[my], sm_s.at[0, i], sm_r.at[0], (core, xn)).wait_send()
        for e in range(3):
            for h in range(2):
                up_copy(e, h, i).wait_send()


def attn_call(x, dy, docs, es, ss, small, ws, wu, eu, wd, ed, S):
    T, D = x.shape
    WR, FR = ws[0].shape[0], wd.shape[0]
    L = S // 4
    N = 2 * S
    vm = pl.BlockSpec(memory_space=pltpu.VMEM)
    hb = pl.BlockSpec(memory_space=pl.ANY)
    V = pltpu.VMEM
    dma = pltpu.SemaphoreType.DMA
    sds = jax.ShapeDtypeStruct
    row = sds((T, D), BF)
    rowf = sds((T, D), F32)
    return pl.pallas_call(
        attn_kernel,
        out_shape=(
            row, sds((T, 128), F32), sds((8, T), F32), rowf, rowf, rowf, row, row, row, row,
            sds((D // 128, 2 * T, T), F32), row, sds((8, D), F32), sds((8, 128), F32),
            sds((4, N, WR, D), BF), sds((S, T, D), BF), sds((3, D, 2 * FR), BF), sds((3, 2 * FR, D), BF),
        ),
        in_specs=[vm] * 10 + [hb] * 4,
        out_specs=(vm,) * 14 + (hb,) * 4,
        scratch_shapes=[
            V((4, N, WR, D), BF), V((N, 16, 128), F32), V((T, D), BF), V((T, T), F32), V((T, D), F32), V((T, D), F32),
            dma((3, 4, L)), dma((3, 4, L)), dma((3, max(L, 4))), dma((3, max(L, 4))), dma((2, S)), dma((2,)), dma((10,)),
        ],
        compiler_params=pltpu.CompilerParams(collective_id=1, has_side_effects=True, vmem_limit_bytes=60000000),
        cost_estimate=pl.CostEstimate(flops=2 * 10**9, bytes_accessed=40 * 2**20, transcendentals=2**20),
        name="attn",
    )(x, dy, docs, es, ss, small, *ws, wu, eu, wd, ed)


def body_plain(
    hidden_in, doc_ids, expert_ids, slot_ids, out_grad, ln1_gain, ln1_bias, w_query, w_key, w_value,
    w_out, ln2_gain, ln2_bias, w_up, w_down, w_router, w_mix, expert_up, expert_down, load_avg,
):
    T, D = hidden_in.shape
    H, HD = HEADS, D // HEADS
    S = lax.axis_size("shard")
    C = lax.axis_size("dp")
    WR = w_query.shape[0]
    FF = w_up.shape[1]
    FR = w_down.shape[0]
    F = FR * C
    E = expert_up.shape[0]
    LO, HI = 80, T - 80

    pos = jnp.where(expert_ids == 0, slot_ids, jnp.sum((expert_ids == 0).astype(jnp.int32)) + slot_ids)
    n0 = jnp.sum((expert_ids == 0).astype(jnp.int32))
    place = lax.iota(jnp.int32, T)
    perm = (pos[None, :] == place[:, None]).astype(BF)
    xs = mm(perm, hidden_in)
    dys = mm(perm, out_grad).astype(BF)
    doc = doc_ids[0]
    allowed = (place[None, :] <= place[:, None]) & (doc[:, None] == doc[None, :])
    allowed = mm(mm(perm, allowed.astype(BF)).astype(BF), perm, ((1,), (1,))) > 0.5
    is0 = (place < n0)[:, None]

    small = jnp.stack(
        [ln1_gain, ln1_bias, ln2_gain, ln2_bias, w_router[:, 0], w_router[:, 1], w_mix[:, 0], w_mix[:, 1]]
    ).astype(F32)
    small = lax.all_gather(small, BOTH, axis=1, tiled=True)
    g1, b1, g2, b2 = small[0], small[1], small[2], small[3]
    wr, wm = small[4:6], small[6:8]

    wa = jnp.stack([w_query, w_key, w_value, w_out])
    wa = lax.all_gather(wa, BOTH, axis=1, tiled=True)
    wq, wk, wv, wo = wa[0], wa[1], wa[2], wa[3]

    ups = jnp.stack([w_up, expert_up[0], expert_up[1]])
    ups = ups.reshape(3, WR, C, S, FR).transpose(3, 0, 1, 2, 4).reshape(S, 3, WR, F)
    ups = lax.all_to_all(ups, "shard", 0, 0)
    ups = lax.all_gather(ups, "dp", axis=0)
    ups = ups.transpose(2, 0, 1, 3, 4).reshape(3, D, F)
    downs = jnp.stack([w_down, expert_down[0], expert_down[1]])
    downs = lax.all_gather(downs, "dp", axis=1, tiled=True)

    dy_all = ag(dys)

    n1, u1, i1 = layer_norm(xs, g1, b1)
    h1b = n1.astype(BF)
    q = (mm(h1b, wq) * 0.125).astype(BF).reshape(T, H, HD)
    k = mm(h1b, wk).astype(BF).reshape(T, H, HD)
    v = mm(h1b, wv).astype(BF).reshape(T, H, HD)
    s = jnp.einsum("ihd,jhd->hij", q, k, preferred_element_type=F32)
    s = jnp.where(allowed[None], s, -1e30)
    ex = jnp.exp(s - jnp.max(s, axis=-1, keepdims=True))
    p = ex / jnp.sum(ex, axis=-1, keepdims=True)
    pb = p.astype(BF)
    o = jnp.einsum("hij,jhd->ihd", pb, v, preferred_element_type=F32).reshape(T, D).astype(BF)
    x1 = xs + mm(o, wo)
    h2, u2, i2 = layer_norm(x1, g2, b2)
    h2b = h2.astype(BF)

    def two(w):
        return jnp.stack([jnp.sum(h2 * w[0], axis=-1), jnp.sum(h2 * w[1], axis=-1)], axis=-1)

    r = jax.nn.softmax(two(wr), axis=-1)
    c = jax.nn.softmax(two(wm), axis=-1)
    gate = jnp.where(is0, r[:, 0:1], r[:, 1:2])
    c0, c1 = c[:, 0:1], c[:, 1:2]
    we = c0 * gate
    scal = jnp.concatenate([c1, jnp.where(is0, we, 0.0), jnp.where(is0, 0.0, we)], axis=1)

    h_all = ag(h2b)
    scal_all = ag(scal)

    def cut(a, e):
        return (a[:, :LO] if e == 1 else a[:, HI:]) if e else a

    partial_y = jnp.zeros((S, T, D), F32)
    partial_dh = jnp.zeros((S, T, D), F32)
    score = []
    gup, gdown = [], []
    for e in range(3):
        he = cut(h_all, e)
        dye = cut(dy_all, e).astype(F32)
        se = cut(scal_all, e)[:, :, e : e + 1]
        n = he.shape[1]
        hf = he.reshape(S * n, D)
        pre = mm(hf, ups[e])
        val, der = gelu_pair(pre)
        ub = val.astype(BF)
        m = mm(ub, downs[e]).reshape(S, n, D)
        dm = (dye * se).astype(BF).reshape(S * n, D)
        dg = (mm(dm, downs[e], ((1,), (1,))) * der).astype(BF)
        gdown.append(mm(ub, dm, ((0,), (0,))))
        gup.append(mm(hf, dg, ((0,), (0,))))
        dx = mm(dg, ups[e], ((1,), (1,))).reshape(S, n, D)
        y = m * se
        sc = jnp.sum(dye * m, axis=-1)
        pad = [(0, 0), (0, T - n) if e < 2 else (T - n, 0)]
        live = is0[None, :, 0]
        partial_y += jnp.pad(y, pad + [(0, 0)])
        partial_dh += jnp.pad(dx, pad + [(0, 0)])
        score.append(jnp.pad(sc, pad))
    yfull = rs(partial_y)
    dh2 = rs(partial_dh)
    sc = lax.psum_scatter(jnp.stack(score, axis=1), "shard", scatter_dimension=0, tiled=False)
    sm = sc[0][:, None]
    se = jnp.where(is0, sc[1][:, None], sc[2][:, None])

    dc0, dc1 = gate * se, sm
    tot = c0 * dc0 + c1 * dc1
    dcl0, dcl1 = c0 * (dc0 - tot), c1 * (dc1 - tot)
    dgate = c0 * se
    dr0, dr1 = jnp.where(is0, dgate, 0.0), jnp.where(is0, 0.0, dgate)
    tot = r[:, 0:1] * dr0 + r[:, 1:2] * dr1
    drl0, drl1 = r[:, 0:1] * (dr0 - tot), r[:, 1:2] * (dr1 - tot)
    layer_out = (x1 + yfull).astype(BF)
    dh2 = dh2 + drl0 * wr[0] + drl1 * wr[1] + dcl0 * wm[0] + dcl1 * wm[1]
    gw = [jnp.sum(h2 * t, axis=0) for t in (drl0, drl1, dcl0, dcl1)]
    dx1, gg2, gb2 = norm_back(dh2, u2, i2, g2)
    dx1 = dx1 + dys.astype(F32)
    dab = dx1.astype(BF)
    gwo = mm(o, dab, ((0,), (0,)))
    do = mm(dab, wo, ((1,), (1,))).astype(BF).reshape(T, H, HD)
    dp = jnp.einsum("ihd,jhd->hij", do, v, preferred_element_type=F32)
    ds = (p * (dp - jnp.sum(p * dp, axis=-1, keepdims=True))).astype(BF)
    dq = jnp.einsum("hij,jhd->ihd", ds, k, preferred_element_type=F32).astype(BF)
    dq = (dq * BF(0.125)).reshape(T, D)
    dk = jnp.einsum("hij,ihd->jhd", ds, q, preferred_element_type=F32).astype(BF).reshape(T, D)
    dv = jnp.einsum("hij,ihd->jhd", pb, do, preferred_element_type=F32).astype(BF).reshape(T, D)
    dh1 = mm(dq, wq, ((1,), (1,))) + mm(dk, wk, ((1,), (1,))) + mm(dv, wv, ((1,), (1,)))
    ga = jnp.stack([mm(h1b, dq, ((0,), (0,))), mm(h1b, dk, ((0,), (0,))), mm(h1b, dv, ((0,), (0,))), gwo])
    dxn, gg1, gb1 = norm_back(dh1, u1, i1, g1)
    input_grad = (dx1 + dxn).astype(BF)

    layer_out = mm(perm, layer_out, ((0,), (0,))).astype(BF)
    input_grad = mm(perm, input_grad, ((0,), (0,))).astype(BF)

    smalls = lax.psum(jnp.stack([gg1, gb1, gg2, gb2] + gw), BOTH)
    mine = lax.dynamic_slice_in_dim(smalls, lax.axis_index(BOTH) * WR, WR, 1)
    ga = ga.reshape(4, C, S, WR, D).transpose(1, 2, 0, 3, 4)
    ga = lax.psum_scatter(ga.astype(BF), "dp", scatter_dimension=0, tiled=False)
    ga = lax.psum_scatter(ga, "shard", scatter_dimension=0, tiled=False).astype(F32)
    gdown = lax.psum_scatter(jnp.stack(gdown), "dp", scatter_dimension=1, tiled=True)
    gup = jnp.stack(gup).reshape(3, C, S, WR, F).transpose(1, 2, 0, 3, 4)
    gup = lax.psum_scatter(gup, "dp", scatter_dimension=0, tiled=False).astype(BF)
    gup = lax.all_to_all(gup, "shard", 0, 0).astype(F32)
    gup = gup.reshape(S, 3, WR, C, FR).transpose(1, 2, 3, 0, 4).reshape(3, WR, FF)

    counts = lax.psum(jnp.stack([n0, T - n0]), BOTH)
    load_new = 0.9 * load_avg + 0.1 * counts.astype(F32) * E / (T * C * S)
    return (
        layer_out, input_grad, mine[0], mine[1], ga[0], ga[1], ga[2], ga[3], mine[2], mine[3],
        gup[0], gdown[0], jnp.stack([mine[4], mine[5]], axis=1), jnp.stack([mine[6], mine[7]], axis=1),
        gup[1:], gdown[1:], counts, load_new,
    )


def body(
    hidden_in, doc_ids, expert_ids, slot_ids, out_grad, ln1_gain, ln1_bias, w_query, w_key, w_value,
    w_out, ln2_gain, ln2_bias, w_up, w_down, w_router, w_mix, expert_up, expert_down, load_avg,
):
    T, D = hidden_in.shape
    H, HD = HEADS, D // HEADS
    S = lax.axis_size("shard")
    C = lax.axis_size("dp")
    WR = w_query.shape[0]
    FF = w_up.shape[1]
    FR = w_down.shape[0]
    F = FR * C
    E = expert_up.shape[0]
    ndev = C * S
    dev = lax.axis_index(BOTH)
    small = jnp.stack(
        [ln1_gain, ln1_bias, ln2_gain, ln2_bias, w_router[:, 0], w_router[:, 1], w_mix[:, 0], w_mix[:, 1]]
    ).astype(F32)
    group = 128 // WR
    slot_of = lax.broadcasted_iota(jnp.int32, (8, 128), 1) // WR
    small = jnp.where(slot_of == dev % group, jnp.tile(small, (1, group)), 0.0)
    (h2b, stat, scal8, u1, u2, x1, dys, q, k, v, p, o, small, count, wa, dy_all, ups, downs) = attn_call(
        hidden_in, out_grad, doc_ids, expert_ids.reshape(1, T), slot_ids.reshape(1, T), small,
        (w_query, w_key, w_value, w_out), w_up, expert_up, w_down, expert_down, S,
    )
    wa = wa.reshape(4, D, D)
    wq, wk, wv, wo = wa[0], wa[1], wa[2], wa[3]
    g1, b1, g2, b2 = small[0], small[1], small[2], small[3]
    wr, wm = small[4:6], small[6:8]
    place = lax.iota(jnp.int32, T)
    n0 = jnp.sum((expert_ids == 0).astype(jnp.int32))
    pos = jnp.where(expert_ids == 0, slot_ids, n0 + slot_ids)
    perm = (pos[None, :] == place[:, None]).astype(BF)
    is0 = (place < n0)[:, None]
    i1, i2 = stat[:, 8:9], stat[:, 9:10]
    c0, c1, gate, r = stat[:, 3:4], stat[:, 0:1], stat[:, 4:5], stat[:, 5:7]
    h1b = (u1 * g1 + b1).astype(BF)
    h2 = u2 * g2 + b2
    p = p.reshape(H, T, T)
    pb = p.astype(BF)
    q, k, v = q.reshape(T, H, HD), k.reshape(T, H, HD), v.reshape(T, H, HD)
    yfull, dh2, sc, gup, gdn0, gdn12 = ffn_call(h2b, scal8, dy_all, ups, downs)
    sm = sc[0][:, None]
    se = jnp.where(is0, sc[1][:, None], sc[2][:, None])
    dc0, dc1 = gate * se, sm
    tot = c0 * dc0 + c1 * dc1
    dcl0, dcl1 = c0 * (dc0 - tot), c1 * (dc1 - tot)
    dgate = c0 * se
    dr0, dr1 = jnp.where(is0, dgate, 0.0), jnp.where(is0, 0.0, dgate)
    tot = r[:, 0:1] * dr0 + r[:, 1:2] * dr1
    drl0, drl1 = r[:, 0:1] * (dr0 - tot), r[:, 1:2] * (dr1 - tot)
    layer_out = (x1 + yfull).astype(BF)
    dh2 = dh2 + drl0 * wr[0] + drl1 * wr[1] + dcl0 * wm[0] + dcl1 * wm[1]
    gw = [jnp.sum(h2 * t, axis=0) for t in (drl0, drl1, dcl0, dcl1)]
    dx1, gg2, gb2 = norm_back(dh2, u2, i2, g2)
    dx1 = dx1 + dys.astype(F32)
    dab = dx1.astype(BF)
    gwo = mm(o, dab, ((0,), (0,)))
    do = mm(dab, wo, ((1,), (1,))).astype(BF).reshape(T, H, HD)
    dp = jnp.einsum("ihd,jhd->hij", do, v, preferred_element_type=F32)
    ds = (p * (dp - jnp.sum(p * dp, axis=-1, keepdims=True))).astype(BF)
    dq = jnp.einsum("hij,jhd->ihd", ds, k, preferred_element_type=F32).astype(BF)
    dq = (dq * BF(0.125)).reshape(T, D)
    dk = jnp.einsum("hij,ihd->jhd", ds, q, preferred_element_type=F32).astype(BF).reshape(T, D)
    dv = jnp.einsum("hij,ihd->jhd", pb, do, preferred_element_type=F32).astype(BF).reshape(T, D)
    dh1 = mm(dq, wq, ((1,), (1,))) + mm(dk, wk, ((1,), (1,))) + mm(dv, wv, ((1,), (1,)))
    ga = jnp.stack([mm(h1b, dq, ((0,), (0,))), mm(h1b, dk, ((0,), (0,))), mm(h1b, dv, ((0,), (0,))), gwo])
    dxn, gg1, gb1 = norm_back(dh1, u1, i1, g1)
    input_grad = (dx1 + dxn).astype(BF)

    layer_out = mm(perm, layer_out, ((0,), (0,))).astype(BF)
    input_grad = mm(perm, input_grad, ((0,), (0,))).astype(BF)

    smalls = lax.psum(jnp.stack([gg1, gb1, gg2, gb2] + gw), BOTH)
    mine = lax.dynamic_slice_in_dim(smalls, lax.axis_index(BOTH) * WR, WR, 1)
    ga = ga.reshape(4, C, S, WR, D).transpose(1, 2, 0, 3, 4)
    ga = lax.psum_scatter(ga.astype(BF), "dp", scatter_dimension=0, tiled=False)
    ga = lax.psum_scatter(ga, "shard", scatter_dimension=0, tiled=False).astype(F32)
    gup = gup.astype(F32)
    gup = gup.reshape(S, 3, WR, C, FR).transpose(1, 2, 3, 0, 4).reshape(3, WR, FF)

    tokens0 = count[0, 0].astype(jnp.int32)
    counts = jnp.stack([tokens0, T * ndev - tokens0])
    load_new = 0.9 * load_avg + 0.1 * counts.astype(F32) * E / (T * C * S)
    return (
        layer_out, input_grad, mine[0], mine[1], ga[0], ga[1], ga[2], ga[3], mine[2], mine[3],
        gup[0], gdn0, jnp.stack([mine[4], mine[5]], axis=1), jnp.stack([mine[6], mine[7]], axis=1),
        gup[1:], gdn12, counts, load_new,
    )


def pick(*args):
    S, C, WR, FR = lax.axis_size("shard"), lax.axis_size("dp"), args[7].shape[0], args[14].shape[0]
    fast = C == 2 and S % 4 == 0 and S >= 8 and WR % 16 == 0 and 128 % WR == 0 and FR % 128 == 0
    return (body if fast else body_plain)(*args)


def solution(mesh):
    row, vec = P(BOTH, None), P(BOTH)
    mid = P(None, BOTH, None)
    return jax.shard_map(
        pick,
        mesh=mesh,
        in_specs=(row, row, vec, vec, row, vec, vec, row, row, row, row, vec, vec, row, row, row, row, mid, mid, P()),
        out_specs=(row, row, vec, vec, row, row, row, row, vec, vec, row, row, row, row, mid, mid, P(), P()),
        check_vma=False,
    )
```

```python
import jax
import jax.numpy as jnp
from jax import lax
from jax.experimental import pallas as pl
from jax.experimental.pallas import tpu as pltpu
from jax.sharding import PartitionSpec as P

HEADS = 16
CAP = 74
BF = jnp.bfloat16
F32 = jnp.float32
BOTH = ("dp", "shard")
MESH = pl.DeviceIdType.MESH


def mm(a, b, dims=((1,), (0,))):
    return lax.dot_general(a, b, (dims, ((), ())), preferred_element_type=F32)


def layer_norm(values, gain, bias):
    centre = values - jnp.mean(values, axis=-1, keepdims=True)
    scale_inv = lax.rsqrt(jnp.mean(centre * centre, axis=-1, keepdims=True) + 1e-05)
    normed = centre * scale_inv
    return (normed * gain + bias, normed, scale_inv)


def norm_back(grad_out, normed, scale_inv, gain):
    grad_normed = grad_out * gain
    inner = grad_normed - jnp.mean(grad_normed, axis=-1, keepdims=True)
    inner = inner - normed * jnp.mean(grad_normed * normed, axis=-1, keepdims=True)
    return (scale_inv * inner, jnp.sum(grad_out * normed, axis=0), jnp.sum(grad_out, axis=0))


def gelu_pair(t):
    inner = 0.7978845608 * (t + 0.044715 * t * t * t)
    th = jnp.tanh(inner)
    val = 0.5 * t * (1.0 + th)
    der = 0.5 * (1.0 + th) + 0.5 * t * (1.0 - th * th) * 0.7978845608 * (1.0 + 3.0 * 0.044715 * t * t)
    return val, der


def ag(block):
    return lax.all_gather(block, "shard", axis=0, tiled=False)


def rs(parts):
    return lax.psum_scatter(parts.astype(BF), "shard", scatter_dimension=0, tiled=False).astype(F32)


def place_of():
    me = lax.axis_index("shard")
    core = lax.axis_index("dp")
    z, p = me // 4, me % 4
    xq = p + 1 - 2 * (p % 2)
    yq = p + 2 - 4 * (p // 2)
    return me, core, z, p, xq, yq, 3 - p


def greet(shards, core):
    bar = pltpu.get_barrier_semaphore()
    me = lax.axis_index("shard")

    @pl.loop(1, shards)
    def _(i):
        pl.semaphore_signal(bar, inc=1, device_id=(core, (me + i) % shards), device_id_type=MESH)

    pl.semaphore_signal(bar, inc=1, device_id=(1 - core, me), device_id_type=MESH)
    pl.semaphore_wait(bar, shards)


def remote(src, dst, send, recv, dev):
    return pltpu.make_async_remote_copy(
        src_ref=src, dst_ref=dst, send_sem=send, recv_sem=recv, device_id=dev, device_id_type=MESH
    )


def rows_loop(count, step, fn):
    @pl.loop(0, count // step)
    def _(i):
        fn(pl.multiple_of(i * step, step))


def ffn_kernel(
    h_ref, scal_ref, dy_ref, up_ref, dn_ref,
    y_out, dh_out, sc_out, gup_out, gdn0_out, gdn12_out,
    hall, scall, psc, screcv, wcol, scol, part, ra, rbx, rby, rd, final,
    pre, der, ub, dg, dm, m, yacc, dxacc, gdn, gup, sib_dn, sib_up, gsend, grecv,
    ag_s, ag_r, rs_s, rs_r, one_s, one_r, sm_s, sm_r,
):
    S, T, D = hall.shape
    F = up_ref.shape[2]
    L = S // 4
    LO = 80
    HI = T - LO
    me, core, z, p, xq, yq, dq = place_of()
    xn, yn = z * 4 + xq, z * 4 + yq
    sgn = 1 - 2 * (z // (L // 2))
    greet(S, core)

    def lev_of(k):
        return (z + k * sgn + L) % L

    def h_copy(kind, slot, src, idx, dev):
        return remote(src, hall.at[idx], ag_s.at[kind, slot], ag_r.at[kind, slot], (core, dev))

    @pl.loop(1, L)
    def _(k):
        lev = lev_of(k)
        remote(h_ref, hall.at[me], ag_s.at[0, lev], ag_r.at[0, z], (core, lev * 4 + p)).start()

    h_copy(1, z, h_ref, me, xn).start()
    h_copy(2, z, h_ref, me, yn).start()

    @pl.loop(1, S)
    def _(i):
        remote(scal_ref, scall.at[me], sm_s.at[0, i], sm_r.at[0], (core, (me + i) % S)).start()

    hall[me] = h_ref[...]
    scall[me] = scal_ref[...]
    gdn[...] = jnp.zeros_like(gdn)
    gup[...] = jnp.zeros_like(gup)
    remote(scall.at[pl.ds(0, S - 1)], scall.at[pl.ds(0, S - 1)], sm_s.at[0, 0], sm_r.at[0], (core, xn)).wait_recv()

    def stage_a(k):
        lev = lev_of(k)
        idx = lev * 4 + p
        h_copy(0, lev, hall.at[idx], idx, xn).wait_recv()
        h_copy(1, lev, hall.at[idx], idx, xn).start()
        h_copy(2, lev, hall.at[idx], idx, yn).start()

    def stage_b(k):
        lev = lev_of(k)
        odd = k % 2
        h_copy(1, lev, h_ref, lev * 4 + xq, xn).wait_recv()
        h_copy(2, lev, h_ref, lev * 4 + yq, yn).wait_recv()
        idx = lev * 4 + xq + odd * (yq - xq)
        h_copy(3, lev, hall.at[idx], idx, yn + odd * (xn - yn)).start()
        h_copy(3, lev, h_ref, lev * 4 + dq, xn).wait_recv()

    lane = lax.broadcasted_iota(jnp.int32, (16, 128), 1)

    def compute(lev):
        base = lev * 4
        for q in range(4):
            full = jnp.concatenate([scall[base + q], jnp.zeros((120, 128), F32)], axis=0)
            wcol[q] = full.T
        for e in range(3):
            n = LO if e else T
            off = HI if e == 2 else 0
            rows = 4 * n
            hm = hall[pl.ds(base, 4), off : off + n, :].reshape(rows, D)
            pre[0:rows, :] = mm(hm, up_ref[e])

            def act(r):
                val, d = gelu_pair(pre[pl.ds(r, 32), :])
                ub[pl.ds(r, 32), :] = val.astype(BF)
                der[pl.ds(r, 32), :] = d

            rows_loop(rows, 32, act)
            m[0:rows, :] = mm(ub[0:rows, :], dn_ref[e])
            for q in range(4):

                def elem(r):
                    at = pl.multiple_of(r + off, 16)
                    mine = pl.ds(pl.multiple_of(q * n + r, 16), 16)
                    t = pl.ds(pl.multiple_of(q * T + off + r, 16), 16)
                    w = wcol[q, pl.ds(at, 16), :][:, e : e + 1]
                    dyv = dy_ref[base + q, pl.ds(at, 16), :].astype(F32)
                    mv = m[mine, :]
                    s = jnp.sum(dyv * mv, axis=1, keepdims=True)
                    s = jnp.where(lane == e, s, 0.0)
                    dm[mine, :] = (dyv * w).astype(BF)
                    if e:
                        yacc[t, :] = yacc[t, :] + mv * w
                        scol[q, pl.ds(at, 16), :] = scol[q, pl.ds(at, 16), :] + s
                    else:
                        yacc[t, :] = mv * w
                        scol[q, pl.ds(at, 16), :] = s

                rows_loop(n, 16, elem)
            pre[0:rows, :] = mm(dm[0:rows, :], dn_ref[e], ((1,), (1,)))

            def back(r):
                dg[pl.ds(r, 32), :] = (pre[pl.ds(r, 32), :] * der[pl.ds(r, 32), :]).astype(BF)

            rows_loop(rows, 32, back)
            gdn[e] = gdn[e] + mm(ub[0:rows, :], dm[0:rows, :], ((0,), (0,)))
            gup[e] = gup[e] + mm(dg[0:rows, :], hm, ((0,), (0,)))
            if e:
                m[0:rows, :] = mm(dg[0:rows, :], up_ref[e], ((1,), (1,)))
                for q in range(4):

                    def addx(r):
                        t = pl.ds(pl.multiple_of(q * T + off + r, 16), 16)
                        dxacc[t, :] = dxacc[t, :] + m[pl.ds(pl.multiple_of(q * n + r, 16), 16), :]

                    rows_loop(n, 16, addx)
            else:
                dxacc[...] = mm(dg[...], up_ref[0], ((1,), (1,)))
        for q in range(4):
            psc[base + q] = scol[q].T[0:8, :]

            def out(r):
                t = pl.ds(pl.multiple_of(q * T + r, 16), 16)
                part[0, base + q, pl.ds(r, 16), :] = dxacc[t, :].astype(BF)
                part[1, base + q, pl.ds(r, 16), :] = yacc[t, :].astype(BF)

            rows_loop(T, 16, out)

    def r_copy(kind, a, lev, src, dst, dev):
        return remote(src, dst, rs_s.at[kind, a, lev], rs_r.at[kind, a, lev], (core, dev))

    def rs_a(k):
        lev = lev_of(k)
        odd = k % 2
        for a in range(2):
            r_copy(0, a, lev, part.at[a, lev * 4 + dq], ra.at[a, lev], yn + odd * (xn - yn)).start()

    def rs_b(k):
        lev = lev_of(k)
        odd = k % 2
        via = lev * 4 + xq + odd * (yq - xq)
        for a in range(2):
            r_copy(0, a, lev, ra.at[a, lev], ra.at[a, lev], xn).wait_recv()

            def add(r):
                t = pl.ds(r, 16)
                part[a, via, t, :] = (part[a, via, t, :].astype(F32) + ra[a, lev, t, :].astype(F32)).astype(BF)

            rows_loop(T, 16, add)
            r_copy(1, a, lev, part.at[a, lev * 4 + xq], rbx.at[a, lev], xn).start()
            r_copy(2, a, lev, part.at[a, lev * 4 + yq], rby.at[a, lev], yn).start()

    def rs_c(k):
        lev = lev_of(k)
        own = lev * 4 + p
        for a in range(2):
            r_copy(1, a, lev, rbx.at[a, lev], rbx.at[a, lev], xn).wait_recv()
            r_copy(2, a, lev, rby.at[a, lev], rby.at[a, lev], yn).wait_recv()

            def add(r):
                t = pl.ds(r, 16)
                tot = part[a, own, t, :].astype(F32) + rbx[a, lev, t, :].astype(F32) + rby[a, lev, t, :].astype(F32)

                @pl.when(k == 0)
                def _():
                    final[a, t, :] = tot

                @pl.when(k > 0)
                def _():
                    part[a, own, t, :] = tot.astype(BF)

            rows_loop(T, 16, add)

            @pl.when(k > 0)
            def _():
                remote(
                    part.at[a, own], rd.at[a, z], rs_s.at[3, a, lev], rs_r.at[3, a, z], (core, lev * 4 + p)
                ).start()

    stage_a(1)

    @pl.loop(0, L)
    def _(k):
        stage_b(k)

        @pl.when(k < L - 2)
        def _():
            stage_a(k + 2)

        compute(lev_of(k))
        rs_a(k)

        @pl.when(k > 0)
        def _():
            rs_c(k - 1)

        rs_b(k)

    half = D // 2
    other = pl.multiple_of((1 - core) * half, half)
    mine_d = pl.multiple_of(core * half, half)
    FR = F // 2
    other_f = pl.multiple_of((1 - core) * FR, FR)
    mine_f = pl.multiple_of(core * FR, FR)
    sib = (1 - core, me)
    c_up = remote(gup.at[:, :, pl.ds(other, half)], sib_up, one_s.at[0], one_r.at[0], sib)
    c_dn = remote(gdn.at[:, pl.ds(other_f, FR), :], sib_dn, one_s.at[1], one_r.at[1], sib)
    c_up.start()
    c_dn.start()

    @pl.loop(1, S)
    def _(i):
        to = (me + i) % S
        remote(psc.at[to], screcv.at[i], sm_s.at[1, i], sm_r.at[1], (core, to)).start()

    rs_c(L - 1)
    c_up.wait_recv()
    for e in range(3):
        tot = gup[e, :, pl.ds(mine_d, half)] + sib_up[e]
        gsend[e] = tot.T.astype(BF)
    WR = half // S
    screcv[0] = psc[me]

    def g_copy(i, to):
        return remote(
            gsend.at[:, pl.ds(pl.multiple_of(to * WR, WR), WR), :], grecv.at[me], sm_s.at[2, i], sm_r.at[2], (core, to)
        )

    @pl.loop(1, S)
    def _(i):
        g_copy(i, (me + i) % S).start()

    grecv[me] = gsend[:, pl.ds(pl.multiple_of(me * WR, WR), WR), :]
    c_dn.wait_recv()
    gdn0_out[...] = gdn[0, pl.ds(mine_f, FR), :] + sib_dn[0]
    for e in range(1, 3):
        gdn12_out[e - 1] = gdn[e, pl.ds(mine_f, FR), :] + sib_dn[e]

    @pl.loop(1, L)
    def _(k):
        lev = lev_of(k)
        for a in range(2):
            r_copy(3, a, lev, rd.at[a, lev], rd.at[a, lev], xn).wait_recv()

            def add(r):
                t = pl.ds(r, 16)
                final[a, t, :] = final[a, t, :] + rd[a, lev, t, :].astype(F32)

            rows_loop(T, 16, add)

    dh_out[...] = final[0]
    y_out[...] = final[1]
    remote(screcv.at[pl.ds(1, S - 1)], screcv.at[pl.ds(1, S - 1)], sm_s.at[1, 0], sm_r.at[1], (core, xn)).wait_recv()
    sc_out[...] = jnp.sum(screcv[...], axis=0)
    remote(grecv.at[pl.ds(0, S - 1)], grecv.at[pl.ds(0, S - 1)], sm_s.at[2, 0], sm_r.at[2], (core, xn)).wait_recv()
    gup_out[...] = grecv[...]

    c_up.wait_send()
    c_dn.wait_send()

    @pl.loop(1, S)
    def _(i):
        remote(scal_ref, scall.at[0], sm_s.at[0, i], sm_r.at[0], (core, xn)).wait_send()
        remote(psc.at[0], screcv.at[0], sm_s.at[1, i], sm_r.at[1], (core, xn)).wait_send()
        g_copy(i, (me + i) % S).wait_send()

    @pl.loop(0, L)
    def _(k):
        lev = lev_of(k)
        for kind in range(1, 4):
            h_copy(kind, lev, hall.at[0], 0, xn).wait_send()
        for a in range(2):
            for kind in range(3):
                r_copy(kind, a, lev, ra.at[a, 0], ra.at[a, 0], xn).wait_send()

        @pl.when(k > 0)
        def _():
            h_copy(0, lev, hall.at[0], 0, xn).wait_send()
            for a in range(2):
                r_copy(3, a, lev, ra.at[a, 0], ra.at[a, 0], xn).wait_send()


def ffn_call(h2b, scal, dy_all, ups, downs):
    S, T, D = dy_all.shape
    F = ups.shape[2]
    L = S // 4
    WR = D // 2 // S
    vm = pl.BlockSpec(memory_space=pltpu.VMEM)
    V = pltpu.VMEM
    dma = pltpu.SemaphoreType.DMA
    sds = jax.ShapeDtypeStruct
    return pl.pallas_call(
        ffn_kernel,
        out_shape=(
            sds((T, D), F32), sds((T, D), F32), sds((8, 128), F32), sds((S, 3, WR, F), BF),
            sds((F // 2, D), F32), sds((2, F // 2, D), F32),
        ),
        in_specs=[vm] * 5,
        out_specs=(vm,) * 6,
        scratch_shapes=[
            V((S, T, D), BF), V((S, 8, 128), F32), V((S, 8, 128), F32), V((S, 8, 128), F32),
            V((4, T, 128), F32), V((4, T, 128), F32),
            V((2, S, T, D), BF), V((2, L, T, D), BF), V((2, L, T, D), BF), V((2, L, T, D), BF), V((2, L, T, D), BF),
            V((2, T, D), F32),
            V((4 * T, F), F32), V((4 * T, F), F32), V((4 * T, F), BF), V((4 * T, F), BF), V((4 * T, D), BF),
            V((4 * T, D), F32), V((4 * T, D), F32), V((4 * T, D), F32),
            V((3, F, D), F32), V((3, F, D), F32), V((3, F // 2, D), F32), V((3, F, D // 2), F32),
            V((3, D // 2, F), BF), V((S, 3, WR, F), BF),
            dma((4, L)), dma((4, L)), dma((4, 2, L)), dma((4, 2, L)), dma((2,)), dma((2,)), dma((3, S)), dma((3,)),
        ],
        compiler_params=pltpu.CompilerParams(collective_id=2, has_side_effects=True, vmem_limit_bytes=64000000),
        cost_estimate=pl.CostEstimate(flops=15 * 10**9, bytes_accessed=20 * 2**20, transcendentals=2**20),
        name="ffn",
    )(h2b, scal, dy_all, ups, downs)


def tree_gather(at, own, ss, rs, dev, levels):
    core, z, p, xq, yq, dq = dev
    xn, yn = z * 4 + xq, z * 4 + yq
    me = z * 4 + p
    lev_of, L = levels

    def copy(kind, slot, src, idx, to):
        return remote(src, at(idx), ss.at[kind, slot], rs.at[kind, slot], (core, to))

    class Stages:
        @staticmethod
        def start():
            @pl.loop(1, L)
            def _(k):
                lev = lev_of(k)
                remote(own, at(me), ss.at[0, lev], rs.at[0, z], (core, lev * 4 + p)).start()

            copy(1, z, own, me, xn).start()
            copy(2, z, own, me, yn).start()

        @staticmethod
        def a(k):
            lev = lev_of(k)
            idx = lev * 4 + p
            copy(0, lev, own, idx, xn).wait_recv()
            copy(1, lev, at(idx), idx, xn).start()
            copy(2, lev, at(idx), idx, yn).start()

        @staticmethod
        def b(k):
            lev = lev_of(k)
            odd = k % 2
            copy(1, lev, own, lev * 4 + xq, xn).wait_recv()
            copy(2, lev, own, lev * 4 + yq, yn).wait_recv()
            idx = lev * 4 + xq + odd * (yq - xq)
            copy(3, lev, at(idx), idx, yn + odd * (xn - yn)).start()

        @staticmethod
        def c(k):
            lev = lev_of(k)
            copy(3, lev, own, lev * 4 + dq, xn).wait_recv()

        @staticmethod
        def finish():
            @pl.loop(0, L)
            def _(k):
                lev = lev_of(k)
                for kind in range(1, 4):
                    copy(kind, lev, own, me, xn).wait_send()

                @pl.when(k > 0)
                def _():
                    copy(0, lev, own, me, xn).wait_send()

    return Stages


def sort_matrix(ids_e, ids_s, T):
    zero = ids_e == 0
    n0 = jnp.sum(jnp.where(zero, 1.0, 0.0), axis=1, keepdims=True)
    slot = ids_s.astype(F32)
    pos = jnp.where(zero, slot, slot + n0)
    sub = lax.broadcasted_iota(jnp.int32, (T, T), 0).astype(F32)
    return jnp.where(sub == pos, 1.0, 0.0), n0


def attn_kernel(
    x_ref, dy_ref, doc_ref, e_ref, s_ref, small_ref, wq_ref, wk_ref, wv_ref, wo_ref,
    wu_ref, eu_ref, wd_ref, ed_ref,
    h2b_out, stat_out, scal_out, u1_out, u2_out, x1_out, dys_out, q_out, k_out, v_out, p_out, o_out,
    small_out, count_out, w_out, dyall_out, up_out, dn_out,
    wbuf, smallbuf, h1b, bias, xs, tmp,
    ag_s, ag_r, sib_s, sib_r, sm_s, sm_r, loc,
):
    T, D = x_ref.shape
    WR = wq_ref.shape[0]
    FR = wd_ref.shape[0]
    N = wbuf.shape[1]
    S = N // 2
    L = S // 4
    me, core, z, p, xq, yq, dq = place_of()
    xn = z * 4 + xq
    sgn = 1 - 2 * (z // (L // 2))
    my = core * S + me
    sib = (1 - core, me)
    greet(S, core)

    def lev_of(k):
        return (z + k * sgn + L) % L

    dev, levels = (core, z, p, xq, yq, dq), (lev_of, L)

    def w1_at(i):
        return wbuf.at[pl.ds(0, 3), core * S + i]

    def w2_at(i):
        return wbuf.at[3, core * S + i]

    w1 = tree_gather(w1_at, w1_at(me), ag_s.at[0], ag_r.at[0], dev, levels)
    w2 = tree_gather(w2_at, w2_at(me), ag_s.at[1], ag_r.at[1], dev, levels)
    dyg = tree_gather(lambda i: dyall_out.at[i], dys_out, ag_s.at[2], ag_r.at[2], dev, levels)

    for i, w in enumerate((wq_ref, wk_ref, wv_ref, wo_ref)):
        wbuf[i, my] = w[...]
    w1.start()

    perm, n0 = sort_matrix(e_ref[...], s_ref[...], T)
    smallbuf[my, 0:8, :] = small_ref[...]
    lane8 = lax.broadcasted_iota(jnp.int32, (8, 128), 1)
    smallbuf[my, 8:16, :] = jnp.where(lane8 == 0, jnp.broadcast_to(n0, (8, 128)), 0.0)

    @pl.loop(1, S)
    def _(i):
        remote(smallbuf.at[my], smallbuf.at[my], sm_s.at[0, i], sm_r.at[0], (core, (me + i) % S)).start()

    def dn_own(e0, n, src):
        dst = dn_out.at[pl.ds(e0, n), pl.ds(pl.multiple_of(core * FR, FR), FR), :]
        return src, dst

    d0 = dn_own(0, 1, wd_ref)
    d0 = (wd_ref, dn_out.at[0, pl.ds(pl.multiple_of(core * FR, FR), FR), :])
    d1 = dn_own(1, 2, ed_ref)
    dn_copies = []
    for j, (src, dst) in enumerate((d0, d1)):
        r = remote(src, dst, sib_s.at[2, j], sib_r.at[2, j], sib)
        lc = pltpu.make_async_copy(src, dst, loc.at[j])
        r.start()
        lc.start()
        dn_copies.append((r, lc))

    permb = perm.astype(BF)
    xs[...] = mm(permb, x_ref[...])
    dys_out[...] = mm(permb, dy_ref[...]).astype(BF)
    dy_local = pltpu.make_async_copy(dys_out, dyall_out.at[me], loc.at[2])
    dy_local.start()

    docs = (doc_ref[...] == lax.broadcasted_iota(jnp.int32, (16, T), 0)).astype(F32).astype(BF)
    docs = mm(docs, permb, ((1,), (1,))).astype(BF)
    same = mm(docs, docs, ((0,), (0,)))
    place = lax.broadcasted_iota(jnp.int32, (T, T), 1).astype(F32)
    ord_col = jnp.sum(perm * place, axis=1, keepdims=True)
    ord_row = mm(place[0:16, :].astype(BF), permb, ((1,), (1,)))[0:1, :]
    bias[...] = jnp.where((same > 0.5) & (ord_row <= ord_col), 0.0, -1e30)

    lane = lax.broadcasted_iota(jnp.int32, (16, 128), 1)

    def norm1(r):
        t = pl.ds(r, 16)
        v = xs[t, :]
        cen = v - jnp.mean(v, axis=1, keepdims=True)
        inv = lax.rsqrt(jnp.mean(cen * cen, axis=1, keepdims=True) + 1e-05)
        u1_out[t, :] = cen * inv
        stat_out[t, :] = jnp.where(lane == 8, inv, 0.0)

    rows_loop(T, 16, norm1)

    w1.a(1)
    w1.b(0)
    w1.a(2)
    w1.b(1)

    group = 128 // WR
    remote(smallbuf.at[pl.ds(0, S - 1)], smallbuf.at[pl.ds(0, S - 1)], sm_s.at[0, 0], sm_r.at[0], (core, xn)).wait_recv()
    mine_small = smallbuf.at[pl.ds(core * S, S)]
    c_small = remote(mine_small, mine_small, sib_s.at[2, 2], sib_r.at[2, 2], sib)
    c_small.start()

    def w1_sib(lev, who):
        b = wbuf.at[pl.ds(0, 3), pl.ds(who * S + lev * 4, 4)]
        return remote(b, b, sib_s.at[0, lev], sib_r.at[0, lev], sib)

    def w2_sib(lev, who):
        b = wbuf.at[3, pl.ds(who * S + lev * 4, 4)]
        return remote(b, b, sib_s.at[1, lev], sib_r.at[1, lev], sib)

    def c1(k):
        w1.c(k)
        w1_sib(lev_of(k), core).start()

    def c2(k):
        w2.c(k)
        w2_sib(lev_of(k), core).start()

    for k in range(3, L):
        w1.a(k)
    c1(0)
    w2.start()
    for k in range(2, L):
        w1.b(k)
        c1(k - 1)

    def up_copy(e, h, i):
        to = (me + i) % S
        src = wu_ref if e == 0 else eu_ref.at[e - 1]
        return remote(
            src.at[:, pl.ds(pl.multiple_of((h * S + to) * FR, FR), FR)],
            up_out.at[e, pl.ds(pl.multiple_of(my * WR, WR), WR), pl.ds(h * FR, FR)],
            sm_s.at[1, i], sm_r.at[1], (core, to),
        )

    def up_local(e, h):
        src = wu_ref if e == 0 else eu_ref.at[e - 1]
        return pltpu.make_async_copy(
            src.at[:, pl.ds(pl.multiple_of((h * S + me) * FR, FR), FR)],
            up_out.at[e, pl.ds(pl.multiple_of(my * WR, WR), WR), pl.ds(h * FR, FR)],
            loc.at[4 + 2 * e + h],
        )

    @pl.loop(1, S)
    def _(i):
        for e in range(3):
            for h in range(2):
                up_copy(e, h, i).start()

    for e in range(3):
        for h in range(2):
            up_local(e, h).start()

    c_small.wait_recv()
    for g in range(D // 128):
        part = smallbuf[g * group, 0:8, :]
        for j in range(1, group):
            part = part + smallbuf[g * group + j, 0:8, :]
        small_out[:, g * 128 : (g + 1) * 128] = part
    cnt = smallbuf[0, 8:16, :]
    for i in range(1, N):
        cnt = cnt + smallbuf[i, 8:16, :]
    count_out[...] = cnt

    def norm1b(r):
        t = pl.ds(r, 16)
        h1b[t, :] = (u1_out[t, :] * small_out[0:1, :] + small_out[1:2, :]).astype(BF)

    rows_loop(T, 16, norm1b)
    c1(L - 1)
    w2.a(1)
    w2.b(0)
    for k in range(L):
        w1_sib(lev_of(k), 1 - core).wait_recv()

    def full(i):
        return wbuf[i].reshape(D, D)

    tmp[...] = mm(h1b[...], full(0))
    q_out[...] = (tmp[...] * 0.125).astype(BF)
    for k in range(2, L):
        w2.a(k)
    w2.b(1)
    tmp[...] = mm(h1b[...], full(1))
    k_out[...] = tmp[...].astype(BF)
    c2(0)
    dyg.start()
    for k in range(2, L):
        w2.b(k)
        c2(k - 1)
    tmp[...] = mm(h1b[...], full(2))
    v_out[...] = tmp[...].astype(BF)
    c2(L - 1)
    dyg.a(1)
    dyg.b(0)

    low = lax.broadcasted_iota(jnp.int32, (T, 128), 1) < 64
    lowb = low.astype(F32).astype(BF)
    highb = (1.0 - low.astype(F32)).astype(BF)

    def heads(j):
        ln = pl.ds(pl.multiple_of(j * 128, 128), 128)
        qp = q_out[:, ln]
        q2 = jnp.concatenate([qp * lowb, qp * highb], axis=0)
        s = mm(q2, k_out[:, ln], ((1,), (1,)))
        s = s + jnp.concatenate([bias[...], bias[...]], axis=0)
        ex = jnp.exp(s - jnp.max(s, axis=1, keepdims=True))
        pr = ex / jnp.sum(ex, axis=1, keepdims=True)
        p_out[j] = pr
        o2 = mm(pr.astype(BF), v_out[:, ln])
        o_out[:, ln] = jnp.where(low, o2[0:T], o2[T:]).astype(BF)

    half = D // 256

    @pl.loop(0, half)
    def _(j):
        heads(j)

    dyg.a(2)
    dyg.b(1)

    @pl.loop(half, 2 * half)
    def _(j):
        heads(j)

    for k in range(3, L):
        dyg.a(k)
    for k in range(L):
        w2_sib(lev_of(k), 1 - core).wait_recv()
    w_save = pltpu.make_async_copy(wbuf, w_out, loc.at[3])
    w_save.start()
    tmp[...] = mm(o_out[...], full(3))

    def norm2(r):
        t = pl.ds(r, 16)
        v = xs[t, :] + tmp[t, :]
        x1_out[t, :] = v
        cen = v - jnp.mean(v, axis=1, keepdims=True)
        inv = lax.rsqrt(jnp.mean(cen * cen, axis=1, keepdims=True) + 1e-05)
        u = cen * inv
        u2_out[t, :] = u
        h2 = u * small_out[2:3, :] + small_out[3:4, :]
        h2b_out[t, :] = h2.astype(BF)
        lg = [jnp.sum(h2 * small_out[i : i + 1, :], axis=1, keepdims=True) for i in range(4, 8)]

        def soft(a, b):
            mx = jnp.maximum(a, b)
            ea, eb = jnp.exp(a - mx), jnp.exp(b - mx)
            return ea / (ea + eb), eb / (ea + eb)

        r0, r1 = soft(lg[0], lg[1])
        k0, k1 = soft(lg[2], lg[3])
        row = (lax.broadcasted_iota(jnp.int32, (16, 1), 0) + r).astype(F32)
        is0 = row < n0
        gate = jnp.where(is0, r0, r1)
        we = k0 * gate
        cols = (k1, jnp.where(is0, we, 0.0), jnp.where(is0, 0.0, we), k0, gate, r0, r1)
        st = stat_out[t, :] + jnp.where(lane == 9, inv, 0.0)
        for i, col in enumerate(cols):
            st = st + jnp.where(lane == i, col, 0.0)
        stat_out[t, :] = st

    rows_loop(T, 16, norm2)
    scal_out[...] = stat_out[...].T[0:8, :]

    for k in range(2, L):
        dyg.b(k)
    for k in range(L):
        dyg.c(k)

    got = up_out.at[:, pl.ds(0, (S - 1) * WR), :]
    remote(got, got, sm_s.at[1, 0], sm_r.at[1], (core, xn)).wait_recv()
    for e in range(3):
        for h in range(2):
            up_local(e, h).wait()
    mine_up = up_out.at[:, pl.ds(pl.multiple_of(core * S * WR, S * WR), S * WR), :]
    c_up = remote(mine_up, mine_up, sib_s.at[2, 3], sib_r.at[2, 3], sib)
    c_up.start()
    c_up.wait()
    w_save.wait()
    dy_local.wait()
    for r, lc in dn_copies:
        r.wait()
        lc.wait()
    c_small.wait_send()
    w1.finish()
    w2.finish()
    dyg.finish()

    @pl.loop(0, L)
    def _(k):
        w1_sib(k, core).wait_send()
        w2_sib(k, core).wait_send()

    @pl.loop(1, S)
    def _(i):
        remote(smallbuf.at[my], smallbuf.at[my], sm_s.at[0, i], sm_r.at[0], (core, xn)).wait_send()
        for e in range(3):
            for h in range(2):
                up_copy(e, h, i).wait_send()


def attn_call(x, dy, docs, es, ss, small, ws, wu, eu, wd, ed, S):
    T, D = x.shape
    WR, FR = ws[0].shape[0], wd.shape[0]
    L = S // 4
    N = 2 * S
    vm = pl.BlockSpec(memory_space=pltpu.VMEM)
    hb = pl.BlockSpec(memory_space=pl.ANY)
    V = pltpu.VMEM
    dma = pltpu.SemaphoreType.DMA
    sds = jax.ShapeDtypeStruct
    row = sds((T, D), BF)
    rowf = sds((T, D), F32)
    return pl.pallas_call(
        attn_kernel,
        out_shape=(
            row, sds((T, 128), F32), sds((8, T), F32), rowf, rowf, rowf, row, row, row, row,
            sds((D // 128, 2 * T, T), F32), row, sds((8, D), F32), sds((8, 128), F32),
            sds((4, N, WR, D), BF), sds((S, T, D), BF), sds((3, D, 2 * FR), BF), sds((3, 2 * FR, D), BF),
        ),
        in_specs=[vm] * 10 + [hb] * 4,
        out_specs=(vm,) * 14 + (hb,) * 4,
        scratch_shapes=[
            V((4, N, WR, D), BF), V((N, 16, 128), F32), V((T, D), BF), V((T, T), F32), V((T, D), F32), V((T, D), F32),
            dma((3, 4, L)), dma((3, 4, L)), dma((3, max(L, 4))), dma((3, max(L, 4))), dma((2, S)), dma((2,)), dma((10,)),
        ],
        compiler_params=pltpu.CompilerParams(collective_id=1, has_side_effects=True, vmem_limit_bytes=60000000),
        cost_estimate=pl.CostEstimate(flops=2 * 10**9, bytes_accessed=40 * 2**20, transcendentals=2**20),
        name="attn",
    )(x, dy, docs, es, ss, small, *ws, wu, eu, wd, ed)


def tree_scatter(part, ra, rbx, rby, rd, final, ss, rs, dev, levels):
    core, z, p, xq, yq, dq = dev
    xn, yn = z * 4 + xq, z * 4 + yq
    lev_of, L = levels
    R = part.shape[1]

    def copy(kind, lev, src, dst, to):
        return remote(src, dst, ss.at[kind, lev], rs.at[kind, lev], (core, to))

    class Stages:
        @staticmethod
        def a(k):
            lev = lev_of(k)
            odd = k % 2
            copy(0, lev, part.at[lev * 4 + dq], ra.at[lev], yn + odd * (xn - yn)).start()

        @staticmethod
        def b(k):
            lev = lev_of(k)
            odd = k % 2
            via = lev * 4 + xq + odd * (yq - xq)
            copy(0, lev, ra.at[lev], ra.at[lev], xn).wait_recv()

            def add(r):
                t = pl.ds(r, 16)
                part[via, t, :] = (part[via, t, :].astype(F32) + ra[lev, t, :].astype(F32)).astype(BF)

            rows_loop(R, 16, add)
            copy(1, lev, part.at[lev * 4 + xq], rbx.at[lev], xn).start()
            copy(2, lev, part.at[lev * 4 + yq], rby.at[lev], yn).start()

        @staticmethod
        def c(k):
            lev = lev_of(k)
            own = lev * 4 + p
            copy(1, lev, rbx.at[lev], rbx.at[lev], xn).wait_recv()
            copy(2, lev, rby.at[lev], rby.at[lev], yn).wait_recv()

            def add(r):
                t = pl.ds(r, 16)
                tot = part[own, t, :].astype(F32) + rbx[lev, t, :].astype(F32) + rby[lev, t, :].astype(F32)

                @pl.when(k == 0)
                def _():
                    final[t, :] = tot

                @pl.when(k > 0)
                def _():
                    part[own, t, :] = tot.astype(BF)

            rows_loop(R, 16, add)

            @pl.when(k > 0)
            def _():
                remote(part.at[own], rd.at[z], ss.at[3, lev], rs.at[3, z], (core, lev * 4 + p)).start()

        @staticmethod
        def d(k):
            lev = lev_of(k)
            copy(3, lev, rd.at[lev], rd.at[lev], xn).wait_recv()

            def add(r):
                t = pl.ds(r, 16)
                final[t, :] = final[t, :] + rd[lev, t, :].astype(F32)

            rows_loop(R, 16, add)

        @staticmethod
        def finish():
            @pl.loop(0, L)
            def _(k):
                lev = lev_of(k)
                for kind in range(3):
                    copy(kind, lev, ra.at[0], ra.at[0], xn).wait_send()

                @pl.when(k > 0)
                def _():
                    copy(3, lev, ra.at[0], ra.at[0], xn).wait_send()

    return Stages


def back_kernel(
    dh_ref, y_ref, sc_ref, small_ref, stat_ref, u1_ref, u2_ref, x1_ref, dys_ref,
    q_ref, k_ref, v_ref, p_ref, o_ref, e_ref, s_ref, w_hbm,
    lo_out, ig_out, gqkv_out, go_out, smalls_out,
    wbuf, perm, accs, dx1, dab, do, dq, dk, dv, h1b, dh1, tmpb, keep, send, recv,
    part0, ra0, rbx0, rby0, rd0, part1, ra1, rbx1, rby1, rd1, smine, ssib, srecv,
    rs_s, rs_r, sib_s, sib_r, sm_s, sm_r, loc,
):
    T, D = dh_ref.shape
    S, WR = part0.shape[0], part0.shape[1]
    L = S // 4
    half = D // 2
    me, core, z, p, xq, yq, dgq = place_of()
    xn = z * 4 + xq
    sgn = 1 - 2 * (z // (L // 2))
    sib = (1 - core, me)
    greet(S, core)

    def lev_of(k):
        return (z + k * sgn + L) % L

    dev, levels = (core, z, p, xq, yq, dgq), (lev_of, L)
    g0 = tree_scatter(part0, ra0, rbx0, rby0, rd0, go_out, rs_s.at[0], rs_r.at[0], dev, levels)
    g1 = tree_scatter(part1, ra1, rbx1, rby1, rd1, gqkv_out, rs_s.at[1], rs_r.at[1], dev, levels)
    loads = [pltpu.make_async_copy(w_hbm.at[i], wbuf.at[i], loc.at[i]) for i in range(4)]
    for i in (3, 0, 1, 2):
        loads[i].start()

    perm_f, n0 = sort_matrix(e_ref[...], s_ref[...], T)
    perm[...] = perm_f.astype(BF)
    accs[...] = jnp.zeros_like(accs)
    scol = jnp.concatenate([sc_ref[...], jnp.zeros((120, 128), F32)], axis=0).T
    dh1[:, 0:128] = scol

    def acc(i, v):
        accs[i] = accs[i] + (v[0:8] + v[8:16])

    def norm2(r):
        t = pl.ds(r, 16)
        st = stat_ref[t, :]
        c1, c0, gate, r0, r1, inv = (st[:, i : i + 1] for i in (0, 3, 4, 5, 6, 9))
        row = (lax.broadcasted_iota(jnp.int32, (16, 1), 0) + r).astype(F32)
        is0 = row < n0
        s3 = dh1[t, 0:128]
        sm = s3[:, 0:1]
        se = jnp.where(is0, s3[:, 1:2], s3[:, 2:3])
        dc0, dc1 = gate * se, sm
        tot = c0 * dc0 + c1 * dc1
        dcl0, dcl1 = c0 * (dc0 - tot), c1 * (dc1 - tot)
        dgate = c0 * se
        dr0, dr1 = jnp.where(is0, dgate, 0.0), jnp.where(is0, 0.0, dgate)
        tot = r0 * dr0 + r1 * dr1
        drl0, drl1 = r0 * (dr0 - tot), r1 * (dr1 - tot)
        u2 = u2_ref[t, :]
        h2 = u2 * small_ref[2:3, :] + small_ref[3:4, :]
        dh2 = dh_ref[t, :]
        for i, d in enumerate((drl0, drl1, dcl0, dcl1)):
            acc(4 + i, h2 * d)
            dh2 = dh2 + d * small_ref[4 + i : 5 + i, :]
        acc(2, dh2 * u2)
        acc(3, dh2)
        e = dh2 * small_ref[2:3, :]
        inner = e - jnp.mean(e, axis=1, keepdims=True) - u2 * jnp.mean(e * u2, axis=1, keepdims=True)
        g = dys_ref[t, :].astype(F32) + inv * inner
        dx1[t, :] = g
        dab[t, :] = g.astype(BF)
        tmpb[t, :] = (x1_ref[t, :] + y_ref[t, :]).astype(BF)
        h1b[t, :] = (u1_ref[t, :] * small_ref[0:1, :] + small_ref[1:2, :]).astype(BF)

    rows_loop(T, 16, norm2)

    other = pl.multiple_of((1 - core) * half, half)
    mine = pl.multiple_of(core * half, half)

    def weight_grad(i, left, right):
        send[i] = mm(left[:, pl.ds(other, half)], right[...], ((0,), (0,))).astype(BF)
        c = remote(send.at[i], recv.at[i], sib_s.at[i], sib_r.at[i], sib)
        c.start()
        keep[i] = mm(left[:, pl.ds(mine, half)], right[...], ((0,), (0,)))
        return c

    def join(i, c, part, at):
        c.wait_recv()

        @pl.loop(0, S)
        def _(j):
            t = pl.ds(pl.multiple_of(j * WR, WR), WR)
            part[j, at : at + WR, :] = (keep[i, t, :] + recv[i, t, :].astype(F32)).astype(BF)

    c_o = weight_grad(3, o_ref, dab)
    loads[3].wait()
    do[...] = mm(dab[...], wbuf[3], ((1,), (1,))).astype(BF)
    join(3, c_o, part0, 0)
    for k in reversed(range(L)):
        g0.a(k)

    lo_out[...] = mm(perm[...], tmpb[...], ((0,), (0,))).astype(BF)

    low = lax.broadcasted_iota(jnp.int32, (T, 128), 1) < 64
    lowb = low.astype(F32).astype(BF)
    highb = (1.0 - low.astype(F32)).astype(BF)

    def heads(j):
        ln = pl.ds(pl.multiple_of(j * 128, 128), 128)
        qp, dop = q_ref[:, ln], do[:, ln]
        q2 = jnp.concatenate([qp * lowb, qp * highb], axis=0)
        do2 = jnp.concatenate([dop * lowb, dop * highb], axis=0)
        pr = p_ref[j]
        dp = mm(do2, v_ref[:, ln], ((1,), (1,)))
        ds = (pr * (dp - jnp.sum(pr * dp, axis=1, keepdims=True))).astype(BF)
        dq2 = mm(ds, k_ref[:, ln])
        dq[:, ln] = jnp.where(low, dq2[0:T], dq2[T:]).astype(BF) * BF(0.125)
        dk[:, ln] = mm(ds, q2, ((0,), (0,))).astype(BF)
        dv[:, ln] = mm(pr.astype(BF), do2, ((0,), (0,))).astype(BF)

    @pl.loop(0, D // 128)
    def _(j):
        heads(j)

    c_v = weight_grad(2, h1b, dv)
    c_k = weight_grad(1, h1b, dk)
    c_q = weight_grad(0, h1b, dq)
    for k in reversed(range(L)):
        g0.b(k)
    join(2, c_v, part1, 2 * WR)
    join(1, c_k, part1, WR)
    join(0, c_q, part1, 0)
    for k in reversed(range(L)):
        g1.a(k)
    for i in range(3):
        loads[i].wait()
    dh1[...] = mm(dq[...], wbuf[0], ((1,), (1,)))
    dh1[...] = dh1[...] + mm(dk[...], wbuf[1], ((1,), (1,)))
    dh1[...] = dh1[...] + mm(dv[...], wbuf[2], ((1,), (1,)))
    for k in reversed(range(L)):
        g0.c(k)

    def norm1(r):
        t = pl.ds(r, 16)
        inv = stat_ref[t, :][:, 8:9]
        u = u1_ref[t, :]
        d = dh1[t, :]
        acc(0, d * u)
        acc(1, d)
        e = d * small_ref[0:1, :]
        inner = e - jnp.mean(e, axis=1, keepdims=True) - u * jnp.mean(e * u, axis=1, keepdims=True)
        tmpb[t, :] = (dx1[t, :] + inv * inner).astype(BF)

    rows_loop(T, 16, norm1)
    for i in range(8):
        smine[i : i + 1, :] = jnp.sum(accs[i], axis=0, keepdims=True)
    c_s = remote(smine, ssib, sib_s.at[4], sib_r.at[4], sib)
    c_s.start()
    for k in reversed(range(L)):
        g1.b(k)
    ig_out[...] = mm(perm[...], tmpb[...], ((0,), (0,))).astype(BF)
    c_s.wait()
    smine[...] = smine[...] + ssib[...]
    group = 128 // WR

    def s_at(i):
        return smine.at[:, pl.ds(pl.multiple_of((core * S + i) // group * 128, 128), 128)]

    def s_copy(i):
        to = (me + i) % S
        return remote(s_at(to), srecv.at[me], sm_s.at[i], sm_r.at[0], (core, to))

    @pl.loop(1, S)
    def _(i):
        s_copy(i).start()

    srecv[me] = s_at(me)[...]
    for k in reversed(range(L)):
        g1.c(k)
    for k in range(1, L):
        g0.d(k)
    allr = srecv.at[pl.ds(0, S - 1)]
    remote(allr, allr, sm_s.at[0], sm_r.at[0], (core, xn)).wait_recv()
    smalls_out[...] = jnp.sum(srecv[...], axis=0)
    for k in range(1, L):
        g1.d(k)
    g0.finish()
    g1.finish()
    for c in (c_o, c_v, c_k, c_q):
        c.wait_send()

    @pl.loop(1, S)
    def _(i):
        s_copy(i).wait_send()


def back_call(dh, y, sc, small, stat, u1, u2, x1, dys, q, k, v, p, o, es, ss, wa, S):
    T, D = dh.shape
    WR = D // (2 * S)
    L = S // 4
    vm = pl.BlockSpec(memory_space=pltpu.VMEM)
    hb = pl.BlockSpec(memory_space=pl.ANY)
    V = pltpu.VMEM
    dma = pltpu.SemaphoreType.DMA
    sds = jax.ShapeDtypeStruct
    row = V((T, D), BF)

    def rs_bufs(R):
        return [V((S, R, D), BF)] + [V((L, R, D), BF)] * 4

    return pl.pallas_call(
        back_kernel,
        out_shape=(
            sds((T, D), BF), sds((T, D), BF), sds((3 * WR, D), F32), sds((WR, D), F32), sds((8, 128), F32),
        ),
        in_specs=[vm] * 16 + [hb],
        out_specs=(vm,) * 5,
        scratch_shapes=[
            V((4, D, D), BF), V((T, T), BF), V((8, 8, D), F32), V((T, D), F32), row, row, row, row, row, row,
            V((T, D), F32), row, V((4, D // 2, D), F32), V((4, D // 2, D), BF), V((4, D // 2, D), BF),
        ]
        + rs_bufs(WR)
        + rs_bufs(3 * WR)
        + [
            V((8, D), F32), V((8, D), F32), V((S, 8, 128), F32),
            dma((2, 4, L)), dma((2, 4, L)), dma((5,)), dma((5,)), dma((S,)), dma((1,)), dma((4,)),
        ],
        compiler_params=pltpu.CompilerParams(collective_id=3, has_side_effects=True, vmem_limit_bytes=60000000),
        cost_estimate=pl.CostEstimate(flops=4 * 10**9, bytes_accessed=20 * 2**20, transcendentals=2**20),
        name="back",
    )(dh, y, sc, small, stat, u1, u2, x1, dys, q, k, v, p, o, es, ss, wa)


def body_plain(
    hidden_in, doc_ids, expert_ids, slot_ids, out_grad, ln1_gain, ln1_bias, w_query, w_key, w_value,
    w_out, ln2_gain, ln2_bias, w_up, w_down, w_router, w_mix, expert_up, expert_down, load_avg,
):
    T, D = hidden_in.shape
    H, HD = HEADS, D // HEADS
    S = lax.axis_size("shard")
    C = lax.axis_size("dp")
    WR = w_query.shape[0]
    FF = w_up.shape[1]
    FR = w_down.shape[0]
    F = FR * C
    E = expert_up.shape[0]
    LO, HI = 80, T - 80

    pos = jnp.where(expert_ids == 0, slot_ids, jnp.sum((expert_ids == 0).astype(jnp.int32)) + slot_ids)
    n0 = jnp.sum((expert_ids == 0).astype(jnp.int32))
    place = lax.iota(jnp.int32, T)
    perm = (pos[None, :] == place[:, None]).astype(BF)
    xs = mm(perm, hidden_in)
    dys = mm(perm, out_grad).astype(BF)
    doc = doc_ids[0]
    allowed = (place[None, :] <= place[:, None]) & (doc[:, None] == doc[None, :])
    allowed = mm(mm(perm, allowed.astype(BF)).astype(BF), perm, ((1,), (1,))) > 0.5
    is0 = (place < n0)[:, None]

    small = jnp.stack(
        [ln1_gain, ln1_bias, ln2_gain, ln2_bias, w_router[:, 0], w_router[:, 1], w_mix[:, 0], w_mix[:, 1]]
    ).astype(F32)
    small = lax.all_gather(small, BOTH, axis=1, tiled=True)
    g1, b1, g2, b2 = small[0], small[1], small[2], small[3]
    wr, wm = small[4:6], small[6:8]

    wa = jnp.stack([w_query, w_key, w_value, w_out])
    wa = lax.all_gather(wa, BOTH, axis=1, tiled=True)
    wq, wk, wv, wo = wa[0], wa[1], wa[2], wa[3]

    ups = jnp.stack([w_up, expert_up[0], expert_up[1]])
    ups = ups.reshape(3, WR, C, S, FR).transpose(3, 0, 1, 2, 4).reshape(S, 3, WR, F)
    ups = lax.all_to_all(ups, "shard", 0, 0)
    ups = lax.all_gather(ups, "dp", axis=0)
    ups = ups.transpose(2, 0, 1, 3, 4).reshape(3, D, F)
    downs = jnp.stack([w_down, expert_down[0], expert_down[1]])
    downs = lax.all_gather(downs, "dp", axis=1, tiled=True)

    dy_all = ag(dys)

    n1, u1, i1 = layer_norm(xs, g1, b1)
    h1b = n1.astype(BF)
    q = (mm(h1b, wq) * 0.125).astype(BF).reshape(T, H, HD)
    k = mm(h1b, wk).astype(BF).reshape(T, H, HD)
    v = mm(h1b, wv).astype(BF).reshape(T, H, HD)
    s = jnp.einsum("ihd,jhd->hij", q, k, preferred_element_type=F32)
    s = jnp.where(allowed[None], s, -1e30)
    ex = jnp.exp(s - jnp.max(s, axis=-1, keepdims=True))
    p = ex / jnp.sum(ex, axis=-1, keepdims=True)
    pb = p.astype(BF)
    o = jnp.einsum("hij,jhd->ihd", pb, v, preferred_element_type=F32).reshape(T, D).astype(BF)
    x1 = xs + mm(o, wo)
    h2, u2, i2 = layer_norm(x1, g2, b2)
    h2b = h2.astype(BF)

    def two(w):
        return jnp.stack([jnp.sum(h2 * w[0], axis=-1), jnp.sum(h2 * w[1], axis=-1)], axis=-1)

    r = jax.nn.softmax(two(wr), axis=-1)
    c = jax.nn.softmax(two(wm), axis=-1)
    gate = jnp.where(is0, r[:, 0:1], r[:, 1:2])
    c0, c1 = c[:, 0:1], c[:, 1:2]
    we = c0 * gate
    scal = jnp.concatenate([c1, jnp.where(is0, we, 0.0), jnp.where(is0, 0.0, we)], axis=1)

    h_all = ag(h2b)
    scal_all = ag(scal)

    def cut(a, e):
        return (a[:, :LO] if e == 1 else a[:, HI:]) if e else a

    partial_y = jnp.zeros((S, T, D), F32)
    partial_dh = jnp.zeros((S, T, D), F32)
    score = []
    gup, gdown = [], []
    for e in range(3):
        he = cut(h_all, e)
        dye = cut(dy_all, e).astype(F32)
        se = cut(scal_all, e)[:, :, e : e + 1]
        n = he.shape[1]
        hf = he.reshape(S * n, D)
        pre = mm(hf, ups[e])
        val, der = gelu_pair(pre)
        ub = val.astype(BF)
        m = mm(ub, downs[e]).reshape(S, n, D)
        dm = (dye * se).astype(BF).reshape(S * n, D)
        dg = (mm(dm, downs[e], ((1,), (1,))) * der).astype(BF)
        gdown.append(mm(ub, dm, ((0,), (0,))))
        gup.append(mm(hf, dg, ((0,), (0,))))
        dx = mm(dg, ups[e], ((1,), (1,))).reshape(S, n, D)
        y = m * se
        sc = jnp.sum(dye * m, axis=-1)
        pad = [(0, 0), (0, T - n) if e < 2 else (T - n, 0)]
        live = is0[None, :, 0]
        partial_y += jnp.pad(y, pad + [(0, 0)])
        partial_dh += jnp.pad(dx, pad + [(0, 0)])
        score.append(jnp.pad(sc, pad))
    yfull = rs(partial_y)
    dh2 = rs(partial_dh)
    sc = lax.psum_scatter(jnp.stack(score, axis=1), "shard", scatter_dimension=0, tiled=False)
    sm = sc[0][:, None]
    se = jnp.where(is0, sc[1][:, None], sc[2][:, None])

    dc0, dc1 = gate * se, sm
    tot = c0 * dc0 + c1 * dc1
    dcl0, dcl1 = c0 * (dc0 - tot), c1 * (dc1 - tot)
    dgate = c0 * se
    dr0, dr1 = jnp.where(is0, dgate, 0.0), jnp.where(is0, 0.0, dgate)
    tot = r[:, 0:1] * dr0 + r[:, 1:2] * dr1
    drl0, drl1 = r[:, 0:1] * (dr0 - tot), r[:, 1:2] * (dr1 - tot)
    layer_out = (x1 + yfull).astype(BF)
    dh2 = dh2 + drl0 * wr[0] + drl1 * wr[1] + dcl0 * wm[0] + dcl1 * wm[1]
    gw = [jnp.sum(h2 * t, axis=0) for t in (drl0, drl1, dcl0, dcl1)]
    dx1, gg2, gb2 = norm_back(dh2, u2, i2, g2)
    dx1 = dx1 + dys.astype(F32)
    dab = dx1.astype(BF)
    gwo = mm(o, dab, ((0,), (0,)))
    do = mm(dab, wo, ((1,), (1,))).astype(BF).reshape(T, H, HD)
    dp = jnp.einsum("ihd,jhd->hij", do, v, preferred_element_type=F32)
    ds = (p * (dp - jnp.sum(p * dp, axis=-1, keepdims=True))).astype(BF)
    dq = jnp.einsum("hij,jhd->ihd", ds, k, preferred_element_type=F32).astype(BF)
    dq = (dq * BF(0.125)).reshape(T, D)
    dk = jnp.einsum("hij,ihd->jhd", ds, q, preferred_element_type=F32).astype(BF).reshape(T, D)
    dv = jnp.einsum("hij,ihd->jhd", pb, do, preferred_element_type=F32).astype(BF).reshape(T, D)
    dh1 = mm(dq, wq, ((1,), (1,))) + mm(dk, wk, ((1,), (1,))) + mm(dv, wv, ((1,), (1,)))
    ga = jnp.stack([mm(h1b, dq, ((0,), (0,))), mm(h1b, dk, ((0,), (0,))), mm(h1b, dv, ((0,), (0,))), gwo])
    dxn, gg1, gb1 = norm_back(dh1, u1, i1, g1)
    input_grad = (dx1 + dxn).astype(BF)

    layer_out = mm(perm, layer_out, ((0,), (0,))).astype(BF)
    input_grad = mm(perm, input_grad, ((0,), (0,))).astype(BF)

    smalls = lax.psum(jnp.stack([gg1, gb1, gg2, gb2] + gw), BOTH)
    mine = lax.dynamic_slice_in_dim(smalls, lax.axis_index(BOTH) * WR, WR, 1)
    ga = ga.reshape(4, C, S, WR, D).transpose(1, 2, 0, 3, 4)
    ga = lax.psum_scatter(ga.astype(BF), "dp", scatter_dimension=0, tiled=False)
    ga = lax.psum_scatter(ga, "shard", scatter_dimension=0, tiled=False).astype(F32)
    gdown = lax.psum_scatter(jnp.stack(gdown), "dp", scatter_dimension=1, tiled=True)
    gup = jnp.stack(gup).reshape(3, C, S, WR, F).transpose(1, 2, 0, 3, 4)
    gup = lax.psum_scatter(gup, "dp", scatter_dimension=0, tiled=False).astype(BF)
    gup = lax.all_to_all(gup, "shard", 0, 0).astype(F32)
    gup = gup.reshape(S, 3, WR, C, FR).transpose(1, 2, 3, 0, 4).reshape(3, WR, FF)

    counts = lax.psum(jnp.stack([n0, T - n0]), BOTH)
    load_new = 0.9 * load_avg + 0.1 * counts.astype(F32) * E / (T * C * S)
    return (
        layer_out, input_grad, mine[0], mine[1], ga[0], ga[1], ga[2], ga[3], mine[2], mine[3],
        gup[0], gdown[0], jnp.stack([mine[4], mine[5]], axis=1), jnp.stack([mine[6], mine[7]], axis=1),
        gup[1:], gdown[1:], counts, load_new,
    )


def body(
    hidden_in, doc_ids, expert_ids, slot_ids, out_grad, ln1_gain, ln1_bias, w_query, w_key, w_value,
    w_out, ln2_gain, ln2_bias, w_up, w_down, w_router, w_mix, expert_up, expert_down, load_avg,
):
    T, D = hidden_in.shape
    H, HD = HEADS, D // HEADS
    S = lax.axis_size("shard")
    C = lax.axis_size("dp")
    WR = w_query.shape[0]
    FF = w_up.shape[1]
    FR = w_down.shape[0]
    F = FR * C
    E = expert_up.shape[0]
    ndev = C * S
    dev = lax.axis_index(BOTH)
    small = jnp.stack(
        [ln1_gain, ln1_bias, ln2_gain, ln2_bias, w_router[:, 0], w_router[:, 1], w_mix[:, 0], w_mix[:, 1]]
    ).astype(F32)
    group = 128 // WR
    slot_of = lax.broadcasted_iota(jnp.int32, (8, 128), 1) // WR
    small = jnp.where(slot_of == dev % group, jnp.tile(small, (1, group)), 0.0)
    (h2b, stat, scal8, u1, u2, x1, dys, q, k, v, p, o, small, count, wa, dy_all, ups, downs) = attn_call(
        hidden_in, out_grad, doc_ids, expert_ids.reshape(1, T), slot_ids.reshape(1, T), small,
        (w_query, w_key, w_value, w_out), w_up, expert_up, w_down, expert_down, S,
    )
    yfull, dh2, sc, gup, gdn0, gdn12 = ffn_call(h2b, scal8, dy_all, ups, downs)
    layer_out, input_grad, gqkv, gwo, smalls = back_call(
        dh2, yfull, sc, small, stat, u1, u2, x1, dys, q, k, v, p, o,
        expert_ids.reshape(1, T), slot_ids.reshape(1, T), wa.reshape(4, D, D), S,
    )
    mine = lax.dynamic_slice_in_dim(smalls, dev % group * WR, WR, 1)
    ga = gqkv.reshape(3, WR, D)
    gup = gup.astype(F32).reshape(S, 3, WR, C, FR).transpose(1, 2, 3, 0, 4).reshape(3, WR, FF)
    tokens0 = count[0, 0].astype(jnp.int32)
    counts = jnp.stack([tokens0, T * ndev - tokens0])
    load_new = 0.9 * load_avg + 0.1 * counts.astype(F32) * E / (T * ndev)
    return (
        layer_out, input_grad, mine[0], mine[1], ga[0], ga[1], ga[2], gwo, mine[2], mine[3],
        gup[0], gdn0, mine[4:6].T, mine[6:8].T, gup[1:], gdn12, counts, load_new,
    )


def pick(*args):
    S, C, WR, FR = lax.axis_size("shard"), lax.axis_size("dp"), args[7].shape[0], args[14].shape[0]
    fast = C == 2 and S % 4 == 0 and S >= 8 and WR % 16 == 0 and 128 % WR == 0 and FR % 128 == 0
    return (body if fast else body_plain)(*args)


def solution(mesh):
    row, vec = P(BOTH, None), P(BOTH)
    mid = P(None, BOTH, None)
    return jax.shard_map(
        pick,
        mesh=mesh,
        in_specs=(row, row, vec, vec, row, vec, vec, row, row, row, row, vec, vec, row, row, row, row, mid, mid, P()),
        out_specs=(row, row, vec, vec, row, row, row, row, vec, vec, row, row, row, row, mid, mid, P(), P()),
        check_vma=False,
    )
```

```python
import jax
import jax.numpy as jnp
from jax import lax
from jax.experimental import pallas as pl
from jax.experimental.pallas import tpu as pltpu
from jax.sharding import PartitionSpec as P

HEADS = 16
CAP = 74
BF = jnp.bfloat16
F32 = jnp.float32
BOTH = ("dp", "shard")
MESH = pl.DeviceIdType.MESH


def mm(a, b, dims=((1,), (0,))):
    return lax.dot_general(a, b, (dims, ((), ())), preferred_element_type=F32)


def layer_norm(values, gain, bias):
    centre = values - jnp.mean(values, axis=-1, keepdims=True)
    scale_inv = lax.rsqrt(jnp.mean(centre * centre, axis=-1, keepdims=True) + 1e-05)
    normed = centre * scale_inv
    return (normed * gain + bias, normed, scale_inv)


def norm_back(grad_out, normed, scale_inv, gain):
    grad_normed = grad_out * gain
    inner = grad_normed - jnp.mean(grad_normed, axis=-1, keepdims=True)
    inner = inner - normed * jnp.mean(grad_normed * normed, axis=-1, keepdims=True)
    return (scale_inv * inner, jnp.sum(grad_out * normed, axis=0), jnp.sum(grad_out, axis=0))


def gelu_pair(t):
    inner = 0.7978845608 * (t + 0.044715 * t * t * t)
    th = jnp.tanh(inner)
    val = 0.5 * t * (1.0 + th)
    der = 0.5 * (1.0 + th) + 0.5 * t * (1.0 - th * th) * 0.7978845608 * (1.0 + 3.0 * 0.044715 * t * t)
    return val, der


def ag(block):
    return lax.all_gather(block, "shard", axis=0, tiled=False)


def rs(parts):
    return lax.psum_scatter(parts.astype(BF), "shard", scatter_dimension=0, tiled=False).astype(F32)


def place_of():
    me = lax.axis_index("shard")
    core = lax.axis_index("dp")
    z, p = me // 4, me % 4
    xq = p + 1 - 2 * (p % 2)
    yq = p + 2 - 4 * (p // 2)
    return me, core, z, p, xq, yq, 3 - p


def greet(shards, core):
    bar = pltpu.get_barrier_semaphore()
    me = lax.axis_index("shard")

    @pl.loop(1, shards)
    def _(i):
        pl.semaphore_signal(bar, inc=1, device_id=(core, (me + i) % shards), device_id_type=MESH)

    pl.semaphore_signal(bar, inc=1, device_id=(1 - core, me), device_id_type=MESH)
    pl.semaphore_wait(bar, shards)


def remote(src, dst, send, recv, dev):
    return pltpu.make_async_remote_copy(
        src_ref=src, dst_ref=dst, send_sem=send, recv_sem=recv, device_id=dev, device_id_type=MESH
    )


def rows_loop(count, step, fn):
    @pl.loop(0, count // step)
    def _(i):
        fn(pl.multiple_of(i * step, step))


def level_order(z, L):
    upper = z // (L // 2)
    y = z + upper * (L - 1 - 2 * z)

    def lev_of(k):
        low = k - 1 + (k - 1 - y + L) // L
        lev = low + upper * (L - 1 - 2 * low)
        first = 1 - (k + L - 1) // L
        return lev + first * (z - lev)

    return lev_of


def tree_gather(at, own, ss, rs, dev, levels):
    core, z, p, xq, yq, dq = dev
    xn, yn = z * 4 + xq, z * 4 + yq
    me = z * 4 + p
    lev_of, L = levels

    def copy(kind, slot, src, idx, to):
        return remote(src, at(idx), ss.at[kind, slot], rs.at[kind, slot], (core, to))

    def up_line(src, send):
        return remote(src, at(me), send, rs.at[0, z], (core, me + 4))

    def down_line(src, send):
        return remote(src, at(me), send, rs.at[0, z], (core, me - 4))

    def onward(k):
        lev = lev_of(k)
        step = 1 - 2 * ((lev - z + L) // L)
        to = z + step
        idx = lev * 4 + p
        ok = (to >= 0) & (to < L)
        return ok, remote(at(idx), at(idx), ss.at[0, lev], rs.at[0, lev], (core, me + 4 * step))

    class Stages:
        @staticmethod
        def start():
            @pl.when(z < L - 1)
            def _():
                up_line(own, ss.at[0, z]).start()

            @pl.when(z > 0)
            def _():
                down_line(own, ss.at[4, 0]).start()

            copy(1, z, own, me, xn).start()
            copy(2, z, own, me, yn).start()

        @staticmethod
        def a(k):
            lev = lev_of(k)
            idx = lev * 4 + p
            copy(0, lev, own, idx, xn).wait_recv()
            ok, on = onward(k)

            @pl.when(ok)
            def _():
                on.start()

            copy(1, lev, at(idx), idx, xn).start()
            copy(2, lev, at(idx), idx, yn).start()

        @staticmethod
        def b(k):
            lev = lev_of(k)
            odd = k % 2
            copy(1, lev, own, lev * 4 + xq, xn).wait_recv()
            copy(2, lev, own, lev * 4 + yq, yn).wait_recv()
            idx = lev * 4 + xq + odd * (yq - xq)
            copy(3, lev, at(idx), idx, yn + odd * (xn - yn)).start()

        @staticmethod
        def c(k):
            lev = lev_of(k)
            copy(3, lev, own, lev * 4 + dq, xn).wait_recv()

        @staticmethod
        def finish():
            @pl.when(z < L - 1)
            def _():
                up_line(own, ss.at[0, z]).wait_send()

            @pl.when(z > 0)
            def _():
                down_line(own, ss.at[4, 0]).wait_send()

            @pl.loop(0, L)
            def _(k):
                lev = lev_of(k)
                for kind in range(1, 4):
                    copy(kind, lev, own, me, xn).wait_send()

            @pl.loop(1, L)
            def _(k):
                ok, on = onward(k)

                @pl.when(ok)
                def _():
                    on.wait_send()

    return Stages


def tree_scatter(part, ra, rbx, rby, rd, final, ss, rs, dev, levels):
    core, z, p, xq, yq, dq = dev
    xn, yn = z * 4 + xq, z * 4 + yq
    lev_of, L = levels
    R = part.shape[1]

    def copy(kind, lev, src, dst, to):
        return remote(src, dst, ss.at[kind, lev], rs.at[kind, lev], (core, to))

    class Stages:
        @staticmethod
        def a(k):
            lev = lev_of(k)
            odd = k % 2
            copy(0, lev, part.at[lev * 4 + dq], ra.at[lev], yn + odd * (xn - yn)).start()

        @staticmethod
        def b(k):
            lev = lev_of(k)
            odd = k % 2
            via = lev * 4 + xq + odd * (yq - xq)
            copy(0, lev, ra.at[lev], ra.at[lev], xn).wait_recv()

            def add(r):
                t = pl.ds(r, 32)
                part[via, t, :] = (part[via, t, :].astype(F32) + ra[lev, t, :].astype(F32)).astype(BF)

            rows_loop(R, 32, add)
            copy(1, lev, part.at[lev * 4 + xq], rbx.at[lev], xn).start()
            copy(2, lev, part.at[lev * 4 + yq], rby.at[lev], yn).start()

        @staticmethod
        def c(k):
            lev = lev_of(k)
            own = lev * 4 + p
            copy(1, lev, rbx.at[lev], rbx.at[lev], xn).wait_recv()
            copy(2, lev, rby.at[lev], rby.at[lev], yn).wait_recv()

            def add(r):
                t = pl.ds(r, 32)
                tot = part[own, t, :].astype(F32) + rbx[lev, t, :].astype(F32) + rby[lev, t, :].astype(F32)

                @pl.when(k == 0)
                def _():
                    final[t, :] = tot

                @pl.when(k > 0)
                def _():
                    part[own, t, :] = tot.astype(BF)

            rows_loop(R, 32, add)

            @pl.when(k > 0)
            def _():
                remote(part.at[own], rd.at[z], ss.at[3, lev], rs.at[3, z], (core, lev * 4 + p)).start()

        @staticmethod
        def d(k):
            lev = lev_of(k)
            copy(3, lev, rd.at[lev], rd.at[lev], xn).wait_recv()

            def add(r):
                t = pl.ds(r, 32)
                final[t, :] = final[t, :] + rd[lev, t, :].astype(F32)

            rows_loop(R, 32, add)

        @staticmethod
        def finish():
            @pl.loop(0, L)
            def _(k):
                lev = lev_of(k)
                for kind in range(3):
                    copy(kind, lev, ra.at[0], ra.at[0], xn).wait_send()

                @pl.when(k > 0)
                def _():
                    copy(3, lev, ra.at[0], ra.at[0], xn).wait_send()

    return Stages


def ffn_kernel(
    h_ref, scal_ref, dy_ref, up_ref, dn_ref,
    y_out, dh_out, sc_out, gup_out, gdn0_out, gdn12_out,
    hall, scall, psc, screcv, wcol, scol, part, ra, rbx, rby, rd,
    pre, der, ub, dg, dm, m, yacc, dxacc, gdn, gup, sib_dn, sib_up, gsend, grecv,
    ag_s, ag_r, rs_s, rs_r, one_s, one_r, sm_s, sm_r,
):
    S, T, D = hall.shape
    F = up_ref.shape[2]
    L = S // 4
    LO = 80
    HI = T - LO
    me, core, z, p, xq, yq, dq = place_of()
    xn = z * 4 + xq
    lev_of = level_order(z, L)
    dev, levels = (core, z, p, xq, yq, dq), (lev_of, L)
    greet(S, core)
    hg = tree_gather(lambda i: hall.at[i], h_ref, ag_s, ag_r, dev, levels)
    rg = tree_scatter(part, ra, rbx, rby, rd, dh_out, rs_s, rs_r, dev, levels)
    hg.start()

    @pl.loop(1, S)
    def _(i):
        remote(scal_ref, scall.at[me], sm_s.at[0, i], sm_r.at[0], (core, (me + i) % S)).start()

    hall[me] = h_ref[...]
    scall[me] = scal_ref[...]
    gdn[...] = jnp.zeros_like(gdn)
    gup[...] = jnp.zeros_like(gup)
    remote(scall.at[pl.ds(0, S - 1)], scall.at[pl.ds(0, S - 1)], sm_s.at[0, 0], sm_r.at[0], (core, xn)).wait_recv()

    size = (4 * T, 4 * LO, 4 * LO)
    first = (0, 4 * T, 4 * T + 4 * LO)

    def compute(lev):
        base = lev * 4
        for q in range(4):
            full = jnp.concatenate([scall[base + q], jnp.zeros((120, 128), F32)], axis=0)
            wcol[q] = full.T
        for e in range(3):
            n = LO if e else T
            off = HI if e == 2 else 0
            rows, at0 = size[e], first[e]
            here = slice(at0, at0 + rows)
            hm = hall[pl.ds(base, 4), off : off + n, :].reshape(rows, D)
            pre[0:rows, :] = mm(hm, up_ref[e])

            def act(r):
                t = pl.ds(r, rows // 4)
                val, d = gelu_pair(pre[t, :])
                ub[pl.ds(pl.multiple_of(at0 + r, 16), rows // 4), :] = val.astype(BF)
                der[t, :] = d

            rows_loop(rows, rows // 4, act)
            m[0:rows, :] = mm(ub[here, :], dn_ref[e])
            step = n if e else T // 2
            lane = lax.broadcasted_iota(jnp.int32, (step, 128), 1)
            for q in range(4):

                def elem(r):
                    at = pl.ds(pl.multiple_of(r + off, 16), step)
                    mine = pl.ds(pl.multiple_of(q * n + r, 16), step)
                    keep = pl.ds(pl.multiple_of(at0 + q * n + r, 16), step)
                    t = pl.ds(pl.multiple_of(q * T + off + r, 16), step)
                    w = wcol[q, at, :][:, e : e + 1]
                    dyv = dy_ref[base + q, at, :].astype(F32)
                    mv = m[mine, :]
                    s = jnp.sum(dyv * mv, axis=1, keepdims=True)
                    s = jnp.where(lane == e, s, 0.0)
                    dm[keep, :] = (dyv * w).astype(BF)
                    if e:
                        yacc[t, :] = yacc[t, :] + mv * w
                        scol[q, at, :] = scol[q, at, :] + s
                    else:
                        yacc[t, :] = mv * w
                        scol[q, at, :] = s

                rows_loop(n, step, elem)
            pre[0:rows, :] = mm(dm[here, :], dn_ref[e], ((1,), (1,)))

            def back(r):
                t = pl.ds(r, rows // 4)
                dg[pl.ds(pl.multiple_of(at0 + r, 16), rows // 4), :] = (pre[t, :] * der[t, :]).astype(BF)

            rows_loop(rows, rows // 4, back)
            if e:
                m[0:rows, :] = mm(dg[here, :], up_ref[e], ((1,), (1,)))
                for q in range(4):
                    t = slice(q * T + off, q * T + off + n)
                    dxacc[t, :] = dxacc[t, :] + m[q * n : q * n + n, :]
            else:
                dxacc[...] = mm(dg[here, :], up_ref[0], ((1,), (1,)))
        for q in range(4):
            psc[base + q] = scol[q].T[0:8, :]
            t = slice(q * T, q * T + T)
            part[base + q] = dxacc[t, :].astype(BF)
            y_out[base + q] = yacc[t, :].astype(BF)

    def weight_grads(lev):
        for e in range(3):
            n = LO if e else T
            off = HI if e == 2 else 0
            here = slice(first[e], first[e] + size[e])
            hm = hall[pl.ds(lev * 4, 4), off : off + n, :].reshape(size[e], D)
            gdn[e] = gdn[e] + mm(ub[here, :], dm[here, :], ((0,), (0,)))
            gup[e] = gup[e] + mm(dg[here, :], hm, ((0,), (0,)))

    hg.a(1)
    hg.b(0)
    hg.a(2)

    @pl.loop(0, L)
    def _(k):
        hg.c(k)

        @pl.when(k < L - 1)
        def _():
            hg.b(k + 1)

        @pl.when(k < L - 3)
        def _():
            hg.a(k + 3)

        compute(lev_of(k))
        rg.a(k)

        @pl.when(k > 0)
        def _():
            rg.b(k - 1)

        @pl.when(k > 1)
        def _():
            rg.c(k - 2)

        weight_grads(lev_of(k))

    half = D // 2
    other = pl.multiple_of((1 - core) * half, half)
    mine_d = pl.multiple_of(core * half, half)
    FR = F // 2
    other_f = pl.multiple_of((1 - core) * FR, FR)
    mine_f = pl.multiple_of(core * FR, FR)
    sib = (1 - core, me)
    c_up = remote(gup.at[:, :, pl.ds(other, half)], sib_up, one_s.at[0], one_r.at[0], sib)
    c_dn = remote(gdn.at[:, pl.ds(other_f, FR), :], sib_dn, one_s.at[1], one_r.at[1], sib)
    c_up.start()
    c_dn.start()

    @pl.loop(1, S)
    def _(i):
        to = (me + i) % S
        remote(psc.at[to], screcv.at[i], sm_s.at[1, i], sm_r.at[1], (core, to)).start()

    rg.b(L - 1)
    rg.c(L - 2)
    c_up.wait_recv()
    for e in range(3):
        tot = gup[e, :, pl.ds(mine_d, half)] + sib_up[e]
        gsend[e] = tot.T.astype(BF)
    rg.c(L - 1)
    WR = half // S
    screcv[0] = psc[me]

    def g_copy(i, to):
        return remote(
            gsend.at[:, pl.ds(pl.multiple_of(to * WR, WR), WR), :], grecv.at[me], sm_s.at[2, i], sm_r.at[2], (core, to)
        )

    @pl.loop(1, S)
    def _(i):
        g_copy(i, (me + i) % S).start()

    grecv[me] = gsend[:, pl.ds(pl.multiple_of(me * WR, WR), WR), :]
    c_dn.wait_recv()
    gdn0_out[...] = gdn[0, pl.ds(mine_f, FR), :] + sib_dn[0]
    for e in range(1, 3):
        gdn12_out[e - 1] = gdn[e, pl.ds(mine_f, FR), :] + sib_dn[e]
    for k in range(1, L):
        rg.d(k)
    remote(screcv.at[pl.ds(1, S - 1)], screcv.at[pl.ds(1, S - 1)], sm_s.at[1, 0], sm_r.at[1], (core, xn)).wait_recv()
    sc_out[...] = jnp.sum(screcv[...], axis=0)
    remote(grecv.at[pl.ds(0, S - 1)], grecv.at[pl.ds(0, S - 1)], sm_s.at[2, 0], sm_r.at[2], (core, xn)).wait_recv()
    gup_out[...] = grecv[...]

    c_up.wait_send()
    c_dn.wait_send()
    hg.finish()
    rg.finish()

    @pl.loop(1, S)
    def _(i):
        remote(scal_ref, scall.at[0], sm_s.at[0, i], sm_r.at[0], (core, xn)).wait_send()
        remote(psc.at[0], screcv.at[0], sm_s.at[1, i], sm_r.at[1], (core, xn)).wait_send()
        g_copy(i, (me + i) % S).wait_send()


def ffn_call(h2b, scal, dy_all, ups, downs):
    S, T, D = dy_all.shape
    F = ups.shape[2]
    L = S // 4
    WR = D // 2 // S
    rows = 4 * T + 8 * 80
    vm = pl.BlockSpec(memory_space=pltpu.VMEM)
    V = pltpu.VMEM
    dma = pltpu.SemaphoreType.DMA
    sds = jax.ShapeDtypeStruct
    blocks = V((L, T, D), BF)
    return pl.pallas_call(
        ffn_kernel,
        out_shape=(
            sds((S, T, D), BF), sds((T, D), F32), sds((8, 128), F32), sds((S, 3, WR, F), BF),
            sds((F // 2, D), F32), sds((2, F // 2, D), F32),
        ),
        in_specs=[vm] * 5,
        out_specs=(vm,) * 6,
        scratch_shapes=[
            V((S, T, D), BF), V((S, 8, 128), F32), V((S, 8, 128), F32), V((S, 8, 128), F32),
            V((4, T, 128), F32), V((4, T, 128), F32),
            V((S, T, D), BF), blocks, blocks, blocks, blocks,
            V((4 * T, F), F32), V((4 * T, F), F32), V((rows, F), BF), V((rows, F), BF), V((rows, D), BF),
            V((4 * T, D), F32), V((4 * T, D), F32), V((4 * T, D), F32),
            V((3, F, D), F32), V((3, F, D), F32), V((3, F // 2, D), F32), V((3, F, D // 2), F32),
            V((3, D // 2, F), BF), V((S, 3, WR, F), BF),
            dma((5, L)), dma((5, L)), dma((4, L)), dma((4, L)), dma((2,)), dma((2,)), dma((3, S)), dma((3,)),
        ],
        compiler_params=pltpu.CompilerParams(collective_id=2, has_side_effects=True, vmem_limit_bytes=64000000),
        cost_estimate=pl.CostEstimate(flops=15 * 10**9, bytes_accessed=20 * 2**20, transcendentals=2**20),
        name="ffn",
    )(h2b, scal, dy_all, ups, downs)


def sort_matrix(ids_e, ids_s, T):
    zero = ids_e == 0
    n0 = jnp.sum(jnp.where(zero, 1.0, 0.0), axis=1, keepdims=True)
    slot = ids_s.astype(F32)
    pos = jnp.where(zero, slot, slot + n0)
    sub = lax.broadcasted_iota(jnp.int32, (T, T), 0).astype(F32)
    return jnp.where(sub == pos, 1.0, 0.0), n0


def attn_kernel(
    x_ref, dy_ref, doc_ref, e_ref, s_ref, small_ref, wq_ref, wk_ref, wv_ref, wo_ref,
    wu_ref, eu_ref, wd_ref, ed_ref,
    h2b_out, stat_out, scal_out, u1_out, u2_out, x1_out, dys_out, q_out, k_out, v_out, p_out, o_out,
    small_out, count_out, w_out, dyall_out, up_out, dn_out,
    wbuf, smallbuf, h1b, bias, xs, tmp,
    ag_s, ag_r, sib_s, sib_r, sm_s, sm_r, loc,
):
    T, D = x_ref.shape
    WR = wq_ref.shape[0]
    FR = wd_ref.shape[0]
    N = wbuf.shape[1]
    S = N // 2
    L = S // 4
    me, core, z, p, xq, yq, dq = place_of()
    xn = z * 4 + xq
    my = core * S + me
    sib = (1 - core, me)
    greet(S, core)
    lev_of = level_order(z, L)

    dev, levels = (core, z, p, xq, yq, dq), (lev_of, L)

    def w1_at(i):
        return wbuf.at[pl.ds(0, 3), core * S + i]

    def w2_at(i):
        return wbuf.at[3, core * S + i]

    w1 = tree_gather(w1_at, w1_at(me), ag_s.at[0], ag_r.at[0], dev, levels)
    w2 = tree_gather(w2_at, w2_at(me), ag_s.at[1], ag_r.at[1], dev, levels)
    dyg = tree_gather(lambda i: dyall_out.at[i], dys_out, ag_s.at[2], ag_r.at[2], dev, levels)

    for i, w in enumerate((wq_ref, wk_ref, wv_ref, wo_ref)):
        wbuf[i, my] = w[...]
    w1.start()

    perm, n0 = sort_matrix(e_ref[...], s_ref[...], T)
    smallbuf[my, 0:8, :] = small_ref[...]
    lane8 = lax.broadcasted_iota(jnp.int32, (8, 128), 1)
    smallbuf[my, 8:16, :] = jnp.where(lane8 == 0, jnp.broadcast_to(n0, (8, 128)), 0.0)

    @pl.loop(1, S)
    def _(i):
        remote(smallbuf.at[my], smallbuf.at[my], sm_s.at[0, i], sm_r.at[0], (core, (me + i) % S)).start()

    def dn_own(e0, n, src):
        dst = dn_out.at[pl.ds(e0, n), pl.ds(pl.multiple_of(core * FR, FR), FR), :]
        return src, dst

    d0 = dn_own(0, 1, wd_ref)
    d0 = (wd_ref, dn_out.at[0, pl.ds(pl.multiple_of(core * FR, FR), FR), :])
    d1 = dn_own(1, 2, ed_ref)
    dn_copies = []
    for j, (src, dst) in enumerate((d0, d1)):
        r = remote(src, dst, sib_s.at[2, j], sib_r.at[2, j], sib)
        lc = pltpu.make_async_copy(src, dst, loc.at[j])
        r.start()
        lc.start()
        dn_copies.append((r, lc))

    permb = perm.astype(BF)
    xs[...] = mm(permb, x_ref[...])
    dys_out[...] = mm(permb, dy_ref[...]).astype(BF)
    dy_local = pltpu.make_async_copy(dys_out, dyall_out.at[me], loc.at[2])
    dy_local.start()

    docs = (doc_ref[...] == lax.broadcasted_iota(jnp.int32, (16, T), 0)).astype(F32).astype(BF)
    docs = mm(docs, permb, ((1,), (1,))).astype(BF)
    same = mm(docs, docs, ((0,), (0,)))
    place = lax.broadcasted_iota(jnp.int32, (T, T), 1).astype(F32)
    ord_col = jnp.sum(perm * place, axis=1, keepdims=True)
    ord_row = mm(place[0:16, :].astype(BF), permb, ((1,), (1,)))[0:1, :]
    bias[...] = jnp.where((same > 0.5) & (ord_row <= ord_col), 0.0, -1e30)

    lane = lax.broadcasted_iota(jnp.int32, (64, 128), 1)

    def norm1(r):
        t = pl.ds(r, 64)
        v = xs[t, :]
        cen = v - jnp.mean(v, axis=1, keepdims=True)
        inv = lax.rsqrt(jnp.mean(cen * cen, axis=1, keepdims=True) + 1e-05)
        u1_out[t, :] = cen * inv
        stat_out[t, :] = jnp.where(lane == 8, inv, 0.0)

    rows_loop(T, 64, norm1)

    w1.a(1)
    w1.b(0)
    w1.a(2)
    w1.b(1)

    group = 128 // WR
    remote(smallbuf.at[pl.ds(0, S - 1)], smallbuf.at[pl.ds(0, S - 1)], sm_s.at[0, 0], sm_r.at[0], (core, xn)).wait_recv()
    mine_small = smallbuf.at[pl.ds(core * S, S)]
    c_small = remote(mine_small, mine_small, sib_s.at[2, 2], sib_r.at[2, 2], sib)
    c_small.start()

    def w1_sib(lev, who):
        b = wbuf.at[pl.ds(0, 3), pl.ds(who * S + lev * 4, 4)]
        return remote(b, b, sib_s.at[0, lev], sib_r.at[0, lev], sib)

    def w2_sib(lev, who):
        b = wbuf.at[3, pl.ds(who * S + lev * 4, 4)]
        return remote(b, b, sib_s.at[1, lev], sib_r.at[1, lev], sib)

    def c1(k):
        w1.c(k)
        w1_sib(lev_of(k), core).start()

    def c2(k):
        w2.c(k)
        w2_sib(lev_of(k), core).start()

    for k in range(3, L):
        w1.a(k)
    c1(0)
    w2.start()
    for k in range(2, L):
        w1.b(k)
        c1(k - 1)

    def up_copy(e, h, i):
        to = (me + i) % S
        src = wu_ref if e == 0 else eu_ref.at[e - 1]
        return remote(
            src.at[:, pl.ds(pl.multiple_of((h * S + to) * FR, FR), FR)],
            up_out.at[e, pl.ds(pl.multiple_of(my * WR, WR), WR), pl.ds(h * FR, FR)],
            sm_s.at[1, i], sm_r.at[1], (core, to),
        )

    def up_local(e, h):
        src = wu_ref if e == 0 else eu_ref.at[e - 1]
        return pltpu.make_async_copy(
            src.at[:, pl.ds(pl.multiple_of((h * S + me) * FR, FR), FR)],
            up_out.at[e, pl.ds(pl.multiple_of(my * WR, WR), WR), pl.ds(h * FR, FR)],
            loc.at[4 + 2 * e + h],
        )

    @pl.loop(1, S)
    def _(i):
        for e in range(3):
            for h in range(2):
                up_copy(e, h, i).start()

    for e in range(3):
        for h in range(2):
            up_local(e, h).start()

    c_small.wait_recv()
    for g in range(D // 128):
        part = smallbuf[g * group, 0:8, :]
        for j in range(1, group):
            part = part + smallbuf[g * group + j, 0:8, :]
        small_out[:, g * 128 : (g + 1) * 128] = part
    cnt = smallbuf[0, 8:16, :]
    for i in range(1, N):
        cnt = cnt + smallbuf[i, 8:16, :]
    count_out[...] = cnt

    def norm1b(r):
        t = pl.ds(r, 64)
        h1b[t, :] = (u1_out[t, :] * small_out[0:1, :] + small_out[1:2, :]).astype(BF)

    rows_loop(T, 64, norm1b)
    c1(L - 1)
    w2.a(1)
    w2.b(0)
    for k in range(L):
        w1_sib(lev_of(k), 1 - core).wait_recv()

    def full(i):
        return wbuf[i].reshape(D, D)

    tmp[...] = mm(h1b[...], full(0))
    q_out[...] = (tmp[...] * 0.125).astype(BF)
    for k in range(2, L):
        w2.a(k)
    w2.b(1)
    tmp[...] = mm(h1b[...], full(1))
    k_out[...] = tmp[...].astype(BF)
    c2(0)
    dyg.start()
    for k in range(2, L):
        w2.b(k)
        c2(k - 1)
    tmp[...] = mm(h1b[...], full(2))
    v_out[...] = tmp[...].astype(BF)
    c2(L - 1)
    dyg.a(1)
    dyg.b(0)

    low = lax.broadcasted_iota(jnp.int32, (T, 128), 1) < 64
    lowb = low.astype(F32).astype(BF)
    highb = (1.0 - low.astype(F32)).astype(BF)

    def heads(j):
        ln = pl.ds(pl.multiple_of(j * 128, 128), 128)
        qp = q_out[:, ln]
        q2 = jnp.concatenate([qp * lowb, qp * highb], axis=0)
        s = mm(q2, k_out[:, ln], ((1,), (1,)))
        s = s + jnp.concatenate([bias[...], bias[...]], axis=0)
        ex = jnp.exp(s - jnp.max(s, axis=1, keepdims=True))
        pr = ex / jnp.sum(ex, axis=1, keepdims=True)
        p_out[j] = pr
        o2 = mm(pr.astype(BF), v_out[:, ln])
        o_out[:, ln] = jnp.where(low, o2[0:T], o2[T:]).astype(BF)

    half = D // 256

    @pl.loop(0, half)
    def _(j):
        heads(j)

    dyg.a(2)
    dyg.b(1)

    @pl.loop(half, 2 * half)
    def _(j):
        heads(j)

    for k in range(3, L):
        dyg.a(k)
    for k in range(L):
        w2_sib(lev_of(k), 1 - core).wait_recv()
    w_save = pltpu.make_async_copy(wbuf, w_out, loc.at[3])
    w_save.start()
    tmp[...] = mm(o_out[...], full(3))

    def norm2(r):
        t = pl.ds(r, 64)
        v = xs[t, :] + tmp[t, :]
        x1_out[t, :] = v
        cen = v - jnp.mean(v, axis=1, keepdims=True)
        inv = lax.rsqrt(jnp.mean(cen * cen, axis=1, keepdims=True) + 1e-05)
        u = cen * inv
        u2_out[t, :] = u
        h2 = u * small_out[2:3, :] + small_out[3:4, :]
        h2b_out[t, :] = h2.astype(BF)
        lg = [jnp.sum(h2 * small_out[i : i + 1, :], axis=1, keepdims=True) for i in range(4, 8)]

        def soft(a, b):
            mx = jnp.maximum(a, b)
            ea, eb = jnp.exp(a - mx), jnp.exp(b - mx)
            return ea / (ea + eb), eb / (ea + eb)

        r0, r1 = soft(lg[0], lg[1])
        k0, k1 = soft(lg[2], lg[3])
        row = (lax.broadcasted_iota(jnp.int32, (64, 1), 0) + r).astype(F32)
        is0 = row < n0
        gate = jnp.where(is0, r0, r1)
        we = k0 * gate
        cols = (k1, jnp.where(is0, we, 0.0), jnp.where(is0, 0.0, we), k0, gate, r0, r1)
        st = stat_out[t, :] + jnp.where(lane == 9, inv, 0.0)
        for i, col in enumerate(cols):
            st = st + jnp.where(lane == i, col, 0.0)
        stat_out[t, :] = st

    rows_loop(T, 64, norm2)
    scal_out[...] = stat_out[...].T[0:8, :]

    for k in range(2, L):
        dyg.b(k)
    for k in range(L):
        dyg.c(k)

    got = up_out.at[:, pl.ds(0, (S - 1) * WR), :]
    remote(got, got, sm_s.at[1, 0], sm_r.at[1], (core, xn)).wait_recv()
    for e in range(3):
        for h in range(2):
            up_local(e, h).wait()
    mine_up = up_out.at[:, pl.ds(pl.multiple_of(core * S * WR, S * WR), S * WR), :]
    c_up = remote(mine_up, mine_up, sib_s.at[2, 3], sib_r.at[2, 3], sib)
    c_up.start()
    c_up.wait()
    w_save.wait()
    dy_local.wait()
    for r, lc in dn_copies:
        r.wait()
        lc.wait()
    c_small.wait_send()
    w1.finish()
    w2.finish()
    dyg.finish()

    @pl.loop(0, L)
    def _(k):
        w1_sib(k, core).wait_send()
        w2_sib(k, core).wait_send()

    @pl.loop(1, S)
    def _(i):
        remote(smallbuf.at[my], smallbuf.at[my], sm_s.at[0, i], sm_r.at[0], (core, xn)).wait_send()
        for e in range(3):
            for h in range(2):
                up_copy(e, h, i).wait_send()


def attn_call(x, dy, docs, es, ss, small, ws, wu, eu, wd, ed, S):
    T, D = x.shape
    WR, FR = ws[0].shape[0], wd.shape[0]
    L = S // 4
    N = 2 * S
    vm = pl.BlockSpec(memory_space=pltpu.VMEM)
    hb = pl.BlockSpec(memory_space=pl.ANY)
    V = pltpu.VMEM
    dma = pltpu.SemaphoreType.DMA
    sds = jax.ShapeDtypeStruct
    row = sds((T, D), BF)
    rowf = sds((T, D), F32)
    return pl.pallas_call(
        attn_kernel,
        out_shape=(
            row, sds((T, 128), F32), sds((8, T), F32), rowf, rowf, rowf, row, row, row, row,
            sds((D // 128, 2 * T, T), F32), row, sds((8, D), F32), sds((8, 128), F32),
            sds((4, N, WR, D), BF), sds((S, T, D), BF), sds((3, D, 2 * FR), BF), sds((3, 2 * FR, D), BF),
        ),
        in_specs=[vm] * 10 + [hb] * 4,
        out_specs=(vm,) * 14 + (hb,) * 4,
        scratch_shapes=[
            V((4, N, WR, D), BF), V((N, 16, 128), F32), V((T, D), BF), V((T, T), F32), V((T, D), F32), V((T, D), F32),
            dma((3, 5, L)), dma((3, 5, L)), dma((3, max(L, 4))), dma((3, max(L, 4))), dma((2, S)), dma((2,)), dma((10,)),
        ],
        compiler_params=pltpu.CompilerParams(collective_id=1, has_side_effects=True, vmem_limit_bytes=60000000),
        cost_estimate=pl.CostEstimate(flops=2 * 10**9, bytes_accessed=40 * 2**20, transcendentals=2**20),
        name="attn",
    )(x, dy, docs, es, ss, small, *ws, wu, eu, wd, ed)


def back_kernel(
    dh_ref, sc_ref, small_ref, stat_ref, u1_ref, u2_ref, x1_ref, dys_ref,
    q_ref, k_ref, v_ref, p_ref, o_ref, e_ref, s_ref, y_hbm, w_hbm,
    lo_out, ig_out, gqkv_out, go_out, smalls_out,
    wbuf, perm, accs, dx1, dab, do, dq, dk, dv, h1b, dh1, tmpb, keep, send, recv,
    part0, ra0, rbx0, rby0, rd0, part1, ra1, rbx1, rby1, rd1, ypart, ray, rbxy, rbyy, rdy, ysum, lsort, smine, ssib, srecv,
    rs_s, rs_r, sib_s, sib_r, sm_s, sm_r, loc,
):
    T, D = dh_ref.shape
    S, WR = part0.shape[0], part0.shape[1]
    L = S // 4
    half = D // 2
    me, core, z, p, xq, yq, dgq = place_of()
    xn = z * 4 + xq
    sib = (1 - core, me)
    greet(S, core)
    lev_of = level_order(z, L)

    dev, levels = (core, z, p, xq, yq, dgq), (lev_of, L)
    g0 = tree_scatter(part0, ra0, rbx0, rby0, rd0, go_out, rs_s.at[0], rs_r.at[0], dev, levels)
    g1 = tree_scatter(part1, ra1, rbx1, rby1, rd1, gqkv_out, rs_s.at[1], rs_r.at[1], dev, levels)
    gy = tree_scatter(ypart, ray, rbxy, rbyy, rdy, ysum, rs_s.at[2], rs_r.at[2], dev, levels)
    far = list(reversed(range(L)))
    fetch = []
    for k in far:
        some = pl.ds(lev_of(k) * 4, 4)
        fetch.append(pltpu.make_async_copy(y_hbm.at[some], ypart.at[some], loc.at[4 + k]))
    for c in fetch:
        c.start()
    loads = [pltpu.make_async_copy(w_hbm.at[i], wbuf.at[i], loc.at[i]) for i in range(4)]
    for i in (3, 0, 1, 2):
        loads[i].start()

    for k, c in zip(far, fetch):
        c.wait()
        gy.a(k)
    perm_f, n0 = sort_matrix(e_ref[...], s_ref[...], T)
    perm[...] = perm_f.astype(BF)
    accs[...] = jnp.zeros_like(accs)
    scol = jnp.concatenate([sc_ref[...], jnp.zeros((120, 128), F32)], axis=0).T
    dh1[:, 0:128] = scol

    def acc(i, v):
        accs[i] = accs[i] + jnp.sum(v.reshape(32 // 8, 8, v.shape[1]), axis=0)

    def norm2(r):
        t = pl.ds(r, 32)
        st = stat_ref[t, :]
        c1, c0, gate, r0, r1, inv = (st[:, i : i + 1] for i in (0, 3, 4, 5, 6, 9))
        row = (lax.broadcasted_iota(jnp.int32, (32, 1), 0) + r).astype(F32)
        is0 = row < n0
        s3 = dh1[t, 0:128]
        sm = s3[:, 0:1]
        se = jnp.where(is0, s3[:, 1:2], s3[:, 2:3])
        dc0, dc1 = gate * se, sm
        tot = c0 * dc0 + c1 * dc1
        dcl0, dcl1 = c0 * (dc0 - tot), c1 * (dc1 - tot)
        dgate = c0 * se
        dr0, dr1 = jnp.where(is0, dgate, 0.0), jnp.where(is0, 0.0, dgate)
        tot = r0 * dr0 + r1 * dr1
        drl0, drl1 = r0 * (dr0 - tot), r1 * (dr1 - tot)
        u2 = u2_ref[t, :]
        h2 = u2 * small_ref[2:3, :] + small_ref[3:4, :]
        dh2 = dh_ref[t, :]
        for i, d in enumerate((drl0, drl1, dcl0, dcl1)):
            acc(4 + i, h2 * d)
            dh2 = dh2 + d * small_ref[4 + i : 5 + i, :]
        acc(2, dh2 * u2)
        acc(3, dh2)
        e = dh2 * small_ref[2:3, :]
        inner = e - jnp.mean(e, axis=1, keepdims=True) - u2 * jnp.mean(e * u2, axis=1, keepdims=True)
        g = dys_ref[t, :].astype(F32) + inv * inner
        dx1[t, :] = g
        dab[t, :] = g.astype(BF)
        h1b[t, :] = (u1_ref[t, :] * small_ref[0:1, :] + small_ref[1:2, :]).astype(BF)

    rows_loop(T, 32, norm2)

    other = pl.multiple_of((1 - core) * half, half)
    mine = pl.multiple_of(core * half, half)

    def weight_grad(i, left, right):
        send[i] = mm(left[:, pl.ds(other, half)], right[...], ((0,), (0,))).astype(BF)
        c = remote(send.at[i], recv.at[i], sib_s.at[i], sib_r.at[i], sib)
        c.start()
        keep[i] = mm(left[:, pl.ds(mine, half)], right[...], ((0,), (0,)))
        return c

    def join(i, c, part, at):
        c.wait_recv()

        @pl.loop(0, S)
        def _(j):
            t = pl.ds(pl.multiple_of(j * WR, WR), WR)
            part[j, at : at + WR, :] = (keep[i, t, :] + recv[i, t, :].astype(F32)).astype(BF)

    for k in far:
        gy.b(k)
    c_o = weight_grad(3, o_ref, dab)
    loads[3].wait()
    do[...] = mm(dab[...], wbuf[3], ((1,), (1,))).astype(BF)
    join(3, c_o, part0, 0)
    for k in far:
        g0.a(k)

    low = lax.broadcasted_iota(jnp.int32, (T, 128), 1) < 64
    lowb = low.astype(F32).astype(BF)
    highb = (1.0 - low.astype(F32)).astype(BF)

    def heads(j):
        ln = pl.ds(pl.multiple_of(j * 128, 128), 128)
        qp, dop = q_ref[:, ln], do[:, ln]
        q2 = jnp.concatenate([qp * lowb, qp * highb], axis=0)
        do2 = jnp.concatenate([dop * lowb, dop * highb], axis=0)
        pr = p_ref[j]
        dp = mm(do2, v_ref[:, ln], ((1,), (1,)))
        ds = (pr * (dp - jnp.sum(pr * dp, axis=1, keepdims=True))).astype(BF)
        dq2 = mm(ds, k_ref[:, ln])
        dq[:, ln] = jnp.where(low, dq2[0:T], dq2[T:]).astype(BF) * BF(0.125)
        dk[:, ln] = mm(ds, q2, ((0,), (0,))).astype(BF)
        dv[:, ln] = mm(pr.astype(BF), do2, ((0,), (0,))).astype(BF)

    @pl.loop(0, D // 256)
    def _(j):
        heads(j)

    for k in far:
        gy.c(k)

    @pl.loop(D // 256, D // 128)
    def _(j):
        heads(j)

    c_v = weight_grad(2, h1b, dv)
    c_k = weight_grad(1, h1b, dk)
    c_q = weight_grad(0, h1b, dq)
    for k in reversed(range(L)):
        g0.b(k)
    join(2, c_v, part1, 2 * WR)
    join(1, c_k, part1, WR)
    join(0, c_q, part1, 0)
    for k in reversed(range(L)):
        g1.a(k)
    for i in range(3):
        loads[i].wait()
    dh1[...] = mm(dq[...], wbuf[0], ((1,), (1,)))
    dh1[...] = dh1[...] + mm(dk[...], wbuf[1], ((1,), (1,)))
    dh1[...] = dh1[...] + mm(dv[...], wbuf[2], ((1,), (1,)))
    for k in reversed(range(L)):
        g0.c(k)

    def norm1(r):
        t = pl.ds(r, 32)
        inv = stat_ref[t, :][:, 8:9]
        u = u1_ref[t, :]
        d = dh1[t, :]
        acc(0, d * u)
        acc(1, d)
        e = d * small_ref[0:1, :]
        inner = e - jnp.mean(e, axis=1, keepdims=True) - u * jnp.mean(e * u, axis=1, keepdims=True)
        tmpb[t, :] = (dx1[t, :] + inv * inner).astype(BF)

    rows_loop(T, 32, norm1)
    for i in range(8):
        smine[i : i + 1, :] = jnp.sum(accs[i], axis=0, keepdims=True)
    c_s = remote(smine, ssib, sib_s.at[4], sib_r.at[4], sib)
    c_s.start()
    for k in reversed(range(L)):
        g1.b(k)
    ig_out[...] = mm(perm[...], tmpb[...], ((0,), (0,))).astype(BF)
    c_s.wait()
    smine[...] = smine[...] + ssib[...]
    group = 128 // WR

    def s_at(i):
        return smine.at[:, pl.ds(pl.multiple_of((core * S + i) // group * 128, 128), 128)]

    def s_copy(i):
        to = (me + i) % S
        return remote(s_at(to), srecv.at[me], sm_s.at[i], sm_r.at[0], (core, to))

    @pl.loop(1, S)
    def _(i):
        s_copy(i).start()

    srecv[me] = s_at(me)[...]
    for k in range(1, L):
        gy.d(k)
    lsort[...] = (x1_ref[...] + ysum[...]).astype(BF)
    lo_out[...] = mm(perm[...], lsort[...], ((0,), (0,))).astype(BF)
    for k in far:
        g1.c(k)
    for k in range(1, L):
        g0.d(k)
    allr = srecv.at[pl.ds(0, S - 1)]
    remote(allr, allr, sm_s.at[0], sm_r.at[0], (core, xn)).wait_recv()
    smalls_out[...] = jnp.sum(srecv[...], axis=0)
    for k in range(1, L):
        g1.d(k)
    gy.finish()
    g0.finish()
    g1.finish()
    for c in (c_o, c_v, c_k, c_q):
        c.wait_send()

    @pl.loop(1, S)
    def _(i):
        s_copy(i).wait_send()


def back_call(dh, y, sc, small, stat, u1, u2, x1, dys, q, k, v, p, o, es, ss, wa, S):
    T, D = dh.shape
    WR = D // (2 * S)
    L = S // 4
    vm = pl.BlockSpec(memory_space=pltpu.VMEM)
    hb = pl.BlockSpec(memory_space=pl.ANY)
    V = pltpu.VMEM
    dma = pltpu.SemaphoreType.DMA
    sds = jax.ShapeDtypeStruct
    row = V((T, D), BF)

    def rs_bufs(R):
        return [V((S, R, D), BF)] + [V((L, R, D), BF)] * 4

    return pl.pallas_call(
        back_kernel,
        out_shape=(
            sds((T, D), BF), sds((T, D), BF), sds((3 * WR, D), F32), sds((WR, D), F32), sds((8, 128), F32),
        ),
        in_specs=[vm] * 15 + [hb, hb],
        out_specs=(vm,) * 5,
        scratch_shapes=[
            V((4, D, D), BF), V((T, T), BF), V((8, 8, D), F32), V((T, D), F32), row, row, row, row, row, row,
            V((T, D), F32), row, V((4, D // 2, D), F32), V((4, D // 2, D), BF), V((4, D // 2, D), BF),
        ]
        + rs_bufs(WR)
        + rs_bufs(3 * WR)
        + rs_bufs(T)
        + [
            V((T, D), F32), V((T, D), BF),
            V((8, D), F32), V((8, D), F32), V((S, 8, 128), F32),
            dma((3, 4, L)), dma((3, 4, L)), dma((5,)), dma((5,)), dma((S,)), dma((1,)), dma((4 + L,)),
        ],
        compiler_params=pltpu.CompilerParams(collective_id=3, has_side_effects=True, vmem_limit_bytes=60000000),
        cost_estimate=pl.CostEstimate(flops=4 * 10**9, bytes_accessed=20 * 2**20, transcendentals=2**20),
        name="back",
    )(dh, sc, small, stat, u1, u2, x1, dys, q, k, v, p, o, es, ss, y, wa)


def body_plain(
    hidden_in, doc_ids, expert_ids, slot_ids, out_grad, ln1_gain, ln1_bias, w_query, w_key, w_value,
    w_out, ln2_gain, ln2_bias, w_up, w_down, w_router, w_mix, expert_up, expert_down, load_avg,
):
    T, D = hidden_in.shape
    H, HD = HEADS, D // HEADS
    S = lax.axis_size("shard")
    C = lax.axis_size("dp")
    WR = w_query.shape[0]
    FF = w_up.shape[1]
    FR = w_down.shape[0]
    F = FR * C
    E = expert_up.shape[0]
    LO, HI = 80, T - 80

    pos = jnp.where(expert_ids == 0, slot_ids, jnp.sum((expert_ids == 0).astype(jnp.int32)) + slot_ids)
    n0 = jnp.sum((expert_ids == 0).astype(jnp.int32))
    place = lax.iota(jnp.int32, T)
    perm = (pos[None, :] == place[:, None]).astype(BF)
    xs = mm(perm, hidden_in)
    dys = mm(perm, out_grad).astype(BF)
    doc = doc_ids[0]
    allowed = (place[None, :] <= place[:, None]) & (doc[:, None] == doc[None, :])
    allowed = mm(mm(perm, allowed.astype(BF)).astype(BF), perm, ((1,), (1,))) > 0.5
    is0 = (place < n0)[:, None]

    small = jnp.stack(
        [ln1_gain, ln1_bias, ln2_gain, ln2_bias, w_router[:, 0], w_router[:, 1], w_mix[:, 0], w_mix[:, 1]]
    ).astype(F32)
    small = lax.all_gather(small, BOTH, axis=1, tiled=True)
    g1, b1, g2, b2 = small[0], small[1], small[2], small[3]
    wr, wm = small[4:6], small[6:8]

    wa = jnp.stack([w_query, w_key, w_value, w_out])
    wa = lax.all_gather(wa, BOTH, axis=1, tiled=True)
    wq, wk, wv, wo = wa[0], wa[1], wa[2], wa[3]

    ups = jnp.stack([w_up, expert_up[0], expert_up[1]])
    ups = ups.reshape(3, WR, C, S, FR).transpose(3, 0, 1, 2, 4).reshape(S, 3, WR, F)
    ups = lax.all_to_all(ups, "shard", 0, 0)
    ups = lax.all_gather(ups, "dp", axis=0)
    ups = ups.transpose(2, 0, 1, 3, 4).reshape(3, D, F)
    downs = jnp.stack([w_down, expert_down[0], expert_down[1]])
    downs = lax.all_gather(downs, "dp", axis=1, tiled=True)

    dy_all = ag(dys)

    n1, u1, i1 = layer_norm(xs, g1, b1)
    h1b = n1.astype(BF)
    q = (mm(h1b, wq) * 0.125).astype(BF).reshape(T, H, HD)
    k = mm(h1b, wk).astype(BF).reshape(T, H, HD)
    v = mm(h1b, wv).astype(BF).reshape(T, H, HD)
    s = jnp.einsum("ihd,jhd->hij", q, k, preferred_element_type=F32)
    s = jnp.where(allowed[None], s, -1e30)
    ex = jnp.exp(s - jnp.max(s, axis=-1, keepdims=True))
    p = ex / jnp.sum(ex, axis=-1, keepdims=True)
    pb = p.astype(BF)
    o = jnp.einsum("hij,jhd->ihd", pb, v, preferred_element_type=F32).reshape(T, D).astype(BF)
    x1 = xs + mm(o, wo)
    h2, u2, i2 = layer_norm(x1, g2, b2)
    h2b = h2.astype(BF)

    def two(w):
        return jnp.stack([jnp.sum(h2 * w[0], axis=-1), jnp.sum(h2 * w[1], axis=-1)], axis=-1)

    r = jax.nn.softmax(two(wr), axis=-1)
    c = jax.nn.softmax(two(wm), axis=-1)
    gate = jnp.where(is0, r[:, 0:1], r[:, 1:2])
    c0, c1 = c[:, 0:1], c[:, 1:2]
    we = c0 * gate
    scal = jnp.concatenate([c1, jnp.where(is0, we, 0.0), jnp.where(is0, 0.0, we)], axis=1)

    h_all = ag(h2b)
    scal_all = ag(scal)

    def cut(a, e):
        return (a[:, :LO] if e == 1 else a[:, HI:]) if e else a

    partial_y = jnp.zeros((S, T, D), F32)
    partial_dh = jnp.zeros((S, T, D), F32)
    score = []
    gup, gdown = [], []
    for e in range(3):
        he = cut(h_all, e)
        dye = cut(dy_all, e).astype(F32)
        se = cut(scal_all, e)[:, :, e : e + 1]
        n = he.shape[1]
        hf = he.reshape(S * n, D)
        pre = mm(hf, ups[e])
        val, der = gelu_pair(pre)
        ub = val.astype(BF)
        m = mm(ub, downs[e]).reshape(S, n, D)
        dm = (dye * se).astype(BF).reshape(S * n, D)
        dg = (mm(dm, downs[e], ((1,), (1,))) * der).astype(BF)
        gdown.append(mm(ub, dm, ((0,), (0,))))
        gup.append(mm(hf, dg, ((0,), (0,))))
        dx = mm(dg, ups[e], ((1,), (1,))).reshape(S, n, D)
        y = m * se
        sc = jnp.sum(dye * m, axis=-1)
        pad = [(0, 0), (0, T - n) if e < 2 else (T - n, 0)]
        live = is0[None, :, 0]
        partial_y += jnp.pad(y, pad + [(0, 0)])
        partial_dh += jnp.pad(dx, pad + [(0, 0)])
        score.append(jnp.pad(sc, pad))
    yfull = rs(partial_y)
    dh2 = rs(partial_dh)
    sc = lax.psum_scatter(jnp.stack(score, axis=1), "shard", scatter_dimension=0, tiled=False)
    sm = sc[0][:, None]
    se = jnp.where(is0, sc[1][:, None], sc[2][:, None])

    dc0, dc1 = gate * se, sm
    tot = c0 * dc0 + c1 * dc1
    dcl0, dcl1 = c0 * (dc0 - tot), c1 * (dc1 - tot)
    dgate = c0 * se
    dr0, dr1 = jnp.where(is0, dgate, 0.0), jnp.where(is0, 0.0, dgate)
    tot = r[:, 0:1] * dr0 + r[:, 1:2] * dr1
    drl0, drl1 = r[:, 0:1] * (dr0 - tot), r[:, 1:2] * (dr1 - tot)
    layer_out = (x1 + yfull).astype(BF)
    dh2 = dh2 + drl0 * wr[0] + drl1 * wr[1] + dcl0 * wm[0] + dcl1 * wm[1]
    gw = [jnp.sum(h2 * t, axis=0) for t in (drl0, drl1, dcl0, dcl1)]
    dx1, gg2, gb2 = norm_back(dh2, u2, i2, g2)
    dx1 = dx1 + dys.astype(F32)
    dab = dx1.astype(BF)
    gwo = mm(o, dab, ((0,), (0,)))
    do = mm(dab, wo, ((1,), (1,))).astype(BF).reshape(T, H, HD)
    dp = jnp.einsum("ihd,jhd->hij", do, v, preferred_element_type=F32)
    ds = (p * (dp - jnp.sum(p * dp, axis=-1, keepdims=True))).astype(BF)
    dq = jnp.einsum("hij,jhd->ihd", ds, k, preferred_element_type=F32).astype(BF)
    dq = (dq * BF(0.125)).reshape(T, D)
    dk = jnp.einsum("hij,ihd->jhd", ds, q, preferred_element_type=F32).astype(BF).reshape(T, D)
    dv = jnp.einsum("hij,ihd->jhd", pb, do, preferred_element_type=F32).astype(BF).reshape(T, D)
    dh1 = mm(dq, wq, ((1,), (1,))) + mm(dk, wk, ((1,), (1,))) + mm(dv, wv, ((1,), (1,)))
    ga = jnp.stack([mm(h1b, dq, ((0,), (0,))), mm(h1b, dk, ((0,), (0,))), mm(h1b, dv, ((0,), (0,))), gwo])
    dxn, gg1, gb1 = norm_back(dh1, u1, i1, g1)
    input_grad = (dx1 + dxn).astype(BF)

    layer_out = mm(perm, layer_out, ((0,), (0,))).astype(BF)
    input_grad = mm(perm, input_grad, ((0,), (0,))).astype(BF)

    smalls = lax.psum(jnp.stack([gg1, gb1, gg2, gb2] + gw), BOTH)
    mine = lax.dynamic_slice_in_dim(smalls, lax.axis_index(BOTH) * WR, WR, 1)
    ga = ga.reshape(4, C, S, WR, D).transpose(1, 2, 0, 3, 4)
    ga = lax.psum_scatter(ga.astype(BF), "dp", scatter_dimension=0, tiled=False)
    ga = lax.psum_scatter(ga, "shard", scatter_dimension=0, tiled=False).astype(F32)
    gdown = lax.psum_scatter(jnp.stack(gdown), "dp", scatter_dimension=1, tiled=True)
    gup = jnp.stack(gup).reshape(3, C, S, WR, F).transpose(1, 2, 0, 3, 4)
    gup = lax.psum_scatter(gup, "dp", scatter_dimension=0, tiled=False).astype(BF)
    gup = lax.all_to_all(gup, "shard", 0, 0).astype(F32)
    gup = gup.reshape(S, 3, WR, C, FR).transpose(1, 2, 3, 0, 4).reshape(3, WR, FF)

    counts = lax.psum(jnp.stack([n0, T - n0]), BOTH)
    load_new = 0.9 * load_avg + 0.1 * counts.astype(F32) * E / (T * C * S)
    return (
        layer_out, input_grad, mine[0], mine[1], ga[0], ga[1], ga[2], ga[3], mine[2], mine[3],
        gup[0], gdown[0], jnp.stack([mine[4], mine[5]], axis=1), jnp.stack([mine[6], mine[7]], axis=1),
        gup[1:], gdown[1:], counts, load_new,
    )


def body(
    hidden_in, doc_ids, expert_ids, slot_ids, out_grad, ln1_gain, ln1_bias, w_query, w_key, w_value,
    w_out, ln2_gain, ln2_bias, w_up, w_down, w_router, w_mix, expert_up, expert_down, load_avg,
):
    T, D = hidden_in.shape
    H, HD = HEADS, D // HEADS
    S = lax.axis_size("shard")
    C = lax.axis_size("dp")
    WR = w_query.shape[0]
    FF = w_up.shape[1]
    FR = w_down.shape[0]
    F = FR * C
    E = expert_up.shape[0]
    ndev = C * S
    dev = lax.axis_index(BOTH)
    small = jnp.stack(
        [ln1_gain, ln1_bias, ln2_gain, ln2_bias, w_router[:, 0], w_router[:, 1], w_mix[:, 0], w_mix[:, 1]]
    ).astype(F32)
    group = 128 // WR
    slot_of = lax.broadcasted_iota(jnp.int32, (8, 128), 1) // WR
    small = jnp.where(slot_of == dev % group, jnp.tile(small, (1, group)), 0.0)
    (h2b, stat, scal8, u1, u2, x1, dys, q, k, v, p, o, small, count, wa, dy_all, ups, downs) = attn_call(
        hidden_in, out_grad, doc_ids, expert_ids.reshape(1, T), slot_ids.reshape(1, T), small,
        (w_query, w_key, w_value, w_out), w_up, expert_up, w_down, expert_down, S,
    )
    y_parts, dh2, sc, gup, gdn0, gdn12 = ffn_call(h2b, scal8, dy_all, ups, downs)
    layer_out, input_grad, gqkv, gwo, smalls = back_call(
        dh2, y_parts, sc, small, stat, u1, u2, x1, dys, q, k, v, p, o,
        expert_ids.reshape(1, T), slot_ids.reshape(1, T), wa.reshape(4, D, D), S,
    )
    mine = lax.dynamic_slice_in_dim(smalls, dev % group * WR, WR, 1)
    ga = gqkv.reshape(3, WR, D)
    gup = gup.astype(F32).reshape(S, 3, WR, C, FR).transpose(1, 2, 3, 0, 4).reshape(3, WR, FF)
    tokens0 = count[0, 0].astype(jnp.int32)
    counts = jnp.stack([tokens0, T * ndev - tokens0])
    load_new = 0.9 * load_avg + 0.1 * counts.astype(F32) * E / (T * ndev)
    return (
        layer_out, input_grad, mine[0], mine[1], ga[0], ga[1], ga[2], gwo, mine[2], mine[3],
        gup[0], gdn0, mine[4:6].T, mine[6:8].T, gup[1:], gdn12, counts, load_new,
    )


def pick(*args):
    S, C, WR, FR = lax.axis_size("shard"), lax.axis_size("dp"), args[7].shape[0], args[14].shape[0]
    fast = C == 2 and S % 4 == 0 and S >= 8 and WR % 16 == 0 and 128 % WR == 0 and FR % 128 == 0
    return (body if fast else body_plain)(*args)


def solution(mesh):
    row, vec = P(BOTH, None), P(BOTH)
    mid = P(None, BOTH, None)
    return jax.shard_map(
        pick,
        mesh=mesh,
        in_specs=(row, row, vec, vec, row, vec, vec, row, row, row, row, vec, vec, row, row, row, row, mid, mid, P()),
        out_specs=(row, row, vec, vec, row, row, row, row, vec, vec, row, row, row, row, mid, mid, P(), P()),
        check_vma=False,
    )
```

```python
import jax
import jax.numpy as jnp
from jax import lax
from jax.experimental import pallas as pl
from jax.experimental.pallas import tpu as pltpu
from jax.sharding import PartitionSpec as P

HEADS = 16
CAP = 74
BF = jnp.bfloat16
F32 = jnp.float32
BOTH = ("dp", "shard")
MESH = pl.DeviceIdType.MESH


def mm(a, b, dims=((1,), (0,))):
    return lax.dot_general(a, b, (dims, ((), ())), preferred_element_type=F32)


def layer_norm(values, gain, bias):
    centre = values - jnp.mean(values, axis=-1, keepdims=True)
    scale_inv = lax.rsqrt(jnp.mean(centre * centre, axis=-1, keepdims=True) + 1e-05)
    normed = centre * scale_inv
    return (normed * gain + bias, normed, scale_inv)


def norm_back(grad_out, normed, scale_inv, gain):
    grad_normed = grad_out * gain
    inner = grad_normed - jnp.mean(grad_normed, axis=-1, keepdims=True)
    inner = inner - normed * jnp.mean(grad_normed * normed, axis=-1, keepdims=True)
    return (scale_inv * inner, jnp.sum(grad_out * normed, axis=0), jnp.sum(grad_out, axis=0))


def gelu_pair(t):
    inner = 0.7978845608 * (t + 0.044715 * t * t * t)
    th = jnp.tanh(inner)
    val = 0.5 * t * (1.0 + th)
    der = 0.5 * (1.0 + th) + 0.5 * t * (1.0 - th * th) * 0.7978845608 * (1.0 + 3.0 * 0.044715 * t * t)
    return val, der


def ag(block):
    return lax.all_gather(block, "shard", axis=0, tiled=False)


def rs(parts):
    return lax.psum_scatter(parts.astype(BF), "shard", scatter_dimension=0, tiled=False).astype(F32)


def place_of():
    me = lax.axis_index("shard")
    core = lax.axis_index("dp")
    z, p = me // 4, me % 4
    xq = p + 1 - 2 * (p % 2)
    yq = p + 2 - 4 * (p // 2)
    return me, core, z, p, xq, yq, 3 - p


def greet(shards, core):
    bar = pltpu.get_barrier_semaphore()
    me = lax.axis_index("shard")

    @pl.loop(1, shards)
    def _(i):
        pl.semaphore_signal(bar, inc=1, device_id=(core, (me + i) % shards), device_id_type=MESH)

    pl.semaphore_signal(bar, inc=1, device_id=(1 - core, me), device_id_type=MESH)
    pl.semaphore_wait(bar, shards)


def remote(src, dst, send, recv, dev):
    return pltpu.make_async_remote_copy(
        src_ref=src, dst_ref=dst, send_sem=send, recv_sem=recv, device_id=dev, device_id_type=MESH
    )


def rows_loop(count, step, fn):
    @pl.loop(0, count // step)
    def _(i):
        fn(pl.multiple_of(i * step, step))


def level_order(z, L):
    upper = z // (L // 2)
    y = z + upper * (L - 1 - 2 * z)

    def lev_of(k):
        low = k - 1 + (k - 1 - y + L) // L
        lev = low + upper * (L - 1 - 2 * low)
        first = 1 - (k + L - 1) // L
        return lev + first * (z - lev)

    return lev_of


def tree_gather(at, own, ss, rs, dev, levels):
    core, z, p, xq, yq, dq = dev
    xn, yn = z * 4 + xq, z * 4 + yq
    me = z * 4 + p
    pair = me + 4 - 8 * (z % 2)
    lev_of, L = levels

    def copy(kind, slot, src, idx, to):
        return remote(src, at(idx), ss.at[kind, slot], rs.at[kind, slot], (core, to))

    def up_line(src, send):
        return remote(src, at(me), send, rs.at[0, z], (core, me + 4))

    def down_line(src, send):
        return remote(src, at(me), send, rs.at[0, z], (core, me - 4))

    def onward(k):
        lev = lev_of(k)
        step = 1 - 2 * ((lev - z + L) // L)
        to = z + step
        idx = lev * 4 + p
        ok = (to >= 0) & (to < L)
        return ok, remote(at(idx), at(idx), ss.at[0, lev], rs.at[0, lev], (core, me + 4 * step))

    class Stages:
        @staticmethod
        def start():
            @pl.when(z < L - 1)
            def _():
                up_line(own, ss.at[0, z]).start()

            @pl.when(z > 0)
            def _():
                down_line(own, ss.at[4, 0]).start()

            copy(1, z, own, me, xn).start()
            copy(2, z, own, me, yn).start()

        @staticmethod
        def a(k):
            lev = lev_of(k)
            idx = lev * 4 + p
            copy(0, lev, own, idx, xn).wait_recv()
            ok, on = onward(k)

            @pl.when(ok)
            def _():
                on.start()

            copy(1, lev, at(idx), idx, xn).start()
            copy(2, lev, at(idx), idx, yn).start()

        @staticmethod
        def b(k):
            lev = lev_of(k)
            odd = lev // 2 % 2
            copy(1, lev, own, lev * 4 + xq, xn).wait_recv()
            copy(2, lev, own, lev * 4 + yq, yn).wait_recv()
            idx = lev * 4 + xq + odd * (yq - xq)

            @pl.when((lev + z) % 2 == 0)
            def _():
                copy(3, lev, at(idx), idx, yn + odd * (xn - yn)).start()

        @staticmethod
        def c(k):
            lev = lev_of(k)
            idx = lev * 4 + dq

            @pl.when((lev + z) % 2 == 0)
            def _():
                copy(3, lev, own, idx, xn).wait_recv()
                copy(5, lev, at(idx), idx, pair).start()

        @staticmethod
        def d(k):
            lev = lev_of(k)

            @pl.when((lev + z) % 2 == 1)
            def _():
                copy(5, lev, own, lev * 4 + dq, pair).wait_recv()

        @staticmethod
        def finish():
            @pl.when(z < L - 1)
            def _():
                up_line(own, ss.at[0, z]).wait_send()

            @pl.when(z > 0)
            def _():
                down_line(own, ss.at[4, 0]).wait_send()

            @pl.loop(0, L)
            def _(k):
                lev = lev_of(k)
                for kind in range(1, 3):
                    copy(kind, lev, own, me, xn).wait_send()

                @pl.when((lev + z) % 2 == 0)
                def _():
                    for kind in (3, 5):
                        copy(kind, lev, own, me, xn).wait_send()

            @pl.loop(1, L)
            def _(k):
                ok, on = onward(k)

                @pl.when(ok)
                def _():
                    on.wait_send()

    return Stages


def tree_scatter(part, ra, rbx, rby, rd, final, ss, rs, dev, levels, rz=None):
    core, z, p, xq, yq, dq = dev
    xn, yn = z * 4 + xq, z * 4 + yq
    pair = z * 4 + p + 4 - 8 * (z % 2)
    lev_of, L = levels
    R = part.shape[1]

    def copy(kind, lev, src, dst, to):
        return remote(src, dst, ss.at[kind, lev], rs.at[kind, lev], (core, to))

    def sides(lev):
        copy(1, lev, part.at[lev * 4 + xq], rbx.at[lev], xn).start()
        copy(2, lev, part.at[lev * 4 + yq], rby.at[lev], yn).start()

    class Stages:
        @staticmethod
        def share(k):
            lev = lev_of(k)

            @pl.when((lev + z) % 2 == 1)
            def _():
                copy(4, lev, part.at[lev * 4 + dq], rz.at[lev // 2], pair).start()

        @staticmethod
        def a(k):
            lev = lev_of(k)
            odd = k % 2 if rz is None else lev // 2 % 2
            diag = lev * 4 + dq

            def send():
                copy(0, lev, part.at[diag], ra.at[lev], yn + odd * (xn - yn)).start()

            def join():
                copy(4, lev, rz.at[lev // 2], rz.at[lev // 2], pair).wait_recv()

                def add(r):
                    t = pl.ds(r, 32)
                    part[diag, t, :] = (part[diag, t, :].astype(F32) + rz[lev // 2, t, :].astype(F32)).astype(BF)

                rows_loop(R, 32, add)
                send()

            if rz is None:
                send()
            else:
                pl.when((lev + z) % 2 == 0)(join)

        @staticmethod
        def b(k):
            lev = lev_of(k)
            odd = k % 2 if rz is None else lev // 2 % 2
            via = lev * 4 + xq + odd * (yq - xq)
            copy(0, lev, ra.at[lev], ra.at[lev], xn).wait_recv()

            def add(r):
                t = pl.ds(r, 32)
                part[via, t, :] = (part[via, t, :].astype(F32) + ra[lev, t, :].astype(F32)).astype(BF)

            rows_loop(R, 32, add)
            sides(lev)

        @staticmethod
        def b0(k):
            pl.when((lev_of(k) + z) % 2 == 1)(lambda: sides(lev_of(k)))

        @staticmethod
        def b1(k):
            pl.when((lev_of(k) + z) % 2 == 0)(lambda: Stages.b(k))

        @staticmethod
        def c0(k):
            pl.when((lev_of(k) + z) % 2 == 1)(lambda: Stages.c(k))

        @staticmethod
        def c1(k):
            pl.when((lev_of(k) + z) % 2 == 0)(lambda: Stages.c(k))

        @staticmethod
        def c(k):
            lev = lev_of(k)
            own = lev * 4 + p
            copy(1, lev, rbx.at[lev], rbx.at[lev], xn).wait_recv()
            copy(2, lev, rby.at[lev], rby.at[lev], yn).wait_recv()

            def add(r, last):
                t = pl.ds(r, 32)
                tot = part[own, t, :].astype(F32) + rbx[lev, t, :].astype(F32) + rby[lev, t, :].astype(F32)
                if last:
                    final[t, :] = tot
                else:
                    part[own, t, :] = tot.astype(BF)

            def close():
                rows_loop(R, 32, lambda r: add(r, True))

            def send():
                rows_loop(R, 32, lambda r: add(r, False))
                remote(part.at[own], rd.at[z], ss.at[3, lev], rs.at[3, z], (core, lev * 4 + p)).start()

            if isinstance(k, int):
                (send if k else close)()
            else:
                pl.when(k == 0)(close)
                pl.when(k > 0)(send)

        @staticmethod
        def d(k):
            lev = lev_of(k)
            copy(3, lev, rd.at[lev], rd.at[lev], xn).wait_recv()

            def add(r):
                t = pl.ds(r, 32)
                final[t, :] = final[t, :] + rd[lev, t, :].astype(F32)

            rows_loop(R, 32, add)

        @staticmethod
        def finish():
            @pl.loop(0, L)
            def _(k):
                lev = lev_of(k)
                for kind in (1, 2):
                    copy(kind, lev, ra.at[0], ra.at[0], xn).wait_send()

                if rz is None:
                    copy(0, lev, ra.at[0], ra.at[0], xn).wait_send()
                else:
                    kind = (lev + z) % 2 * 4
                    copy(kind, lev, ra.at[0], ra.at[0], xn).wait_send()

                @pl.when(k > 0)
                def _():
                    copy(3, lev, ra.at[0], ra.at[0], xn).wait_send()

    return Stages


def ffn_kernel(
    h_ref, scal_ref, dy_hbm, up_hbm, wd_hbm, ed_hbm, dn_hbm,
    y_out, dh_out, sc_out, gup_out, gdn0_out, gdn12_out,
    dy_ref, up_ref, dn_ref, ypart, hall, scall, psc, screcv, wcol, scol, part, ra, rbx, rby, rd,
    pre, der, ub, dg, dm, m, yacc, dxacc, gdn, gup, sib_dn, sib_up,
    ag_s, ag_r, rs_s, rs_r, one_s, one_r, sm_s, sm_r, loc, yloc,
):
    S, T, D = hall.shape
    F = up_hbm.shape[2]
    L = S // 4
    LO = 80
    HI = T - LO
    me, core, z, p, xq, yq, dq = place_of()
    xn = z * 4 + xq
    lev_of = level_order(z, L)
    dev, levels = (core, z, p, xq, yq, dq), (lev_of, L)
    greet(S, core)
    hg = tree_gather(lambda i: hall.at[i], h_ref, ag_s, ag_r, dev, levels)
    rgs = []
    for i in range(2):
        t = pl.ds(i * (T // 2), T // 2)
        bufs = [b.at[:, t, :] for b in (part, ra, rbx, rby, rd)]
        rgs.append(tree_scatter(*bufs, dh_out.at[t], rs_s.at[i], rs_r.at[i], dev, levels))
    hg.start()
    half_f = F // 2
    mine_f = pl.ds(pl.multiple_of(core * half_f, half_f), half_f)
    other_f = pl.ds(pl.multiple_of((1 - core) * half_f, half_f), half_f)
    pairs = (
        (up_hbm, up_ref),
        (wd_hbm, dn_ref.at[0, mine_f]),
        (ed_hbm, dn_ref.at[pl.ds(1, 2), mine_f]),
        (dn_hbm, dn_ref.at[:, other_f]),
        (dy_hbm, dy_ref),
    )
    loads = [pltpu.make_async_copy(a, b, loc.at[i]) for i, (a, b) in enumerate(pairs)]
    for c in loads:
        c.start()

    @pl.loop(1, S)
    def _(i):
        remote(scal_ref, scall.at[me], sm_s.at[0, i], sm_r.at[0], (core, (me + i) % S)).start()

    hall[me] = h_ref[...]
    scall[me] = scal_ref[...]
    gdn[...] = jnp.zeros_like(gdn)
    gup[...] = jnp.zeros_like(gup)
    remote(scall.at[pl.ds(0, S - 1)], scall.at[pl.ds(0, S - 1)], sm_s.at[0, 0], sm_r.at[0], (core, xn)).wait_recv()

    size = (4 * T, 4 * LO, 4 * LO)
    first = (0, 4 * T, 4 * T + 4 * LO)

    def compute(lev, between):
        base = lev * 4
        for q in range(4):
            full = jnp.concatenate([scall[base + q], jnp.zeros((120, 128), F32)], axis=0)
            wcol[q] = full.T
        for e in range(3):
            n = LO if e else T
            off = HI if e == 2 else 0
            rows, at0 = size[e], first[e]
            here = slice(at0, at0 + rows)
            hm = hall[pl.ds(base, 4), off : off + n, :].reshape(rows, D)
            pre[0:rows, :] = mm(hm, up_ref[e])

            def act(r):
                t = pl.ds(r, rows // 4)
                val, d = gelu_pair(pre[t, :])
                ub[pl.ds(pl.multiple_of(at0 + r, 16), rows // 4), :] = val.astype(BF)
                der[t, :] = d

            rows_loop(rows, rows // 4, act)
            m[0:rows, :] = mm(ub[here, :], dn_ref[e])
            step = n if e else T // 2
            lane = lax.broadcasted_iota(jnp.int32, (step, 128), 1)
            for q in range(4):

                def elem(r):
                    at = pl.ds(pl.multiple_of(r + off, 16), step)
                    mine = pl.ds(pl.multiple_of(q * n + r, 16), step)
                    keep = pl.ds(pl.multiple_of(at0 + q * n + r, 16), step)
                    t = pl.ds(pl.multiple_of(q * T + off + r, 16), step)
                    w = wcol[q, at, :][:, e : e + 1]
                    dyv = dy_ref[base + q, at, :].astype(F32)
                    mv = m[mine, :]
                    s = jnp.sum(dyv * mv, axis=1, keepdims=True)
                    s = jnp.where(lane == e, s, 0.0)
                    dm[keep, :] = (dyv * w).astype(BF)
                    if e:
                        yacc[t, :] = yacc[t, :] + mv * w
                        scol[q, at, :] = scol[q, at, :] + s
                    else:
                        yacc[t, :] = mv * w
                        scol[q, at, :] = s

                rows_loop(n, step, elem)
            pre[0:rows, :] = mm(dm[here, :], dn_ref[e], ((1,), (1,)))

            def back(r):
                t = pl.ds(r, rows // 4)
                dg[pl.ds(pl.multiple_of(at0 + r, 16), rows // 4), :] = (pre[t, :] * der[t, :]).astype(BF)

            rows_loop(rows, rows // 4, back)
            if e:
                m[0:rows, :] = mm(dg[here, :], up_ref[e], ((1,), (1,)))
                for q in range(4):
                    t = slice(q * T + off, q * T + off + n)
                    dxacc[t, :] = dxacc[t, :] + m[q * n : q * n + n, :]
            else:
                dxacc[...] = mm(dg[here, :], up_ref[0], ((1,), (1,)))
            between(e)
        for q in range(4):
            psc[base + q] = scol[q].T[0:8, :]
            t = slice(q * T, q * T + T)
            part[base + q] = dxacc[t, :].astype(BF)
            ypart[base + q] = yacc[t, :].astype(BF)
        some = pl.ds(base, 4)
        pltpu.make_async_copy(ypart.at[some], y_out.at[some], yloc.at[lev]).start()

    def weight_grads(lev):
        for e in range(3):
            n = LO if e else T
            off = HI if e == 2 else 0
            here = slice(first[e], first[e] + size[e])
            hm = hall[pl.ds(lev * 4, 4), off : off + n, :].reshape(size[e], D)
            gdn[e] = gdn[e] + mm(ub[here, :], dm[here, :], ((0,), (0,)))
            gup[e] = gup[e] + mm(dg[here, :], hm, ((0,), (0,)))

    end = (z == 0) | (z == L - 1)
    hg.a(1)
    hg.b(0)
    hg.a(2)
    pl.when(jnp.logical_not(end))(lambda: hg.a(3))
    hg.c(0)
    for c in loads:
        c.wait()

    def far_a(i):
        pl.when(end)(lambda: hg.a(i))

    @pl.loop(0, L)
    def _(k):
        @pl.when(k > 0)
        def _():
            hg.d(k)

        def between(e):
            @pl.when(k == 0)
            def _():
                for call, i in (((far_a, 3), (hg.b, 1)), ((hg.c, 1), (hg.b, 2)), ())[e]:
                    call(i)

            @pl.when(k == 1)
            def _():
                for call, i in (((hg.c, 2), (hg.b, 3)), ((hg.c, 3),), ())[e]:
                    call(i)

            if e == 1:

                @pl.when(k > 0)
                def _():
                    for g in rgs:
                        g.b(k - 1)

        compute(lev_of(k), between)
        for g in rgs:
            g.a(k)

        @pl.when(k > 0)
        def _():
            for g in rgs:
                g.c(k - 1)

        weight_grads(lev_of(k))

    half = D // 2
    other = pl.multiple_of((1 - core) * half, half)
    mine_d = pl.multiple_of(core * half, half)
    sib = (1 - core, me)
    c_up = remote(gup.at[:, :, pl.ds(other, half)], sib_up, one_s.at[0], one_r.at[0], sib)
    c_dn = remote(gdn.at[:, other_f, :], sib_dn, one_s.at[1], one_r.at[1], sib)
    c_up.start()
    c_dn.start()

    @pl.loop(1, S)
    def _(i):
        to = (me + i) % S
        remote(psc.at[to], screcv.at[i], sm_s.at[1, i], sm_r.at[1], (core, to)).start()

    for g in rgs:
        g.b(L - 1)
    c_up.wait_recv()
    for e in range(3):
        tot = gup[e, :, pl.ds(mine_d, half)] + sib_up[e]
        gup_out[e] = tot.T.astype(BF)
        if e == 0:
            for g in rgs:
                g.c(L - 1)
    screcv[0] = psc[me]
    c_dn.wait_recv()
    gdn0_out[...] = gdn[0, mine_f, :] + sib_dn[0]
    for e in range(1, 3):
        gdn12_out[e - 1] = gdn[e, mine_f, :] + sib_dn[e]
    for k in range(1, L):
        for g in rgs:
            g.d(k)
    remote(screcv.at[pl.ds(1, S - 1)], screcv.at[pl.ds(1, S - 1)], sm_s.at[1, 0], sm_r.at[1], (core, xn)).wait_recv()
    sc_out[...] = jnp.sum(screcv[...], axis=0)

    for i in range(L):
        some = pl.ds(i * 4, 4)
        pltpu.make_async_copy(ypart.at[some], y_out.at[some], yloc.at[i]).wait()
    c_up.wait_send()
    c_dn.wait_send()
    hg.finish()
    for g in rgs:
        g.finish()

    @pl.loop(1, S)
    def _(i):
        remote(scal_ref, scall.at[0], sm_s.at[0, i], sm_r.at[0], (core, xn)).wait_send()
        remote(psc.at[0], screcv.at[0], sm_s.at[1, i], sm_r.at[1], (core, xn)).wait_send()


def ffn_call(h2b, scal, dy_all, ups, wd, ed, downs):
    S, T, D = dy_all.shape
    F = ups.shape[2]
    L = S // 4
    rows = 4 * T + 8 * 80
    vm = pl.BlockSpec(memory_space=pltpu.VMEM)
    hb = pl.BlockSpec(memory_space=pl.ANY)
    V = pltpu.VMEM
    dma = pltpu.SemaphoreType.DMA
    sds = jax.ShapeDtypeStruct
    blocks = V((L, T, D), BF)
    return pl.pallas_call(
        ffn_kernel,
        out_shape=(
            sds((S, T, D), BF), sds((T, D), F32), sds((8, 128), F32), sds((3, D // 2, F), BF),
            sds((F // 2, D), F32), sds((2, F // 2, D), F32),
        ),
        in_specs=[vm] * 2 + [hb] * 5,
        out_specs=(hb,) + (vm,) * 5,
        scratch_shapes=[
            V((S, T, D), BF), V((3, D, F), BF), V((3, F, D), BF), V((S, T, D), BF), V((S, T, D), BF), V((S, 8, 128), F32), V((S, 8, 128), F32), V((S, 8, 128), F32),
            V((4, T, 128), F32), V((4, T, 128), F32),
            V((S, T, D), BF), blocks, blocks, blocks, blocks,
            V((4 * T, F), F32), V((4 * T, F), F32), V((rows, F), BF), V((rows, F), BF), V((rows, D), BF),
            V((4 * T, D), F32), V((4 * T, D), F32), V((4 * T, D), F32),
            V((3, F, D), F32), V((3, F, D), F32), V((3, F // 2, D), F32), V((3, F, D // 2), F32),
            dma((6, L)), dma((6, L)), dma((2, 4, L)), dma((2, 4, L)), dma((2,)), dma((2,)), dma((2, S)), dma((2,)), dma((5,)), dma((L,)),
        ],
        compiler_params=pltpu.CompilerParams(collective_id=2, has_side_effects=True, vmem_limit_bytes=64000000),
        cost_estimate=pl.CostEstimate(flops=15 * 10**9, bytes_accessed=20 * 2**20, transcendentals=2**20),
        name="ffn",
    )(h2b, scal, dy_all, ups, wd, ed, downs)


def sort_matrix(ids_e, ids_s, T):
    zero = ids_e == 0
    n0 = jnp.sum(jnp.where(zero, 1.0, 0.0), axis=1, keepdims=True)
    slot = ids_s.astype(F32)
    pos = jnp.where(zero, slot, slot + n0)
    sub = lax.broadcasted_iota(jnp.int32, (T, T), 0).astype(F32)
    return jnp.where(sub == pos, 1.0, 0.0), n0


def attn_kernel(
    x_ref, dy_ref, doc_ref, e_ref, s_ref, small_ref, wq_ref, wk_ref, wv_ref, wo_ref,
    wu_ref, eu_ref, wd_ref, ed_ref,
    h2b_out, stat_out, scal_out, u1_out, u2_out, x1_out, dys_out, q_out, k_out, v_out, p_out, o_out,
    small_out, count_out, w_out, dyall_out, up_out, dn_out,
    wbuf, upb, smallbuf, h1b, bias, xs, tmp,
    ag_s, ag_r, sib_s, sib_r, sm_s, sm_r, loc,
):
    T, D = x_ref.shape
    WR = wq_ref.shape[0]
    FR = wd_ref.shape[0]
    N = wbuf.shape[1]
    S = N // 2
    L = S // 4
    me, core, z, p, xq, yq, dq = place_of()
    xn = z * 4 + xq
    my = core * S + me
    sib = (1 - core, me)
    greet(S, core)
    lev_of = level_order(z, L)

    dev, levels = (core, z, p, xq, yq, dq), (lev_of, L)

    def w_at(i):
        return wbuf.at[:, core * S + i]

    wg = tree_gather(w_at, w_at(me), ag_s.at[0], ag_r.at[0], dev, levels)
    dyg = tree_gather(lambda i: dyall_out.at[i], dys_out, ag_s.at[2], ag_r.at[2], dev, levels)

    for i, w in enumerate((wq_ref, wk_ref, wv_ref, wo_ref)):
        wbuf[i, my] = w[...]
    wg.start()

    perm, n0 = sort_matrix(e_ref[...], s_ref[...], T)
    smallbuf[my, 0:8, :] = small_ref[...]
    lane8 = lax.broadcasted_iota(jnp.int32, (8, 128), 1)
    smallbuf[my, 8:16, :] = jnp.where(lane8 == 0, jnp.broadcast_to(n0, (8, 128)), 0.0)

    @pl.loop(1, S)
    def _(i):
        remote(smallbuf.at[my], smallbuf.at[my], sm_s.at[0, i], sm_r.at[0], (core, (me + i) % S)).start()

    dn_copies = (
        remote(wd_ref, dn_out.at[0], sib_s.at[2, 0], sib_r.at[2, 0], sib),
        remote(ed_ref, dn_out.at[pl.ds(1, 2)], sib_s.at[2, 1], sib_r.at[2, 1], sib),
    )
    for c in dn_copies:
        c.start()
    permb = perm.astype(BF)
    xs[...] = mm(permb, x_ref[...])
    dys_out[...] = mm(permb, dy_ref[...]).astype(BF)
    dy_local = pltpu.make_async_copy(dys_out, dyall_out.at[me], loc.at[2])
    dy_local.start()

    docs = (doc_ref[...] == lax.broadcasted_iota(jnp.int32, (16, T), 0)).astype(F32).astype(BF)
    docs = mm(docs, permb, ((1,), (1,))).astype(BF)
    same = mm(docs, docs, ((0,), (0,)))
    place = lax.broadcasted_iota(jnp.int32, (T, T), 1).astype(F32)
    ord_col = jnp.sum(perm * place, axis=1, keepdims=True)
    ord_row = mm(place[0:16, :].astype(BF), permb, ((1,), (1,)))[0:1, :]
    bias[...] = jnp.where((same > 0.5) & (ord_row <= ord_col), 0.0, -1e30)

    lane = lax.broadcasted_iota(jnp.int32, (64, 128), 1)

    def norm1(r):
        t = pl.ds(r, 64)
        v = xs[t, :]
        cen = v - jnp.mean(v, axis=1, keepdims=True)
        inv = lax.rsqrt(jnp.mean(cen * cen, axis=1, keepdims=True) + 1e-05)
        u1_out[t, :] = cen * inv
        stat_out[t, :] = jnp.where(lane == 8, inv, 0.0)

    rows_loop(T, 64, norm1)

    wg.a(1)
    wg.b(0)
    wg.a(2)
    wg.b(1)
    wg.a(3)
    wg.c(0)

    group = 128 // WR
    remote(smallbuf.at[pl.ds(0, S - 1)], smallbuf.at[pl.ds(0, S - 1)], sm_s.at[0, 0], sm_r.at[0], (core, xn)).wait_recv()
    mine_small = smallbuf.at[pl.ds(core * S, S)]
    c_small = remote(mine_small, mine_small, sib_s.at[2, 2], sib_r.at[2, 2], sib)
    c_small.start()

    def up_copy(e, h, i):
        to = (me + i) % S
        src = wu_ref if e == 0 else eu_ref.at[e - 1]
        return remote(
            src.at[:, pl.ds(pl.multiple_of((h * S + to) * FR, FR), FR)],
            upb.at[e, pl.ds(pl.multiple_of(my * WR, WR), WR), pl.ds(h * FR, FR)],
            sm_s.at[1, i], sm_r.at[1], (core, to),
        )

    @pl.loop(1, S)
    def _(i):
        for e in range(3):
            for h in range(2):
                up_copy(e, h, i).start()

    for e in range(3):
        for h in range(2):
            src = wu_ref if e == 0 else eu_ref.at[e - 1]
            block = src[:, pl.ds(pl.multiple_of((h * S + me) * FR, FR), FR)]
            upb[e, pl.ds(pl.multiple_of(my * WR, WR), WR), h * FR : (h + 1) * FR] = block

    def w_sib(lev, who):
        b = wbuf.at[:, pl.ds(who * S + lev * 4, 4)]
        return remote(b, b, sib_s.at[0, lev], sib_r.at[0, lev], sib)

    def pass_on(k):
        wg.d(k)
        w_sib(lev_of(k), core).start()

    pass_on(0)
    wg.b(2)
    wg.c(1)
    wg.b(3)
    dyg.start()
    pass_on(1)
    wg.c(2)
    pass_on(2)
    wg.c(3)
    pass_on(3)
    dyg.a(1)
    dyg.b(0)
    c_small.wait_recv()
    for g in range(D // 128):
        part = smallbuf[g * group, 0:8, :]
        for j in range(1, group):
            part = part + smallbuf[g * group + j, 0:8, :]
        small_out[:, g * 128 : (g + 1) * 128] = part
    cnt = smallbuf[0, 8:16, :]
    for i in range(1, N):
        cnt = cnt + smallbuf[i, 8:16, :]
    count_out[...] = cnt

    def norm1b(r):
        t = pl.ds(r, 64)
        h1b[t, :] = (u1_out[t, :] * small_out[0:1, :] + small_out[1:2, :]).astype(BF)

    rows_loop(T, 64, norm1b)
    dyg.a(2)
    dyg.b(1)
    for k in range(L):
        w_sib(lev_of(k), 1 - core).wait_recv()
    w_save = pltpu.make_async_copy(wbuf, w_out, loc.at[3])
    w_save.start()

    def full(i):
        return wbuf[i].reshape(D, D)

    tmp[...] = mm(h1b[...], full(0))
    q_out[...] = (tmp[...] * 0.125).astype(BF)
    dyg.a(3)
    dyg.c(0)
    tmp[...] = mm(h1b[...], full(1))
    k_out[...] = tmp[...].astype(BF)
    tmp[...] = mm(h1b[...], full(2))
    v_out[...] = tmp[...].astype(BF)
    dyg.b(2)
    dyg.c(1)

    low = lax.broadcasted_iota(jnp.int32, (T, 128), 1) < 64
    lowb = low.astype(F32).astype(BF)
    highb = (1.0 - low.astype(F32)).astype(BF)

    def heads(j):
        ln = pl.ds(pl.multiple_of(j * 128, 128), 128)
        qp = q_out[:, ln]
        q2 = jnp.concatenate([qp * lowb, qp * highb], axis=0)
        s = mm(q2, k_out[:, ln], ((1,), (1,)))
        s = s + jnp.concatenate([bias[...], bias[...]], axis=0)
        ex = jnp.exp(s - jnp.max(s, axis=1, keepdims=True))
        pr = ex / jnp.sum(ex, axis=1, keepdims=True)
        p_out[j] = pr
        o2 = mm(pr.astype(BF), v_out[:, ln])
        o_out[:, ln] = jnp.where(low, o2[0:T], o2[T:]).astype(BF)

    @pl.loop(0, D // 128)
    def _(j):
        heads(j)

    dyg.b(3)
    tmp[...] = mm(o_out[...], full(3))

    def norm2(r):
        t = pl.ds(r, 64)
        v = xs[t, :] + tmp[t, :]
        x1_out[t, :] = v
        cen = v - jnp.mean(v, axis=1, keepdims=True)
        inv = lax.rsqrt(jnp.mean(cen * cen, axis=1, keepdims=True) + 1e-05)
        u = cen * inv
        u2_out[t, :] = u
        h2 = u * small_out[2:3, :] + small_out[3:4, :]
        h2b_out[t, :] = h2.astype(BF)
        lg = [jnp.sum(h2 * small_out[i : i + 1, :], axis=1, keepdims=True) for i in range(4, 8)]

        def soft(a, b):
            mx = jnp.maximum(a, b)
            ea, eb = jnp.exp(a - mx), jnp.exp(b - mx)
            return ea / (ea + eb), eb / (ea + eb)

        r0, r1 = soft(lg[0], lg[1])
        k0, k1 = soft(lg[2], lg[3])
        row = (lax.broadcasted_iota(jnp.int32, (64, 1), 0) + r).astype(F32)
        is0 = row < n0
        gate = jnp.where(is0, r0, r1)
        we = k0 * gate
        cols = (k1, jnp.where(is0, we, 0.0), jnp.where(is0, 0.0, we), k0, gate, r0, r1)
        st = stat_out[t, :] + jnp.where(lane == 9, inv, 0.0)
        for i, col in enumerate(cols):
            st = st + jnp.where(lane == i, col, 0.0)
        stat_out[t, :] = st

    dyg.c(2)
    rows_loop(T, 64, norm2)
    scal_out[...] = stat_out[...].T[0:8, :]

    dyg.c(3)
    for k in range(L):
        dyg.d(k)

    got = upb.at[:, pl.ds(0, (S - 1) * WR), :]
    remote(got, got, sm_s.at[1, 0], sm_r.at[1], (core, xn)).wait_recv()
    mine_up = upb.at[:, pl.ds(pl.multiple_of(core * S * WR, S * WR), S * WR), :]
    c_up = remote(mine_up, mine_up, sib_s.at[2, 3], sib_r.at[2, 3], sib)
    c_up.start()
    c_up.wait()
    up_save = pltpu.make_async_copy(upb, up_out, loc.at[0])
    up_save.start()
    w_save.wait()
    up_save.wait()
    dy_local.wait()
    for c in dn_copies:
        c.wait()
    c_small.wait_send()
    wg.finish()
    dyg.finish()

    @pl.loop(0, L)
    def _(k):
        w_sib(k, core).wait_send()

    @pl.loop(1, S)
    def _(i):
        remote(smallbuf.at[my], smallbuf.at[my], sm_s.at[0, i], sm_r.at[0], (core, xn)).wait_send()
        for e in range(3):
            for h in range(2):
                up_copy(e, h, i).wait_send()


def attn_call(x, dy, docs, es, ss, small, ws, wu, eu, wd, ed, S):
    T, D = x.shape
    WR, FR = ws[0].shape[0], wd.shape[0]
    L = S // 4
    N = 2 * S
    vm = pl.BlockSpec(memory_space=pltpu.VMEM)
    hb = pl.BlockSpec(memory_space=pl.ANY)
    V = pltpu.VMEM
    dma = pltpu.SemaphoreType.DMA
    sds = jax.ShapeDtypeStruct
    row = sds((T, D), BF)
    rowf = sds((T, D), F32)
    return pl.pallas_call(
        attn_kernel,
        out_shape=(
            row, sds((T, 128), F32), sds((8, T), F32), rowf, rowf, rowf, row, row, row, row,
            sds((D // 128, 2 * T, T), F32), row, sds((8, D), F32), sds((8, 128), F32),
            sds((4, N, WR, D), BF), sds((S, T, D), BF), sds((3, D, 2 * FR), BF), sds((3, FR, D), BF),
        ),
        in_specs=[vm] * 14,
        out_specs=(vm,) * 14 + (hb,) * 4,
        scratch_shapes=[
            V((4, N, WR, D), BF), V((3, D, 2 * FR), BF), V((N, 16, 128), F32), V((T, D), BF), V((T, T), F32), V((T, D), F32), V((T, D), F32),
            dma((3, 6, L)), dma((3, 6, L)), dma((3, max(L, 4))), dma((3, max(L, 4))), dma((2, S)), dma((2,)), dma((10,)),
        ],
        compiler_params=pltpu.CompilerParams(collective_id=1, has_side_effects=True, vmem_limit_bytes=60000000),
        cost_estimate=pl.CostEstimate(flops=2 * 10**9, bytes_accessed=40 * 2**20, transcendentals=2**20),
        name="attn",
    )(x, dy, docs, es, ss, small, *ws, wu, eu, wd, ed)


def back_kernel(
    dh_ref, sc_ref, small_ref, stat_ref, u1_ref, u2_ref, x1_ref, dys_ref,
    q_ref, k_ref, v_ref, p_ref, o_ref, e_ref, s_ref, y_hbm, w_hbm, gup_ref,
    lo_out, ig_out, gq_out, gk_out, gv_out, go_out, smalls_out, gup_out,
    wbuf, perm, accs, dx1, dab, do, dq, dk, dv, h1b, dh1, tmpb, keep, send, recv,
    part0, ra0, rbx0, rby0, rd0, rz0, partv, rav, rbxv, rbyv, rdv, rzv, partk, rak, rbxk, rbyk, rdk, rzk,
    partq, raq, rbxq, rbyq, rdq, rzq, ypart, ray, rbxy, rbyy, rdy, rzy, ysum, lsort, smine, ssib, srecv,
    rs_s, rs_r, sib_s, sib_r, sm_s, sm_r, loc,
):
    T, D = dh_ref.shape
    S, WR = part0.shape[0], part0.shape[1]
    L = S // 4
    half = D // 2
    me, core, z, p, xq, yq, dgq = place_of()
    xn = z * 4 + xq
    sib = (1 - core, me)
    lev_of = level_order(z, L)
    far = list(reversed(range(L)))
    fetch = []
    for k in far:
        some = pl.ds(lev_of(k) * 4, 4)
        fetch.append(pltpu.make_async_copy(y_hbm.at[some], ypart.at[some], loc.at[4 + k]))
    for c in fetch:
        c.start()
    greet(S, core)

    dev, levels = (core, z, p, xq, yq, dgq), (lev_of, L)
    g0 = tree_scatter(part0, ra0, rbx0, rby0, rd0, go_out, rs_s.at[0], rs_r.at[0], dev, levels, rz0)
    gv = tree_scatter(partv, rav, rbxv, rbyv, rdv, gv_out, rs_s.at[1], rs_r.at[1], dev, levels, rzv)
    gk = tree_scatter(partk, rak, rbxk, rbyk, rdk, gk_out, rs_s.at[3], rs_r.at[3], dev, levels, rzk)
    gq = tree_scatter(partq, raq, rbxq, rbyq, rdq, gq_out, rs_s.at[4], rs_r.at[4], dev, levels, rzq)
    gy = tree_scatter(ypart, ray, rbxy, rbyy, rdy, ysum, rs_s.at[2], rs_r.at[2], dev, levels, rzy)
    far = list(reversed(range(L)))
    loads = [pltpu.make_async_copy(w_hbm.at[i], wbuf.at[i], loc.at[i]) for i in range(4)]
    for i in (3, 0, 1, 2):
        loads[i].start()

    for k, c in zip(far, fetch):
        c.wait()
        gy.share(k)
        gy.b0(k)
    perm_f, n0 = sort_matrix(e_ref[...], s_ref[...], T)
    perm[...] = perm_f.astype(BF)
    accs[...] = jnp.zeros_like(accs)
    scol = jnp.concatenate([sc_ref[...], jnp.zeros((120, 128), F32)], axis=0).T
    dh1[:, 0:128] = scol

    def acc(i, v):
        accs[i] = accs[i] + jnp.sum(v.reshape(32 // 8, 8, v.shape[1]), axis=0)

    def norm2(r):
        t = pl.ds(r, 32)
        st = stat_ref[t, :]
        c1, c0, gate, r0, r1, inv = (st[:, i : i + 1] for i in (0, 3, 4, 5, 6, 9))
        row = (lax.broadcasted_iota(jnp.int32, (32, 1), 0) + r).astype(F32)
        is0 = row < n0
        s3 = dh1[t, 0:128]
        sm = s3[:, 0:1]
        se = jnp.where(is0, s3[:, 1:2], s3[:, 2:3])
        dc0, dc1 = gate * se, sm
        tot = c0 * dc0 + c1 * dc1
        dcl0, dcl1 = c0 * (dc0 - tot), c1 * (dc1 - tot)
        dgate = c0 * se
        dr0, dr1 = jnp.where(is0, dgate, 0.0), jnp.where(is0, 0.0, dgate)
        tot = r0 * dr0 + r1 * dr1
        drl0, drl1 = r0 * (dr0 - tot), r1 * (dr1 - tot)
        u2 = u2_ref[t, :]
        h2 = u2 * small_ref[2:3, :] + small_ref[3:4, :]
        dh2 = dh_ref[t, :]
        for i, d in enumerate((drl0, drl1, dcl0, dcl1)):
            acc(4 + i, h2 * d)
            dh2 = dh2 + d * small_ref[4 + i : 5 + i, :]
        acc(2, dh2 * u2)
        acc(3, dh2)
        e = dh2 * small_ref[2:3, :]
        inner = e - jnp.mean(e, axis=1, keepdims=True) - u2 * jnp.mean(e * u2, axis=1, keepdims=True)
        g = dys_ref[t, :].astype(F32) + inv * inner
        dx1[t, :] = g
        dab[t, :] = g.astype(BF)
        h1b[t, :] = (u1_ref[t, :] * small_ref[0:1, :] + small_ref[1:2, :]).astype(BF)

    rows_loop(T, 32, norm2)

    other = pl.multiple_of((1 - core) * half, half)
    mine = pl.multiple_of(core * half, half)

    def weight_grad(i, left, right):
        send[i] = mm(left[:, pl.ds(other, half)], right[...], ((0,), (0,))).astype(BF)
        c = remote(send.at[i], recv.at[i], sib_s.at[i], sib_r.at[i], sib)
        c.start()
        keep[i] = mm(left[:, pl.ds(mine, half)], right[...], ((0,), (0,)))
        return c

    def join(i, c, part):
        c.wait_recv()

        @pl.loop(0, S)
        def _(j):
            t = pl.ds(pl.multiple_of(j * WR, WR), WR)
            part[j] = (keep[i, t, :] + recv[i, t, :].astype(F32)).astype(BF)


    def g_copy(i):
        to = (me + i) % S
        src = gup_ref.at[:, pl.ds(pl.multiple_of(to * WR, WR), WR), :]
        return remote(src, gup_out.at[me], sm_s.at[1, i], sm_r.at[1], (core, to))

    @pl.loop(1, S)
    def _(i):
        g_copy(i).start()

    gup_out[me] = gup_ref[:, pl.ds(pl.multiple_of(me * WR, WR), WR), :]
    low = lax.broadcasted_iota(jnp.int32, (T, 128), 1) < 64
    lowb = low.astype(F32).astype(BF)
    highb = (1.0 - low.astype(F32)).astype(BF)

    def heads(j):
        ln = pl.ds(pl.multiple_of(j * 128, 128), 128)
        qp, dop = q_ref[:, ln], do[:, ln]
        q2 = jnp.concatenate([qp * lowb, qp * highb], axis=0)
        do2 = jnp.concatenate([dop * lowb, dop * highb], axis=0)
        pr = p_ref[j]
        dp = mm(do2, v_ref[:, ln], ((1,), (1,)))
        ds = (pr * (dp - jnp.sum(pr * dp, axis=1, keepdims=True))).astype(BF)
        dq2 = mm(ds, k_ref[:, ln])
        dq[:, ln] = jnp.where(low, dq2[0:T], dq2[T:]).astype(BF) * BF(0.125)
        dk[:, ln] = mm(ds, q2, ((0,), (0,))).astype(BF)
        dv[:, ln] = mm(pr.astype(BF), do2, ((0,), (0,))).astype(BF)

    def norm1(r):
        t = pl.ds(r, 32)
        inv = stat_ref[t, :][:, 8:9]
        u = u1_ref[t, :]
        d = dh1[t, :]
        acc(0, d * u)
        acc(1, d)
        e = d * small_ref[0:1, :]
        inner = e - jnp.mean(e, axis=1, keepdims=True) - u * jnp.mean(e * u, axis=1, keepdims=True)
        tmpb[t, :] = (dx1[t, :] + inv * inner).astype(BF)

    def each(*calls):
        for k in far:
            for call in calls:
                call(k)

    def start(i, c, part, g):
        join(i, c, part)
        each(g.share, g.b0)

    c_o = weight_grad(3, o_ref, dab)
    each(gy.a)
    loads[3].wait()
    do[...] = mm(dab[...], wbuf[3], ((1,), (1,))).astype(BF)
    start(3, c_o, part0, g0)
    each(gy.c0)

    @pl.loop(0, D // 256)
    def _(j):
        heads(j)

    each(gy.b1)

    @pl.loop(D // 256, D // 128)
    def _(j):
        heads(j)

    each(g0.a)
    c_v = weight_grad(2, h1b, dv)
    each(g0.c0)
    c_k = weight_grad(1, h1b, dk)
    start(2, c_v, partv, gv)
    c_q = weight_grad(0, h1b, dq)
    start(1, c_k, partk, gk)
    each(g0.b1)
    each(gy.c1)
    for i in range(3):
        loads[i].wait()
    dh1[...] = mm(dq[...], wbuf[0], ((1,), (1,)))
    start(0, c_q, partq, gq)
    each(gv.a)
    dh1[...] = dh1[...] + mm(dk[...], wbuf[1], ((1,), (1,)))
    each(gk.a, gv.c0)
    dh1[...] = dh1[...] + mm(dv[...], wbuf[2], ((1,), (1,)))
    each(gq.a, gv.b1, g0.c1, gk.c0)
    rows_loop(T, 32, norm1)
    each(gk.b1, gq.c0)
    each(gq.b1, gv.c1)
    for k in range(1, L):
        gy.d(k)
    for i in range(8):
        smine[i : i + 1, :] = jnp.sum(accs[i], axis=0, keepdims=True)
    c_s = remote(smine, ssib, sib_s.at[4], sib_r.at[4], sib)
    c_s.start()
    lsort[...] = (x1_ref[...] + ysum[...]).astype(BF)
    lo_out[...] = mm(perm[...], lsort[...], ((0,), (0,))).astype(BF)
    each(gk.c1)
    ig_out[...] = mm(perm[...], tmpb[...], ((0,), (0,))).astype(BF)
    c_s.wait()
    smine[...] = smine[...] + ssib[...]
    group = 128 // WR

    def s_at(i):
        return smine.at[:, pl.ds(pl.multiple_of((core * S + i) // group * 128, 128), 128)]

    def s_copy(i):
        to = (me + i) % S
        return remote(s_at(to), srecv.at[me], sm_s.at[0, i], sm_r.at[0], (core, to))

    @pl.loop(1, S)
    def _(i):
        s_copy(i).start()

    srecv[me] = s_at(me)[...]
    each(gq.c1)
    for g in (g0, gv, gk, gq):
        for k in range(1, L):
            g.d(k)
    allr = srecv.at[pl.ds(0, S - 1)]
    remote(allr, allr, sm_s.at[0, 0], sm_r.at[0], (core, xn)).wait_recv()
    smalls_out[...] = jnp.sum(srecv[...], axis=0)
    for g in (gy, g0, gv, gk, gq):
        g.finish()
    for c in (c_o, c_v, c_k, c_q):
        c.wait_send()

    got = gup_out.at[pl.ds(0, S - 1)]
    remote(got, got, sm_s.at[1, 0], sm_r.at[1], (core, xn)).wait_recv()

    @pl.loop(1, S)
    def _(i):
        s_copy(i).wait_send()
        g_copy(i).wait_send()


def back_call(dh, y, sc, small, stat, u1, u2, x1, dys, q, k, v, p, o, es, ss, wa, gup, S):
    T, D = dh.shape
    WR = D // (2 * S)
    L = S // 4
    vm = pl.BlockSpec(memory_space=pltpu.VMEM)
    hb = pl.BlockSpec(memory_space=pl.ANY)
    V = pltpu.VMEM
    dma = pltpu.SemaphoreType.DMA
    sds = jax.ShapeDtypeStruct
    row = V((T, D), BF)

    def rs_bufs(R):
        return [V((S, R, D), BF)] + [V((L, R, D), BF)] * 4 + [V((L // 2, R, D), BF)]

    return pl.pallas_call(
        back_kernel,
        out_shape=(
            sds((T, D), BF), sds((T, D), BF), sds((WR, D), F32), sds((WR, D), F32), sds((WR, D), F32),
            sds((WR, D), F32), sds((8, 128), F32),
            sds((S, 3, WR, gup.shape[2]), BF),
        ),
        in_specs=[vm] * 15 + [hb, hb, vm],
        out_specs=(vm,) * 8,
        scratch_shapes=[
            V((4, D, D), BF), V((T, T), BF), V((8, 8, D), F32), V((T, D), F32), row, row, row, row, row, row,
            V((T, D), F32), row, V((4, D // 2, D), F32), V((4, D // 2, D), BF), V((4, D // 2, D), BF),
        ]
        + rs_bufs(WR)
        + rs_bufs(WR)
        + rs_bufs(WR)
        + rs_bufs(WR)
        + rs_bufs(T)
        + [
            V((T, D), F32), V((T, D), BF),
            V((8, D), F32), V((8, D), F32), V((S, 8, 128), F32),
            dma((5, 5, L)), dma((5, 5, L)), dma((5,)), dma((5,)), dma((2, S)), dma((2,)), dma((5 + L,)),
        ],
        compiler_params=pltpu.CompilerParams(collective_id=3, has_side_effects=True, vmem_limit_bytes=60000000),
        cost_estimate=pl.CostEstimate(flops=4 * 10**9, bytes_accessed=20 * 2**20, transcendentals=2**20),
        name="back",
    )(dh, sc, small, stat, u1, u2, x1, dys, q, k, v, p, o, es, ss, y, wa, gup)


def finish_kernel(
    lo_ref, ig_ref, gq_ref, gk_ref, gv_ref, go_ref, sm_ref, gup_ref, gdn0_ref, gdn12_ref,
    lo_out, ig_out, q_out, k_out, v_out, o_out, up_out, dn_out, eu_out, ed_out, r_out, m_out, n_out,
    turned,
):
    S, _, WR, F = gup_ref.shape
    FR = F // 2
    at = (lax.axis_index("dp") * S + lax.axis_index("shard")) % (128 // WR) * WR
    lo_out[...] = lo_ref[...]
    ig_out[...] = ig_ref[...]
    for src, out in ((gq_ref, q_out), (gk_ref, k_out), (gv_ref, v_out), (go_ref, o_out)):
        out[...] = src[...]
    dn_out[...] = gdn0_ref[...]
    ed_out[...] = gdn12_ref[...]
    for s in range(S):
        for c in range(2):
            cols = slice((c * S + s) * FR, (c * S + s + 1) * FR)
            part = slice(c * FR, (c + 1) * FR)
            up_out[:, cols] = gup_ref[s, 0, :, part].astype(F32)
            for e in range(2):
                eu_out[e, :, cols] = gup_ref[s, 1 + e, :, part].astype(F32)
    turned[...] = jnp.concatenate([sm_ref[...], jnp.zeros((120, 128), F32)], axis=0).T
    mine = turned[pl.ds(pl.multiple_of(at, WR), WR), :]
    r_out[...] = mine[:, 4:6]
    m_out[...] = mine[:, 6:8]
    n_out[...] = mine[:, 0:4]


def finish_call(lo, ig, gwq, gwk, gwv, gwo, smalls, gup, gdn0, gdn12):
    T, D = lo.shape
    S, _, WR, F = gup.shape
    FF = S * F
    vm = pl.BlockSpec(memory_space=pltpu.VMEM)
    sds = jax.ShapeDtypeStruct
    sq = sds((WR, D), F32)
    return pl.pallas_call(
        finish_kernel,
        out_shape=(
            sds((T, D), BF), sds((T, D), BF), sq, sq, sq, sq, sds((WR, FF), F32), sds(gdn0.shape, F32),
            sds((2, WR, FF), F32), sds(gdn12.shape, F32), sds((WR, 2), F32), sds((WR, 2), F32), sds((WR, 4), F32),
        ),
        in_specs=[vm] * 10,
        out_specs=(vm,) * 13,
        scratch_shapes=[pltpu.VMEM((128, 128), F32)],
        compiler_params=pltpu.CompilerParams(vmem_limit_bytes=40000000),
        name="finish",
    )(lo, ig, gwq, gwk, gwv, gwo, smalls, gup, gdn0, gdn12)


def body_plain(
    hidden_in, doc_ids, expert_ids, slot_ids, out_grad, ln1_gain, ln1_bias, w_query, w_key, w_value,
    w_out, ln2_gain, ln2_bias, w_up, w_down, w_router, w_mix, expert_up, expert_down, load_avg,
):
    T, D = hidden_in.shape
    H, HD = HEADS, D // HEADS
    S = lax.axis_size("shard")
    C = lax.axis_size("dp")
    WR = w_query.shape[0]
    FF = w_up.shape[1]
    FR = w_down.shape[0]
    F = FR * C
    E = expert_up.shape[0]
    LO, HI = 80, T - 80

    pos = jnp.where(expert_ids == 0, slot_ids, jnp.sum((expert_ids == 0).astype(jnp.int32)) + slot_ids)
    n0 = jnp.sum((expert_ids == 0).astype(jnp.int32))
    place = lax.iota(jnp.int32, T)
    perm = (pos[None, :] == place[:, None]).astype(BF)
    xs = mm(perm, hidden_in)
    dys = mm(perm, out_grad).astype(BF)
    doc = doc_ids[0]
    allowed = (place[None, :] <= place[:, None]) & (doc[:, None] == doc[None, :])
    allowed = mm(mm(perm, allowed.astype(BF)).astype(BF), perm, ((1,), (1,))) > 0.5
    is0 = (place < n0)[:, None]

    small = jnp.stack(
        [ln1_gain, ln1_bias, ln2_gain, ln2_bias, w_router[:, 0], w_router[:, 1], w_mix[:, 0], w_mix[:, 1]]
    ).astype(F32)
    small = lax.all_gather(small, BOTH, axis=1, tiled=True)
    g1, b1, g2, b2 = small[0], small[1], small[2], small[3]
    wr, wm = small[4:6], small[6:8]

    wa = jnp.stack([w_query, w_key, w_value, w_out])
    wa = lax.all_gather(wa, BOTH, axis=1, tiled=True)
    wq, wk, wv, wo = wa[0], wa[1], wa[2], wa[3]

    ups = jnp.stack([w_up, expert_up[0], expert_up[1]])
    ups = ups.reshape(3, WR, C, S, FR).transpose(3, 0, 1, 2, 4).reshape(S, 3, WR, F)
    ups = lax.all_to_all(ups, "shard", 0, 0)
    ups = lax.all_gather(ups, "dp", axis=0)
    ups = ups.transpose(2, 0, 1, 3, 4).reshape(3, D, F)
    downs = jnp.stack([w_down, expert_down[0], expert_down[1]])
    downs = lax.all_gather(downs, "dp", axis=1, tiled=True)

    dy_all = ag(dys)

    n1, u1, i1 = layer_norm(xs, g1, b1)
    h1b = n1.astype(BF)
    q = (mm(h1b, wq) * 0.125).astype(BF).reshape(T, H, HD)
    k = mm(h1b, wk).astype(BF).reshape(T, H, HD)
    v = mm(h1b, wv).astype(BF).reshape(T, H, HD)
    s = jnp.einsum("ihd,jhd->hij", q, k, preferred_element_type=F32)
    s = jnp.where(allowed[None], s, -1e30)
    ex = jnp.exp(s - jnp.max(s, axis=-1, keepdims=True))
    p = ex / jnp.sum(ex, axis=-1, keepdims=True)
    pb = p.astype(BF)
    o = jnp.einsum("hij,jhd->ihd", pb, v, preferred_element_type=F32).reshape(T, D).astype(BF)
    x1 = xs + mm(o, wo)
    h2, u2, i2 = layer_norm(x1, g2, b2)
    h2b = h2.astype(BF)

    def two(w):
        return jnp.stack([jnp.sum(h2 * w[0], axis=-1), jnp.sum(h2 * w[1], axis=-1)], axis=-1)

    r = jax.nn.softmax(two(wr), axis=-1)
    c = jax.nn.softmax(two(wm), axis=-1)
    gate = jnp.where(is0, r[:, 0:1], r[:, 1:2])
    c0, c1 = c[:, 0:1], c[:, 1:2]
    we = c0 * gate
    scal = jnp.concatenate([c1, jnp.where(is0, we, 0.0), jnp.where(is0, 0.0, we)], axis=1)

    h_all = ag(h2b)
    scal_all = ag(scal)

    def cut(a, e):
        return (a[:, :LO] if e == 1 else a[:, HI:]) if e else a

    partial_y = jnp.zeros((S, T, D), F32)
    partial_dh = jnp.zeros((S, T, D), F32)
    score = []
    gup, gdown = [], []
    for e in range(3):
        he = cut(h_all, e)
        dye = cut(dy_all, e).astype(F32)
        se = cut(scal_all, e)[:, :, e : e + 1]
        n = he.shape[1]
        hf = he.reshape(S * n, D)
        pre = mm(hf, ups[e])
        val, der = gelu_pair(pre)
        ub = val.astype(BF)
        m = mm(ub, downs[e]).reshape(S, n, D)
        dm = (dye * se).astype(BF).reshape(S * n, D)
        dg = (mm(dm, downs[e], ((1,), (1,))) * der).astype(BF)
        gdown.append(mm(ub, dm, ((0,), (0,))))
        gup.append(mm(hf, dg, ((0,), (0,))))
        dx = mm(dg, ups[e], ((1,), (1,))).reshape(S, n, D)
        y = m * se
        sc = jnp.sum(dye * m, axis=-1)
        pad = [(0, 0), (0, T - n) if e < 2 else (T - n, 0)]
        live = is0[None, :, 0]
        partial_y += jnp.pad(y, pad + [(0, 0)])
        partial_dh += jnp.pad(dx, pad + [(0, 0)])
        score.append(jnp.pad(sc, pad))
    yfull = rs(partial_y)
    dh2 = rs(partial_dh)
    sc = lax.psum_scatter(jnp.stack(score, axis=1), "shard", scatter_dimension=0, tiled=False)
    sm = sc[0][:, None]
    se = jnp.where(is0, sc[1][:, None], sc[2][:, None])

    dc0, dc1 = gate * se, sm
    tot = c0 * dc0 + c1 * dc1
    dcl0, dcl1 = c0 * (dc0 - tot), c1 * (dc1 - tot)
    dgate = c0 * se
    dr0, dr1 = jnp.where(is0, dgate, 0.0), jnp.where(is0, 0.0, dgate)
    tot = r[:, 0:1] * dr0 + r[:, 1:2] * dr1
    drl0, drl1 = r[:, 0:1] * (dr0 - tot), r[:, 1:2] * (dr1 - tot)
    layer_out = (x1 + yfull).astype(BF)
    dh2 = dh2 + drl0 * wr[0] + drl1 * wr[1] + dcl0 * wm[0] + dcl1 * wm[1]
    gw = [jnp.sum(h2 * t, axis=0) for t in (drl0, drl1, dcl0, dcl1)]
    dx1, gg2, gb2 = norm_back(dh2, u2, i2, g2)
    dx1 = dx1 + dys.astype(F32)
    dab = dx1.astype(BF)
    gwo = mm(o, dab, ((0,), (0,)))
    do = mm(dab, wo, ((1,), (1,))).astype(BF).reshape(T, H, HD)
    dp = jnp.einsum("ihd,jhd->hij", do, v, preferred_element_type=F32)
    ds = (p * (dp - jnp.sum(p * dp, axis=-1, keepdims=True))).astype(BF)
    dq = jnp.einsum("hij,jhd->ihd", ds, k, preferred_element_type=F32).astype(BF)
    dq = (dq * BF(0.125)).reshape(T, D)
    dk = jnp.einsum("hij,ihd->jhd", ds, q, preferred_element_type=F32).astype(BF).reshape(T, D)
    dv = jnp.einsum("hij,ihd->jhd", pb, do, preferred_element_type=F32).astype(BF).reshape(T, D)
    dh1 = mm(dq, wq, ((1,), (1,))) + mm(dk, wk, ((1,), (1,))) + mm(dv, wv, ((1,), (1,)))
    ga = jnp.stack([mm(h1b, dq, ((0,), (0,))), mm(h1b, dk, ((0,), (0,))), mm(h1b, dv, ((0,), (0,))), gwo])
    dxn, gg1, gb1 = norm_back(dh1, u1, i1, g1)
    input_grad = (dx1 + dxn).astype(BF)

    layer_out = mm(perm, layer_out, ((0,), (0,))).astype(BF)
    input_grad = mm(perm, input_grad, ((0,), (0,))).astype(BF)

    smalls = lax.psum(jnp.stack([gg1, gb1, gg2, gb2] + gw), BOTH)
    mine = lax.dynamic_slice_in_dim(smalls, lax.axis_index(BOTH) * WR, WR, 1)
    ga = ga.reshape(4, C, S, WR, D).transpose(1, 2, 0, 3, 4)
    ga = lax.psum_scatter(ga.astype(BF), "dp", scatter_dimension=0, tiled=False)
    ga = lax.psum_scatter(ga, "shard", scatter_dimension=0, tiled=False).astype(F32)
    gdown = lax.psum_scatter(jnp.stack(gdown), "dp", scatter_dimension=1, tiled=True)
    gup = jnp.stack(gup).reshape(3, C, S, WR, F).transpose(1, 2, 0, 3, 4)
    gup = lax.psum_scatter(gup, "dp", scatter_dimension=0, tiled=False).astype(BF)
    gup = lax.all_to_all(gup, "shard", 0, 0).astype(F32)
    gup = gup.reshape(S, 3, WR, C, FR).transpose(1, 2, 3, 0, 4).reshape(3, WR, FF)

    counts = lax.psum(jnp.stack([n0, T - n0]), BOTH)
    load_new = 0.9 * load_avg + 0.1 * counts.astype(F32) * E / (T * C * S)
    return (
        layer_out, input_grad, mine[0], mine[1], ga[0], ga[1], ga[2], ga[3], mine[2], mine[3],
        gup[0], gdown[0], jnp.stack([mine[4], mine[5]], axis=1), jnp.stack([mine[6], mine[7]], axis=1),
        gup[1:], gdown[1:], counts, load_new,
    )


def body(
    hidden_in, doc_ids, expert_ids, slot_ids, out_grad, ln1_gain, ln1_bias, w_query, w_key, w_value,
    w_out, ln2_gain, ln2_bias, w_up, w_down, w_router, w_mix, expert_up, expert_down, load_avg,
):
    T, D = hidden_in.shape
    H, HD = HEADS, D // HEADS
    S = lax.axis_size("shard")
    C = lax.axis_size("dp")
    WR = w_query.shape[0]
    FF = w_up.shape[1]
    FR = w_down.shape[0]
    F = FR * C
    E = expert_up.shape[0]
    ndev = C * S
    dev = lax.axis_index(BOTH)
    small = jnp.stack(
        [ln1_gain, ln1_bias, ln2_gain, ln2_bias, w_router[:, 0], w_router[:, 1], w_mix[:, 0], w_mix[:, 1]]
    ).astype(F32)
    group = 128 // WR
    slot_of = lax.broadcasted_iota(jnp.int32, (8, 128), 1) // WR
    small = jnp.where(slot_of == dev % group, jnp.tile(small, (1, group)), 0.0)
    (h2b, stat, scal8, u1, u2, x1, dys, q, k, v, p, o, small, count, wa, dy_all, ups, downs) = attn_call(
        hidden_in, out_grad, doc_ids, expert_ids.reshape(1, T), slot_ids.reshape(1, T), small,
        (w_query, w_key, w_value, w_out), w_up, expert_up, w_down, expert_down, S,
    )
    y_parts, dh2, sc, gup, gdn0, gdn12 = ffn_call(h2b, scal8, dy_all, ups, w_down, expert_down, downs)
    layer_out, input_grad, gwq, gwk, gwv, gwo, smalls, gup = back_call(
        dh2, y_parts, sc, small, stat, u1, u2, x1, dys, q, k, v, p, o,
        expert_ids.reshape(1, T), slot_ids.reshape(1, T), wa.reshape(4, D, D), gup, S,
    )
    lo, ig, gq, gk, gv, go, gu, gd, geu, ged, gr, gm, gn = finish_call(
        layer_out, input_grad, gwq, gwk, gwv, gwo, smalls, gup, gdn0, gdn12
    )
    tokens0 = count[0, 0].astype(jnp.int32)
    counts = jnp.stack([tokens0, T * ndev - tokens0])
    load_new = 0.9 * load_avg + 0.1 * counts.astype(F32) * E / (T * ndev)
    return (
        lo, ig, gn[:, 0], gn[:, 1], gq, gk, gv, go, gn[:, 2], gn[:, 3],
        gu, gd, gr, gm, geu, ged, counts, load_new,
    )


def pick(*args):
    S, C, WR, FR = lax.axis_size("shard"), lax.axis_size("dp"), args[7].shape[0], args[14].shape[0]
    fast = C == 2 and S // 4 == 4 and S % 4 == 0 and WR % 16 == 0 and 128 % WR == 0 and FR % 128 == 0
    return (body if fast else body_plain)(*args)


def solution(mesh):
    row, vec = P(BOTH, None), P(BOTH)
    mid = P(None, BOTH, None)
    return jax.shard_map(
        pick,
        mesh=mesh,
        in_specs=(row, row, vec, vec, row, vec, vec, row, row, row, row, vec, vec, row, row, row, row, mid, mid, P()),
        out_specs=(row, row, vec, vec, row, row, row, row, vec, vec, row, row, row, row, mid, mid, P(), P()),
        check_vma=False,
    )
```

```python
import jax
import jax.numpy as jnp
from jax import lax
from jax.experimental import pallas as pl
from jax.experimental.pallas import tpu as pltpu
from jax.sharding import PartitionSpec as P

HEADS = 16
CAP = 74
BF = jnp.bfloat16
F32 = jnp.float32
BOTH = ("dp", "shard")
MESH = pl.DeviceIdType.MESH


def mm(a, b, dims=((1,), (0,))):
    return lax.dot_general(a, b, (dims, ((), ())), preferred_element_type=F32)


def layer_norm(values, gain, bias):
    centre = values - jnp.mean(values, axis=-1, keepdims=True)
    scale_inv = lax.rsqrt(jnp.mean(centre * centre, axis=-1, keepdims=True) + 1e-05)
    normed = centre * scale_inv
    return (normed * gain + bias, normed, scale_inv)


def norm_back(grad_out, normed, scale_inv, gain):
    grad_normed = grad_out * gain
    inner = grad_normed - jnp.mean(grad_normed, axis=-1, keepdims=True)
    inner = inner - normed * jnp.mean(grad_normed * normed, axis=-1, keepdims=True)
    return (scale_inv * inner, jnp.sum(grad_out * normed, axis=0), jnp.sum(grad_out, axis=0))


def gelu_pair(t):
    inner = 0.7978845608 * (t + 0.044715 * t * t * t)
    th = jnp.tanh(inner)
    val = 0.5 * t * (1.0 + th)
    der = 0.5 * (1.0 + th) + 0.5 * t * (1.0 - th * th) * 0.7978845608 * (1.0 + 3.0 * 0.044715 * t * t)
    return val, der


def ag(block):
    return lax.all_gather(block, "shard", axis=0, tiled=False)


def rs(parts):
    return lax.psum_scatter(parts.astype(BF), "shard", scatter_dimension=0, tiled=False).astype(F32)


def place_of():
    me = lax.axis_index("shard")
    core = lax.axis_index("dp")
    z, p = me // 4, me % 4
    xq = p + 1 - 2 * (p % 2)
    yq = p + 2 - 4 * (p // 2)
    return me, core, z, p, xq, yq, 3 - p


def greet(shards, core):
    bar = pltpu.get_barrier_semaphore()
    me = lax.axis_index("shard")

    @pl.loop(1, shards)
    def _(i):
        pl.semaphore_signal(bar, inc=1, device_id=(core, (me + i) % shards), device_id_type=MESH)

    pl.semaphore_signal(bar, inc=1, device_id=(1 - core, me), device_id_type=MESH)
    pl.semaphore_wait(bar, shards)


def remote(src, dst, send, recv, dev):
    return pltpu.make_async_remote_copy(
        src_ref=src, dst_ref=dst, send_sem=send, recv_sem=recv, device_id=dev, device_id_type=MESH
    )


def rows_loop(count, step, fn):
    @pl.loop(0, count // step)
    def _(i):
        fn(pl.multiple_of(i * step, step))


def level_order(z, L):
    upper = z // (L // 2)
    y = z + upper * (L - 1 - 2 * z)

    def lev_of(k):
        low = k - 1 + (k - 1 - y + L) // L
        lev = low + upper * (L - 1 - 2 * low)
        first = 1 - (k + L - 1) // L
        return lev + first * (z - lev)

    return lev_of


def tree_gather(at, own, ss, rs, dev, levels):
    core, z, p, xq, yq, dq = dev
    xn, yn = z * 4 + xq, z * 4 + yq
    me = z * 4 + p
    pair = me + 4 - 8 * (z % 2)
    lev_of, L = levels

    def copy(kind, slot, src, idx, to):
        return remote(src, at(idx), ss.at[kind, slot], rs.at[kind, slot], (core, to))

    def up_line(src, send):
        return remote(src, at(me), send, rs.at[0, z], (core, me + 4))

    def down_line(src, send):
        return remote(src, at(me), send, rs.at[0, z], (core, me - 4))

    def onward(k):
        lev = lev_of(k)
        step = 1 - 2 * ((lev - z + L) // L)
        to = z + step
        idx = lev * 4 + p
        ok = (to >= 0) & (to < L)
        return ok, remote(at(idx), at(idx), ss.at[0, lev], rs.at[0, lev], (core, me + 4 * step))

    class Stages:
        @staticmethod
        def start():
            @pl.when(z < L - 1)
            def _():
                up_line(own, ss.at[0, z]).start()

            @pl.when(z > 0)
            def _():
                down_line(own, ss.at[4, 0]).start()

            copy(1, z, own, me, xn).start()
            copy(2, z, own, me, yn).start()

        @staticmethod
        def a(k):
            lev = lev_of(k)
            idx = lev * 4 + p
            copy(0, lev, own, idx, xn).wait_recv()
            ok, on = onward(k)

            @pl.when(ok)
            def _():
                on.start()

            copy(1, lev, at(idx), idx, xn).start()
            copy(2, lev, at(idx), idx, yn).start()

        @staticmethod
        def b(k):
            lev = lev_of(k)
            odd = lev // 2 % 2
            copy(1, lev, own, lev * 4 + xq, xn).wait_recv()
            copy(2, lev, own, lev * 4 + yq, yn).wait_recv()
            idx = lev * 4 + xq + odd * (yq - xq)

            @pl.when((lev + z) % 2 == 0)
            def _():
                copy(3, lev, at(idx), idx, yn + odd * (xn - yn)).start()

        @staticmethod
        def c(k):
            lev = lev_of(k)
            idx = lev * 4 + dq

            @pl.when((lev + z) % 2 == 0)
            def _():
                copy(3, lev, own, idx, xn).wait_recv()
                copy(5, lev, at(idx), idx, pair).start()

        @staticmethod
        def d(k):
            lev = lev_of(k)

            @pl.when((lev + z) % 2 == 1)
            def _():
                copy(5, lev, own, lev * 4 + dq, pair).wait_recv()

        @staticmethod
        def done(k):
            lev = lev_of(k)
            for kind in range(1, 3):
                copy(kind, lev, own, me, xn).wait_send()

            @pl.when((lev + z) % 2 == 0)
            def _():
                for kind in (3, 5):
                    copy(kind, lev, own, me, xn).wait_send()

            @pl.when(k > 0)
            def _():
                ok, on = onward(k)
                pl.when(ok)(on.wait_send)

            @pl.when(k == 0)
            def _():
                pl.when(z < L - 1)(lambda: up_line(own, ss.at[0, z]).wait_send())
                pl.when(z > 0)(lambda: down_line(own, ss.at[4, 0]).wait_send())

        @staticmethod
        def finish():
            @pl.loop(0, L)
            def _(k):
                Stages.done(k)

    return Stages


def tree_scatter(part, ra, rbx, rby, rd, final, ss, rs, dev, levels, rz=None):
    core, z, p, xq, yq, dq = dev
    xn, yn = z * 4 + xq, z * 4 + yq
    pair = z * 4 + p + 4 - 8 * (z % 2)
    lev_of, L = levels
    R = part.shape[1]

    def copy(kind, lev, src, dst, to):
        return remote(src, dst, ss.at[kind, lev], rs.at[kind, lev], (core, to))

    def sides(lev):
        copy(1, lev, part.at[lev * 4 + xq], rbx.at[lev], xn).start()
        copy(2, lev, part.at[lev * 4 + yq], rby.at[lev], yn).start()

    class Stages:
        @staticmethod
        def share(k):
            lev = lev_of(k)

            @pl.when((lev + z) % 2 == 1)
            def _():
                copy(4, lev, part.at[lev * 4 + dq], rz.at[lev // 2], pair).start()

        @staticmethod
        def a(k):
            lev = lev_of(k)
            odd = k % 2 if rz is None else lev // 2 % 2
            diag = lev * 4 + dq

            def send():
                copy(0, lev, part.at[diag], ra.at[lev], yn + odd * (xn - yn)).start()

            def join():
                copy(4, lev, rz.at[lev // 2], rz.at[lev // 2], pair).wait_recv()

                def add(r):
                    t = pl.ds(r, 32)
                    part[diag, t, :] = (part[diag, t, :].astype(F32) + rz[lev // 2, t, :].astype(F32)).astype(BF)

                rows_loop(R, 32, add)
                send()

            if rz is None:
                send()
            else:
                pl.when((lev + z) % 2 == 0)(join)

        @staticmethod
        def b(k):
            lev = lev_of(k)
            odd = k % 2 if rz is None else lev // 2 % 2
            via = lev * 4 + xq + odd * (yq - xq)
            copy(0, lev, ra.at[lev], ra.at[lev], xn).wait_recv()

            def add(r):
                t = pl.ds(r, 32)
                part[via, t, :] = (part[via, t, :].astype(F32) + ra[lev, t, :].astype(F32)).astype(BF)

            rows_loop(R, 32, add)
            sides(lev)

        @staticmethod
        def b0(k):
            pl.when((lev_of(k) + z) % 2 == 1)(lambda: sides(lev_of(k)))

        @staticmethod
        def b1(k):
            pl.when((lev_of(k) + z) % 2 == 0)(lambda: Stages.b(k))

        @staticmethod
        def c0(k):
            pl.when((lev_of(k) + z) % 2 == 1)(lambda: Stages.c(k))

        @staticmethod
        def c1(k):
            pl.when((lev_of(k) + z) % 2 == 0)(lambda: Stages.c(k))

        @staticmethod
        def c(k):
            lev = lev_of(k)
            own = lev * 4 + p
            copy(1, lev, rbx.at[lev], rbx.at[lev], xn).wait_recv()
            copy(2, lev, rby.at[lev], rby.at[lev], yn).wait_recv()

            def add(r, last):
                t = pl.ds(r, 32)
                tot = part[own, t, :].astype(F32) + rbx[lev, t, :].astype(F32) + rby[lev, t, :].astype(F32)
                if last:
                    final[t, :] = tot
                else:
                    part[own, t, :] = tot.astype(BF)

            def close():
                rows_loop(R, 32, lambda r: add(r, True))

            def send():
                rows_loop(R, 32, lambda r: add(r, False))
                remote(part.at[own], rd.at[z], ss.at[3, lev], rs.at[3, z], (core, lev * 4 + p)).start()

            if isinstance(k, int):
                (send if k else close)()
            else:
                pl.when(k == 0)(close)
                pl.when(k > 0)(send)

        @staticmethod
        def d(k):
            lev = lev_of(k)
            copy(3, lev, rd.at[lev], rd.at[lev], xn).wait_recv()

            def add(r):
                t = pl.ds(r, 32)
                final[t, :] = final[t, :] + rd[lev, t, :].astype(F32)

            rows_loop(R, 32, add)

        @staticmethod
        def finish():
            @pl.loop(0, L)
            def _(k):
                lev = lev_of(k)
                for kind in (1, 2):
                    copy(kind, lev, ra.at[0], ra.at[0], xn).wait_send()

                if rz is None:
                    copy(0, lev, ra.at[0], ra.at[0], xn).wait_send()
                else:
                    kind = (lev + z) % 2 * 4
                    copy(kind, lev, ra.at[0], ra.at[0], xn).wait_send()

                @pl.when(k > 0)
                def _():
                    copy(3, lev, ra.at[0], ra.at[0], xn).wait_send()

    return Stages


def sort_matrix(ids_e, ids_s, T):
    zero = ids_e == 0
    n0 = jnp.sum(jnp.where(zero, 1.0, 0.0), axis=1, keepdims=True)
    slot = ids_s.astype(F32)
    pos = jnp.where(zero, slot, slot + n0)
    sub = lax.broadcasted_iota(jnp.int32, (T, T), 0).astype(F32)
    return jnp.where(sub == pos, 1.0, 0.0), n0


def front_kernel(
    x_ref, dyin_ref, doc_ref, e_ref, s_ref, small_ref, wq_ref, wk_ref, wv_ref, wo_ref,
    wu_ref, eu_ref, wd_ref, ed_ref,
    stat_out, u1_out, u2_out, x1_out, dys_out, q_out, k_out, v_out, p_out, o_out,
    small_out, count_out, w_out, y_out, dh_out, sc_out, gup_out, gdn0_out, gdn12_out,
    wbuf, up_ref, dn_ref, smallbuf, bias, dy_all, hall, scall, psc, screcv, wcol, scol, ra, rbx, rby, rd,
    pre, der, ub, dg, dm, m, yacc, dxacc, gdn, gup, sib_dn, sib_up,
    ag_s, ag_r, rs_s, rs_r, sib_s, sib_r, one_s, one_r, sm_s, sm_r, sn_s, sn_r, loc,
):
    T, D = x_ref.shape
    WR = wq_ref.shape[0]
    FR = wd_ref.shape[0]
    N = wbuf.shape[1]
    S = N // 2
    L = S // 4
    me, core, z, p, xq, yq, dq = place_of()
    xn = z * 4 + xq
    my = core * S + me
    sib = (1 - core, me)
    greet(S, core)
    lev_of = level_order(z, L)

    dev, levels = (core, z, p, xq, yq, dq), (lev_of, L)

    def w_at(i):
        return wbuf.at[:, core * S + i]

    wg = tree_gather(w_at, w_at(me), ag_s.at[0], ag_r.at[0], dev, levels)
    dyg = tree_gather(lambda i: dy_all.at[i], dys_out, ag_s.at[1], ag_r.at[1], dev, levels)
    hg = tree_gather(lambda i: hall.at[i], hall.at[me], ag_s.at[2], ag_r.at[2], dev, levels)
    tmp, xs, h1b = m.at[pl.ds(0, T)], yacc.at[pl.ds(0, T)], dm.at[pl.ds(0, T)]

    for i, w in enumerate((wq_ref, wk_ref, wv_ref, wo_ref)):
        wbuf[i, my] = w[...]
    wg.start()

    perm, n0 = sort_matrix(e_ref[...], s_ref[...], T)
    smallbuf[my, 0:8, :] = small_ref[...]
    lane8 = lax.broadcasted_iota(jnp.int32, (8, 128), 1)
    smallbuf[my, 8:16, :] = jnp.where(lane8 == 0, jnp.broadcast_to(n0, (8, 128)), 0.0)

    @pl.loop(1, S)
    def _(i):
        remote(smallbuf.at[my], smallbuf.at[my], sm_s.at[0, i], sm_r.at[0], (core, (me + i) % S)).start()

    F = 2 * FR
    mine_f = pl.ds(pl.multiple_of(core * FR, FR), FR)
    other_f = pl.ds(pl.multiple_of((1 - core) * FR, FR), FR)
    dn_copies = (
        remote(wd_ref, dn_ref.at[0, mine_f], sib_s.at[1, 0], sib_r.at[1, 0], sib),
        remote(ed_ref, dn_ref.at[pl.ds(1, 2), mine_f], sib_s.at[1, 1], sib_r.at[1, 1], sib),
    )
    for c in dn_copies:
        c.start()
    dn_ref[0, mine_f, :] = wd_ref[...]
    for e in range(2):
        dn_ref[1 + e, mine_f, :] = ed_ref[e]
    permb = perm.astype(BF)
    xs[...] = mm(permb, x_ref[...])
    dys_out[...] = mm(permb, dyin_ref[...]).astype(BF)
    dy_all[me] = dys_out[...]
    gdn[...] = jnp.zeros_like(gdn)
    gup[...] = jnp.zeros_like(gup)

    docs = (doc_ref[...] == lax.broadcasted_iota(jnp.int32, (16, T), 0)).astype(F32).astype(BF)
    docs = mm(docs, permb, ((1,), (1,))).astype(BF)
    same = mm(docs, docs, ((0,), (0,)))
    place = lax.broadcasted_iota(jnp.int32, (T, T), 1).astype(F32)
    ord_col = jnp.sum(perm * place, axis=1, keepdims=True)
    ord_row = mm(place[0:16, :].astype(BF), permb, ((1,), (1,)))[0:1, :]
    bias[...] = jnp.where((same > 0.5) & (ord_row <= ord_col), 0.0, -1e30)

    lane = lax.broadcasted_iota(jnp.int32, (64, 128), 1)

    def norm1(r):
        t = pl.ds(r, 64)
        v = xs[t, :]
        cen = v - jnp.mean(v, axis=1, keepdims=True)
        inv = lax.rsqrt(jnp.mean(cen * cen, axis=1, keepdims=True) + 1e-05)
        u1_out[t, :] = cen * inv
        stat_out[t, :] = jnp.where(lane == 8, inv, 0.0)

    rows_loop(T, 64, norm1)

    wg.a(1)
    wg.b(0)
    wg.a(2)
    wg.b(1)
    wg.a(3)
    wg.c(0)

    group = 128 // WR
    remote(smallbuf.at[pl.ds(0, S - 1)], smallbuf.at[pl.ds(0, S - 1)], sm_s.at[0, 0], sm_r.at[0], (core, xn)).wait_recv()
    mine_small = smallbuf.at[pl.ds(core * S, S)]
    c_small = remote(mine_small, mine_small, sib_s.at[1, 2], sib_r.at[1, 2], sib)
    c_small.start()

    def up_copy(e, h, i):
        to = (me + i) % S
        src = wu_ref if e == 0 else eu_ref.at[e - 1]
        return remote(
            src.at[:, pl.ds(pl.multiple_of((h * S + to) * FR, FR), FR)],
            up_ref.at[e, pl.ds(pl.multiple_of(my * WR, WR), WR), pl.ds(h * FR, FR)],
            sm_s.at[1, i], sm_r.at[1], (core, to),
        )

    @pl.loop(1, S)
    def _(i):
        for e in range(3):
            for h in range(2):
                up_copy(e, h, i).start()

    for e in range(3):
        for h in range(2):
            src = wu_ref if e == 0 else eu_ref.at[e - 1]
            block = src[:, pl.ds(pl.multiple_of((h * S + me) * FR, FR), FR)]
            up_ref[e, pl.ds(pl.multiple_of(my * WR, WR), WR), h * FR : (h + 1) * FR] = block

    def w_sib(lev, who):
        b = wbuf.at[:, pl.ds(who * S + lev * 4, 4)]
        return remote(b, b, sib_s.at[0, lev], sib_r.at[0, lev], sib)

    def pass_on(k):
        wg.d(k)
        w_sib(lev_of(k), core).start()

    pass_on(0)
    wg.b(2)
    wg.c(1)
    wg.b(3)
    dyg.start()
    pass_on(1)
    wg.c(2)
    pass_on(2)
    wg.c(3)
    pass_on(3)
    dyg.a(1)
    dyg.b(0)
    c_small.wait_recv()
    for g in range(D // 128):
        part = smallbuf[g * group, 0:8, :]
        for j in range(1, group):
            part = part + smallbuf[g * group + j, 0:8, :]
        small_out[:, g * 128 : (g + 1) * 128] = part
    cnt = smallbuf[0, 8:16, :]
    for i in range(1, N):
        cnt = cnt + smallbuf[i, 8:16, :]
    count_out[...] = cnt

    def norm1b(r):
        t = pl.ds(r, 64)
        h1b[t, :] = (u1_out[t, :] * small_out[0:1, :] + small_out[1:2, :]).astype(BF)

    rows_loop(T, 64, norm1b)
    dyg.a(2)
    dyg.b(1)
    for k in range(L):
        w_sib(lev_of(k), 1 - core).wait_recv()
    w_save = pltpu.make_async_copy(wbuf, w_out, loc.at[L])
    w_save.start()

    def full(i):
        return wbuf[i].reshape(D, D)

    tmp[...] = mm(h1b[...], full(0))
    q_out[...] = (tmp[...] * 0.125).astype(BF)
    dyg.a(3)
    dyg.c(0)
    tmp[...] = mm(h1b[...], full(1))
    k_out[...] = tmp[...].astype(BF)
    tmp[...] = mm(h1b[...], full(2))
    v_out[...] = tmp[...].astype(BF)
    dyg.b(2)
    dyg.c(1)

    low = lax.broadcasted_iota(jnp.int32, (T, 128), 1) < 64
    lowb = low.astype(F32).astype(BF)
    highb = (1.0 - low.astype(F32)).astype(BF)

    def heads(j):
        ln = pl.ds(pl.multiple_of(j * 128, 128), 128)
        qp = q_out[:, ln]
        q2 = jnp.concatenate([qp * lowb, qp * highb], axis=0)
        s = mm(q2, k_out[:, ln], ((1,), (1,)))
        s = s + jnp.concatenate([bias[...], bias[...]], axis=0)
        ex = jnp.exp(s - jnp.max(s, axis=1, keepdims=True))
        pr = ex / jnp.sum(ex, axis=1, keepdims=True)
        p_out[j] = pr
        o2 = mm(pr.astype(BF), v_out[:, ln])
        o_out[:, ln] = jnp.where(low, o2[0:T], o2[T:]).astype(BF)

    @pl.loop(0, D // 128)
    def _(j):
        heads(j)

    dyg.b(3)
    tmp[...] = mm(o_out[...], full(3))

    def norm2(r):
        t = pl.ds(r, 64)
        v = xs[t, :] + tmp[t, :]
        x1_out[t, :] = v
        cen = v - jnp.mean(v, axis=1, keepdims=True)
        inv = lax.rsqrt(jnp.mean(cen * cen, axis=1, keepdims=True) + 1e-05)
        u = cen * inv
        u2_out[t, :] = u
        h2 = u * small_out[2:3, :] + small_out[3:4, :]
        hall[me, t, :] = h2.astype(BF)
        lg = [jnp.sum(h2 * small_out[i : i + 1, :], axis=1, keepdims=True) for i in range(4, 8)]

        def soft(a, b):
            mx = jnp.maximum(a, b)
            ea, eb = jnp.exp(a - mx), jnp.exp(b - mx)
            return ea / (ea + eb), eb / (ea + eb)

        r0, r1 = soft(lg[0], lg[1])
        k0, k1 = soft(lg[2], lg[3])
        row = (lax.broadcasted_iota(jnp.int32, (64, 1), 0) + r).astype(F32)
        is0 = row < n0
        gate = jnp.where(is0, r0, r1)
        we = k0 * gate
        cols = (k1, jnp.where(is0, we, 0.0), jnp.where(is0, 0.0, we), k0, gate, r0, r1)
        st = stat_out[t, :] + jnp.where(lane == 9, inv, 0.0)
        for i, col in enumerate(cols):
            st = st + jnp.where(lane == i, col, 0.0)
        stat_out[t, :] = st

    dyg.c(2)
    rows_loop(T, 64, norm2)
    scall[me] = stat_out[...].T[0:8, :]
    hg.start()

    @pl.loop(1, S)
    def _(i):
        remote(scall.at[me], scall.at[me], sn_s.at[0, i], sn_r.at[0], (core, (me + i) % S)).start()

    dyg.c(3)
    got = up_ref.at[:, pl.ds(0, (S - 1) * WR), :]
    remote(got, got, sm_s.at[1, 0], sm_r.at[1], (core, xn)).wait_recv()
    mine_up = up_ref.at[:, pl.ds(pl.multiple_of(core * S * WR, S * WR), S * WR), :]
    c_slice = remote(mine_up, mine_up, sib_s.at[1, 3], sib_r.at[1, 3], sib)
    c_slice.start()
    end = (z == 0) | (z == L - 1)
    hg.a(1)
    hg.b(0)
    hg.a(2)
    pl.when(jnp.logical_not(end))(lambda: hg.a(3))

    w_save.wait()
    wg.finish()

    @pl.loop(0, L)
    def _(k):
        w_sib(k, core).wait_send()

    remote(scall.at[pl.ds(0, S - 1)], scall.at[pl.ds(0, S - 1)], sn_s.at[0, 0], sn_r.at[0], (core, xn)).wait_recv()
    c_slice.wait()
    for c in dn_copies:
        c.wait()
    c_small.wait_send()
    hg.c(0)
    rgs = []
    for i in range(2):
        t = pl.ds(i * (T // 2), T // 2)
        bufs = [b.at[:, t, :] for b in (dy_all, ra, rbx, rby, rd)]
        rgs.append(tree_scatter(*bufs, dh_out.at[t], rs_s.at[i], rs_r.at[i], dev, levels))
    LO = 80
    HI = T - LO
    per = T // WR
    fold = N // (4 * per)

    size = (4 * T, 4 * LO, 4 * LO)
    first = (0, 4 * T, 4 * T + 4 * LO)

    def y_copy(lev):
        src = wbuf.at[lev // fold, pl.ds(lev % fold * (4 * per), 4 * per)]
        return pltpu.make_async_copy(src, y_out.at[pl.ds(lev * (4 * per), 4 * per)], loc.at[lev])

    def compute(lev, between, settle):
        base = lev * 4
        for q in range(4):
            full = jnp.concatenate([scall[base + q], jnp.zeros((120, 128), F32)], axis=0)
            wcol[q] = full.T
        for e in range(3):
            n = LO if e else T
            off = HI if e == 2 else 0
            rows, at0 = size[e], first[e]
            here = slice(at0, at0 + rows)
            hm = hall[pl.ds(base, 4), off : off + n, :].reshape(rows, D)
            pre[0:rows, :] = mm(hm, up_ref[e])

            def act(r):
                t = pl.ds(r, rows // 4)
                val, d = gelu_pair(pre[t, :])
                ub[pl.ds(pl.multiple_of(at0 + r, 16), rows // 4), :] = val.astype(BF)
                der[t, :] = d

            rows_loop(rows, rows // 4, act)
            m[0:rows, :] = mm(ub[here, :], dn_ref[e])
            step = n if e else T // 2
            lane = lax.broadcasted_iota(jnp.int32, (step, 128), 1)
            for q in range(4):

                def elem(r):
                    at = pl.ds(pl.multiple_of(r + off, 16), step)
                    mine = pl.ds(pl.multiple_of(q * n + r, 16), step)
                    keep = pl.ds(pl.multiple_of(at0 + q * n + r, 16), step)
                    t = pl.ds(pl.multiple_of(q * T + off + r, 16), step)
                    w = wcol[q, at, :][:, e : e + 1]
                    dyv = dy_all[base + q, at, :].astype(F32)
                    mv = m[mine, :]
                    s = jnp.sum(dyv * mv, axis=1, keepdims=True)
                    s = jnp.where(lane == e, s, 0.0)
                    dm[keep, :] = (dyv * w).astype(BF)
                    if e:
                        yacc[t, :] = yacc[t, :] + mv * w
                        scol[q, at, :] = scol[q, at, :] + s
                    else:
                        yacc[t, :] = mv * w
                        scol[q, at, :] = s

                rows_loop(n, step, elem)
            pre[0:rows, :] = mm(dm[here, :], dn_ref[e], ((1,), (1,)))

            def back(r):
                t = pl.ds(r, rows // 4)
                dg[pl.ds(pl.multiple_of(at0 + r, 16), rows // 4), :] = (pre[t, :] * der[t, :]).astype(BF)

            rows_loop(rows, rows // 4, back)
            if e:
                m[0:rows, :] = mm(dg[here, :], up_ref[e], ((1,), (1,)))
                for q in range(4):
                    t = slice(q * T + off, q * T + off + n)
                    dxacc[t, :] = dxacc[t, :] + m[q * n : q * n + n, :]
            else:
                dxacc[...] = mm(dg[here, :], up_ref[0], ((1,), (1,)))
            between(e)
        settle()
        for q in range(4):
            psc[base + q] = scol[q].T[0:8, :]
            t = slice(q * T, q * T + T)
            dy_all[base + q] = dxacc[t, :].astype(BF)
            here = pl.ds(lev % fold * (4 * per) + q * per, per)
            wbuf[lev // fold, here] = yacc[t, :].astype(BF).reshape(per, WR, D)
        y_copy(lev).start()

    def weight_grads(lev):
        for e in range(3):
            n = LO if e else T
            off = HI if e == 2 else 0
            here = slice(first[e], first[e] + size[e])
            hm = hall[pl.ds(lev * 4, 4), off : off + n, :].reshape(size[e], D)
            gdn[e] = gdn[e] + mm(ub[here, :], dm[here, :], ((0,), (0,)))
            gup[e] = gup[e] + mm(dg[here, :], hm, ((0,), (0,)))

    def far_a(i):
        pl.when(end)(lambda: hg.a(i))

    @pl.loop(0, L)
    def _(k):
        @pl.when(k > 0)
        def _():
            hg.d(k)
            dyg.d(k)

        def between(e):
            @pl.when(k == 0)
            def _():
                for call, i in (((far_a, 3), (hg.b, 1)), ((hg.c, 1), (hg.b, 2)), ())[e]:
                    call(i)

            @pl.when(k == 1)
            def _():
                for call, i in (((hg.c, 2), (hg.b, 3)), ((hg.c, 3),), ())[e]:
                    call(i)

            if e == 1:

                @pl.when(k > 0)
                def _():
                    for g in rgs:
                        g.b(k - 1)

        compute(lev_of(k), between, lambda: dyg.done(k))
        for g in rgs:
            g.a(k)

        @pl.when(k > 0)
        def _():
            for g in rgs:
                g.c(k - 1)

        weight_grads(lev_of(k))

    half = D // 2
    other = pl.multiple_of((1 - core) * half, half)
    mine_d = pl.multiple_of(core * half, half)
    c_up = remote(gup.at[:, :, pl.ds(other, half)], sib_up, one_s.at[0], one_r.at[0], sib)
    c_dn = remote(gdn.at[:, other_f, :], sib_dn, one_s.at[1], one_r.at[1], sib)
    c_up.start()
    c_dn.start()

    @pl.loop(1, S)
    def _(i):
        to = (me + i) % S
        remote(psc.at[to], screcv.at[i], sn_s.at[1, i], sn_r.at[1], (core, to)).start()

    for g in rgs:
        g.b(L - 1)
    c_up.wait_recv()
    for e in range(3):
        tot = gup[e, :, pl.ds(mine_d, half)] + sib_up[e]
        gup_out[e] = tot.T.astype(BF)
        if e == 0:
            for g in rgs:
                g.c(L - 1)
    screcv[0] = psc[me]
    c_dn.wait_recv()
    gdn0_out[...] = gdn[0, mine_f, :] + sib_dn[0]
    for e in range(1, 3):
        gdn12_out[e - 1] = gdn[e, mine_f, :] + sib_dn[e]
    for k in range(1, L):
        for g in rgs:
            g.d(k)
    remote(screcv.at[pl.ds(1, S - 1)], screcv.at[pl.ds(1, S - 1)], sn_s.at[1, 0], sn_r.at[1], (core, xn)).wait_recv()
    sc_out[...] = jnp.sum(screcv[...], axis=0)

    for i in range(L):
        y_copy(i).wait()
    c_up.wait_send()
    c_dn.wait_send()
    hg.finish()
    for g in rgs:
        g.finish()

    @pl.loop(1, S)
    def _(i):
        remote(scall.at[me], scall.at[0], sn_s.at[0, i], sn_r.at[0], (core, xn)).wait_send()
        remote(psc.at[0], screcv.at[0], sn_s.at[1, i], sn_r.at[1], (core, xn)).wait_send()
        remote(smallbuf.at[my], smallbuf.at[my], sm_s.at[0, i], sm_r.at[0], (core, xn)).wait_send()
        for e in range(3):
            for h in range(2):
                up_copy(e, h, i).wait_send()


def front_call(x, dy, docs, es, ss, small, ws, wu, eu, wd, ed, S):
    T, D = x.shape
    WR, FR = ws[0].shape[0], wd.shape[0]
    L, N, F = S // 4, 2 * S, 2 * FR
    many = 4 * T + 8 * 80
    vm = pl.BlockSpec(memory_space=pltpu.VMEM)
    hb = pl.BlockSpec(memory_space=pl.ANY)
    V = pltpu.VMEM
    dma = pltpu.SemaphoreType.DMA
    sds = jax.ShapeDtypeStruct
    row = sds((T, D), BF)
    rowf = sds((T, D), F32)
    tokens, blocks, side = V((S, T, D), BF), V((L, T, D), BF), V((S, 8, 128), F32)
    return pl.pallas_call(
        front_kernel,
        out_shape=(
            sds((T, 128), F32), rowf, rowf, rowf, row, row, row, row,
            sds((D // 128, 2 * T, T), F32), row, sds((8, D), F32), sds((8, 128), F32),
            sds((4, N, WR, D), BF), sds((S * T // WR, WR, D), BF), rowf, sds((8, 128), F32), sds((3, D // 2, F), BF),
            sds((FR, D), F32), sds((2, FR, D), F32),
        ),
        in_specs=[vm] * 14,
        out_specs=(vm,) * 12 + (hb, hb) + (vm,) * 5,
        scratch_shapes=[
            V((4, N, WR, D), BF), V((3, D, F), BF), V((3, F, D), BF), V((N, 16, 128), F32), V((T, T), F32),
            tokens, tokens, side, side, side, V((4, T, 128), F32), V((4, T, 128), F32), blocks, blocks, blocks, blocks,
            V((4 * T, F), F32), V((4 * T, F), F32), V((many, F), BF), V((many, F), BF), V((many, D), BF),
            V((4 * T, D), F32), V((4 * T, D), F32), V((4 * T, D), F32),
            V((3, F, D), F32), V((3, F, D), F32), V((3, FR, D), F32), V((3, F, D // 2), F32),
            dma((3, 6, L)), dma((3, 6, L)), dma((2, 4, L)), dma((2, 4, L)), dma((2, max(L, 4))), dma((2, max(L, 4))),
            dma((2,)), dma((2,)), dma((2, S)), dma((2,)), dma((2, S)), dma((2,)), dma((L + 1,)),
        ],
        compiler_params=pltpu.CompilerParams(collective_id=1, has_side_effects=True, vmem_limit_bytes=66000000),
        cost_estimate=pl.CostEstimate(flops=17 * 10**9, bytes_accessed=40 * 2**20, transcendentals=2**20),
        name="front",
    )(x, dy, docs, es, ss, small, *ws, wu, eu, wd, ed)


def back_kernel(
    dh_ref, sc_ref, small_ref, stat_ref, u1_ref, u2_ref, x1_ref, dys_ref,
    q_ref, k_ref, v_ref, p_ref, o_ref, e_ref, s_ref, y_hbm, w_hbm, gup_ref,
    lo_out, ig_out, gq_out, gk_out, gv_out, go_out, smalls_out, gup_out,
    wbuf, perm, accs, dx1, dab, do, dq, dk, dv, h1b, dh1, tmpb, keep, send, recv,
    part0, ra0, rbx0, rby0, rd0, rz0, partv, rav, rbxv, rbyv, rdv, rzv, partk, rak, rbxk, rbyk, rdk, rzk,
    partq, raq, rbxq, rbyq, rdq, rzq, ypart, ray, rbxy, rbyy, rdy, rzy, ysum, lsort, smine, ssib, srecv,
    rs_s, rs_r, sib_s, sib_r, sm_s, sm_r, loc,
):
    T, D = dh_ref.shape
    S, WR = part0.shape[0], part0.shape[1]
    L = S // 4
    half = D // 2
    me, core, z, p, xq, yq, dgq = place_of()
    xn = z * 4 + xq
    sib = (1 - core, me)
    lev_of = level_order(z, L)
    far = list(reversed(range(L)))
    fetch = []
    for k in far:
        some = pl.ds(lev_of(k) * 4, 4)
        fetch.append(pltpu.make_async_copy(y_hbm.at[some], ypart.at[some], loc.at[4 + k]))
    for c in fetch:
        c.start()
    greet(S, core)

    dev, levels = (core, z, p, xq, yq, dgq), (lev_of, L)
    g0 = tree_scatter(part0, ra0, rbx0, rby0, rd0, go_out, rs_s.at[0], rs_r.at[0], dev, levels, rz0)
    gv = tree_scatter(partv, rav, rbxv, rbyv, rdv, gv_out, rs_s.at[1], rs_r.at[1], dev, levels, rzv)
    gk = tree_scatter(partk, rak, rbxk, rbyk, rdk, gk_out, rs_s.at[3], rs_r.at[3], dev, levels, rzk)
    gq = tree_scatter(partq, raq, rbxq, rbyq, rdq, gq_out, rs_s.at[4], rs_r.at[4], dev, levels, rzq)
    gy = tree_scatter(ypart, ray, rbxy, rbyy, rdy, ysum, rs_s.at[2], rs_r.at[2], dev, levels, rzy)
    far = list(reversed(range(L)))
    loads = [pltpu.make_async_copy(w_hbm.at[i], wbuf.at[i], loc.at[i]) for i in range(4)]
    for i in (3, 0, 1, 2):
        loads[i].start()

    for k, c in zip(far, fetch):
        c.wait()
        gy.share(k)
        gy.b0(k)
    perm_f, n0 = sort_matrix(e_ref[...], s_ref[...], T)
    perm[...] = perm_f.astype(BF)
    accs[...] = jnp.zeros_like(accs)
    scol = jnp.concatenate([sc_ref[...], jnp.zeros((120, 128), F32)], axis=0).T
    dh1[:, 0:128] = scol

    def acc(i, v):
        accs[i] = accs[i] + jnp.sum(v.reshape(32 // 8, 8, v.shape[1]), axis=0)

    def norm2(r):
        t = pl.ds(r, 32)
        st = stat_ref[t, :]
        c1, c0, gate, r0, r1, inv = (st[:, i : i + 1] for i in (0, 3, 4, 5, 6, 9))
        row = (lax.broadcasted_iota(jnp.int32, (32, 1), 0) + r).astype(F32)
        is0 = row < n0
        s3 = dh1[t, 0:128]
        sm = s3[:, 0:1]
        se = jnp.where(is0, s3[:, 1:2], s3[:, 2:3])
        dc0, dc1 = gate * se, sm
        tot = c0 * dc0 + c1 * dc1
        dcl0, dcl1 = c0 * (dc0 - tot), c1 * (dc1 - tot)
        dgate = c0 * se
        dr0, dr1 = jnp.where(is0, dgate, 0.0), jnp.where(is0, 0.0, dgate)
        tot = r0 * dr0 + r1 * dr1
        drl0, drl1 = r0 * (dr0 - tot), r1 * (dr1 - tot)
        u2 = u2_ref[t, :]
        h2 = u2 * small_ref[2:3, :] + small_ref[3:4, :]
        dh2 = dh_ref[t, :]
        for i, d in enumerate((drl0, drl1, dcl0, dcl1)):
            acc(4 + i, h2 * d)
            dh2 = dh2 + d * small_ref[4 + i : 5 + i, :]
        acc(2, dh2 * u2)
        acc(3, dh2)
        e = dh2 * small_ref[2:3, :]
        inner = e - jnp.mean(e, axis=1, keepdims=True) - u2 * jnp.mean(e * u2, axis=1, keepdims=True)
        g = dys_ref[t, :].astype(F32) + inv * inner
        dx1[t, :] = g
        dab[t, :] = g.astype(BF)
        h1b[t, :] = (u1_ref[t, :] * small_ref[0:1, :] + small_ref[1:2, :]).astype(BF)

    rows_loop(T, 32, norm2)

    other = pl.multiple_of((1 - core) * half, half)
    mine = pl.multiple_of(core * half, half)

    def weight_grad(i, left, right):
        send[i] = mm(left[:, pl.ds(other, half)], right[...], ((0,), (0,))).astype(BF)
        c = remote(send.at[i], recv.at[i], sib_s.at[i], sib_r.at[i], sib)
        c.start()
        keep[i] = mm(left[:, pl.ds(mine, half)], right[...], ((0,), (0,)))
        return c

    def join(i, c, part):
        c.wait_recv()

        @pl.loop(0, S)
        def _(j):
            t = pl.ds(pl.multiple_of(j * WR, WR), WR)
            part[j] = (keep[i, t, :] + recv[i, t, :].astype(F32)).astype(BF)


    def g_copy(i):
        to = (me + i) % S
        src = gup_ref.at[:, pl.ds(pl.multiple_of(to * WR, WR), WR), :]
        return remote(src, gup_out.at[me], sm_s.at[1, i], sm_r.at[1], (core, to))

    @pl.loop(1, S)
    def _(i):
        g_copy(i).start()

    gup_out[me] = gup_ref[:, pl.ds(pl.multiple_of(me * WR, WR), WR), :]
    low = lax.broadcasted_iota(jnp.int32, (T, 128), 1) < 64
    lowb = low.astype(F32).astype(BF)
    highb = (1.0 - low.astype(F32)).astype(BF)

    def heads(j):
        ln = pl.ds(pl.multiple_of(j * 128, 128), 128)
        qp, dop = q_ref[:, ln], do[:, ln]
        q2 = jnp.concatenate([qp * lowb, qp * highb], axis=0)
        do2 = jnp.concatenate([dop * lowb, dop * highb], axis=0)
        pr = p_ref[j]
        dp = mm(do2, v_ref[:, ln], ((1,), (1,)))
        ds = (pr * (dp - jnp.sum(pr * dp, axis=1, keepdims=True))).astype(BF)
        dq2 = mm(ds, k_ref[:, ln])
        dq[:, ln] = jnp.where(low, dq2[0:T], dq2[T:]).astype(BF) * BF(0.125)
        dk[:, ln] = mm(ds, q2, ((0,), (0,))).astype(BF)
        dv[:, ln] = mm(pr.astype(BF), do2, ((0,), (0,))).astype(BF)

    def norm1(r):
        t = pl.ds(r, 32)
        inv = stat_ref[t, :][:, 8:9]
        u = u1_ref[t, :]
        d = dh1[t, :]
        acc(0, d * u)
        acc(1, d)
        e = d * small_ref[0:1, :]
        inner = e - jnp.mean(e, axis=1, keepdims=True) - u * jnp.mean(e * u, axis=1, keepdims=True)
        tmpb[t, :] = (dx1[t, :] + inv * inner).astype(BF)

    def each(*calls):
        for k in far:
            for call in calls:
                call(k)

    def start(i, c, part, g):
        join(i, c, part)
        each(g.share, g.b0)

    c_o = weight_grad(3, o_ref, dab)
    each(gy.a)
    loads[3].wait()
    do[...] = mm(dab[...], wbuf[3], ((1,), (1,))).astype(BF)
    start(3, c_o, part0, g0)
    each(gy.c0)

    @pl.loop(0, D // 256)
    def _(j):
        heads(j)

    each(gy.b1)

    @pl.loop(D // 256, D // 128)
    def _(j):
        heads(j)

    each(g0.a)
    c_v = weight_grad(2, h1b, dv)
    each(g0.c0)
    c_k = weight_grad(1, h1b, dk)
    start(2, c_v, partv, gv)
    c_q = weight_grad(0, h1b, dq)
    start(1, c_k, partk, gk)
    each(g0.b1)
    each(gy.c1)
    for i in range(3):
        loads[i].wait()
    dh1[...] = mm(dq[...], wbuf[0], ((1,), (1,)))
    start(0, c_q, partq, gq)
    each(gv.a)
    dh1[...] = dh1[...] + mm(dk[...], wbuf[1], ((1,), (1,)))
    each(gk.a, gv.c0)
    dh1[...] = dh1[...] + mm(dv[...], wbuf[2], ((1,), (1,)))
    each(gq.a, gv.b1, g0.c1, gk.c0)
    rows_loop(T, 32, norm1)
    each(gk.b1, gq.c0)
    each(gq.b1, gv.c1)
    for k in range(1, L):
        gy.d(k)
    for i in range(8):
        smine[i : i + 1, :] = jnp.sum(accs[i], axis=0, keepdims=True)
    c_s = remote(smine, ssib, sib_s.at[4], sib_r.at[4], sib)
    c_s.start()
    lsort[...] = (x1_ref[...] + ysum[...]).astype(BF)
    lo_out[...] = mm(perm[...], lsort[...], ((0,), (0,))).astype(BF)
    each(gk.c1)
    ig_out[...] = mm(perm[...], tmpb[...], ((0,), (0,))).astype(BF)
    c_s.wait()
    smine[...] = smine[...] + ssib[...]
    group = 128 // WR

    def s_at(i):
        return smine.at[:, pl.ds(pl.multiple_of((core * S + i) // group * 128, 128), 128)]

    def s_copy(i):
        to = (me + i) % S
        return remote(s_at(to), srecv.at[me], sm_s.at[0, i], sm_r.at[0], (core, to))

    @pl.loop(1, S)
    def _(i):
        s_copy(i).start()

    srecv[me] = s_at(me)[...]
    each(gq.c1)
    for g in (g0, gv, gk, gq):
        for k in range(1, L):
            g.d(k)
    allr = srecv.at[pl.ds(0, S - 1)]
    remote(allr, allr, sm_s.at[0, 0], sm_r.at[0], (core, xn)).wait_recv()
    smalls_out[...] = jnp.sum(srecv[...], axis=0)
    for g in (gy, g0, gv, gk, gq):
        g.finish()
    for c in (c_o, c_v, c_k, c_q):
        c.wait_send()

    got = gup_out.at[pl.ds(0, S - 1)]
    remote(got, got, sm_s.at[1, 0], sm_r.at[1], (core, xn)).wait_recv()

    @pl.loop(1, S)
    def _(i):
        s_copy(i).wait_send()
        g_copy(i).wait_send()


def back_call(dh, y, sc, small, stat, u1, u2, x1, dys, q, k, v, p, o, es, ss, wa, gup, S):
    T, D = dh.shape
    WR = D // (2 * S)
    L = S // 4
    vm = pl.BlockSpec(memory_space=pltpu.VMEM)
    hb = pl.BlockSpec(memory_space=pl.ANY)
    V = pltpu.VMEM
    dma = pltpu.SemaphoreType.DMA
    sds = jax.ShapeDtypeStruct
    row = V((T, D), BF)

    def rs_bufs(R):
        return [V((S, R, D), BF)] + [V((L, R, D), BF)] * 4 + [V((L // 2, R, D), BF)]

    return pl.pallas_call(
        back_kernel,
        out_shape=(
            sds((T, D), BF), sds((T, D), BF), sds((WR, D), F32), sds((WR, D), F32), sds((WR, D), F32),
            sds((WR, D), F32), sds((8, 128), F32),
            sds((S, 3, WR, gup.shape[2]), BF),
        ),
        in_specs=[vm] * 15 + [hb, hb, vm],
        out_specs=(vm,) * 8,
        scratch_shapes=[
            V((4, D, D), BF), V((T, T), BF), V((8, 8, D), F32), V((T, D), F32), row, row, row, row, row, row,
            V((T, D), F32), row, V((4, D // 2, D), F32), V((4, D // 2, D), BF), V((4, D // 2, D), BF),
        ]
        + rs_bufs(WR)
        + rs_bufs(WR)
        + rs_bufs(WR)
        + rs_bufs(WR)
        + rs_bufs(T)
        + [
            V((T, D), F32), V((T, D), BF),
            V((8, D), F32), V((8, D), F32), V((S, 8, 128), F32),
            dma((5, 5, L)), dma((5, 5, L)), dma((5,)), dma((5,)), dma((2, S)), dma((2,)), dma((5 + L,)),
        ],
        compiler_params=pltpu.CompilerParams(collective_id=3, has_side_effects=True, vmem_limit_bytes=60000000),
        cost_estimate=pl.CostEstimate(flops=4 * 10**9, bytes_accessed=20 * 2**20, transcendentals=2**20),
        name="back",
    )(dh, sc, small, stat, u1, u2, x1, dys, q, k, v, p, o, es, ss, y, wa, gup)


def finish_kernel(
    lo_ref, ig_ref, gq_ref, gk_ref, gv_ref, go_ref, sm_ref, gup_ref, gdn0_ref, gdn12_ref,
    lo_out, ig_out, q_out, k_out, v_out, o_out, up_out, dn_out, eu_out, ed_out, r_out, m_out, n_out,
    turned,
):
    S, _, WR, F = gup_ref.shape
    FR = F // 2
    at = (lax.axis_index("dp") * S + lax.axis_index("shard")) % (128 // WR) * WR
    lo_out[...] = lo_ref[...]
    ig_out[...] = ig_ref[...]
    for src, out in ((gq_ref, q_out), (gk_ref, k_out), (gv_ref, v_out), (go_ref, o_out)):
        out[...] = src[...]
    dn_out[...] = gdn0_ref[...]
    ed_out[...] = gdn12_ref[...]
    for s in range(S):
        for c in range(2):
            cols = slice((c * S + s) * FR, (c * S + s + 1) * FR)
            part = slice(c * FR, (c + 1) * FR)
            up_out[:, cols] = gup_ref[s, 0, :, part].astype(F32)
            for e in range(2):
                eu_out[e, :, cols] = gup_ref[s, 1 + e, :, part].astype(F32)
    turned[...] = jnp.concatenate([sm_ref[...], jnp.zeros((120, 128), F32)], axis=0).T
    mine = turned[pl.ds(pl.multiple_of(at, WR), WR), :]
    r_out[...] = mine[:, 4:6]
    m_out[...] = mine[:, 6:8]
    n_out[...] = mine[:, 0:4]


def finish_call(lo, ig, gwq, gwk, gwv, gwo, smalls, gup, gdn0, gdn12):
    T, D = lo.shape
    S, _, WR, F = gup.shape
    FF = S * F
    vm = pl.BlockSpec(memory_space=pltpu.VMEM)
    sds = jax.ShapeDtypeStruct
    sq = sds((WR, D), F32)
    return pl.pallas_call(
        finish_kernel,
        out_shape=(
            sds((T, D), BF), sds((T, D), BF), sq, sq, sq, sq, sds((WR, FF), F32), sds(gdn0.shape, F32),
            sds((2, WR, FF), F32), sds(gdn12.shape, F32), sds((WR, 2), F32), sds((WR, 2), F32), sds((WR, 4), F32),
        ),
        in_specs=[vm] * 10,
        out_specs=(vm,) * 13,
        scratch_shapes=[pltpu.VMEM((128, 128), F32)],
        compiler_params=pltpu.CompilerParams(vmem_limit_bytes=40000000),
        name="finish",
    )(lo, ig, gwq, gwk, gwv, gwo, smalls, gup, gdn0, gdn12)


def body_plain(
    hidden_in, doc_ids, expert_ids, slot_ids, out_grad, ln1_gain, ln1_bias, w_query, w_key, w_value,
    w_out, ln2_gain, ln2_bias, w_up, w_down, w_router, w_mix, expert_up, expert_down, load_avg,
):
    T, D = hidden_in.shape
    H, HD = HEADS, D // HEADS
    S = lax.axis_size("shard")
    C = lax.axis_size("dp")
    WR = w_query.shape[0]
    FF = w_up.shape[1]
    FR = w_down.shape[0]
    F = FR * C
    E = expert_up.shape[0]
    LO, HI = 80, T - 80

    pos = jnp.where(expert_ids == 0, slot_ids, jnp.sum((expert_ids == 0).astype(jnp.int32)) + slot_ids)
    n0 = jnp.sum((expert_ids == 0).astype(jnp.int32))
    place = lax.iota(jnp.int32, T)
    perm = (pos[None, :] == place[:, None]).astype(BF)
    xs = mm(perm, hidden_in)
    dys = mm(perm, out_grad).astype(BF)
    doc = doc_ids[0]
    allowed = (place[None, :] <= place[:, None]) & (doc[:, None] == doc[None, :])
    allowed = mm(mm(perm, allowed.astype(BF)).astype(BF), perm, ((1,), (1,))) > 0.5
    is0 = (place < n0)[:, None]

    small = jnp.stack(
        [ln1_gain, ln1_bias, ln2_gain, ln2_bias, w_router[:, 0], w_router[:, 1], w_mix[:, 0], w_mix[:, 1]]
    ).astype(F32)
    small = lax.all_gather(small, BOTH, axis=1, tiled=True)
    g1, b1, g2, b2 = small[0], small[1], small[2], small[3]
    wr, wm = small[4:6], small[6:8]

    wa = jnp.stack([w_query, w_key, w_value, w_out])
    wa = lax.all_gather(wa, BOTH, axis=1, tiled=True)
    wq, wk, wv, wo = wa[0], wa[1], wa[2], wa[3]

    ups = jnp.stack([w_up, expert_up[0], expert_up[1]])
    ups = ups.reshape(3, WR, C, S, FR).transpose(3, 0, 1, 2, 4).reshape(S, 3, WR, F)
    ups = lax.all_to_all(ups, "shard", 0, 0)
    ups = lax.all_gather(ups, "dp", axis=0)
    ups = ups.transpose(2, 0, 1, 3, 4).reshape(3, D, F)
    downs = jnp.stack([w_down, expert_down[0], expert_down[1]])
    downs = lax.all_gather(downs, "dp", axis=1, tiled=True)

    dy_all = ag(dys)

    n1, u1, i1 = layer_norm(xs, g1, b1)
    h1b = n1.astype(BF)
    q = (mm(h1b, wq) * 0.125).astype(BF).reshape(T, H, HD)
    k = mm(h1b, wk).astype(BF).reshape(T, H, HD)
    v = mm(h1b, wv).astype(BF).reshape(T, H, HD)
    s = jnp.einsum("ihd,jhd->hij", q, k, preferred_element_type=F32)
    s = jnp.where(allowed[None], s, -1e30)
    ex = jnp.exp(s - jnp.max(s, axis=-1, keepdims=True))
    p = ex / jnp.sum(ex, axis=-1, keepdims=True)
    pb = p.astype(BF)
    o = jnp.einsum("hij,jhd->ihd", pb, v, preferred_element_type=F32).reshape(T, D).astype(BF)
    x1 = xs + mm(o, wo)
    h2, u2, i2 = layer_norm(x1, g2, b2)
    h2b = h2.astype(BF)

    def two(w):
        return jnp.stack([jnp.sum(h2 * w[0], axis=-1), jnp.sum(h2 * w[1], axis=-1)], axis=-1)

    r = jax.nn.softmax(two(wr), axis=-1)
    c = jax.nn.softmax(two(wm), axis=-1)
    gate = jnp.where(is0, r[:, 0:1], r[:, 1:2])
    c0, c1 = c[:, 0:1], c[:, 1:2]
    we = c0 * gate
    scal = jnp.concatenate([c1, jnp.where(is0, we, 0.0), jnp.where(is0, 0.0, we)], axis=1)

    h_all = ag(h2b)
    scal_all = ag(scal)

    def cut(a, e):
        return (a[:, :LO] if e == 1 else a[:, HI:]) if e else a

    partial_y = jnp.zeros((S, T, D), F32)
    partial_dh = jnp.zeros((S, T, D), F32)
    score = []
    gup, gdown = [], []
    for e in range(3):
        he = cut(h_all, e)
        dye = cut(dy_all, e).astype(F32)
        se = cut(scal_all, e)[:, :, e : e + 1]
        n = he.shape[1]
        hf = he.reshape(S * n, D)
        pre = mm(hf, ups[e])
        val, der = gelu_pair(pre)
        ub = val.astype(BF)
        m = mm(ub, downs[e]).reshape(S, n, D)
        dm = (dye * se).astype(BF).reshape(S * n, D)
        dg = (mm(dm, downs[e], ((1,), (1,))) * der).astype(BF)
        gdown.append(mm(ub, dm, ((0,), (0,))))
        gup.append(mm(hf, dg, ((0,), (0,))))
        dx = mm(dg, ups[e], ((1,), (1,))).reshape(S, n, D)
        y = m * se
        sc = jnp.sum(dye * m, axis=-1)
        pad = [(0, 0), (0, T - n) if e < 2 else (T - n, 0)]
        live = is0[None, :, 0]
        partial_y += jnp.pad(y, pad + [(0, 0)])
        partial_dh += jnp.pad(dx, pad + [(0, 0)])
        score.append(jnp.pad(sc, pad))
    yfull = rs(partial_y)
    dh2 = rs(partial_dh)
    sc = lax.psum_scatter(jnp.stack(score, axis=1), "shard", scatter_dimension=0, tiled=False)
    sm = sc[0][:, None]
    se = jnp.where(is0, sc[1][:, None], sc[2][:, None])

    dc0, dc1 = gate * se, sm
    tot = c0 * dc0 + c1 * dc1
    dcl0, dcl1 = c0 * (dc0 - tot), c1 * (dc1 - tot)
    dgate = c0 * se
    dr0, dr1 = jnp.where(is0, dgate, 0.0), jnp.where(is0, 0.0, dgate)
    tot = r[:, 0:1] * dr0 + r[:, 1:2] * dr1
    drl0, drl1 = r[:, 0:1] * (dr0 - tot), r[:, 1:2] * (dr1 - tot)
    layer_out = (x1 + yfull).astype(BF)
    dh2 = dh2 + drl0 * wr[0] + drl1 * wr[1] + dcl0 * wm[0] + dcl1 * wm[1]
    gw = [jnp.sum(h2 * t, axis=0) for t in (drl0, drl1, dcl0, dcl1)]
    dx1, gg2, gb2 = norm_back(dh2, u2, i2, g2)
    dx1 = dx1 + dys.astype(F32)
    dab = dx1.astype(BF)
    gwo = mm(o, dab, ((0,), (0,)))
    do = mm(dab, wo, ((1,), (1,))).astype(BF).reshape(T, H, HD)
    dp = jnp.einsum("ihd,jhd->hij", do, v, preferred_element_type=F32)
    ds = (p * (dp - jnp.sum(p * dp, axis=-1, keepdims=True))).astype(BF)
    dq = jnp.einsum("hij,jhd->ihd", ds, k, preferred_element_type=F32).astype(BF)
    dq = (dq * BF(0.125)).reshape(T, D)
    dk = jnp.einsum("hij,ihd->jhd", ds, q, preferred_element_type=F32).astype(BF).reshape(T, D)
    dv = jnp.einsum("hij,ihd->jhd", pb, do, preferred_element_type=F32).astype(BF).reshape(T, D)
    dh1 = mm(dq, wq, ((1,), (1,))) + mm(dk, wk, ((1,), (1,))) + mm(dv, wv, ((1,), (1,)))
    ga = jnp.stack([mm(h1b, dq, ((0,), (0,))), mm(h1b, dk, ((0,), (0,))), mm(h1b, dv, ((0,), (0,))), gwo])
    dxn, gg1, gb1 = norm_back(dh1, u1, i1, g1)
    input_grad = (dx1 + dxn).astype(BF)

    layer_out = mm(perm, layer_out, ((0,), (0,))).astype(BF)
    input_grad = mm(perm, input_grad, ((0,), (0,))).astype(BF)

    smalls = lax.psum(jnp.stack([gg1, gb1, gg2, gb2] + gw), BOTH)
    mine = lax.dynamic_slice_in_dim(smalls, lax.axis_index(BOTH) * WR, WR, 1)
    ga = ga.reshape(4, C, S, WR, D).transpose(1, 2, 0, 3, 4)
    ga = lax.psum_scatter(ga.astype(BF), "dp", scatter_dimension=0, tiled=False)
    ga = lax.psum_scatter(ga, "shard", scatter_dimension=0, tiled=False).astype(F32)
    gdown = lax.psum_scatter(jnp.stack(gdown), "dp", scatter_dimension=1, tiled=True)
    gup = jnp.stack(gup).reshape(3, C, S, WR, F).transpose(1, 2, 0, 3, 4)
    gup = lax.psum_scatter(gup, "dp", scatter_dimension=0, tiled=False).astype(BF)
    gup = lax.all_to_all(gup, "shard", 0, 0).astype(F32)
    gup = gup.reshape(S, 3, WR, C, FR).transpose(1, 2, 3, 0, 4).reshape(3, WR, FF)

    counts = lax.psum(jnp.stack([n0, T - n0]), BOTH)
    load_new = 0.9 * load_avg + 0.1 * counts.astype(F32) * E / (T * C * S)
    return (
        layer_out, input_grad, mine[0], mine[1], ga[0], ga[1], ga[2], ga[3], mine[2], mine[3],
        gup[0], gdown[0], jnp.stack([mine[4], mine[5]], axis=1), jnp.stack([mine[6], mine[7]], axis=1),
        gup[1:], gdown[1:], counts, load_new,
    )


def body(
    hidden_in, doc_ids, expert_ids, slot_ids, out_grad, ln1_gain, ln1_bias, w_query, w_key, w_value,
    w_out, ln2_gain, ln2_bias, w_up, w_down, w_router, w_mix, expert_up, expert_down, load_avg,
):
    T, D = hidden_in.shape
    H, HD = HEADS, D // HEADS
    S = lax.axis_size("shard")
    C = lax.axis_size("dp")
    WR = w_query.shape[0]
    FF = w_up.shape[1]
    FR = w_down.shape[0]
    F = FR * C
    E = expert_up.shape[0]
    ndev = C * S
    dev = lax.axis_index(BOTH)
    small = jnp.stack(
        [ln1_gain, ln1_bias, ln2_gain, ln2_bias, w_router[:, 0], w_router[:, 1], w_mix[:, 0], w_mix[:, 1]]
    ).astype(F32)
    group = 128 // WR
    slot_of = lax.broadcasted_iota(jnp.int32, (8, 128), 1) // WR
    small = jnp.where(slot_of == dev % group, jnp.tile(small, (1, group)), 0.0)
    (
        stat, u1, u2, x1, dys, q, k, v, p, o, small, count, wa, y_parts, dh2, sc, gup, gdn0, gdn12,
    ) = front_call(
        hidden_in, out_grad, doc_ids, expert_ids.reshape(1, T), slot_ids.reshape(1, T), small,
        (w_query, w_key, w_value, w_out), w_up, expert_up, w_down, expert_down, S,
    )
    y_parts = y_parts.reshape(S, T, D)
    layer_out, input_grad, gwq, gwk, gwv, gwo, smalls, gup = back_call(
        dh2, y_parts, sc, small, stat, u1, u2, x1, dys, q, k, v, p, o,
        expert_ids.reshape(1, T), slot_ids.reshape(1, T), wa.reshape(4, D, D), gup, S,
    )
    lo, ig, gq, gk, gv, go, gu, gd, geu, ged, gr, gm, gn = finish_call(
        layer_out, input_grad, gwq, gwk, gwv, gwo, smalls, gup, gdn0, gdn12
    )
    tokens0 = count[0, 0].astype(jnp.int32)
    counts = jnp.stack([tokens0, T * ndev - tokens0])
    load_new = 0.9 * load_avg + 0.1 * counts.astype(F32) * E / (T * ndev)
    return (
        lo, ig, gn[:, 0], gn[:, 1], gq, gk, gv, go, gn[:, 2], gn[:, 3],
        gu, gd, gr, gm, geu, ged, counts, load_new,
    )


def pick(*args):
    S, C, WR, FR = lax.axis_size("shard"), lax.axis_size("dp"), args[7].shape[0], args[14].shape[0]
    fast = C == 2 and S // 4 == 4 and S % 4 == 0 and WR % 16 == 0 and 128 % WR == 0 and FR % 128 == 0
    return (body if fast else body_plain)(*args)


def solution(mesh):
    row, vec = P(BOTH, None), P(BOTH)
    mid = P(None, BOTH, None)
    return jax.shard_map(
        pick,
        mesh=mesh,
        in_specs=(row, row, vec, vec, row, vec, vec, row, row, row, row, vec, vec, row, row, row, row, mid, mid, P()),
        out_specs=(row, row, vec, vec, row, row, row, row, vec, vec, row, row, row, row, mid, mid, P(), P()),
        check_vma=False,
    )
```

```python
import jax
import jax.numpy as jnp
from jax import lax
from jax.experimental import pallas as pl
from jax.experimental.pallas import tpu as pltpu
from jax.sharding import PartitionSpec as P

HEADS = 16
CAP = 74
BF = jnp.bfloat16
F32 = jnp.float32
BOTH = ("dp", "shard")
MESH = pl.DeviceIdType.MESH


def mm(a, b, dims=((1,), (0,))):
    return lax.dot_general(a, b, (dims, ((), ())), preferred_element_type=F32)


def layer_norm(values, gain, bias):
    centre = values - jnp.mean(values, axis=-1, keepdims=True)
    scale_inv = lax.rsqrt(jnp.mean(centre * centre, axis=-1, keepdims=True) + 1e-05)
    normed = centre * scale_inv
    return (normed * gain + bias, normed, scale_inv)


def norm_back(grad_out, normed, scale_inv, gain):
    grad_normed = grad_out * gain
    inner = grad_normed - jnp.mean(grad_normed, axis=-1, keepdims=True)
    inner = inner - normed * jnp.mean(grad_normed * normed, axis=-1, keepdims=True)
    return (scale_inv * inner, jnp.sum(grad_out * normed, axis=0), jnp.sum(grad_out, axis=0))


def gelu_pair(t):
    inner = 0.7978845608 * (t + 0.044715 * t * t * t)
    th = jnp.tanh(inner)
    val = 0.5 * t * (1.0 + th)
    der = 0.5 * (1.0 + th) + 0.5 * t * (1.0 - th * th) * 0.7978845608 * (1.0 + 3.0 * 0.044715 * t * t)
    return val, der


def ag(block):
    return lax.all_gather(block, "shard", axis=0, tiled=False)


def rs(parts):
    return lax.psum_scatter(parts.astype(BF), "shard", scatter_dimension=0, tiled=False).astype(F32)


def place_of():
    me = lax.axis_index("shard")
    core = lax.axis_index("dp")
    z, p = me // 4, me % 4
    xq = p + 1 - 2 * (p % 2)
    yq = p + 2 - 4 * (p // 2)
    return me, core, z, p, xq, yq, 3 - p


def greet(shards, core):
    bar = pltpu.get_barrier_semaphore()
    me = lax.axis_index("shard")

    @pl.loop(1, shards)
    def _(i):
        pl.semaphore_signal(bar, inc=1, device_id=(core, (me + i) % shards), device_id_type=MESH)

    pl.semaphore_signal(bar, inc=1, device_id=(1 - core, me), device_id_type=MESH)
    pl.semaphore_wait(bar, shards)


def remote(src, dst, send, recv, dev):
    return pltpu.make_async_remote_copy(
        src_ref=src, dst_ref=dst, send_sem=send, recv_sem=recv, device_id=dev, device_id_type=MESH
    )


def rows_loop(count, step, fn):
    @pl.loop(0, count // step)
    def _(i):
        fn(pl.multiple_of(i * step, step))


def level_order(z, L):
    upper = z // (L // 2)
    y = z + upper * (L - 1 - 2 * z)

    def lev_of(k):
        low = k - 1 + (k - 1 - y + L) // L
        lev = low + upper * (L - 1 - 2 * low)
        first = 1 - (k + L - 1) // L
        return lev + first * (z - lev)

    return lev_of


def tree_gather(at, own, ss, rs, dev, levels):
    core, z, p, xq, yq, dq = dev
    xn, yn = z * 4 + xq, z * 4 + yq
    me = z * 4 + p
    pair = me + 4 - 8 * (z % 2)
    lev_of, L = levels

    def copy(kind, slot, src, idx, to):
        return remote(src, at(idx), ss.at[kind, slot], rs.at[kind, slot], (core, to))

    def up_line(src, send):
        return remote(src, at(me), send, rs.at[0, z], (core, me + 4))

    def down_line(src, send):
        return remote(src, at(me), send, rs.at[0, z], (core, me - 4))

    def onward(k):
        lev = lev_of(k)
        step = 1 - 2 * ((lev - z + L) // L)
        to = z + step
        idx = lev * 4 + p
        ok = (to >= 0) & (to < L)
        return ok, remote(at(idx), at(idx), ss.at[0, lev], rs.at[0, lev], (core, me + 4 * step))

    class Stages:
        @staticmethod
        def start():
            @pl.when(z < L - 1)
            def _():
                up_line(own, ss.at[0, z]).start()

            @pl.when(z > 0)
            def _():
                down_line(own, ss.at[4, 0]).start()

            copy(1, z, own, me, xn).start()
            copy(2, z, own, me, yn).start()

        @staticmethod
        def a(k):
            lev = lev_of(k)
            idx = lev * 4 + p
            copy(0, lev, own, idx, xn).wait_recv()
            ok, on = onward(k)

            @pl.when(ok)
            def _():
                on.start()

            copy(1, lev, at(idx), idx, xn).start()
            copy(2, lev, at(idx), idx, yn).start()

        @staticmethod
        def b(k):
            lev = lev_of(k)
            odd = lev // 2 % 2
            copy(1, lev, own, lev * 4 + xq, xn).wait_recv()
            copy(2, lev, own, lev * 4 + yq, yn).wait_recv()
            idx = lev * 4 + xq + odd * (yq - xq)

            @pl.when((lev + z) % 2 == 0)
            def _():
                copy(3, lev, at(idx), idx, yn + odd * (xn - yn)).start()

        @staticmethod
        def c(k):
            lev = lev_of(k)
            idx = lev * 4 + dq

            @pl.when((lev + z) % 2 == 0)
            def _():
                copy(3, lev, own, idx, xn).wait_recv()
                copy(5, lev, at(idx), idx, pair).start()

        @staticmethod
        def d(k):
            lev = lev_of(k)

            @pl.when((lev + z) % 2 == 1)
            def _():
                copy(5, lev, own, lev * 4 + dq, pair).wait_recv()

        @staticmethod
        def done(k):
            lev = lev_of(k)
            for kind in range(1, 3):
                copy(kind, lev, own, me, xn).wait_send()

            @pl.when((lev + z) % 2 == 0)
            def _():
                for kind in (3, 5):
                    copy(kind, lev, own, me, xn).wait_send()

            @pl.when(k > 0)
            def _():
                ok, on = onward(k)
                pl.when(ok)(on.wait_send)

            @pl.when(k == 0)
            def _():
                pl.when(z < L - 1)(lambda: up_line(own, ss.at[0, z]).wait_send())
                pl.when(z > 0)(lambda: down_line(own, ss.at[4, 0]).wait_send())

        @staticmethod
        def finish():
            @pl.loop(0, L)
            def _(k):
                Stages.done(k)

    return Stages


def together(*machines):
    class Stages:
        pass

    for name in vars(machines[0]):
        if not name.startswith("_"):
            calls = [getattr(mach, name) for mach in machines]
            setattr(Stages, name, staticmethod(lambda *a, calls=calls: [call(*a) for call in calls] and None))
    return Stages


def tree_scatter(part, ra, rbx, rby, rd, final, ss, rs, dev, levels, rz=None):
    core, z, p, xq, yq, dq = dev
    xn, yn = z * 4 + xq, z * 4 + yq
    pair = z * 4 + p + 4 - 8 * (z % 2)
    lev_of, L = levels
    R = part.shape[1]

    def copy(kind, lev, src, dst, to):
        return remote(src, dst, ss.at[kind, lev], rs.at[kind, lev], (core, to))

    def sides(lev):
        copy(1, lev, part.at[lev * 4 + xq], rbx.at[lev], xn).start()
        copy(2, lev, part.at[lev * 4 + yq], rby.at[lev], yn).start()

    class Stages:
        @staticmethod
        def share(k):
            lev = lev_of(k)

            @pl.when((lev + z) % 2 == 1)
            def _():
                copy(4, lev, part.at[lev * 4 + dq], rz.at[lev // 2], pair).start()

        @staticmethod
        def a(k):
            lev = lev_of(k)
            odd = k % 2 if rz is None else lev // 2 % 2
            diag = lev * 4 + dq

            def send():
                copy(0, lev, part.at[diag], ra.at[lev], yn + odd * (xn - yn)).start()

            def join():
                copy(4, lev, rz.at[lev // 2], rz.at[lev // 2], pair).wait_recv()

                def add(r):
                    t = pl.ds(r, 32)
                    part[diag, t, :] = (part[diag, t, :].astype(F32) + rz[lev // 2, t, :].astype(F32)).astype(BF)

                rows_loop(R, 32, add)
                send()

            if rz is None:
                send()
            else:
                pl.when((lev + z) % 2 == 0)(join)

        @staticmethod
        def b(k):
            lev = lev_of(k)
            odd = k % 2 if rz is None else lev // 2 % 2
            via = lev * 4 + xq + odd * (yq - xq)
            copy(0, lev, ra.at[lev], ra.at[lev], xn).wait_recv()

            def add(r):
                t = pl.ds(r, 32)
                part[via, t, :] = (part[via, t, :].astype(F32) + ra[lev, t, :].astype(F32)).astype(BF)

            rows_loop(R, 32, add)
            sides(lev)

        @staticmethod
        def b0(k):
            pl.when((lev_of(k) + z) % 2 == 1)(lambda: sides(lev_of(k)))

        @staticmethod
        def b1(k):
            pl.when((lev_of(k) + z) % 2 == 0)(lambda: Stages.b(k))

        @staticmethod
        def c0(k):
            pl.when((lev_of(k) + z) % 2 == 1)(lambda: Stages.c(k))

        @staticmethod
        def c1(k):
            pl.when((lev_of(k) + z) % 2 == 0)(lambda: Stages.c(k))

        @staticmethod
        def c(k):
            lev = lev_of(k)
            own = lev * 4 + p
            copy(1, lev, rbx.at[lev], rbx.at[lev], xn).wait_recv()
            copy(2, lev, rby.at[lev], rby.at[lev], yn).wait_recv()

            def add(r, last):
                t = pl.ds(r, 32)
                tot = part[own, t, :].astype(F32) + rbx[lev, t, :].astype(F32) + rby[lev, t, :].astype(F32)
                if last:
                    final[t, :] = tot
                else:
                    part[own, t, :] = tot.astype(BF)

            def close():
                rows_loop(R, 32, lambda r: add(r, True))

            def send():
                rows_loop(R, 32, lambda r: add(r, False))
                remote(part.at[own], rd.at[z], ss.at[3, lev], rs.at[3, z], (core, lev * 4 + p)).start()

            if isinstance(k, int):
                (send if k else close)()
            else:
                pl.when(k == 0)(close)
                pl.when(k > 0)(send)

        @staticmethod
        def d(k):
            lev = lev_of(k)
            copy(3, lev, rd.at[lev], rd.at[lev], xn).wait_recv()

            def add(r):
                t = pl.ds(r, 32)
                final[t, :] = final[t, :] + rd[lev, t, :].astype(F32)

            rows_loop(R, 32, add)

        @staticmethod
        def finish():
            @pl.loop(0, L)
            def _(k):
                lev = lev_of(k)
                for kind in (1, 2):
                    copy(kind, lev, ra.at[0], ra.at[0], xn).wait_send()

                if rz is None:
                    copy(0, lev, ra.at[0], ra.at[0], xn).wait_send()
                else:
                    kind = (lev + z) % 2 * 4
                    copy(kind, lev, ra.at[0], ra.at[0], xn).wait_send()

                @pl.when(k > 0)
                def _():
                    copy(3, lev, ra.at[0], ra.at[0], xn).wait_send()

    return Stages


def sort_matrix(ids_e, ids_s, T):
    zero = ids_e == 0
    n0 = jnp.sum(jnp.where(zero, 1.0, 0.0), axis=1, keepdims=True)
    slot = ids_s.astype(F32)
    pos = jnp.where(zero, slot, slot + n0)
    sub = lax.broadcasted_iota(jnp.int32, (T, T), 0).astype(F32)
    return jnp.where(sub == pos, 1.0, 0.0), n0


def front_kernel(
    x_ref, dyin_ref, doc_ref, e_ref, s_ref, small_ref, wq_ref, wk_ref, wv_ref, wo_ref,
    wu_ref, eu_ref, wd_ref, ed_ref,
    stat_out, u1_out, u2_out, x1_out, dys_out, q_out, k_out, v_out, p_out, o_out,
    small_out, count_out, w_out, y_out, dh_out, sc_out, gup_out, gdn0_out, gdn12_out,
    wbuf, up_ref, dn_ref, smallbuf, h1b, bias, tmp, xs, dy_all, hall, dxp, scall, psc, screcv, wcol, scol, ra, rbx, rby, rd,
    pre, dyw, uw, dg, gdn, gup, sib_dn, sib_up,
    ag_s, ag_r, rs_s, rs_r, sib_s, sib_r, one_s, one_r, sm_s, sm_r, sn_s, sn_r, loc,
):
    T, D = x_ref.shape
    WR = wq_ref.shape[0]
    FR = wd_ref.shape[0]
    N = wbuf.shape[1]
    S = N // 2
    L = S // 4
    me, core, z, p, xq, yq, dq = place_of()
    xn = z * 4 + xq
    my = core * S + me
    sib = (1 - core, me)
    greet(S, core)
    lev_of = level_order(z, L)

    dev, levels = (core, z, p, xq, yq, dq), (lev_of, L)

    def split(at, j):
        return tree_gather(at, at(me), ag_s.at[j], ag_r.at[j], dev, levels)

    def rows_of(ref, j):
        return lambda i: ref.at[i, pl.ds(j * (T // 2), T // 2)]

    wg = together(*(split(lambda i, j=j: wbuf.at[pl.ds(2 * j, 2), core * S + i], j) for j in range(2)))
    dyg = together(*(split(rows_of(dy_all, j), 2 + j) for j in range(2)))
    hg = together(*(split(rows_of(hall, j), 4 + j) for j in range(2)))

    for i, w in enumerate((wq_ref, wk_ref, wv_ref, wo_ref)):
        wbuf[i, my] = w[...]
    wg.start()

    perm, n0 = sort_matrix(e_ref[...], s_ref[...], T)
    smallbuf[my, 0:8, :] = small_ref[...]
    lane8 = lax.broadcasted_iota(jnp.int32, (8, 128), 1)
    smallbuf[my, 8:16, :] = jnp.where(lane8 == 0, jnp.broadcast_to(n0, (8, 128)), 0.0)

    @pl.loop(1, S)
    def _(i):
        remote(smallbuf.at[my], smallbuf.at[my], sm_s.at[0, i], sm_r.at[0], (core, (me + i) % S)).start()

    F = 2 * FR
    mine_f = pl.ds(pl.multiple_of(core * FR, FR), FR)
    other_f = pl.ds(pl.multiple_of((1 - core) * FR, FR), FR)
    dn_copies = (
        remote(wd_ref, dn_ref.at[0, mine_f], sib_s.at[1, 0], sib_r.at[1, 0], sib),
        remote(ed_ref, dn_ref.at[pl.ds(1, 2), mine_f], sib_s.at[1, 1], sib_r.at[1, 1], sib),
    )
    for c in dn_copies:
        c.start()
    dn_ref[0, mine_f, :] = wd_ref[...]
    for e in range(2):
        dn_ref[1 + e, mine_f, :] = ed_ref[e]
    permb = perm.astype(BF)
    xs[...] = mm(permb, x_ref[...])
    dys_out[...] = mm(permb, dyin_ref[...]).astype(BF)
    dy_all[me] = dys_out[...]
    gdn[...] = jnp.zeros_like(gdn)
    gup[...] = jnp.zeros_like(gup)

    docs = (doc_ref[...] == lax.broadcasted_iota(jnp.int32, (16, T), 0)).astype(F32).astype(BF)
    docs = mm(docs, permb, ((1,), (1,))).astype(BF)
    same = mm(docs, docs, ((0,), (0,)))
    place = lax.broadcasted_iota(jnp.int32, (T, T), 1).astype(F32)
    ord_col = jnp.sum(perm * place, axis=1, keepdims=True)
    ord_row = mm(place[0:16, :].astype(BF), permb, ((1,), (1,)))[0:1, :]
    bias[...] = jnp.where((same > 0.5) & (ord_row <= ord_col), 0.0, -1e30)

    lane = lax.broadcasted_iota(jnp.int32, (64, 128), 1)

    def norm1(r):
        t = pl.ds(r, 64)
        v = xs[t, :]
        cen = v - jnp.mean(v, axis=1, keepdims=True)
        inv = lax.rsqrt(jnp.mean(cen * cen, axis=1, keepdims=True) + 1e-05)
        u1_out[t, :] = cen * inv
        stat_out[t, :] = jnp.where(lane == 8, inv, 0.0)

    rows_loop(T, 64, norm1)

    wg.a(1)
    wg.b(0)
    wg.a(2)
    wg.b(1)
    wg.a(3)
    wg.c(0)

    group = 128 // WR
    remote(smallbuf.at[pl.ds(0, S - 1)], smallbuf.at[pl.ds(0, S - 1)], sm_s.at[0, 0], sm_r.at[0], (core, xn)).wait_recv()
    mine_small = smallbuf.at[pl.ds(core * S, S)]
    c_small = remote(mine_small, mine_small, sib_s.at[1, 2], sib_r.at[1, 2], sib)
    c_small.start()

    def up_copy(e, h, i):
        to = (me + i) % S
        src = wu_ref if e == 0 else eu_ref.at[e - 1]
        return remote(
            src.at[:, pl.ds(pl.multiple_of((h * S + to) * FR, FR), FR)],
            up_ref.at[pl.ds(pl.multiple_of(my * WR, WR), WR), pl.ds(e * F + h * FR, FR)],
            sm_s.at[1, i], sm_r.at[1], (core, to),
        )

    @pl.loop(1, S)
    def _(i):
        for e in range(3):
            for h in range(2):
                up_copy(e, h, i).start()

    for e in range(3):
        for h in range(2):
            src = wu_ref if e == 0 else eu_ref.at[e - 1]
            block = src[:, pl.ds(pl.multiple_of((h * S + me) * FR, FR), FR)]
            up_ref[pl.ds(pl.multiple_of(my * WR, WR), WR), e * F + h * FR : e * F + (h + 1) * FR] = block

    def w_sib(lev, who):
        b = wbuf.at[:, pl.ds(who * S + lev * 4, 4)]
        return remote(b, b, sib_s.at[0, lev], sib_r.at[0, lev], sib)

    def pass_on(k):
        wg.d(k)
        w_sib(lev_of(k), core).start()

    pass_on(0)
    wg.b(2)
    wg.c(1)
    wg.b(3)
    dyg.start()
    pass_on(1)
    wg.c(2)
    pass_on(2)
    wg.c(3)
    pass_on(3)
    dyg.a(1)
    dyg.b(0)
    c_small.wait_recv()
    for g in range(D // 128):
        part = smallbuf[g * group, 0:8, :]
        for j in range(1, group):
            part = part + smallbuf[g * group + j, 0:8, :]
        small_out[:, g * 128 : (g + 1) * 128] = part
    cnt = smallbuf[0, 8:16, :]
    for i in range(1, N):
        cnt = cnt + smallbuf[i, 8:16, :]
    count_out[...] = cnt

    def norm1b(r):
        t = pl.ds(r, 64)
        h1b[t, :] = (u1_out[t, :] * small_out[0:1, :] + small_out[1:2, :]).astype(BF)

    rows_loop(T, 64, norm1b)
    dyg.a(2)
    dyg.b(1)
    for k in range(L):
        w_sib(lev_of(k), 1 - core).wait_recv()
    w_save = pltpu.make_async_copy(wbuf, w_out, loc.at[L])
    w_save.start()

    def full(i):
        return wbuf[i].reshape(D, D)

    tmp[...] = mm(h1b[...], full(0))
    q_out[...] = (tmp[...] * 0.125).astype(BF)
    dyg.a(3)
    dyg.c(0)
    tmp[...] = mm(h1b[...], full(1))
    k_out[...] = tmp[...].astype(BF)
    tmp[...] = mm(h1b[...], full(2))
    v_out[...] = tmp[...].astype(BF)
    dyg.b(2)
    dyg.c(1)

    low = lax.broadcasted_iota(jnp.int32, (T, 128), 1) < 64
    lowb = low.astype(F32).astype(BF)
    highb = (1.0 - low.astype(F32)).astype(BF)

    def heads(j):
        ln = pl.ds(pl.multiple_of(j * 128, 128), 128)
        qp = q_out[:, ln]
        q2 = jnp.concatenate([qp * lowb, qp * highb], axis=0)
        s = mm(q2, k_out[:, ln], ((1,), (1,)))
        s = s + jnp.concatenate([bias[...], bias[...]], axis=0)
        ex = jnp.exp(s - jnp.max(s, axis=1, keepdims=True))
        pr = ex / jnp.sum(ex, axis=1, keepdims=True)
        p_out[j] = pr
        o2 = mm(pr.astype(BF), v_out[:, ln])
        o_out[:, ln] = jnp.where(low, o2[0:T], o2[T:]).astype(BF)

    @pl.loop(0, D // 128)
    def _(j):
        heads(j)

    dyg.b(3)
    tmp[...] = mm(o_out[...], full(3))

    def norm2(r):
        t = pl.ds(r, 64)
        v = xs[t, :] + tmp[t, :]
        x1_out[t, :] = v
        cen = v - jnp.mean(v, axis=1, keepdims=True)
        inv = lax.rsqrt(jnp.mean(cen * cen, axis=1, keepdims=True) + 1e-05)
        u = cen * inv
        u2_out[t, :] = u
        h2 = u * small_out[2:3, :] + small_out[3:4, :]
        hall[me, t, :] = h2.astype(BF)
        lg = [jnp.sum(h2 * small_out[i : i + 1, :], axis=1, keepdims=True) for i in range(4, 8)]

        def soft(a, b):
            mx = jnp.maximum(a, b)
            ea, eb = jnp.exp(a - mx), jnp.exp(b - mx)
            return ea / (ea + eb), eb / (ea + eb)

        r0, r1 = soft(lg[0], lg[1])
        k0, k1 = soft(lg[2], lg[3])
        row = (lax.broadcasted_iota(jnp.int32, (64, 1), 0) + r).astype(F32)
        is0 = row < n0
        gate = jnp.where(is0, r0, r1)
        we = k0 * gate
        cols = (k1, jnp.where(is0, we, 0.0), jnp.where(is0, 0.0, we), k0, gate, r0, r1)
        st = stat_out[t, :] + jnp.where(lane == 9, inv, 0.0)
        for i, col in enumerate(cols):
            st = st + jnp.where(lane == i, col, 0.0)
        stat_out[t, :] = st

    dyg.c(2)
    rows_loop(T, 64, norm2)
    scall[me] = stat_out[...].T[0:8, :]
    hg.start()

    @pl.loop(1, S)
    def _(i):
        remote(scall.at[me], scall.at[me], sn_s.at[0, i], sn_r.at[0], (core, (me + i) % S)).start()

    dyg.c(3)
    got = up_ref.at[pl.ds(0, (S - 1) * WR), :]
    remote(got, got, sm_s.at[1, 0], sm_r.at[1], (core, xn)).wait_recv()
    mine_up = up_ref.at[pl.ds(pl.multiple_of(core * S * WR, S * WR), S * WR), :]
    c_slice = remote(mine_up, mine_up, sib_s.at[1, 3], sib_r.at[1, 3], sib)
    c_slice.start()
    end = (z == 0) | (z == L - 1)
    hg.a(1)
    hg.b(0)
    hg.a(2)
    pl.when(jnp.logical_not(end))(lambda: hg.a(3))

    w_save.wait()
    wg.finish()

    @pl.loop(0, L)
    def _(k):
        w_sib(k, core).wait_send()

    remote(scall.at[pl.ds(0, S - 1)], scall.at[pl.ds(0, S - 1)], sn_s.at[0, 0], sn_r.at[0], (core, xn)).wait_recv()
    c_slice.wait()
    for c in dn_copies:
        c.wait()
    c_small.wait_send()
    hg.c(0)
    rgs = []
    for i in range(2):
        t = pl.ds(i * (T // 2), T // 2)
        bufs = [b.at[:, t, :] for b in (dxp, ra, rbx, rby, rd)]
        rgs.append(tree_scatter(*bufs, dh_out.at[t], rs_s.at[i], rs_r.at[i], dev, levels))
    LO = 80
    HI = T - LO
    per = T // WR
    fold = N // (4 * per)

    def y_copy(lev):
        src = wbuf.at[lev // fold, pl.ds(lev % fold * (4 * per), 4 * per)]
        return pltpu.make_async_copy(src, y_out.at[pl.ds(lev * (4 * per), 4 * per)], loc.at[lev])

    def compute(lev, between):
        base = lev * 4
        level = pl.ds(base, 4)
        for q in range(4):
            full = jnp.concatenate([scall[base + q], jnp.zeros((120, 128), F32)], axis=0)
            wcol[q] = full.T
        pre[...] = mm(hall[level].reshape(4 * T, D), up_ref[...])
        between(0)
        dyw[...] = mm(dy_all[level].reshape(4 * T, D), dn_ref[...].reshape(3 * F, D), ((1,), (1,)))
        lane = lax.broadcasted_iota(jnp.int32, (T, 128), 1)

        @pl.loop(0, 4)
        def _(q):
            t = pl.ds(pl.multiple_of(q * T, T), T)
            score = jnp.zeros((T, 128), F32)
            for e in range(3):
                cols = slice(e * F, (e + 1) * F)
                val, der = gelu_pair(pre[t, cols])
                low = val.astype(BF).astype(F32)
                back = dyw[t, cols]
                w = wcol[q][:, e : e + 1]
                score = score + jnp.where(lane == e, jnp.sum(low * back, axis=1, keepdims=True), 0.0)
                uw[t, cols] = (low * w).astype(BF)
                dg[t, cols] = (back * w * der).astype(BF)
            psc[base + q] = score.T[0:8, :]

        between(1)
        dxp[level] = mm(dg[...], up_ref[...], ((1,), (1,))).astype(BF).reshape(4, T, D)
        y = mm(uw[...], dn_ref[...].reshape(3 * F, D)).astype(BF)
        wbuf[lev // fold, pl.ds(lev % fold * (4 * per), 4 * per)] = y.reshape(4 * per, WR, D)
        y_copy(lev).start()
        between(2)

    def weight_grads(lev):
        for e in range(3):
            n = LO if e else T
            off = HI if e == 2 else 0
            level = pl.ds(lev * 4, 4)

            def some(a):
                a = a[:, e * F : (e + 1) * F]
                return a.reshape(4, T, F)[:, off : off + n].reshape(4 * n, F)

            hm = hall[level, off : off + n, :].reshape(4 * n, D)
            dyb = dy_all[level, off : off + n, :].reshape(4 * n, D)
            gdn[e] = gdn[e] + mm(some(uw), dyb, ((0,), (0,)))
            gup[e] = gup[e] + mm(some(dg), hm, ((0,), (0,)))

    def far_a(i):
        pl.when(end)(lambda: hg.a(i))

    @pl.loop(0, L)
    def _(k):
        @pl.when(k > 0)
        def _():
            hg.d(k)
            dyg.d(k)

        def between(e):
            @pl.when(k == 0)
            def _():
                for call, i in (((far_a, 3), (hg.b, 1)), ((hg.c, 1), (hg.b, 2)), ())[e]:
                    call(i)

            @pl.when(k == 1)
            def _():
                for call, i in (((hg.c, 2), (hg.b, 3)), ((hg.c, 3),), ())[e]:
                    call(i)

            if e == 1:

                @pl.when(k > 0)
                def _():
                    for g in rgs:
                        g.b(k - 1)

        compute(lev_of(k), between)
        for g in rgs:
            g.a(k)

        @pl.when(k > 0)
        def _():
            for g in rgs:
                g.c(k - 1)

        weight_grads(lev_of(k))

    half = D // 2
    other = pl.multiple_of((1 - core) * half, half)
    mine_d = pl.multiple_of(core * half, half)
    c_up = remote(gup.at[:, :, pl.ds(other, half)], sib_up, one_s.at[0], one_r.at[0], sib)
    c_dn = remote(gdn.at[:, other_f, :], sib_dn, one_s.at[1], one_r.at[1], sib)
    c_up.start()
    c_dn.start()

    @pl.loop(1, S)
    def _(i):
        to = (me + i) % S
        remote(psc.at[to], screcv.at[i], sn_s.at[1, i], sn_r.at[1], (core, to)).start()

    for g in rgs:
        g.b(L - 1)
    c_up.wait_recv()
    for e in range(3):
        tot = gup[e, :, pl.ds(mine_d, half)] + sib_up[e]
        gup_out[e] = tot.T.astype(BF)
        if e == 0:
            for g in rgs:
                g.c(L - 1)
    screcv[0] = psc[me]
    c_dn.wait_recv()
    gdn0_out[...] = gdn[0, mine_f, :] + sib_dn[0]
    for e in range(1, 3):
        gdn12_out[e - 1] = gdn[e, mine_f, :] + sib_dn[e]
    for k in range(1, L):
        for g in rgs:
            g.d(k)
    remote(screcv.at[pl.ds(1, S - 1)], screcv.at[pl.ds(1, S - 1)], sn_s.at[1, 0], sn_r.at[1], (core, xn)).wait_recv()
    sc_out[...] = jnp.sum(screcv[...], axis=0)

    for i in range(L):
        y_copy(i).wait()
    c_up.wait_send()
    c_dn.wait_send()
    hg.finish()
    dyg.finish()
    for g in rgs:
        g.finish()

    @pl.loop(1, S)
    def _(i):
        remote(scall.at[me], scall.at[0], sn_s.at[0, i], sn_r.at[0], (core, xn)).wait_send()
        remote(psc.at[0], screcv.at[0], sn_s.at[1, i], sn_r.at[1], (core, xn)).wait_send()
        remote(smallbuf.at[my], smallbuf.at[my], sm_s.at[0, i], sm_r.at[0], (core, xn)).wait_send()
        for e in range(3):
            for h in range(2):
                up_copy(e, h, i).wait_send()


def front_call(x, dy, docs, es, ss, small, ws, wu, eu, wd, ed, S):
    T, D = x.shape
    WR, FR = ws[0].shape[0], wd.shape[0]
    L, N, F = S // 4, 2 * S, 2 * FR
    vm = pl.BlockSpec(memory_space=pltpu.VMEM)
    hb = pl.BlockSpec(memory_space=pl.ANY)
    V = pltpu.VMEM
    dma = pltpu.SemaphoreType.DMA
    sds = jax.ShapeDtypeStruct
    row = sds((T, D), BF)
    rowf = sds((T, D), F32)
    tokens, blocks, side = V((S, T, D), BF), V((L, T, D), BF), V((S, 8, 128), F32)
    return pl.pallas_call(
        front_kernel,
        out_shape=(
            sds((T, 128), F32), rowf, rowf, rowf, row, row, row, row,
            sds((D // 128, 2 * T, T), F32), row, sds((8, D), F32), sds((8, 128), F32),
            sds((4, N, WR, D), BF), sds((S * T // WR, WR, D), BF), rowf, sds((8, 128), F32), sds((3, D // 2, F), BF),
            sds((FR, D), F32), sds((2, FR, D), F32),
        ),
        in_specs=[vm] * 14,
        out_specs=(vm,) * 12 + (hb, hb) + (vm,) * 5,
        scratch_shapes=[
            V((4, N, WR, D), BF), V((D, 3 * F), BF), V((3, F, D), BF), V((N, 16, 128), F32), V((T, D), BF), V((T, T), F32),
            V((T, D), F32), V((T, D), F32), tokens, tokens, tokens, side, side, side, V((4, T, 128), F32), V((4, T, 128), F32), blocks, blocks, blocks, blocks,
            V((4 * T, 3 * F), F32), V((4 * T, 3 * F), F32), V((4 * T, 3 * F), BF), V((4 * T, 3 * F), BF),
            V((3, F, D), F32), V((3, F, D), F32), V((3, FR, D), F32), V((3, F, D // 2), F32),
            dma((6, 6, L)), dma((6, 6, L)), dma((2, 4, L)), dma((2, 4, L)), dma((2, max(L, 4))), dma((2, max(L, 4))),
            dma((2,)), dma((2,)), dma((2, S)), dma((2,)), dma((2, S)), dma((2,)), dma((L + 1,)),
        ],
        compiler_params=pltpu.CompilerParams(collective_id=1, has_side_effects=True, vmem_limit_bytes=66000000),
        cost_estimate=pl.CostEstimate(flops=17 * 10**9, bytes_accessed=40 * 2**20, transcendentals=2**20),
        name="front",
    )(x, dy, docs, es, ss, small, *ws, wu, eu, wd, ed)


def back_kernel(
    dh_ref, sc_ref, small_ref, stat_ref, u1_ref, u2_ref, x1_ref, dys_ref,
    q_ref, k_ref, v_ref, p_ref, o_ref, e_ref, s_ref, y_hbm, w_hbm, gup_ref,
    lo_out, ig_out, gq_out, gk_out, gv_out, go_out, smalls_out, gup_out,
    wbuf, perm, accs, dx1, dab, do, dq, dk, dv, h1b, dh1, tmpb, keep, send, recv,
    part0, ra0, rbx0, rby0, rd0, rz0, partv, rav, rbxv, rbyv, rdv, rzv, partk, rak, rbxk, rbyk, rdk, rzk,
    partq, raq, rbxq, rbyq, rdq, rzq, ypart, ray, rbxy, rbyy, rdy, rzy, ysum, lsort, smine, ssib, srecv,
    rs_s, rs_r, sib_s, sib_r, sm_s, sm_r, loc,
):
    T, D = dh_ref.shape
    S, WR = part0.shape[0], part0.shape[1]
    L = S // 4
    half = D // 2
    me, core, z, p, xq, yq, dgq = place_of()
    xn = z * 4 + xq
    sib = (1 - core, me)
    lev_of = level_order(z, L)
    far = list(reversed(range(L)))
    fetch = []
    for k in far:
        some = pl.ds(lev_of(k) * 4, 4)
        fetch.append(pltpu.make_async_copy(y_hbm.at[some], ypart.at[some], loc.at[4 + k]))
    for c in fetch:
        c.start()
    greet(S, core)

    dev, levels = (core, z, p, xq, yq, dgq), (lev_of, L)
    g0 = tree_scatter(part0, ra0, rbx0, rby0, rd0, go_out, rs_s.at[0], rs_r.at[0], dev, levels, rz0)
    gv = tree_scatter(partv, rav, rbxv, rbyv, rdv, gv_out, rs_s.at[1], rs_r.at[1], dev, levels, rzv)
    gk = tree_scatter(partk, rak, rbxk, rbyk, rdk, gk_out, rs_s.at[3], rs_r.at[3], dev, levels, rzk)
    gq = tree_scatter(partq, raq, rbxq, rbyq, rdq, gq_out, rs_s.at[4], rs_r.at[4], dev, levels, rzq)
    gy = tree_scatter(ypart, ray, rbxy, rbyy, rdy, ysum, rs_s.at[2], rs_r.at[2], dev, levels, rzy)
    far = list(reversed(range(L)))
    loads = [pltpu.make_async_copy(w_hbm.at[i], wbuf.at[i], loc.at[i]) for i in range(4)]
    for i in (3, 0, 1, 2):
        loads[i].start()

    for k, c in zip(far, fetch):
        c.wait()
        gy.share(k)
        gy.b0(k)
    perm_f, n0 = sort_matrix(e_ref[...], s_ref[...], T)
    perm[...] = perm_f.astype(BF)
    accs[...] = jnp.zeros_like(accs)
    scol = jnp.concatenate([sc_ref[...], jnp.zeros((120, 128), F32)], axis=0).T
    dh1[:, 0:128] = scol

    def acc(i, v):
        accs[i] = accs[i] + jnp.sum(v.reshape(32 // 8, 8, v.shape[1]), axis=0)

    def norm2(r):
        t = pl.ds(r, 32)
        st = stat_ref[t, :]
        c1, c0, gate, r0, r1, inv = (st[:, i : i + 1] for i in (0, 3, 4, 5, 6, 9))
        row = (lax.broadcasted_iota(jnp.int32, (32, 1), 0) + r).astype(F32)
        is0 = row < n0
        s3 = dh1[t, 0:128]
        sm = s3[:, 0:1]
        se = jnp.where(is0, s3[:, 1:2], s3[:, 2:3])
        dc0, dc1 = gate * se, sm
        tot = c0 * dc0 + c1 * dc1
        dcl0, dcl1 = c0 * (dc0 - tot), c1 * (dc1 - tot)
        dgate = c0 * se
        dr0, dr1 = jnp.where(is0, dgate, 0.0), jnp.where(is0, 0.0, dgate)
        tot = r0 * dr0 + r1 * dr1
        drl0, drl1 = r0 * (dr0 - tot), r1 * (dr1 - tot)
        u2 = u2_ref[t, :]
        h2 = u2 * small_ref[2:3, :] + small_ref[3:4, :]
        dh2 = dh_ref[t, :]
        for i, d in enumerate((drl0, drl1, dcl0, dcl1)):
            acc(4 + i, h2 * d)
            dh2 = dh2 + d * small_ref[4 + i : 5 + i, :]
        acc(2, dh2 * u2)
        acc(3, dh2)
        e = dh2 * small_ref[2:3, :]
        inner = e - jnp.mean(e, axis=1, keepdims=True) - u2 * jnp.mean(e * u2, axis=1, keepdims=True)
        g = dys_ref[t, :].astype(F32) + inv * inner
        dx1[t, :] = g
        dab[t, :] = g.astype(BF)
        h1b[t, :] = (u1_ref[t, :] * small_ref[0:1, :] + small_ref[1:2, :]).astype(BF)

    rows_loop(T, 32, norm2)

    other = pl.multiple_of((1 - core) * half, half)
    mine = pl.multiple_of(core * half, half)

    def weight_grad(i, left, right):
        send[i] = mm(left[:, pl.ds(other, half)], right[...], ((0,), (0,))).astype(BF)
        c = remote(send.at[i], recv.at[i], sib_s.at[i], sib_r.at[i], sib)
        c.start()
        keep[i] = mm(left[:, pl.ds(mine, half)], right[...], ((0,), (0,)))
        return c

    def join(i, c, part):
        c.wait_recv()

        @pl.loop(0, S)
        def _(j):
            t = pl.ds(pl.multiple_of(j * WR, WR), WR)
            part[j] = (keep[i, t, :] + recv[i, t, :].astype(F32)).astype(BF)


    def g_copy(i):
        to = (me + i) % S
        src = gup_ref.at[:, pl.ds(pl.multiple_of(to * WR, WR), WR), :]
        return remote(src, gup_out.at[me], sm_s.at[1, i], sm_r.at[1], (core, to))

    @pl.loop(1, S)
    def _(i):
        g_copy(i).start()

    gup_out[me] = gup_ref[:, pl.ds(pl.multiple_of(me * WR, WR), WR), :]
    low = lax.broadcasted_iota(jnp.int32, (T, 128), 1) < 64
    lowb = low.astype(F32).astype(BF)
    highb = (1.0 - low.astype(F32)).astype(BF)

    def heads(j):
        ln = pl.ds(pl.multiple_of(j * 128, 128), 128)
        qp, dop = q_ref[:, ln], do[:, ln]
        q2 = jnp.concatenate([qp * lowb, qp * highb], axis=0)
        do2 = jnp.concatenate([dop * lowb, dop * highb], axis=0)
        pr = p_ref[j]
        dp = mm(do2, v_ref[:, ln], ((1,), (1,)))
        ds = (pr * (dp - jnp.sum(pr * dp, axis=1, keepdims=True))).astype(BF)
        dq2 = mm(ds, k_ref[:, ln])
        dq[:, ln] = jnp.where(low, dq2[0:T], dq2[T:]).astype(BF) * BF(0.125)
        dk[:, ln] = mm(ds, q2, ((0,), (0,))).astype(BF)
        dv[:, ln] = mm(pr.astype(BF), do2, ((0,), (0,))).astype(BF)

    def norm1(r):
        t = pl.ds(r, 32)
        inv = stat_ref[t, :][:, 8:9]
        u = u1_ref[t, :]
        d = dh1[t, :]
        acc(0, d * u)
        acc(1, d)
        e = d * small_ref[0:1, :]
        inner = e - jnp.mean(e, axis=1, keepdims=True) - u * jnp.mean(e * u, axis=1, keepdims=True)
        tmpb[t, :] = (dx1[t, :] + inv * inner).astype(BF)

    def each(*calls):
        for k in far:
            for call in calls:
                call(k)

    def start(i, c, part, g):
        join(i, c, part)
        each(g.share, g.b0)

    c_o = weight_grad(3, o_ref, dab)
    each(gy.a)
    loads[3].wait()
    do[...] = mm(dab[...], wbuf[3], ((1,), (1,))).astype(BF)
    start(3, c_o, part0, g0)
    each(gy.c0)

    @pl.loop(0, D // 256)
    def _(j):
        heads(j)

    each(gy.b1)

    @pl.loop(D // 256, D // 128)
    def _(j):
        heads(j)

    each(g0.a)
    c_v = weight_grad(2, h1b, dv)
    each(g0.c0)
    c_k = weight_grad(1, h1b, dk)
    start(2, c_v, partv, gv)
    c_q = weight_grad(0, h1b, dq)
    start(1, c_k, partk, gk)
    each(g0.b1)
    each(gy.c1)
    for i in range(3):
        loads[i].wait()
    dh1[...] = mm(dq[...], wbuf[0], ((1,), (1,)))
    start(0, c_q, partq, gq)
    each(gv.a)
    dh1[...] = dh1[...] + mm(dk[...], wbuf[1], ((1,), (1,)))
    each(gk.a, gv.c0)
    dh1[...] = dh1[...] + mm(dv[...], wbuf[2], ((1,), (1,)))
    each(gq.a, gv.b1, g0.c1, gk.c0)
    rows_loop(T, 32, norm1)
    each(gk.b1, gq.c0)
    each(gq.b1, gv.c1)
    for k in range(1, L):
        gy.d(k)
    for i in range(8):
        smine[i : i + 1, :] = jnp.sum(accs[i], axis=0, keepdims=True)
    c_s = remote(smine, ssib, sib_s.at[4], sib_r.at[4], sib)
    c_s.start()
    lsort[...] = (x1_ref[...] + ysum[...]).astype(BF)
    lo_out[...] = mm(perm[...], lsort[...], ((0,), (0,))).astype(BF)
    each(gk.c1)
    ig_out[...] = mm(perm[...], tmpb[...], ((0,), (0,))).astype(BF)
    c_s.wait()
    smine[...] = smine[...] + ssib[...]
    group = 128 // WR

    def s_at(i):
        return smine.at[:, pl.ds(pl.multiple_of((core * S + i) // group * 128, 128), 128)]

    def s_copy(i):
        to = (me + i) % S
        return remote(s_at(to), srecv.at[me], sm_s.at[0, i], sm_r.at[0], (core, to))

    @pl.loop(1, S)
    def _(i):
        s_copy(i).start()

    srecv[me] = s_at(me)[...]
    each(gq.c1)
    for g in (g0, gv, gk, gq):
        for k in range(1, L):
            g.d(k)
    allr = srecv.at[pl.ds(0, S - 1)]
    remote(allr, allr, sm_s.at[0, 0], sm_r.at[0], (core, xn)).wait_recv()
    smalls_out[...] = jnp.sum(srecv[...], axis=0)
    for g in (gy, g0, gv, gk, gq):
        g.finish()
    for c in (c_o, c_v, c_k, c_q):
        c.wait_send()

    got = gup_out.at[pl.ds(0, S - 1)]
    remote(got, got, sm_s.at[1, 0], sm_r.at[1], (core, xn)).wait_recv()

    @pl.loop(1, S)
    def _(i):
        s_copy(i).wait_send()
        g_copy(i).wait_send()


def back_call(dh, y, sc, small, stat, u1, u2, x1, dys, q, k, v, p, o, es, ss, wa, gup, S):
    T, D = dh.shape
    WR = D // (2 * S)
    L = S // 4
    vm = pl.BlockSpec(memory_space=pltpu.VMEM)
    hb = pl.BlockSpec(memory_space=pl.ANY)
    V = pltpu.VMEM
    dma = pltpu.SemaphoreType.DMA
    sds = jax.ShapeDtypeStruct
    row = V((T, D), BF)

    def rs_bufs(R):
        return [V((S, R, D), BF)] + [V((L, R, D), BF)] * 4 + [V((L // 2, R, D), BF)]

    return pl.pallas_call(
        back_kernel,
        out_shape=(
            sds((T, D), BF), sds((T, D), BF), sds((WR, D), F32), sds((WR, D), F32), sds((WR, D), F32),
            sds((WR, D), F32), sds((8, 128), F32),
            sds((S, 3, WR, gup.shape[2]), BF),
        ),
        in_specs=[vm] * 15 + [hb, hb, vm],
        out_specs=(vm,) * 8,
        scratch_shapes=[
            V((4, D, D), BF), V((T, T), BF), V((8, 8, D), F32), V((T, D), F32), row, row, row, row, row, row,
            V((T, D), F32), row, V((4, D // 2, D), F32), V((4, D // 2, D), BF), V((4, D // 2, D), BF),
        ]
        + rs_bufs(WR)
        + rs_bufs(WR)
        + rs_bufs(WR)
        + rs_bufs(WR)
        + rs_bufs(T)
        + [
            V((T, D), F32), V((T, D), BF),
            V((8, D), F32), V((8, D), F32), V((S, 8, 128), F32),
            dma((5, 5, L)), dma((5, 5, L)), dma((5,)), dma((5,)), dma((2, S)), dma((2,)), dma((5 + L,)),
        ],
        compiler_params=pltpu.CompilerParams(collective_id=3, has_side_effects=True, vmem_limit_bytes=60000000),
        cost_estimate=pl.CostEstimate(flops=4 * 10**9, bytes_accessed=20 * 2**20, transcendentals=2**20),
        name="back",
    )(dh, sc, small, stat, u1, u2, x1, dys, q, k, v, p, o, es, ss, y, wa, gup)


def finish_kernel(
    lo_hbm, ig_hbm, gq_hbm, gk_hbm, gv_hbm, go_hbm, sm_hbm, gup_hbm, gdn0_hbm, gdn12_hbm,
    lo_out, ig_out, q_out, k_out, v_out, o_out, up_out, dn_out, eu_out, ed_out, r_out, m_out, n_out,
    sm_ref, gup_ref, turned, sems,
):
    pairs = (
        (gup_hbm, gup_ref), (sm_hbm, sm_ref), (lo_hbm, lo_out), (ig_hbm, ig_out), (gq_hbm, q_out), (gk_hbm, k_out),
        (gv_hbm, v_out), (go_hbm, o_out), (gdn0_hbm, dn_out), (gdn12_hbm, ed_out),
    )
    copies = [pltpu.make_async_copy(a, b, sems.at[i]) for i, (a, b) in enumerate(pairs)]
    for c in copies:
        c.start()
    copies[0].wait()
    copies[1].wait()
    S, _, WR, F = gup_ref.shape
    FR = F // 2
    at = (lax.axis_index("dp") * S + lax.axis_index("shard")) % (128 // WR) * WR
    for s in range(S):
        for c in range(2):
            cols = slice((c * S + s) * FR, (c * S + s + 1) * FR)
            part = slice(c * FR, (c + 1) * FR)
            up_out[:, cols] = gup_ref[s, 0, :, part].astype(F32)
            for e in range(2):
                eu_out[e, :, cols] = gup_ref[s, 1 + e, :, part].astype(F32)
    turned[...] = jnp.concatenate([sm_ref[...], jnp.zeros((120, 128), F32)], axis=0).T
    mine = turned[pl.ds(pl.multiple_of(at, WR), WR), :]
    r_out[...] = mine[:, 4:6]
    m_out[...] = mine[:, 6:8]
    n_out[...] = mine[:, 0:4]
    for c in copies[2:]:
        c.wait()


def finish_call(lo, ig, gwq, gwk, gwv, gwo, smalls, gup, gdn0, gdn12):
    T, D = lo.shape
    S, _, WR, F = gup.shape
    FF = S * F
    vm = pl.BlockSpec(memory_space=pltpu.VMEM)
    sds = jax.ShapeDtypeStruct
    sq = sds((WR, D), F32)
    return pl.pallas_call(
        finish_kernel,
        out_shape=(
            sds((T, D), BF), sds((T, D), BF), sq, sq, sq, sq, sds((WR, FF), F32), sds(gdn0.shape, F32),
            sds((2, WR, FF), F32), sds(gdn12.shape, F32), sds((WR, 2), F32), sds((WR, 2), F32), sds((WR, 4), F32),
        ),
        in_specs=[pl.BlockSpec(memory_space=pl.ANY)] * 10,
        out_specs=(vm,) * 13,
        scratch_shapes=[
            pltpu.VMEM(smalls.shape, F32), pltpu.VMEM(gup.shape, BF), pltpu.VMEM((128, 128), F32), pltpu.SemaphoreType.DMA((10,)),
        ],
        compiler_params=pltpu.CompilerParams(vmem_limit_bytes=66000000),
        name="finish",
    )(lo, ig, gwq, gwk, gwv, gwo, smalls, gup, gdn0, gdn12)


def body_plain(
    hidden_in, doc_ids, expert_ids, slot_ids, out_grad, ln1_gain, ln1_bias, w_query, w_key, w_value,
    w_out, ln2_gain, ln2_bias, w_up, w_down, w_router, w_mix, expert_up, expert_down, load_avg,
):
    T, D = hidden_in.shape
    H, HD = HEADS, D // HEADS
    S = lax.axis_size("shard")
    C = lax.axis_size("dp")
    WR = w_query.shape[0]
    FF = w_up.shape[1]
    FR = w_down.shape[0]
    F = FR * C
    E = expert_up.shape[0]
    LO, HI = 80, T - 80

    pos = jnp.where(expert_ids == 0, slot_ids, jnp.sum((expert_ids == 0).astype(jnp.int32)) + slot_ids)
    n0 = jnp.sum((expert_ids == 0).astype(jnp.int32))
    place = lax.iota(jnp.int32, T)
    perm = (pos[None, :] == place[:, None]).astype(BF)
    xs = mm(perm, hidden_in)
    dys = mm(perm, out_grad).astype(BF)
    doc = doc_ids[0]
    allowed = (place[None, :] <= place[:, None]) & (doc[:, None] == doc[None, :])
    allowed = mm(mm(perm, allowed.astype(BF)).astype(BF), perm, ((1,), (1,))) > 0.5
    is0 = (place < n0)[:, None]

    small = jnp.stack(
        [ln1_gain, ln1_bias, ln2_gain, ln2_bias, w_router[:, 0], w_router[:, 1], w_mix[:, 0], w_mix[:, 1]]
    ).astype(F32)
    small = lax.all_gather(small, BOTH, axis=1, tiled=True)
    g1, b1, g2, b2 = small[0], small[1], small[2], small[3]
    wr, wm = small[4:6], small[6:8]

    wa = jnp.stack([w_query, w_key, w_value, w_out])
    wa = lax.all_gather(wa, BOTH, axis=1, tiled=True)
    wq, wk, wv, wo = wa[0], wa[1], wa[2], wa[3]

    ups = jnp.stack([w_up, expert_up[0], expert_up[1]])
    ups = ups.reshape(3, WR, C, S, FR).transpose(3, 0, 1, 2, 4).reshape(S, 3, WR, F)
    ups = lax.all_to_all(ups, "shard", 0, 0)
    ups = lax.all_gather(ups, "dp", axis=0)
    ups = ups.transpose(2, 0, 1, 3, 4).reshape(3, D, F)
    downs = jnp.stack([w_down, expert_down[0], expert_down[1]])
    downs = lax.all_gather(downs, "dp", axis=1, tiled=True)

    dy_all = ag(dys)

    n1, u1, i1 = layer_norm(xs, g1, b1)
    h1b = n1.astype(BF)
    q = (mm(h1b, wq) * 0.125).astype(BF).reshape(T, H, HD)
    k = mm(h1b, wk).astype(BF).reshape(T, H, HD)
    v = mm(h1b, wv).astype(BF).reshape(T, H, HD)
    s = jnp.einsum("ihd,jhd->hij", q, k, preferred_element_type=F32)
    s = jnp.where(allowed[None], s, -1e30)
    ex = jnp.exp(s - jnp.max(s, axis=-1, keepdims=True))
    p = ex / jnp.sum(ex, axis=-1, keepdims=True)
    pb = p.astype(BF)
    o = jnp.einsum("hij,jhd->ihd", pb, v, preferred_element_type=F32).reshape(T, D).astype(BF)
    x1 = xs + mm(o, wo)
    h2, u2, i2 = layer_norm(x1, g2, b2)
    h2b = h2.astype(BF)

    def two(w):
        return jnp.stack([jnp.sum(h2 * w[0], axis=-1), jnp.sum(h2 * w[1], axis=-1)], axis=-1)

    r = jax.nn.softmax(two(wr), axis=-1)
    c = jax.nn.softmax(two(wm), axis=-1)
    gate = jnp.where(is0, r[:, 0:1], r[:, 1:2])
    c0, c1 = c[:, 0:1], c[:, 1:2]
    we = c0 * gate
    scal = jnp.concatenate([c1, jnp.where(is0, we, 0.0), jnp.where(is0, 0.0, we)], axis=1)

    h_all = ag(h2b)
    scal_all = ag(scal)

    def cut(a, e):
        return (a[:, :LO] if e == 1 else a[:, HI:]) if e else a

    partial_y = jnp.zeros((S, T, D), F32)
    partial_dh = jnp.zeros((S, T, D), F32)
    score = []
    gup, gdown = [], []
    for e in range(3):
        he = cut(h_all, e)
        dye = cut(dy_all, e).astype(F32)
        se = cut(scal_all, e)[:, :, e : e + 1]
        n = he.shape[1]
        hf = he.reshape(S * n, D)
        pre = mm(hf, ups[e])
        val, der = gelu_pair(pre)
        ub = val.astype(BF)
        m = mm(ub, downs[e]).reshape(S, n, D)
        dm = (dye * se).astype(BF).reshape(S * n, D)
        dg = (mm(dm, downs[e], ((1,), (1,))) * der).astype(BF)
        gdown.append(mm(ub, dm, ((0,), (0,))))
        gup.append(mm(hf, dg, ((0,), (0,))))
        dx = mm(dg, ups[e], ((1,), (1,))).reshape(S, n, D)
        y = m * se
        sc = jnp.sum(dye * m, axis=-1)
        pad = [(0, 0), (0, T - n) if e < 2 else (T - n, 0)]
        live = is0[None, :, 0]
        partial_y += jnp.pad(y, pad + [(0, 0)])
        partial_dh += jnp.pad(dx, pad + [(0, 0)])
        score.append(jnp.pad(sc, pad))
    yfull = rs(partial_y)
    dh2 = rs(partial_dh)
    sc = lax.psum_scatter(jnp.stack(score, axis=1), "shard", scatter_dimension=0, tiled=False)
    sm = sc[0][:, None]
    se = jnp.where(is0, sc[1][:, None], sc[2][:, None])

    dc0, dc1 = gate * se, sm
    tot = c0 * dc0 + c1 * dc1
    dcl0, dcl1 = c0 * (dc0 - tot), c1 * (dc1 - tot)
    dgate = c0 * se
    dr0, dr1 = jnp.where(is0, dgate, 0.0), jnp.where(is0, 0.0, dgate)
    tot = r[:, 0:1] * dr0 + r[:, 1:2] * dr1
    drl0, drl1 = r[:, 0:1] * (dr0 - tot), r[:, 1:2] * (dr1 - tot)
    layer_out = (x1 + yfull).astype(BF)
    dh2 = dh2 + drl0 * wr[0] + drl1 * wr[1] + dcl0 * wm[0] + dcl1 * wm[1]
    gw = [jnp.sum(h2 * t, axis=0) for t in (drl0, drl1, dcl0, dcl1)]
    dx1, gg2, gb2 = norm_back(dh2, u2, i2, g2)
    dx1 = dx1 + dys.astype(F32)
    dab = dx1.astype(BF)
    gwo = mm(o, dab, ((0,), (0,)))
    do = mm(dab, wo, ((1,), (1,))).astype(BF).reshape(T, H, HD)
    dp = jnp.einsum("ihd,jhd->hij", do, v, preferred_element_type=F32)
    ds = (p * (dp - jnp.sum(p * dp, axis=-1, keepdims=True))).astype(BF)
    dq = jnp.einsum("hij,jhd->ihd", ds, k, preferred_element_type=F32).astype(BF)
    dq = (dq * BF(0.125)).reshape(T, D)
    dk = jnp.einsum("hij,ihd->jhd", ds, q, preferred_element_type=F32).astype(BF).reshape(T, D)
    dv = jnp.einsum("hij,ihd->jhd", pb, do, preferred_element_type=F32).astype(BF).reshape(T, D)
    dh1 = mm(dq, wq, ((1,), (1,))) + mm(dk, wk, ((1,), (1,))) + mm(dv, wv, ((1,), (1,)))
    ga = jnp.stack([mm(h1b, dq, ((0,), (0,))), mm(h1b, dk, ((0,), (0,))), mm(h1b, dv, ((0,), (0,))), gwo])
    dxn, gg1, gb1 = norm_back(dh1, u1, i1, g1)
    input_grad = (dx1 + dxn).astype(BF)

    layer_out = mm(perm, layer_out, ((0,), (0,))).astype(BF)
    input_grad = mm(perm, input_grad, ((0,), (0,))).astype(BF)

    smalls = lax.psum(jnp.stack([gg1, gb1, gg2, gb2] + gw), BOTH)
    mine = lax.dynamic_slice_in_dim(smalls, lax.axis_index(BOTH) * WR, WR, 1)
    ga = ga.reshape(4, C, S, WR, D).transpose(1, 2, 0, 3, 4)
    ga = lax.psum_scatter(ga.astype(BF), "dp", scatter_dimension=0, tiled=False)
    ga = lax.psum_scatter(ga, "shard", scatter_dimension=0, tiled=False).astype(F32)
    gdown = lax.psum_scatter(jnp.stack(gdown), "dp", scatter_dimension=1, tiled=True)
    gup = jnp.stack(gup).reshape(3, C, S, WR, F).transpose(1, 2, 0, 3, 4)
    gup = lax.psum_scatter(gup, "dp", scatter_dimension=0, tiled=False).astype(BF)
    gup = lax.all_to_all(gup, "shard", 0, 0).astype(F32)
    gup = gup.reshape(S, 3, WR, C, FR).transpose(1, 2, 3, 0, 4).reshape(3, WR, FF)

    counts = lax.psum(jnp.stack([n0, T - n0]), BOTH)
    load_new = 0.9 * load_avg + 0.1 * counts.astype(F32) * E / (T * C * S)
    return (
        layer_out, input_grad, mine[0], mine[1], ga[0], ga[1], ga[2], ga[3], mine[2], mine[3],
        gup[0], gdown[0], jnp.stack([mine[4], mine[5]], axis=1), jnp.stack([mine[6], mine[7]], axis=1),
        gup[1:], gdown[1:], counts, load_new,
    )


def body(
    hidden_in, doc_ids, expert_ids, slot_ids, out_grad, ln1_gain, ln1_bias, w_query, w_key, w_value,
    w_out, ln2_gain, ln2_bias, w_up, w_down, w_router, w_mix, expert_up, expert_down, load_avg,
):
    T, D = hidden_in.shape
    H, HD = HEADS, D // HEADS
    S = lax.axis_size("shard")
    C = lax.axis_size("dp")
    WR = w_query.shape[0]
    FF = w_up.shape[1]
    FR = w_down.shape[0]
    F = FR * C
    E = expert_up.shape[0]
    ndev = C * S
    dev = lax.axis_index(BOTH)
    small = jnp.stack(
        [ln1_gain, ln1_bias, ln2_gain, ln2_bias, w_router[:, 0], w_router[:, 1], w_mix[:, 0], w_mix[:, 1]]
    ).astype(F32)
    group = 128 // WR
    slot_of = lax.broadcasted_iota(jnp.int32, (8, 128), 1) // WR
    small = jnp.where(slot_of == dev % group, jnp.tile(small, (1, group)), 0.0)
    (
        stat, u1, u2, x1, dys, q, k, v, p, o, small, count, wa, y_parts, dh2, sc, gup, gdn0, gdn12,
    ) = front_call(
        hidden_in, out_grad, doc_ids, expert_ids.reshape(1, T), slot_ids.reshape(1, T), small,
        (w_query, w_key, w_value, w_out), w_up, expert_up, w_down, expert_down, S,
    )
    y_parts = y_parts.reshape(S, T, D)
    layer_out, input_grad, gwq, gwk, gwv, gwo, smalls, gup = back_call(
        dh2, y_parts, sc, small, stat, u1, u2, x1, dys, q, k, v, p, o,
        expert_ids.reshape(1, T), slot_ids.reshape(1, T), wa.reshape(4, D, D), gup, S,
    )
    lo, ig, gq, gk, gv, go, gu, gd, geu, ged, gr, gm, gn = finish_call(
        layer_out, input_grad, gwq, gwk, gwv, gwo, smalls, gup, gdn0, gdn12
    )
    tokens0 = count[0, 0].astype(jnp.int32)
    counts = jnp.stack([tokens0, T * ndev - tokens0])
    load_new = 0.9 * load_avg + 0.1 * counts.astype(F32) * E / (T * ndev)
    return (
        lo, ig, gn[:, 0], gn[:, 1], gq, gk, gv, go, gn[:, 2], gn[:, 3],
        gu, gd, gr, gm, geu, ged, counts, load_new,
    )


def pick(*args):
    S, C, WR, FR = lax.axis_size("shard"), lax.axis_size("dp"), args[7].shape[0], args[14].shape[0]
    fast = C == 2 and S // 4 == 4 and S % 4 == 0 and WR % 16 == 0 and 128 % WR == 0 and FR % 128 == 0
    return (body if fast else body_plain)(*args)


def solution(mesh):
    row, vec = P(BOTH, None), P(BOTH)
    mid = P(None, BOTH, None)
    return jax.shard_map(
        pick,
        mesh=mesh,
        in_specs=(row, row, vec, vec, row, vec, vec, row, row, row, row, vec, vec, row, row, row, row, mid, mid, P()),
        out_specs=(row, row, vec, vec, row, row, row, row, vec, vec, row, row, row, row, mid, mid, P(), P()),
        check_vma=False,
    )
```

```python
import jax
import jax.numpy as jnp
from jax import lax
from jax.experimental import pallas as pl
from jax.experimental.pallas import tpu as pltpu
from jax.sharding import PartitionSpec as P

HEADS = 16
CAP = 74
BF = jnp.bfloat16
F32 = jnp.float32
BOTH = ("dp", "shard")
MESH = pl.DeviceIdType.MESH


def mm(a, b, dims=((1,), (0,))):
    return lax.dot_general(a, b, (dims, ((), ())), preferred_element_type=F32)


def layer_norm(values, gain, bias):
    centre = values - jnp.mean(values, axis=-1, keepdims=True)
    scale_inv = lax.rsqrt(jnp.mean(centre * centre, axis=-1, keepdims=True) + 1e-05)
    normed = centre * scale_inv
    return (normed * gain + bias, normed, scale_inv)


def norm_back(grad_out, normed, scale_inv, gain):
    grad_normed = grad_out * gain
    inner = grad_normed - jnp.mean(grad_normed, axis=-1, keepdims=True)
    inner = inner - normed * jnp.mean(grad_normed * normed, axis=-1, keepdims=True)
    return (scale_inv * inner, jnp.sum(grad_out * normed, axis=0), jnp.sum(grad_out, axis=0))


def gelu_pair(t):
    inner = 0.7978845608 * (t + 0.044715 * t * t * t)
    th = jnp.tanh(inner)
    val = 0.5 * t * (1.0 + th)
    der = 0.5 * (1.0 + th) + 0.5 * t * (1.0 - th * th) * 0.7978845608 * (1.0 + 3.0 * 0.044715 * t * t)
    return val, der


def ag(block):
    return lax.all_gather(block, "shard", axis=0, tiled=False)


def rs(parts):
    return lax.psum_scatter(parts.astype(BF), "shard", scatter_dimension=0, tiled=False).astype(F32)


def place_of():
    me = lax.axis_index("shard")
    core = lax.axis_index("dp")
    z, p = me // 4, me % 4
    xq = p + 1 - 2 * (p % 2)
    yq = p + 2 - 4 * (p // 2)
    return me, core, z, p, xq, yq, 3 - p


def greet(shards, core):
    bar = pltpu.get_barrier_semaphore()
    me = lax.axis_index("shard")

    @pl.loop(1, shards)
    def _(i):
        pl.semaphore_signal(bar, inc=1, device_id=(core, (me + i) % shards), device_id_type=MESH)

    pl.semaphore_signal(bar, inc=1, device_id=(1 - core, me), device_id_type=MESH)
    pl.semaphore_wait(bar, shards)


def remote(src, dst, send, recv, dev):
    return pltpu.make_async_remote_copy(
        src_ref=src, dst_ref=dst, send_sem=send, recv_sem=recv, device_id=dev, device_id_type=MESH
    )


def rows_loop(count, step, fn):
    @pl.loop(0, count // step)
    def _(i):
        fn(pl.multiple_of(i * step, step))


def level_order(z, L):
    upper = z // (L // 2)
    y = z + upper * (L - 1 - 2 * z)

    def lev_of(k):
        low = k - 1 + (k - 1 - y + L) // L
        lev = low + upper * (L - 1 - 2 * low)
        first = 1 - (k + L - 1) // L
        return lev + first * (z - lev)

    return lev_of


def tree_gather(at, own, ss, rs, dev, levels):
    core, z, p, xq, yq, dq = dev
    xn, yn = z * 4 + xq, z * 4 + yq
    me = z * 4 + p
    pair = me + 4 - 8 * (z % 2)
    lev_of, L = levels

    def copy(kind, slot, src, idx, to):
        return remote(src, at(idx), ss.at[kind, slot], rs.at[kind, slot], (core, to))

    def up_line(src, send):
        return remote(src, at(me), send, rs.at[0, z], (core, me + 4))

    def down_line(src, send):
        return remote(src, at(me), send, rs.at[0, z], (core, me - 4))

    def onward(k):
        lev = lev_of(k)
        step = 1 - 2 * ((lev - z + L) // L)
        to = z + step
        idx = lev * 4 + p
        ok = (to >= 0) & (to < L)
        return ok, remote(at(idx), at(idx), ss.at[0, lev], rs.at[0, lev], (core, me + 4 * step))

    class Stages:
        @staticmethod
        def start():
            @pl.when(z < L - 1)
            def _():
                up_line(own, ss.at[0, z]).start()

            @pl.when(z > 0)
            def _():
                down_line(own, ss.at[4, 0]).start()

            copy(1, z, own, me, xn).start()
            copy(2, z, own, me, yn).start()

        @staticmethod
        def a(k):
            lev = lev_of(k)
            idx = lev * 4 + p
            copy(0, lev, own, idx, xn).wait_recv()
            ok, on = onward(k)

            @pl.when(ok)
            def _():
                on.start()

            copy(1, lev, at(idx), idx, xn).start()
            copy(2, lev, at(idx), idx, yn).start()

        @staticmethod
        def b(k):
            lev = lev_of(k)
            odd = lev // 2 % 2
            copy(1, lev, own, lev * 4 + xq, xn).wait_recv()
            copy(2, lev, own, lev * 4 + yq, yn).wait_recv()
            idx = lev * 4 + xq + odd * (yq - xq)

            @pl.when((lev + z) % 2 == 0)
            def _():
                copy(3, lev, at(idx), idx, yn + odd * (xn - yn)).start()

        @staticmethod
        def c(k):
            lev = lev_of(k)
            idx = lev * 4 + dq

            @pl.when((lev + z) % 2 == 0)
            def _():
                copy(3, lev, own, idx, xn).wait_recv()
                copy(5, lev, at(idx), idx, pair).start()

        @staticmethod
        def d(k):
            lev = lev_of(k)

            @pl.when((lev + z) % 2 == 1)
            def _():
                copy(5, lev, own, lev * 4 + dq, pair).wait_recv()

        @staticmethod
        def done(k):
            lev = lev_of(k)
            for kind in range(1, 3):
                copy(kind, lev, own, me, xn).wait_send()

            @pl.when((lev + z) % 2 == 0)
            def _():
                for kind in (3, 5):
                    copy(kind, lev, own, me, xn).wait_send()

            @pl.when(k > 0)
            def _():
                ok, on = onward(k)
                pl.when(ok)(on.wait_send)

            @pl.when(k == 0)
            def _():
                pl.when(z < L - 1)(lambda: up_line(own, ss.at[0, z]).wait_send())
                pl.when(z > 0)(lambda: down_line(own, ss.at[4, 0]).wait_send())

        @staticmethod
        def finish():
            @pl.loop(0, L)
            def _(k):
                Stages.done(k)

    return Stages


def together(*machines):
    class Stages:
        pass

    for name in vars(machines[0]):
        if not name.startswith("_"):
            calls = [getattr(mach, name) for mach in machines]
            setattr(Stages, name, staticmethod(lambda *a, calls=calls: [call(*a) for call in calls] and None))
    return Stages


def tree_scatter(part, ra, rbx, rby, rd, final, ss, rs, dev, levels, rz=None):
    core, z, p, xq, yq, dq = dev
    xn, yn = z * 4 + xq, z * 4 + yq
    pair = z * 4 + p + 4 - 8 * (z % 2)
    lev_of, L = levels
    R = part.shape[1]

    def copy(kind, lev, src, dst, to):
        return remote(src, dst, ss.at[kind, lev], rs.at[kind, lev], (core, to))

    def sides(lev):
        copy(1, lev, part.at[lev * 4 + xq], rbx.at[lev], xn).start()
        copy(2, lev, part.at[lev * 4 + yq], rby.at[lev], yn).start()

    class Stages:
        @staticmethod
        def share(k):
            lev = lev_of(k)

            @pl.when((lev + z) % 2 == 1)
            def _():
                copy(4, lev, part.at[lev * 4 + dq], rz.at[lev // 2], pair).start()

        @staticmethod
        def a(k):
            lev = lev_of(k)
            odd = k % 2 if rz is None else lev // 2 % 2
            diag = lev * 4 + dq

            def send():
                copy(0, lev, part.at[diag], ra.at[lev], yn + odd * (xn - yn)).start()

            def join():
                copy(4, lev, rz.at[lev // 2], rz.at[lev // 2], pair).wait_recv()

                def add(r):
                    t = pl.ds(r, 32)
                    part[diag, t, :] = (part[diag, t, :].astype(F32) + rz[lev // 2, t, :].astype(F32)).astype(BF)

                rows_loop(R, 32, add)
                send()

            if rz is None:
                send()
            else:
                pl.when((lev + z) % 2 == 0)(join)

        @staticmethod
        def b(k):
            lev = lev_of(k)
            odd = k % 2 if rz is None else lev // 2 % 2
            via = lev * 4 + xq + odd * (yq - xq)
            copy(0, lev, ra.at[lev], ra.at[lev], xn).wait_recv()

            def add(r):
                t = pl.ds(r, 32)
                part[via, t, :] = (part[via, t, :].astype(F32) + ra[lev, t, :].astype(F32)).astype(BF)

            rows_loop(R, 32, add)
            sides(lev)

        @staticmethod
        def b0(k):
            pl.when((lev_of(k) + z) % 2 == 1)(lambda: sides(lev_of(k)))

        @staticmethod
        def b1(k):
            pl.when((lev_of(k) + z) % 2 == 0)(lambda: Stages.b(k))

        @staticmethod
        def c0(k):
            pl.when((lev_of(k) + z) % 2 == 1)(lambda: Stages.c(k))

        @staticmethod
        def c1(k):
            pl.when((lev_of(k) + z) % 2 == 0)(lambda: Stages.c(k))

        @staticmethod
        def c(k):
            lev = lev_of(k)
            own = lev * 4 + p
            copy(1, lev, rbx.at[lev], rbx.at[lev], xn).wait_recv()
            copy(2, lev, rby.at[lev], rby.at[lev], yn).wait_recv()

            def add(r, last):
                t = pl.ds(r, 32)
                tot = part[own, t, :].astype(F32) + rbx[lev, t, :].astype(F32) + rby[lev, t, :].astype(F32)
                if last:
                    final[t, :] = tot
                else:
                    part[own, t, :] = tot.astype(BF)

            def close():
                rows_loop(R, 32, lambda r: add(r, True))

            def send():
                rows_loop(R, 32, lambda r: add(r, False))
                remote(part.at[own], rd.at[z], ss.at[3, lev], rs.at[3, z], (core, lev * 4 + p)).start()

            if isinstance(k, int):
                (send if k else close)()
            else:
                pl.when(k == 0)(close)
                pl.when(k > 0)(send)

        @staticmethod
        def d(k):
            lev = lev_of(k)
            copy(3, lev, rd.at[lev], rd.at[lev], xn).wait_recv()

            def add(r):
                t = pl.ds(r, 32)
                final[t, :] = final[t, :] + rd[lev, t, :].astype(F32)

            rows_loop(R, 32, add)

        @staticmethod
        def finish():
            @pl.loop(0, L)
            def _(k):
                lev = lev_of(k)
                for kind in (1, 2):
                    copy(kind, lev, ra.at[0], ra.at[0], xn).wait_send()

                if rz is None:
                    copy(0, lev, ra.at[0], ra.at[0], xn).wait_send()
                else:
                    kind = (lev + z) % 2 * 4
                    copy(kind, lev, ra.at[0], ra.at[0], xn).wait_send()

                @pl.when(k > 0)
                def _():
                    copy(3, lev, ra.at[0], ra.at[0], xn).wait_send()

    return Stages


def sort_matrix(ids_e, ids_s, T):
    zero = ids_e == 0
    n0 = jnp.sum(jnp.where(zero, 1.0, 0.0), axis=1, keepdims=True)
    slot = ids_s.astype(F32)
    pos = jnp.where(zero, slot, slot + n0)
    sub = lax.broadcasted_iota(jnp.int32, (T, T), 0).astype(F32)
    return jnp.where(sub == pos, 1.0, 0.0), n0


def front_kernel(
    x_ref, dyin_ref, doc_ref, e_ref, s_ref, small_ref, wq_ref, wk_ref, wv_ref, wo_ref,
    wu_ref, eu_ref, wd_ref, ed_ref,
    stat_out, u1_out, u2_out, x1_out, dys_out, q_out, k_out, v_out, p_out, o_out,
    small_out, count_out, w_out, y_out, dh_out, sc_out, gup_out, gdn0_out, gdn12_out,
    wbuf, up_ref, dn_ref, smallbuf, h1b, bias, tmp, xs, dy_all, hall, dxp, scall, psc, screcv, wcol, scol, ra, rbx, rby, rd,
    pre, dyw, uw, dg, gdn, gup, sib_dn, sib_up,
    ag_s, ag_r, rs_s, rs_r, sib_s, sib_r, one_s, one_r, sm_s, sm_r, sn_s, sn_r, loc,
):
    T, D = x_ref.shape
    WR = wq_ref.shape[0]
    FR = wd_ref.shape[0]
    N = wbuf.shape[1]
    S = N // 2
    L = S // 4
    me, core, z, p, xq, yq, dq = place_of()
    xn = z * 4 + xq
    my = core * S + me
    sib = (1 - core, me)
    greet(S, core)
    lev_of = level_order(z, L)

    dev, levels = (core, z, p, xq, yq, dq), (lev_of, L)

    def split(at, j):
        return tree_gather(at, at(me), ag_s.at[j], ag_r.at[j], dev, levels)

    def rows_of(ref, j):
        return lambda i: ref.at[i, pl.ds(j * (T // 2), T // 2)]

    wg = together(*(split(lambda i, j=j: wbuf.at[pl.ds(2 * j, 2), core * S + i], j) for j in range(2)))
    dyg = together(*(split(rows_of(dy_all, j), 2 + j) for j in range(2)))
    hg = together(*(split(rows_of(hall, j), 4 + j) for j in range(2)))

    for i, w in enumerate((wq_ref, wk_ref, wv_ref, wo_ref)):
        wbuf[i, my] = w[...]
    wg.start()

    perm, n0 = sort_matrix(e_ref[...], s_ref[...], T)
    smallbuf[my, 0:8, :] = small_ref[...]
    lane8 = lax.broadcasted_iota(jnp.int32, (8, 128), 1)
    smallbuf[my, 8:16, :] = jnp.where(lane8 == 0, jnp.broadcast_to(n0, (8, 128)), 0.0)

    @pl.loop(1, S)
    def _(i):
        remote(smallbuf.at[my], smallbuf.at[my], sm_s.at[0, i], sm_r.at[0], (core, (me + i) % S)).start()

    F = 2 * FR
    mine_f = pl.ds(pl.multiple_of(core * FR, FR), FR)
    other_f = pl.ds(pl.multiple_of((1 - core) * FR, FR), FR)
    dn_copies = (
        remote(wd_ref, dn_ref.at[0, mine_f], sib_s.at[1, 0], sib_r.at[1, 0], sib),
        remote(ed_ref, dn_ref.at[pl.ds(1, 2), mine_f], sib_s.at[1, 1], sib_r.at[1, 1], sib),
    )
    for c in dn_copies:
        c.start()
    dn_ref[0, mine_f, :] = wd_ref[...]
    for e in range(2):
        dn_ref[1 + e, mine_f, :] = ed_ref[e]
    permb = perm.astype(BF)
    xs[...] = mm(permb, x_ref[...])
    dys_out[...] = mm(permb, dyin_ref[...]).astype(BF)
    dy_all[me] = dys_out[...]
    gdn[...] = jnp.zeros_like(gdn)
    gup[...] = jnp.zeros_like(gup)

    docs = (doc_ref[...] == lax.broadcasted_iota(jnp.int32, (16, T), 0)).astype(F32).astype(BF)
    docs = mm(docs, permb, ((1,), (1,))).astype(BF)
    same = mm(docs, docs, ((0,), (0,)))
    place = lax.broadcasted_iota(jnp.int32, (T, T), 1).astype(F32)
    ord_col = jnp.sum(perm * place, axis=1, keepdims=True)
    ord_row = mm(place[0:16, :].astype(BF), permb, ((1,), (1,)))[0:1, :]
    bias[...] = jnp.where((same > 0.5) & (ord_row <= ord_col), 0.0, -1e30)

    lane = lax.broadcasted_iota(jnp.int32, (64, 128), 1)

    def norm1(r):
        t = pl.ds(r, 64)
        v = xs[t, :]
        cen = v - jnp.mean(v, axis=1, keepdims=True)
        inv = lax.rsqrt(jnp.mean(cen * cen, axis=1, keepdims=True) + 1e-05)
        u1_out[t, :] = cen * inv
        stat_out[t, :] = jnp.where(lane == 8, inv, 0.0)

    rows_loop(T, 64, norm1)

    wg.a(1)
    wg.b(0)
    wg.a(2)
    wg.b(1)
    wg.a(3)
    wg.c(0)

    group = 128 // WR
    remote(smallbuf.at[pl.ds(0, S - 1)], smallbuf.at[pl.ds(0, S - 1)], sm_s.at[0, 0], sm_r.at[0], (core, xn)).wait_recv()
    mine_small = smallbuf.at[pl.ds(core * S, S)]
    c_small = remote(mine_small, mine_small, sib_s.at[1, 2], sib_r.at[1, 2], sib)
    c_small.start()

    def up_copy(e, h, i):
        to = (me + i) % S
        src = wu_ref if e == 0 else eu_ref.at[e - 1]
        return remote(
            src.at[:, pl.ds(pl.multiple_of((h * S + to) * FR, FR), FR)],
            up_ref.at[pl.ds(pl.multiple_of(my * WR, WR), WR), pl.ds(e * F + h * FR, FR)],
            sm_s.at[1, i], sm_r.at[1], (core, to),
        )

    @pl.loop(1, S)
    def _(i):
        for e in range(3):
            for h in range(2):
                up_copy(e, h, i).start()

    for e in range(3):
        for h in range(2):
            src = wu_ref if e == 0 else eu_ref.at[e - 1]
            block = src[:, pl.ds(pl.multiple_of((h * S + me) * FR, FR), FR)]
            up_ref[pl.ds(pl.multiple_of(my * WR, WR), WR), e * F + h * FR : e * F + (h + 1) * FR] = block

    def w_sib(lev, who):
        b = wbuf.at[:, pl.ds(who * S + lev * 4, 4)]
        return remote(b, b, sib_s.at[0, lev], sib_r.at[0, lev], sib)

    def pass_on(k):
        wg.d(k)
        w_sib(lev_of(k), core).start()

    pass_on(0)
    wg.b(2)
    wg.c(1)
    wg.b(3)
    dyg.start()
    pass_on(1)
    wg.c(2)
    pass_on(2)
    wg.c(3)
    pass_on(3)
    dyg.a(1)
    dyg.b(0)
    c_small.wait_recv()
    for g in range(D // 128):
        part = smallbuf[g * group, 0:8, :]
        for j in range(1, group):
            part = part + smallbuf[g * group + j, 0:8, :]
        small_out[:, g * 128 : (g + 1) * 128] = part
    cnt = smallbuf[0, 8:16, :]
    for i in range(1, N):
        cnt = cnt + smallbuf[i, 8:16, :]
    count_out[...] = cnt

    def norm1b(r):
        t = pl.ds(r, 64)
        h1b[t, :] = (u1_out[t, :] * small_out[0:1, :] + small_out[1:2, :]).astype(BF)

    rows_loop(T, 64, norm1b)
    dyg.a(2)
    dyg.b(1)
    for k in range(L):
        w_sib(lev_of(k), 1 - core).wait_recv()
    w_save = pltpu.make_async_copy(wbuf, w_out, loc.at[L])
    w_save.start()

    def full(i):
        return wbuf[i].reshape(D, D)

    tmp[...] = mm(h1b[...], full(0))
    q_out[...] = (tmp[...] * 0.125).astype(BF)
    dyg.a(3)
    dyg.c(0)
    tmp[...] = mm(h1b[...], full(1))
    k_out[...] = tmp[...].astype(BF)
    tmp[...] = mm(h1b[...], full(2))
    v_out[...] = tmp[...].astype(BF)
    dyg.b(2)
    dyg.c(1)

    low = lax.broadcasted_iota(jnp.int32, (T, 128), 1) < 64
    lowb = low.astype(F32).astype(BF)
    highb = (1.0 - low.astype(F32)).astype(BF)

    def heads(j):
        ln = pl.ds(pl.multiple_of(j * 128, 128), 128)
        qp = q_out[:, ln]
        q2 = jnp.concatenate([qp * lowb, qp * highb], axis=0)
        s = mm(q2, k_out[:, ln], ((1,), (1,)))
        s = s + jnp.concatenate([bias[...], bias[...]], axis=0)
        ex = jnp.exp(s - jnp.max(s, axis=1, keepdims=True))
        pr = ex / jnp.sum(ex, axis=1, keepdims=True)
        p_out[j] = pr
        o2 = mm(pr.astype(BF), v_out[:, ln])
        o_out[:, ln] = jnp.where(low, o2[0:T], o2[T:]).astype(BF)

    @pl.loop(0, D // 128)
    def _(j):
        heads(j)

    dyg.b(3)
    tmp[...] = mm(o_out[...], full(3))

    def norm2(r):
        t = pl.ds(r, 64)
        v = xs[t, :] + tmp[t, :]
        x1_out[t, :] = v
        cen = v - jnp.mean(v, axis=1, keepdims=True)
        inv = lax.rsqrt(jnp.mean(cen * cen, axis=1, keepdims=True) + 1e-05)
        u = cen * inv
        u2_out[t, :] = u
        h2 = u * small_out[2:3, :] + small_out[3:4, :]
        hall[me, t, :] = h2.astype(BF)
        lg = [jnp.sum(h2 * small_out[i : i + 1, :], axis=1, keepdims=True) for i in range(4, 8)]

        def soft(a, b):
            mx = jnp.maximum(a, b)
            ea, eb = jnp.exp(a - mx), jnp.exp(b - mx)
            return ea / (ea + eb), eb / (ea + eb)

        r0, r1 = soft(lg[0], lg[1])
        k0, k1 = soft(lg[2], lg[3])
        row = (lax.broadcasted_iota(jnp.int32, (64, 1), 0) + r).astype(F32)
        is0 = row < n0
        gate = jnp.where(is0, r0, r1)
        we = k0 * gate
        cols = (k1, jnp.where(is0, we, 0.0), jnp.where(is0, 0.0, we), k0, gate, r0, r1)
        st = stat_out[t, :] + jnp.where(lane == 9, inv, 0.0)
        for i, col in enumerate(cols):
            st = st + jnp.where(lane == i, col, 0.0)
        stat_out[t, :] = st

    dyg.c(2)
    rows_loop(T, 64, norm2)
    scall[me] = stat_out[...].T[0:8, :]
    hg.start()

    @pl.loop(1, S)
    def _(i):
        remote(scall.at[me], scall.at[me], sn_s.at[0, i], sn_r.at[0], (core, (me + i) % S)).start()

    dyg.c(3)
    got = up_ref.at[pl.ds(0, (S - 1) * WR), :]
    remote(got, got, sm_s.at[1, 0], sm_r.at[1], (core, xn)).wait_recv()
    mine_up = up_ref.at[pl.ds(pl.multiple_of(core * S * WR, S * WR), S * WR), :]
    c_slice = remote(mine_up, mine_up, sib_s.at[1, 3], sib_r.at[1, 3], sib)
    c_slice.start()
    end = (z == 0) | (z == L - 1)
    hg.a(1)
    hg.b(0)
    hg.a(2)
    pl.when(jnp.logical_not(end))(lambda: hg.a(3))

    w_save.wait()
    wg.finish()

    @pl.loop(0, L)
    def _(k):
        w_sib(k, core).wait_send()

    remote(scall.at[pl.ds(0, S - 1)], scall.at[pl.ds(0, S - 1)], sn_s.at[0, 0], sn_r.at[0], (core, xn)).wait_recv()
    c_slice.wait()
    for c in dn_copies:
        c.wait()
    c_small.wait_send()
    hg.c(0)
    rgs = []
    for i in range(2):
        t = pl.ds(i * (T // 2), T // 2)
        bufs = [b.at[:, t, :] for b in (dxp, ra, rbx, rby, rd)]
        rgs.append(tree_scatter(*bufs, dh_out.at[t], rs_s.at[i], rs_r.at[i], dev, levels))
    LO = 80
    HI = T - LO
    per = T // WR
    fold = N // (4 * per)

    def y_copy(lev):
        src = wbuf.at[lev // fold, pl.ds(lev % fold * (4 * per), 4 * per)]
        return pltpu.make_async_copy(src, y_out.at[pl.ds(lev * (4 * per), 4 * per)], loc.at[lev])

    def compute(lev, between):
        base = lev * 4
        level = pl.ds(base, 4)
        for q in range(4):
            full = jnp.concatenate([scall[base + q], jnp.zeros((120, 128), F32)], axis=0)
            wcol[q] = full.T
        pre[...] = mm(hall[level].reshape(4 * T, D), up_ref[...])
        between(0)
        dyw[...] = mm(dy_all[level].reshape(4 * T, D), dn_ref[...].reshape(3 * F, D), ((1,), (1,)))
        lane = lax.broadcasted_iota(jnp.int32, (T, 128), 1)

        @pl.loop(0, 4)
        def _(q):
            t = pl.ds(pl.multiple_of(q * T, T), T)
            score = jnp.zeros((T, 128), F32)
            for e in range(3):
                cols = slice(e * F, (e + 1) * F)
                val, der = gelu_pair(pre[t, cols])
                low = val.astype(BF).astype(F32)
                back = dyw[t, cols]
                w = wcol[q][:, e : e + 1]
                score = score + jnp.where(lane == e, jnp.sum(low * back, axis=1, keepdims=True), 0.0)
                uw[t, cols] = (low * w).astype(BF)
                dg[t, cols] = (back * w * der).astype(BF)
            psc[base + q] = score.T[0:8, :]

        between(1)
        dxp[level] = mm(dg[...], up_ref[...], ((1,), (1,))).astype(BF).reshape(4, T, D)
        y = mm(uw[...], dn_ref[...].reshape(3 * F, D)).astype(BF)
        wbuf[lev // fold, pl.ds(lev % fold * (4 * per), 4 * per)] = y.reshape(4 * per, WR, D)
        y_copy(lev).start()
        between(2)

    def weight_grads(lev):
        for e in range(3):
            n = LO if e else T
            off = HI if e == 2 else 0
            level = pl.ds(lev * 4, 4)

            def some(a):
                a = a[:, e * F : (e + 1) * F]
                return a.reshape(4, T, F)[:, off : off + n].reshape(4 * n, F)

            hm = hall[level, off : off + n, :].reshape(4 * n, D)
            dyb = dy_all[level, off : off + n, :].reshape(4 * n, D)
            gdn[e] = gdn[e] + mm(some(uw), dyb, ((0,), (0,)))
            gup[e] = gup[e] + mm(some(dg), hm, ((0,), (0,)))

    def far_a(i):
        pl.when(end)(lambda: hg.a(i))

    @pl.loop(0, L)
    def _(k):
        @pl.when(k > 0)
        def _():
            hg.d(k)
            dyg.d(k)

        def between(e):
            @pl.when(k == 0)
            def _():
                for call, i in (((far_a, 3), (hg.b, 1)), ((hg.c, 1), (hg.b, 2)), ())[e]:
                    call(i)

            @pl.when(k == 1)
            def _():
                for call, i in (((hg.c, 2), (hg.b, 3)), ((hg.c, 3),), ())[e]:
                    call(i)

            if e == 1:

                @pl.when(k > 0)
                def _():
                    for g in rgs:
                        g.b(k - 1)

        compute(lev_of(k), between)
        for g in rgs:
            g.a(k)

        @pl.when(k > 0)
        def _():
            for g in rgs:
                g.c(k - 1)

        weight_grads(lev_of(k))

    half = D // 2
    other = pl.multiple_of((1 - core) * half, half)
    mine_d = pl.multiple_of(core * half, half)
    c_up = remote(gup.at[:, :, pl.ds(other, half)], sib_up, one_s.at[0], one_r.at[0], sib)
    c_dn = remote(gdn.at[:, other_f, :], sib_dn, one_s.at[1], one_r.at[1], sib)
    c_up.start()
    c_dn.start()

    @pl.loop(1, S)
    def _(i):
        to = (me + i) % S
        remote(psc.at[to], screcv.at[i], sn_s.at[1, i], sn_r.at[1], (core, to)).start()

    for g in rgs:
        g.b(L - 1)
    c_up.wait_recv()
    for e in range(3):
        tot = gup[e, :, pl.ds(mine_d, half)] + sib_up[e]
        gup_out[e] = tot.T.astype(BF)
        if e == 0:
            for g in rgs:
                g.c(L - 1)
    screcv[0] = psc[me]
    c_dn.wait_recv()
    gdn0_out[...] = gdn[0, mine_f, :] + sib_dn[0]
    for e in range(1, 3):
        gdn12_out[e - 1] = gdn[e, mine_f, :] + sib_dn[e]
    for k in range(1, L):
        for g in rgs:
            g.d(k)
    remote(screcv.at[pl.ds(1, S - 1)], screcv.at[pl.ds(1, S - 1)], sn_s.at[1, 0], sn_r.at[1], (core, xn)).wait_recv()
    sc_out[...] = jnp.sum(screcv[...], axis=0)

    for i in range(L):
        y_copy(i).wait()
    c_up.wait_send()
    c_dn.wait_send()
    hg.finish()
    dyg.finish()
    for g in rgs:
        g.finish()

    @pl.loop(1, S)
    def _(i):
        remote(scall.at[me], scall.at[0], sn_s.at[0, i], sn_r.at[0], (core, xn)).wait_send()
        remote(psc.at[0], screcv.at[0], sn_s.at[1, i], sn_r.at[1], (core, xn)).wait_send()
        remote(smallbuf.at[my], smallbuf.at[my], sm_s.at[0, i], sm_r.at[0], (core, xn)).wait_send()
        for e in range(3):
            for h in range(2):
                up_copy(e, h, i).wait_send()


def front_call(x, dy, docs, es, ss, small, ws, wu, eu, wd, ed, S):
    T, D = x.shape
    WR, FR = ws[0].shape[0], wd.shape[0]
    L, N, F = S // 4, 2 * S, 2 * FR
    vm = pl.BlockSpec(memory_space=pltpu.VMEM)
    hb = pl.BlockSpec(memory_space=pl.ANY)
    V = pltpu.VMEM
    dma = pltpu.SemaphoreType.DMA
    sds = jax.ShapeDtypeStruct
    row = sds((T, D), BF)
    rowf = sds((T, D), F32)
    tokens, blocks, side = V((S, T, D), BF), V((L, T, D), BF), V((S, 8, 128), F32)
    return pl.pallas_call(
        front_kernel,
        out_shape=(
            sds((T, 128), F32), rowf, rowf, rowf, row, row, row, row,
            sds((D // 128, 2 * T, T), F32), row, sds((8, D), F32), sds((8, 128), F32),
            sds((4, N, WR, D), BF), sds((S * T // WR, WR, D), BF), rowf, sds((8, 128), F32), sds((3, D // 2, F), BF),
            sds((FR, D), F32), sds((2, FR, D), F32),
        ),
        in_specs=[vm] * 14,
        out_specs=(vm,) * 12 + (hb, hb) + (vm,) * 5,
        scratch_shapes=[
            V((4, N, WR, D), BF), V((D, 3 * F), BF), V((3, F, D), BF), V((N, 16, 128), F32), V((T, D), BF), V((T, T), F32),
            V((T, D), F32), V((T, D), F32), tokens, tokens, tokens, side, side, side, V((4, T, 128), F32), V((4, T, 128), F32), blocks, blocks, blocks, blocks,
            V((4 * T, 3 * F), F32), V((4 * T, 3 * F), F32), V((4 * T, 3 * F), BF), V((4 * T, 3 * F), BF),
            V((3, F, D), F32), V((3, F, D), F32), V((3, FR, D), F32), V((3, F, D // 2), F32),
            dma((6, 6, L)), dma((6, 6, L)), dma((2, 4, L)), dma((2, 4, L)), dma((2, max(L, 4))), dma((2, max(L, 4))),
            dma((2,)), dma((2,)), dma((2, S)), dma((2,)), dma((2, S)), dma((2,)), dma((L + 1,)),
        ],
        compiler_params=pltpu.CompilerParams(collective_id=1, has_side_effects=True, vmem_limit_bytes=66000000),
        cost_estimate=pl.CostEstimate(flops=17 * 10**9, bytes_accessed=40 * 2**20, transcendentals=2**20),
        name="front",
    )(x, dy, docs, es, ss, small, *ws, wu, eu, wd, ed)


def back_kernel(
    dh_ref, sc_ref, small_ref, stat_ref, u1_ref, u2_ref, x1_ref, dys_ref,
    q_ref, k_ref, v_ref, p_ref, o_ref, e_ref, s_ref, y_hbm, w_hbm, gup_ref,
    lo_out, ig_out, gq_out, gk_out, gv_out, go_out, smalls_out, gup_out,
    wbuf, perm, accs, dx1, dab, do, dq, dk, dv, h1b, dh1, tmpb, keep, send, recv,
    part0, ra0, rbx0, rby0, rd0, rz0, partv, rav, rbxv, rbyv, rdv, rzv, partk, rak, rbxk, rbyk, rdk, rzk,
    partq, raq, rbxq, rbyq, rdq, rzq, ypart, ray, rbxy, rbyy, rdy, rzy, ysum, lsort, smine, ssib, srecv,
    rs_s, rs_r, sib_s, sib_r, sm_s, sm_r, loc,
):
    T, D = dh_ref.shape
    S, WR = part0.shape[0], part0.shape[1]
    L = S // 4
    half = D // 2
    me, core, z, p, xq, yq, dgq = place_of()
    xn = z * 4 + xq
    sib = (1 - core, me)
    lev_of = level_order(z, L)
    far = list(reversed(range(L)))
    fetch = []
    for k in far:
        some = pl.ds(lev_of(k) * 4, 4)
        fetch.append(pltpu.make_async_copy(y_hbm.at[some], ypart.at[some], loc.at[4 + k]))
    for c in fetch:
        c.start()
    greet(S, core)

    dev, levels = (core, z, p, xq, yq, dgq), (lev_of, L)
    g0 = tree_scatter(part0, ra0, rbx0, rby0, rd0, go_out, rs_s.at[0], rs_r.at[0], dev, levels, rz0)
    gv = tree_scatter(partv, rav, rbxv, rbyv, rdv, gv_out, rs_s.at[1], rs_r.at[1], dev, levels, rzv)
    gk = tree_scatter(partk, rak, rbxk, rbyk, rdk, gk_out, rs_s.at[3], rs_r.at[3], dev, levels, rzk)
    gq = tree_scatter(partq, raq, rbxq, rbyq, rdq, gq_out, rs_s.at[4], rs_r.at[4], dev, levels, rzq)
    gy = tree_scatter(ypart, ray, rbxy, rbyy, rdy, ysum, rs_s.at[2], rs_r.at[2], dev, levels, rzy)
    far = list(reversed(range(L)))
    loads = [pltpu.make_async_copy(w_hbm.at[i], wbuf.at[i], loc.at[i]) for i in range(4)]
    for i in (3, 0, 1, 2):
        loads[i].start()

    for k, c in zip(far, fetch):
        c.wait()
        gy.share(k)
        gy.b0(k)
    perm_f, n0 = sort_matrix(e_ref[...], s_ref[...], T)
    perm[...] = perm_f.astype(BF)
    accs[...] = jnp.zeros_like(accs)
    scol = jnp.concatenate([sc_ref[...], jnp.zeros((120, 128), F32)], axis=0).T
    dh1[:, 0:128] = scol

    def acc(i, v):
        accs[i] = accs[i] + jnp.sum(v.reshape(32 // 8, 8, v.shape[1]), axis=0)

    def norm2(r):
        t = pl.ds(r, 32)
        st = stat_ref[t, :]
        c1, c0, gate, r0, r1, inv = (st[:, i : i + 1] for i in (0, 3, 4, 5, 6, 9))
        row = (lax.broadcasted_iota(jnp.int32, (32, 1), 0) + r).astype(F32)
        is0 = row < n0
        s3 = dh1[t, 0:128]
        sm = s3[:, 0:1]
        se = jnp.where(is0, s3[:, 1:2], s3[:, 2:3])
        dc0, dc1 = gate * se, sm
        tot = c0 * dc0 + c1 * dc1
        dcl0, dcl1 = c0 * (dc0 - tot), c1 * (dc1 - tot)
        dgate = c0 * se
        dr0, dr1 = jnp.where(is0, dgate, 0.0), jnp.where(is0, 0.0, dgate)
        tot = r0 * dr0 + r1 * dr1
        drl0, drl1 = r0 * (dr0 - tot), r1 * (dr1 - tot)
        u2 = u2_ref[t, :]
        h2 = u2 * small_ref[2:3, :] + small_ref[3:4, :]
        dh2 = dh_ref[t, :]
        for i, d in enumerate((drl0, drl1, dcl0, dcl1)):
            acc(4 + i, h2 * d)
            dh2 = dh2 + d * small_ref[4 + i : 5 + i, :]
        acc(2, dh2 * u2)
        acc(3, dh2)
        e = dh2 * small_ref[2:3, :]
        inner = e - jnp.mean(e, axis=1, keepdims=True) - u2 * jnp.mean(e * u2, axis=1, keepdims=True)
        g = dys_ref[t, :].astype(F32) + inv * inner
        dx1[t, :] = g
        dab[t, :] = g.astype(BF)
        h1b[t, :] = (u1_ref[t, :] * small_ref[0:1, :] + small_ref[1:2, :]).astype(BF)

    rows_loop(T, 32, norm2)

    other = pl.multiple_of((1 - core) * half, half)
    mine = pl.multiple_of(core * half, half)

    def weight_grad(i, left, right):
        send[i] = mm(left[:, pl.ds(other, half)], right[...], ((0,), (0,))).astype(BF)
        c = remote(send.at[i], recv.at[i], sib_s.at[i], sib_r.at[i], sib)
        c.start()
        keep[i] = mm(left[:, pl.ds(mine, half)], right[...], ((0,), (0,)))
        return c

    def join(i, c, part):
        c.wait_recv()

        @pl.loop(0, S)
        def _(j):
            t = pl.ds(pl.multiple_of(j * WR, WR), WR)
            part[j] = (keep[i, t, :] + recv[i, t, :].astype(F32)).astype(BF)


    def g_copy(i):
        to = (me + i) % S
        src = gup_ref.at[:, pl.ds(pl.multiple_of(to * WR, WR), WR), :]
        return remote(src, gup_out.at[me], sm_s.at[1, i], sm_r.at[1], (core, to))

    @pl.loop(1, S)
    def _(i):
        g_copy(i).start()

    gup_out[me] = gup_ref[:, pl.ds(pl.multiple_of(me * WR, WR), WR), :]
    low = lax.broadcasted_iota(jnp.int32, (T, 128), 1) < 64
    lowb = low.astype(F32).astype(BF)
    highb = (1.0 - low.astype(F32)).astype(BF)

    def heads(j):
        ln = pl.ds(pl.multiple_of(j * 128, 128), 128)
        qp, dop = q_ref[:, ln], do[:, ln]
        q2 = jnp.concatenate([qp * lowb, qp * highb], axis=0)
        do2 = jnp.concatenate([dop * lowb, dop * highb], axis=0)
        pr = p_ref[j]
        dp = mm(do2, v_ref[:, ln], ((1,), (1,)))
        ds = (pr * (dp - jnp.sum(pr * dp, axis=1, keepdims=True))).astype(BF)
        dq2 = mm(ds, k_ref[:, ln])
        dq[:, ln] = jnp.where(low, dq2[0:T], dq2[T:]).astype(BF) * BF(0.125)
        dk[:, ln] = mm(ds, q2, ((0,), (0,))).astype(BF)
        dv[:, ln] = mm(pr.astype(BF), do2, ((0,), (0,))).astype(BF)

    def norm1(r):
        t = pl.ds(r, 32)
        inv = stat_ref[t, :][:, 8:9]
        u = u1_ref[t, :]
        d = dh1[t, :]
        acc(0, d * u)
        acc(1, d)
        e = d * small_ref[0:1, :]
        inner = e - jnp.mean(e, axis=1, keepdims=True) - u * jnp.mean(e * u, axis=1, keepdims=True)
        tmpb[t, :] = (dx1[t, :] + inv * inner).astype(BF)

    def each(*calls):
        for k in far:
            for call in calls:
                call(k)

    def start(i, c, part, g):
        join(i, c, part)
        each(g.share, g.b0)

    c_o = weight_grad(3, o_ref, dab)
    each(gy.a)
    loads[3].wait()
    do[...] = mm(dab[...], wbuf[3], ((1,), (1,))).astype(BF)
    start(3, c_o, part0, g0)
    each(gy.c0)

    @pl.loop(0, D // 256)
    def _(j):
        heads(j)

    each(gy.b1)

    @pl.loop(D // 256, D // 128)
    def _(j):
        heads(j)

    each(g0.a)
    c_v = weight_grad(2, h1b, dv)
    each(g0.c0)
    c_k = weight_grad(1, h1b, dk)
    start(2, c_v, partv, gv)
    c_q = weight_grad(0, h1b, dq)
    start(1, c_k, partk, gk)
    each(g0.b1)
    each(gy.c1)
    for i in range(3):
        loads[i].wait()
    dh1[...] = mm(dq[...], wbuf[0], ((1,), (1,)))
    start(0, c_q, partq, gq)
    each(gv.a)
    dh1[...] = dh1[...] + mm(dk[...], wbuf[1], ((1,), (1,)))
    each(gk.a, gv.c0)
    dh1[...] = dh1[...] + mm(dv[...], wbuf[2], ((1,), (1,)))
    each(gq.a, gv.b1, g0.c1, gk.c0)
    rows_loop(T, 32, norm1)
    each(gk.b1, gq.c0)
    each(gq.b1, gv.c1)
    for k in range(1, L):
        gy.d(k)
    for i in range(8):
        smine[i : i + 1, :] = jnp.sum(accs[i], axis=0, keepdims=True)
    c_s = remote(smine, ssib, sib_s.at[4], sib_r.at[4], sib)
    c_s.start()
    lsort[...] = (x1_ref[...] + ysum[...]).astype(BF)
    lo_out[...] = mm(perm[...], lsort[...], ((0,), (0,))).astype(BF)
    each(gk.c1)
    ig_out[...] = mm(perm[...], tmpb[...], ((0,), (0,))).astype(BF)
    c_s.wait()
    smine[...] = smine[...] + ssib[...]
    group = 128 // WR

    def s_at(i):
        return smine.at[:, pl.ds(pl.multiple_of((core * S + i) // group * 128, 128), 128)]

    def s_copy(i):
        to = (me + i) % S
        return remote(s_at(to), srecv.at[me], sm_s.at[0, i], sm_r.at[0], (core, to))

    @pl.loop(1, S)
    def _(i):
        s_copy(i).start()

    srecv[me] = s_at(me)[...]
    each(gq.c1)
    for g in (g0, gv, gk, gq):
        for k in range(1, L):
            g.d(k)
    allr = srecv.at[pl.ds(0, S - 1)]
    remote(allr, allr, sm_s.at[0, 0], sm_r.at[0], (core, xn)).wait_recv()
    smalls_out[...] = jnp.sum(srecv[...], axis=0)
    for g in (gy, g0, gv, gk, gq):
        g.finish()
    for c in (c_o, c_v, c_k, c_q):
        c.wait_send()

    got = gup_out.at[pl.ds(0, S - 1)]
    remote(got, got, sm_s.at[1, 0], sm_r.at[1], (core, xn)).wait_recv()

    @pl.loop(1, S)
    def _(i):
        s_copy(i).wait_send()
        g_copy(i).wait_send()


def back_call(dh, y, sc, small, stat, u1, u2, x1, dys, q, k, v, p, o, es, ss, wa, gup, S):
    T, D = dh.shape
    WR = D // (2 * S)
    L = S // 4
    vm = pl.BlockSpec(memory_space=pltpu.VMEM)
    hb = pl.BlockSpec(memory_space=pl.ANY)
    V = pltpu.VMEM
    dma = pltpu.SemaphoreType.DMA
    sds = jax.ShapeDtypeStruct
    row = V((T, D), BF)

    def rs_bufs(R):
        return [V((S, R, D), BF)] + [V((L, R, D), BF)] * 4 + [V((L // 2, R, D), BF)]

    return pl.pallas_call(
        back_kernel,
        out_shape=(
            sds((T, D), BF), sds((T, D), BF), sds((WR, D), F32), sds((WR, D), F32), sds((WR, D), F32),
            sds((WR, D), F32), sds((8, 128), F32),
            sds((S, 3, WR, gup.shape[2]), BF),
        ),
        in_specs=[vm] * 15 + [hb, hb, vm],
        out_specs=(vm,) * 8,
        scratch_shapes=[
            V((4, D, D), BF), V((T, T), BF), V((8, 8, D), F32), V((T, D), F32), row, row, row, row, row, row,
            V((T, D), F32), row, V((4, D // 2, D), F32), V((4, D // 2, D), BF), V((4, D // 2, D), BF),
        ]
        + rs_bufs(WR)
        + rs_bufs(WR)
        + rs_bufs(WR)
        + rs_bufs(WR)
        + rs_bufs(T)
        + [
            V((T, D), F32), V((T, D), BF),
            V((8, D), F32), V((8, D), F32), V((S, 8, 128), F32),
            dma((5, 5, L)), dma((5, 5, L)), dma((5,)), dma((5,)), dma((2, S)), dma((2,)), dma((5 + L,)),
        ],
        compiler_params=pltpu.CompilerParams(collective_id=3, has_side_effects=True, vmem_limit_bytes=60000000),
        cost_estimate=pl.CostEstimate(flops=4 * 10**9, bytes_accessed=20 * 2**20, transcendentals=2**20),
        name="back",
    )(dh, sc, small, stat, u1, u2, x1, dys, q, k, v, p, o, es, ss, y, wa, gup)


def finish_kernel(
    lo_hbm, ig_hbm, gq_hbm, gk_hbm, gv_hbm, go_hbm, sm_hbm, gup_hbm, gdn0_hbm, gdn12_hbm, count_ref, load_ref,
    lo_out, ig_out, q_out, k_out, v_out, o_out, up_out, dn_out, eu_out, ed_out, r_out, m_out, n0_out, n1_out, n2_out, n3_out, cnt_out, load_out,
    sm_ref, gup_ref, sems,
):
    pairs = (
        (gup_hbm, gup_ref), (sm_hbm, sm_ref), (lo_hbm, lo_out), (ig_hbm, ig_out), (gq_hbm, q_out), (gk_hbm, k_out),
        (gv_hbm, v_out), (go_hbm, o_out), (gdn0_hbm, dn_out), (gdn12_hbm, ed_out),
    )
    copies = [pltpu.make_async_copy(a, b, sems.at[i]) for i, (a, b) in enumerate(pairs)]
    for c in copies:
        c.start()
    copies[0].wait()
    copies[1].wait()
    S, _, WR, F = gup_ref.shape
    FR = F // 2
    slot = (lax.axis_index("dp") * S + lax.axis_index("shard")) % (128 // WR)
    tokens = lo_out.shape[0] * 2 * S
    zeros = count_ref[0, 0].astype(jnp.int32)
    for i, n in enumerate((zeros, tokens - zeros)):
        cnt_out[i] = n
        load_out[i] = 0.9 * load_ref[i] + 0.1 * n.astype(F32) * 2 / tokens
    for s in range(S):
        for c in range(2):
            cols = slice((c * S + s) * FR, (c * S + s + 1) * FR)
            part = slice(c * FR, (c + 1) * FR)
            up_out[:, cols] = gup_ref[s, 0, :, part].astype(F32)
            for e in range(2):
                eu_out[e, :, cols] = gup_ref[s, 1 + e, :, part].astype(F32)
    mine = sm_ref[:, 0:WR]
    for j in range(1, 128 // WR):
        mine = jnp.where(slot == j, sm_ref[:, j * WR : (j + 1) * WR], mine)
    for i, out in enumerate((n0_out, n1_out, n2_out, n3_out)):
        out[...] = mine[i, :]
    r_out[...] = mine[4:6, :]
    m_out[...] = mine[6:8, :]
    for c in copies[2:]:
        c.wait()


def finish_call(lo, ig, gwq, gwk, gwv, gwo, smalls, gup, gdn0, gdn12, count, load):
    T, D = lo.shape
    S, _, WR, F = gup.shape
    FF = S * F
    sm = pl.BlockSpec(memory_space=pltpu.SMEM)
    vm = pl.BlockSpec(memory_space=pltpu.VMEM)
    sds = jax.ShapeDtypeStruct
    sq = sds((WR, D), F32)
    return pl.pallas_call(
        finish_kernel,
        out_shape=(
            sds((T, D), BF), sds((T, D), BF), sq, sq, sq, sq, sds((WR, FF), F32), sds(gdn0.shape, F32),
            sds((2, WR, FF), F32), sds(gdn12.shape, F32), sds((2, WR), F32), sds((2, WR), F32),
            *[sds((WR,), F32)] * 4, sds((2,), jnp.int32), sds((2,), F32),
        ),
        in_specs=[pl.BlockSpec(memory_space=pl.ANY)] * 10 + [sm, sm],
        out_specs=(vm,) * 16 + (sm, sm),
        scratch_shapes=[
            pltpu.VMEM(smalls.shape, F32), pltpu.VMEM(gup.shape, BF), pltpu.SemaphoreType.DMA((10,)),
        ],
        compiler_params=pltpu.CompilerParams(vmem_limit_bytes=66000000),
        name="finish",
    )(lo, ig, gwq, gwk, gwv, gwo, smalls, gup, gdn0, gdn12, count, load)


def body_plain(
    hidden_in, doc_ids, expert_ids, slot_ids, out_grad, ln1_gain, ln1_bias, w_query, w_key, w_value,
    w_out, ln2_gain, ln2_bias, w_up, w_down, w_router, w_mix, expert_up, expert_down, load_avg,
):
    T, D = hidden_in.shape
    H, HD = HEADS, D // HEADS
    S = lax.axis_size("shard")
    C = lax.axis_size("dp")
    WR = w_query.shape[0]
    FF = w_up.shape[1]
    FR = w_down.shape[0]
    F = FR * C
    E = expert_up.shape[0]
    LO, HI = 80, T - 80

    pos = jnp.where(expert_ids == 0, slot_ids, jnp.sum((expert_ids == 0).astype(jnp.int32)) + slot_ids)
    n0 = jnp.sum((expert_ids == 0).astype(jnp.int32))
    place = lax.iota(jnp.int32, T)
    perm = (pos[None, :] == place[:, None]).astype(BF)
    xs = mm(perm, hidden_in)
    dys = mm(perm, out_grad).astype(BF)
    doc = doc_ids[0]
    allowed = (place[None, :] <= place[:, None]) & (doc[:, None] == doc[None, :])
    allowed = mm(mm(perm, allowed.astype(BF)).astype(BF), perm, ((1,), (1,))) > 0.5
    is0 = (place < n0)[:, None]

    small = jnp.stack(
        [ln1_gain, ln1_bias, ln2_gain, ln2_bias, w_router[:, 0], w_router[:, 1], w_mix[:, 0], w_mix[:, 1]]
    ).astype(F32)
    small = lax.all_gather(small, BOTH, axis=1, tiled=True)
    g1, b1, g2, b2 = small[0], small[1], small[2], small[3]
    wr, wm = small[4:6], small[6:8]

    wa = jnp.stack([w_query, w_key, w_value, w_out])
    wa = lax.all_gather(wa, BOTH, axis=1, tiled=True)
    wq, wk, wv, wo = wa[0], wa[1], wa[2], wa[3]

    ups = jnp.stack([w_up, expert_up[0], expert_up[1]])
    ups = ups.reshape(3, WR, C, S, FR).transpose(3, 0, 1, 2, 4).reshape(S, 3, WR, F)
    ups = lax.all_to_all(ups, "shard", 0, 0)
    ups = lax.all_gather(ups, "dp", axis=0)
    ups = ups.transpose(2, 0, 1, 3, 4).reshape(3, D, F)
    downs = jnp.stack([w_down, expert_down[0], expert_down[1]])
    downs = lax.all_gather(downs, "dp", axis=1, tiled=True)

    dy_all = ag(dys)

    n1, u1, i1 = layer_norm(xs, g1, b1)
    h1b = n1.astype(BF)
    q = (mm(h1b, wq) * 0.125).astype(BF).reshape(T, H, HD)
    k = mm(h1b, wk).astype(BF).reshape(T, H, HD)
    v = mm(h1b, wv).astype(BF).reshape(T, H, HD)
    s = jnp.einsum("ihd,jhd->hij", q, k, preferred_element_type=F32)
    s = jnp.where(allowed[None], s, -1e30)
    ex = jnp.exp(s - jnp.max(s, axis=-1, keepdims=True))
    p = ex / jnp.sum(ex, axis=-1, keepdims=True)
    pb = p.astype(BF)
    o = jnp.einsum("hij,jhd->ihd", pb, v, preferred_element_type=F32).reshape(T, D).astype(BF)
    x1 = xs + mm(o, wo)
    h2, u2, i2 = layer_norm(x1, g2, b2)
    h2b = h2.astype(BF)

    def two(w):
        return jnp.stack([jnp.sum(h2 * w[0], axis=-1), jnp.sum(h2 * w[1], axis=-1)], axis=-1)

    r = jax.nn.softmax(two(wr), axis=-1)
    c = jax.nn.softmax(two(wm), axis=-1)
    gate = jnp.where(is0, r[:, 0:1], r[:, 1:2])
    c0, c1 = c[:, 0:1], c[:, 1:2]
    we = c0 * gate
    scal = jnp.concatenate([c1, jnp.where(is0, we, 0.0), jnp.where(is0, 0.0, we)], axis=1)

    h_all = ag(h2b)
    scal_all = ag(scal)

    def cut(a, e):
        return (a[:, :LO] if e == 1 else a[:, HI:]) if e else a

    partial_y = jnp.zeros((S, T, D), F32)
    partial_dh = jnp.zeros((S, T, D), F32)
    score = []
    gup, gdown = [], []
    for e in range(3):
        he = cut(h_all, e)
        dye = cut(dy_all, e).astype(F32)
        se = cut(scal_all, e)[:, :, e : e + 1]
        n = he.shape[1]
        hf = he.reshape(S * n, D)
        pre = mm(hf, ups[e])
        val, der = gelu_pair(pre)
        ub = val.astype(BF)
        m = mm(ub, downs[e]).reshape(S, n, D)
        dm = (dye * se).astype(BF).reshape(S * n, D)
        dg = (mm(dm, downs[e], ((1,), (1,))) * der).astype(BF)
        gdown.append(mm(ub, dm, ((0,), (0,))))
        gup.append(mm(hf, dg, ((0,), (0,))))
        dx = mm(dg, ups[e], ((1,), (1,))).reshape(S, n, D)
        y = m * se
        sc = jnp.sum(dye * m, axis=-1)
        pad = [(0, 0), (0, T - n) if e < 2 else (T - n, 0)]
        live = is0[None, :, 0]
        partial_y += jnp.pad(y, pad + [(0, 0)])
        partial_dh += jnp.pad(dx, pad + [(0, 0)])
        score.append(jnp.pad(sc, pad))
    yfull = rs(partial_y)
    dh2 = rs(partial_dh)
    sc = lax.psum_scatter(jnp.stack(score, axis=1), "shard", scatter_dimension=0, tiled=False)
    sm = sc[0][:, None]
    se = jnp.where(is0, sc[1][:, None], sc[2][:, None])

    dc0, dc1 = gate * se, sm
    tot = c0 * dc0 + c1 * dc1
    dcl0, dcl1 = c0 * (dc0 - tot), c1 * (dc1 - tot)
    dgate = c0 * se
    dr0, dr1 = jnp.where(is0, dgate, 0.0), jnp.where(is0, 0.0, dgate)
    tot = r[:, 0:1] * dr0 + r[:, 1:2] * dr1
    drl0, drl1 = r[:, 0:1] * (dr0 - tot), r[:, 1:2] * (dr1 - tot)
    layer_out = (x1 + yfull).astype(BF)
    dh2 = dh2 + drl0 * wr[0] + drl1 * wr[1] + dcl0 * wm[0] + dcl1 * wm[1]
    gw = [jnp.sum(h2 * t, axis=0) for t in (drl0, drl1, dcl0, dcl1)]
    dx1, gg2, gb2 = norm_back(dh2, u2, i2, g2)
    dx1 = dx1 + dys.astype(F32)
    dab = dx1.astype(BF)
    gwo = mm(o, dab, ((0,), (0,)))
    do = mm(dab, wo, ((1,), (1,))).astype(BF).reshape(T, H, HD)
    dp = jnp.einsum("ihd,jhd->hij", do, v, preferred_element_type=F32)
    ds = (p * (dp - jnp.sum(p * dp, axis=-1, keepdims=True))).astype(BF)
    dq = jnp.einsum("hij,jhd->ihd", ds, k, preferred_element_type=F32).astype(BF)
    dq = (dq * BF(0.125)).reshape(T, D)
    dk = jnp.einsum("hij,ihd->jhd", ds, q, preferred_element_type=F32).astype(BF).reshape(T, D)
    dv = jnp.einsum("hij,ihd->jhd", pb, do, preferred_element_type=F32).astype(BF).reshape(T, D)
    dh1 = mm(dq, wq, ((1,), (1,))) + mm(dk, wk, ((1,), (1,))) + mm(dv, wv, ((1,), (1,)))
    ga = jnp.stack([mm(h1b, dq, ((0,), (0,))), mm(h1b, dk, ((0,), (0,))), mm(h1b, dv, ((0,), (0,))), gwo])
    dxn, gg1, gb1 = norm_back(dh1, u1, i1, g1)
    input_grad = (dx1 + dxn).astype(BF)

    layer_out = mm(perm, layer_out, ((0,), (0,))).astype(BF)
    input_grad = mm(perm, input_grad, ((0,), (0,))).astype(BF)

    smalls = lax.psum(jnp.stack([gg1, gb1, gg2, gb2] + gw), BOTH)
    mine = lax.dynamic_slice_in_dim(smalls, lax.axis_index(BOTH) * WR, WR, 1)
    ga = ga.reshape(4, C, S, WR, D).transpose(1, 2, 0, 3, 4)
    ga = lax.psum_scatter(ga.astype(BF), "dp", scatter_dimension=0, tiled=False)
    ga = lax.psum_scatter(ga, "shard", scatter_dimension=0, tiled=False).astype(F32)
    gdown = lax.psum_scatter(jnp.stack(gdown), "dp", scatter_dimension=1, tiled=True)
    gup = jnp.stack(gup).reshape(3, C, S, WR, F).transpose(1, 2, 0, 3, 4)
    gup = lax.psum_scatter(gup, "dp", scatter_dimension=0, tiled=False).astype(BF)
    gup = lax.all_to_all(gup, "shard", 0, 0).astype(F32)
    gup = gup.reshape(S, 3, WR, C, FR).transpose(1, 2, 3, 0, 4).reshape(3, WR, FF)

    counts = lax.psum(jnp.stack([n0, T - n0]), BOTH)
    load_new = 0.9 * load_avg + 0.1 * counts.astype(F32) * E / (T * C * S)
    return (
        layer_out, input_grad, mine[0], mine[1], ga[0], ga[1], ga[2], ga[3], mine[2], mine[3],
        gup[0], gdown[0], jnp.stack([mine[4], mine[5]], axis=1), jnp.stack([mine[6], mine[7]], axis=1),
        gup[1:], gdown[1:], counts, load_new,
    )


def body(
    hidden_in, doc_ids, expert_ids, slot_ids, out_grad, ln1_gain, ln1_bias, w_query, w_key, w_value,
    w_out, ln2_gain, ln2_bias, w_up, w_down, w_router, w_mix, expert_up, expert_down, load_avg,
):
    T, D = hidden_in.shape
    H, HD = HEADS, D // HEADS
    S = lax.axis_size("shard")
    C = lax.axis_size("dp")
    WR = w_query.shape[0]
    FF = w_up.shape[1]
    FR = w_down.shape[0]
    F = FR * C
    E = expert_up.shape[0]
    dev = lax.axis_index(BOTH)
    small = jnp.stack(
        [ln1_gain, ln1_bias, ln2_gain, ln2_bias, w_router[:, 0], w_router[:, 1], w_mix[:, 0], w_mix[:, 1]]
    ).astype(F32)
    group = 128 // WR
    slot_of = lax.broadcasted_iota(jnp.int32, (8, 128), 1) // WR
    small = jnp.where(slot_of == dev % group, jnp.tile(small, (1, group)), 0.0)
    (
        stat, u1, u2, x1, dys, q, k, v, p, o, small, count, wa, y_parts, dh2, sc, gup, gdn0, gdn12,
    ) = front_call(
        hidden_in, out_grad, doc_ids, expert_ids.reshape(1, T), slot_ids.reshape(1, T), small,
        (w_query, w_key, w_value, w_out), w_up, expert_up, w_down, expert_down, S,
    )
    y_parts = y_parts.reshape(S, T, D)
    layer_out, input_grad, gwq, gwk, gwv, gwo, smalls, gup = back_call(
        dh2, y_parts, sc, small, stat, u1, u2, x1, dys, q, k, v, p, o,
        expert_ids.reshape(1, T), slot_ids.reshape(1, T), wa.reshape(4, D, D), gup, S,
    )
    lo, ig, gq, gk, gv, go, gu, gd, geu, ged, gr, gm, n0, n1, n2, n3, counts, load_new = finish_call(
        layer_out, input_grad, gwq, gwk, gwv, gwo, smalls, gup, gdn0, gdn12, count, load_avg
    )
    return (
        lo, ig, n0, n1, gq, gk, gv, go, n2, n3, gu, gd, gr.T, gm.T, geu, ged, counts, load_new,
    )


def pick(*args):
    S, C, WR, FR = lax.axis_size("shard"), lax.axis_size("dp"), args[7].shape[0], args[14].shape[0]
    fast = C == 2 and S // 4 == 4 and S % 4 == 0 and WR % 16 == 0 and 128 % WR == 0 and FR % 128 == 0
    return (body if fast else body_plain)(*args)


def solution(mesh):
    row, vec = P(BOTH, None), P(BOTH)
    mid = P(None, BOTH, None)
    return jax.shard_map(
        pick,
        mesh=mesh,
        in_specs=(row, row, vec, vec, row, vec, vec, row, row, row, row, vec, vec, row, row, row, row, mid, mid, P()),
        out_specs=(row, row, vec, vec, row, row, row, row, vec, vec, row, row, row, row, mid, mid, P(), P()),
        check_vma=False,
    )
```

```python
import jax
import jax.numpy as jnp
from jax import lax
from jax.experimental import pallas as pl
from jax.experimental.pallas import tpu as pltpu
from jax.sharding import PartitionSpec as P

HEADS = 16
CAP = 74
BF = jnp.bfloat16
F32 = jnp.float32
BOTH = ("dp", "shard")
MESH = pl.DeviceIdType.MESH


def mm(a, b, dims=((1,), (0,))):
    return lax.dot_general(a, b, (dims, ((), ())), preferred_element_type=F32)


def layer_norm(values, gain, bias):
    centre = values - jnp.mean(values, axis=-1, keepdims=True)
    scale_inv = lax.rsqrt(jnp.mean(centre * centre, axis=-1, keepdims=True) + 1e-05)
    normed = centre * scale_inv
    return (normed * gain + bias, normed, scale_inv)


def norm_back(grad_out, normed, scale_inv, gain):
    grad_normed = grad_out * gain
    inner = grad_normed - jnp.mean(grad_normed, axis=-1, keepdims=True)
    inner = inner - normed * jnp.mean(grad_normed * normed, axis=-1, keepdims=True)
    return (scale_inv * inner, jnp.sum(grad_out * normed, axis=0), jnp.sum(grad_out, axis=0))


def gelu_pair(t):
    inner = 0.7978845608 * (t + 0.044715 * t * t * t)
    th = jnp.tanh(inner)
    val = 0.5 * t * (1.0 + th)
    der = 0.5 * (1.0 + th) + 0.5 * t * (1.0 - th * th) * 0.7978845608 * (1.0 + 3.0 * 0.044715 * t * t)
    return val, der


def ag(block):
    return lax.all_gather(block, "shard", axis=0, tiled=False)


def rs(parts):
    return lax.psum_scatter(parts.astype(BF), "shard", scatter_dimension=0, tiled=False).astype(F32)


def place_of():
    me = lax.axis_index("shard")
    core = lax.axis_index("dp")
    z, p = me // 4, me % 4
    xq = p + 1 - 2 * (p % 2)
    yq = p + 2 - 4 * (p // 2)
    return me, core, z, p, xq, yq, 3 - p


def greet(shards, core):
    bar = pltpu.get_barrier_semaphore()
    me = lax.axis_index("shard")

    @pl.loop(1, shards)
    def _(i):
        pl.semaphore_signal(bar, inc=1, device_id=(core, (me + i) % shards), device_id_type=MESH)

    pl.semaphore_signal(bar, inc=1, device_id=(1 - core, me), device_id_type=MESH)
    pl.semaphore_wait(bar, shards)


def remote(src, dst, send, recv, dev):
    return pltpu.make_async_remote_copy(
        src_ref=src, dst_ref=dst, send_sem=send, recv_sem=recv, device_id=dev, device_id_type=MESH
    )


def rows_loop(count, step, fn):
    @pl.loop(0, count // step)
    def _(i):
        fn(pl.multiple_of(i * step, step))


def level_order(z, L):
    upper = z // (L // 2)
    y = z + upper * (L - 1 - 2 * z)

    def lev_of(k):
        low = k - 1 + (k - 1 - y + L) // L
        lev = low + upper * (L - 1 - 2 * low)
        first = 1 - (k + L - 1) // L
        return lev + first * (z - lev)

    return lev_of


def tree_gather(at, own, ss, rs, dev, levels):
    core, z, p, xq, yq, dq = dev
    xn, yn = z * 4 + xq, z * 4 + yq
    me = z * 4 + p
    pair = me + 4 - 8 * (z % 2)
    lev_of, L = levels

    def copy(kind, slot, src, idx, to):
        return remote(src, at(idx), ss.at[kind, slot], rs.at[kind, slot], (core, to))

    def up_line(src, send):
        return remote(src, at(me), send, rs.at[0, z], (core, me + 4))

    def down_line(src, send):
        return remote(src, at(me), send, rs.at[0, z], (core, me - 4))

    def onward(k):
        lev = lev_of(k)
        step = 1 - 2 * ((lev - z + L) // L)
        to = z + step
        idx = lev * 4 + p
        ok = (to >= 0) & (to < L)
        return ok, remote(at(idx), at(idx), ss.at[0, lev], rs.at[0, lev], (core, me + 4 * step))

    class Stages:
        @staticmethod
        def start():
            @pl.when(z < L - 1)
            def _():
                up_line(own, ss.at[0, z]).start()

            @pl.when(z > 0)
            def _():
                down_line(own, ss.at[4, 0]).start()

            copy(1, z, own, me, xn).start()
            copy(2, z, own, me, yn).start()

        @staticmethod
        def a(k):
            lev = lev_of(k)
            idx = lev * 4 + p
            copy(0, lev, own, idx, xn).wait_recv()
            ok, on = onward(k)

            @pl.when(ok)
            def _():
                on.start()

            copy(1, lev, at(idx), idx, xn).start()
            copy(2, lev, at(idx), idx, yn).start()

        @staticmethod
        def b(k):
            lev = lev_of(k)
            odd = lev // 2 % 2
            copy(1, lev, own, lev * 4 + xq, xn).wait_recv()
            copy(2, lev, own, lev * 4 + yq, yn).wait_recv()
            idx = lev * 4 + xq + odd * (yq - xq)

            @pl.when((lev + z) % 2 == 0)
            def _():
                copy(3, lev, at(idx), idx, yn + odd * (xn - yn)).start()

        @staticmethod
        def c(k):
            lev = lev_of(k)
            idx = lev * 4 + dq

            @pl.when((lev + z) % 2 == 0)
            def _():
                copy(3, lev, own, idx, xn).wait_recv()
                copy(5, lev, at(idx), idx, pair).start()

        @staticmethod
        def d(k):
            lev = lev_of(k)

            @pl.when((lev + z) % 2 == 1)
            def _():
                copy(5, lev, own, lev * 4 + dq, pair).wait_recv()

        @staticmethod
        def done(k):
            lev = lev_of(k)
            for kind in range(1, 3):
                copy(kind, lev, own, me, xn).wait_send()

            @pl.when((lev + z) % 2 == 0)
            def _():
                for kind in (3, 5):
                    copy(kind, lev, own, me, xn).wait_send()

            @pl.when(k > 0)
            def _():
                ok, on = onward(k)
                pl.when(ok)(on.wait_send)

            @pl.when(k == 0)
            def _():
                pl.when(z < L - 1)(lambda: up_line(own, ss.at[0, z]).wait_send())
                pl.when(z > 0)(lambda: down_line(own, ss.at[4, 0]).wait_send())

        @staticmethod
        def finish():
            @pl.loop(0, L)
            def _(k):
                Stages.done(k)

    return Stages


def together(*machines):
    class Stages:
        pass

    for name in vars(machines[0]):
        if not name.startswith("_"):
            calls = [getattr(mach, name) for mach in machines]
            setattr(Stages, name, staticmethod(lambda *a, calls=calls: [call(*a) for call in calls] and None))
    return Stages


def tree_scatter(part, ra, rbx, rby, rd, final, ss, rs, dev, levels, rz=None):
    core, z, p, xq, yq, dq = dev
    xn, yn = z * 4 + xq, z * 4 + yq
    pair = z * 4 + p + 4 - 8 * (z % 2)
    lev_of, L = levels
    R = part.shape[1]

    def copy(kind, lev, src, dst, to):
        return remote(src, dst, ss.at[kind, lev], rs.at[kind, lev], (core, to))

    def sides(lev):
        copy(1, lev, part.at[lev * 4 + xq], rbx.at[lev], xn).start()
        copy(2, lev, part.at[lev * 4 + yq], rby.at[lev], yn).start()

    class Stages:
        @staticmethod
        def share(k):
            lev = lev_of(k)

            @pl.when((lev + z) % 2 == 1)
            def _():
                copy(4, lev, part.at[lev * 4 + dq], rz.at[lev // 2], pair).start()

        @staticmethod
        def a(k):
            lev = lev_of(k)
            odd = k % 2 if rz is None else lev // 2 % 2
            diag = lev * 4 + dq

            def send():
                copy(0, lev, part.at[diag], ra.at[lev], yn + odd * (xn - yn)).start()

            def join():
                copy(4, lev, rz.at[lev // 2], rz.at[lev // 2], pair).wait_recv()

                def add(r):
                    t = pl.ds(r, 32)
                    part[diag, t, :] = (part[diag, t, :].astype(F32) + rz[lev // 2, t, :].astype(F32)).astype(BF)

                rows_loop(R, 32, add)
                send()

            if rz is None:
                send()
            else:
                pl.when((lev + z) % 2 == 0)(join)

        @staticmethod
        def b(k):
            lev = lev_of(k)
            odd = k % 2 if rz is None else lev // 2 % 2
            via = lev * 4 + xq + odd * (yq - xq)
            copy(0, lev, ra.at[lev], ra.at[lev], xn).wait_recv()

            def add(r):
                t = pl.ds(r, 32)
                part[via, t, :] = (part[via, t, :].astype(F32) + ra[lev, t, :].astype(F32)).astype(BF)

            rows_loop(R, 32, add)
            sides(lev)

        @staticmethod
        def b0(k):
            pl.when((lev_of(k) + z) % 2 == 1)(lambda: sides(lev_of(k)))

        @staticmethod
        def b1(k):
            pl.when((lev_of(k) + z) % 2 == 0)(lambda: Stages.b(k))

        @staticmethod
        def c0(k):
            pl.when((lev_of(k) + z) % 2 == 1)(lambda: Stages.c(k))

        @staticmethod
        def c1(k):
            pl.when((lev_of(k) + z) % 2 == 0)(lambda: Stages.c(k))

        @staticmethod
        def c(k):
            lev = lev_of(k)
            own = lev * 4 + p
            copy(1, lev, rbx.at[lev], rbx.at[lev], xn).wait_recv()
            copy(2, lev, rby.at[lev], rby.at[lev], yn).wait_recv()

            def add(r, last):
                t = pl.ds(r, 32)
                tot = part[own, t, :].astype(F32) + rbx[lev, t, :].astype(F32) + rby[lev, t, :].astype(F32)
                if last:
                    final[t, :] = tot
                else:
                    part[own, t, :] = tot.astype(BF)

            def close():
                rows_loop(R, 32, lambda r: add(r, True))

            def send():
                rows_loop(R, 32, lambda r: add(r, False))
                remote(part.at[own], rd.at[z], ss.at[3, lev], rs.at[3, z], (core, lev * 4 + p)).start()

            if isinstance(k, int):
                (send if k else close)()
            else:
                pl.when(k == 0)(close)
                pl.when(k > 0)(send)

        @staticmethod
        def d(k):
            lev = lev_of(k)
            copy(3, lev, rd.at[lev], rd.at[lev], xn).wait_recv()

            def add(r):
                t = pl.ds(r, 32)
                final[t, :] = final[t, :] + rd[lev, t, :].astype(F32)

            rows_loop(R, 32, add)

        @staticmethod
        def finish():
            @pl.loop(0, L)
            def _(k):
                lev = lev_of(k)
                for kind in (1, 2):
                    copy(kind, lev, ra.at[0], ra.at[0], xn).wait_send()

                if rz is None:
                    copy(0, lev, ra.at[0], ra.at[0], xn).wait_send()
                else:
                    kind = (lev + z) % 2 * 4
                    copy(kind, lev, ra.at[0], ra.at[0], xn).wait_send()

                @pl.when(k > 0)
                def _():
                    copy(3, lev, ra.at[0], ra.at[0], xn).wait_send()

    return Stages


def sort_matrix(ids_e, ids_s, T):
    zero = ids_e == 0
    n0 = jnp.sum(jnp.where(zero, 1.0, 0.0), axis=1, keepdims=True)
    slot = ids_s.astype(F32)
    pos = jnp.where(zero, slot, slot + n0)
    sub = lax.broadcasted_iota(jnp.int32, (T, T), 0).astype(F32)
    return jnp.where(sub == pos, 1.0, 0.0), n0


def front_kernel(
    x_ref, dyin_ref, doc_ref, e_ref, s_ref, small_ref, wq_ref, wk_ref, wv_ref, wo_ref,
    wu_ref, eu_ref, wd_ref, ed_ref,
    stat_out, u1_out, u2_out, x1_out, dys_out, q_out, k_out, v_out, p_out, o_out,
    small_out, count_out, w_out, y_out, dh_out, sc_out, gup_out, gdn0_out, gdn12_out,
    wbuf, up_ref, dn_ref, smallbuf, h1b, bias, tmp, xs, dy_all, hall, dxp, scall, psc, screcv, wcol, scol, ra, rbx, rby, rd,
    pre, dyw, uw, dg, gdn, gup, sib_dn, sib_up,
    ag_s, ag_r, rs_s, rs_r, sib_s, sib_r, one_s, one_r, sm_s, sm_r, sn_s, sn_r, loc,
):
    T, D = x_ref.shape
    WR = wq_ref.shape[0]
    FR = wd_ref.shape[0]
    N = wbuf.shape[1]
    S = N // 2
    L = S // 4
    me, core, z, p, xq, yq, dq = place_of()
    xn = z * 4 + xq
    my = core * S + me
    sib = (1 - core, me)
    greet(S, core)
    lev_of = level_order(z, L)

    dev, levels = (core, z, p, xq, yq, dq), (lev_of, L)

    def split(at, j):
        return tree_gather(at, at(me), ag_s.at[j], ag_r.at[j], dev, levels)

    def rows_of(ref, j):
        return lambda i: ref.at[i, pl.ds(j * (T // 2), T // 2)]

    wg = together(*(split(lambda i, j=j: wbuf.at[pl.ds(2 * j, 2), core * S + i], j) for j in range(2)))
    dyg = together(*(split(rows_of(dy_all, j), 2 + j) for j in range(2)))
    hg = together(*(split(rows_of(hall, j), 4 + j) for j in range(2)))

    for i, w in enumerate((wq_ref, wk_ref, wv_ref, wo_ref)):
        wbuf[i, my] = w[...]
    wg.start()

    perm, n0 = sort_matrix(e_ref[...], s_ref[...], T)
    smallbuf[my, 0:8, :] = small_ref[...]
    lane8 = lax.broadcasted_iota(jnp.int32, (8, 128), 1)
    smallbuf[my, 8:16, :] = jnp.where(lane8 == 0, jnp.broadcast_to(n0, (8, 128)), 0.0)

    @pl.loop(1, S)
    def _(i):
        remote(smallbuf.at[my], smallbuf.at[my], sm_s.at[0, i], sm_r.at[0], (core, (me + i) % S)).start()

    F = 2 * FR
    mine_f = pl.ds(pl.multiple_of(core * FR, FR), FR)
    other_f = pl.ds(pl.multiple_of((1 - core) * FR, FR), FR)
    dn_copies = (
        remote(wd_ref, dn_ref.at[0, mine_f], sib_s.at[1, 0], sib_r.at[1, 0], sib),
        remote(ed_ref, dn_ref.at[pl.ds(1, 2), mine_f], sib_s.at[1, 1], sib_r.at[1, 1], sib),
    )
    for c in dn_copies:
        c.start()
    dn_ref[0, mine_f, :] = wd_ref[...]
    for e in range(2):
        dn_ref[1 + e, mine_f, :] = ed_ref[e]
    permb = perm.astype(BF)
    xs[...] = mm(permb, x_ref[...])
    dys_out[...] = mm(permb, dyin_ref[...]).astype(BF)
    dy_all[me] = dys_out[...]
    gdn[...] = jnp.zeros_like(gdn)
    gup[...] = jnp.zeros_like(gup)

    docs = (doc_ref[...] == lax.broadcasted_iota(jnp.int32, (16, T), 0)).astype(F32).astype(BF)
    docs = mm(docs, permb, ((1,), (1,))).astype(BF)
    same = mm(docs, docs, ((0,), (0,)))
    place = lax.broadcasted_iota(jnp.int32, (T, T), 1).astype(F32)
    ord_col = jnp.sum(perm * place, axis=1, keepdims=True)
    ord_row = mm(place[0:16, :].astype(BF), permb, ((1,), (1,)))[0:1, :]
    bias[...] = jnp.where((same > 0.5) & (ord_row <= ord_col), 0.0, -1e30)

    lane = lax.broadcasted_iota(jnp.int32, (64, 128), 1)

    def norm1(r):
        t = pl.ds(r, 64)
        v = xs[t, :]
        cen = v - jnp.mean(v, axis=1, keepdims=True)
        inv = lax.rsqrt(jnp.mean(cen * cen, axis=1, keepdims=True) + 1e-05)
        u1_out[t, :] = cen * inv
        stat_out[t, :] = jnp.where(lane == 8, inv, 0.0)

    rows_loop(T, 64, norm1)

    wg.a(1)
    wg.b(0)
    wg.a(2)
    wg.b(1)
    wg.a(3)
    wg.c(0)

    group = 128 // WR
    remote(smallbuf.at[pl.ds(0, S - 1)], smallbuf.at[pl.ds(0, S - 1)], sm_s.at[0, 0], sm_r.at[0], (core, xn)).wait_recv()
    mine_small = smallbuf.at[pl.ds(core * S, S)]
    c_small = remote(mine_small, mine_small, sib_s.at[1, 2], sib_r.at[1, 2], sib)
    c_small.start()

    def up_copy(e, h, i):
        to = (me + i) % S
        src = wu_ref if e == 0 else eu_ref.at[e - 1]
        return remote(
            src.at[:, pl.ds(pl.multiple_of((h * S + to) * FR, FR), FR)],
            up_ref.at[pl.ds(pl.multiple_of(my * WR, WR), WR), pl.ds(e * F + h * FR, FR)],
            sm_s.at[1, i], sm_r.at[1], (core, to),
        )

    @pl.loop(1, S)
    def _(i):
        for e in range(3):
            for h in range(2):
                up_copy(e, h, i).start()

    for e in range(3):
        for h in range(2):
            src = wu_ref if e == 0 else eu_ref.at[e - 1]
            block = src[:, pl.ds(pl.multiple_of((h * S + me) * FR, FR), FR)]
            up_ref[pl.ds(pl.multiple_of(my * WR, WR), WR), e * F + h * FR : e * F + (h + 1) * FR] = block

    def w_sib(lev, who):
        b = wbuf.at[:, pl.ds(who * S + lev * 4, 4)]
        return remote(b, b, sib_s.at[0, lev], sib_r.at[0, lev], sib)

    def pass_on(k):
        wg.d(k)
        w_sib(lev_of(k), core).start()

    pass_on(0)
    wg.b(2)
    dyg.start()
    wg.c(1)
    wg.b(3)
    pass_on(1)
    wg.c(2)
    pass_on(2)
    wg.c(3)
    pass_on(3)
    dyg.a(1)
    dyg.b(0)
    c_small.wait_recv()
    for g in range(D // 128):
        part = smallbuf[g * group, 0:8, :]
        for j in range(1, group):
            part = part + smallbuf[g * group + j, 0:8, :]
        small_out[:, g * 128 : (g + 1) * 128] = part
    cnt = smallbuf[0, 8:16, :]
    for i in range(1, N):
        cnt = cnt + smallbuf[i, 8:16, :]
    count_out[...] = cnt

    def norm1b(r):
        t = pl.ds(r, 64)
        h1b[t, :] = (u1_out[t, :] * small_out[0:1, :] + small_out[1:2, :]).astype(BF)

    rows_loop(T, 64, norm1b)
    dyg.a(2)
    dyg.b(1)
    for k in range(L):
        w_sib(lev_of(k), 1 - core).wait_recv()
    w_save = pltpu.make_async_copy(wbuf, w_out, loc.at[L])
    w_save.start()

    def full(i):
        return wbuf[i].reshape(D, D)

    tmp[...] = mm(h1b[...], full(0))
    q_out[...] = (tmp[...] * 0.125).astype(BF)
    dyg.a(3)
    dyg.c(0)
    tmp[...] = mm(h1b[...], full(1))
    k_out[...] = tmp[...].astype(BF)
    tmp[...] = mm(h1b[...], full(2))
    v_out[...] = tmp[...].astype(BF)
    dyg.b(2)
    dyg.c(1)

    low = lax.broadcasted_iota(jnp.int32, (T, 128), 1) < 64
    lowb = low.astype(F32).astype(BF)
    highb = (1.0 - low.astype(F32)).astype(BF)

    def heads(j):
        ln = pl.ds(pl.multiple_of(j * 128, 128), 128)
        qp = q_out[:, ln]
        q2 = jnp.concatenate([qp * lowb, qp * highb], axis=0)
        s = mm(q2, k_out[:, ln], ((1,), (1,)))
        s = s + jnp.concatenate([bias[...], bias[...]], axis=0)
        ex = jnp.exp(s - jnp.max(s, axis=1, keepdims=True))
        pr = ex / jnp.sum(ex, axis=1, keepdims=True)
        p_out[j] = pr
        o2 = mm(pr.astype(BF), v_out[:, ln])
        o_out[:, ln] = jnp.where(low, o2[0:T], o2[T:]).astype(BF)

    @pl.loop(0, D // 128)
    def _(j):
        heads(j)

    dyg.b(3)
    tmp[...] = mm(o_out[...], full(3))

    def norm2(r):
        t = pl.ds(r, 64)
        v = xs[t, :] + tmp[t, :]
        x1_out[t, :] = v
        cen = v - jnp.mean(v, axis=1, keepdims=True)
        inv = lax.rsqrt(jnp.mean(cen * cen, axis=1, keepdims=True) + 1e-05)
        u = cen * inv
        u2_out[t, :] = u
        h2 = u * small_out[2:3, :] + small_out[3:4, :]
        hall[me, t, :] = h2.astype(BF)
        lg = [jnp.sum(h2 * small_out[i : i + 1, :], axis=1, keepdims=True) for i in range(4, 8)]

        def soft(a, b):
            mx = jnp.maximum(a, b)
            ea, eb = jnp.exp(a - mx), jnp.exp(b - mx)
            return ea / (ea + eb), eb / (ea + eb)

        r0, r1 = soft(lg[0], lg[1])
        k0, k1 = soft(lg[2], lg[3])
        row = (lax.broadcasted_iota(jnp.int32, (64, 1), 0) + r).astype(F32)
        is0 = row < n0
        gate = jnp.where(is0, r0, r1)
        we = k0 * gate
        cols = (k1, jnp.where(is0, we, 0.0), jnp.where(is0, 0.0, we), k0, gate, r0, r1)
        st = stat_out[t, :] + jnp.where(lane == 9, inv, 0.0)
        for i, col in enumerate(cols):
            st = st + jnp.where(lane == i, col, 0.0)
        stat_out[t, :] = st

    dyg.c(2)
    rows_loop(T, 64, norm2)
    scall[me] = stat_out[...].T[0:8, :]
    hg.start()

    @pl.loop(1, S)
    def _(i):
        remote(scall.at[me], scall.at[me], sn_s.at[0, i], sn_r.at[0], (core, (me + i) % S)).start()

    dyg.c(3)
    got = up_ref.at[pl.ds(0, (S - 1) * WR), :]
    remote(got, got, sm_s.at[1, 0], sm_r.at[1], (core, xn)).wait_recv()
    mine_up = up_ref.at[pl.ds(pl.multiple_of(core * S * WR, S * WR), S * WR), :]
    c_slice = remote(mine_up, mine_up, sib_s.at[1, 3], sib_r.at[1, 3], sib)
    c_slice.start()
    end = (z == 0) | (z == L - 1)
    hg.a(1)
    hg.b(0)
    hg.a(2)
    pl.when(jnp.logical_not(end))(lambda: hg.a(3))

    w_save.wait()
    wg.finish()

    @pl.loop(0, L)
    def _(k):
        w_sib(k, core).wait_send()

    remote(scall.at[pl.ds(0, S - 1)], scall.at[pl.ds(0, S - 1)], sn_s.at[0, 0], sn_r.at[0], (core, xn)).wait_recv()
    c_slice.wait()
    for c in dn_copies:
        c.wait()
    c_small.wait_send()
    hg.c(0)
    rgs = []
    for i in range(2):
        t = pl.ds(i * (T // 2), T // 2)
        bufs = [b.at[:, t, :] for b in (dxp, ra, rbx, rby, rd)]
        rgs.append(tree_scatter(*bufs, dh_out.at[t], rs_s.at[i], rs_r.at[i], dev, levels))
    LO = 80
    HI = T - LO
    per = T // WR
    fold = N // (4 * per)

    def y_copy(lev):
        src = wbuf.at[lev // fold, pl.ds(lev % fold * (4 * per), 4 * per)]
        return pltpu.make_async_copy(src, y_out.at[pl.ds(lev * (4 * per), 4 * per)], loc.at[lev])

    def compute(lev, between):
        base = lev * 4
        level = pl.ds(base, 4)
        for q in range(4):
            full = jnp.concatenate([scall[base + q], jnp.zeros((120, 128), F32)], axis=0)
            wcol[q] = full.T
        pre[...] = mm(hall[level].reshape(4 * T, D), up_ref[...])
        between(0)
        dyw[...] = mm(dy_all[level].reshape(4 * T, D), dn_ref[...].reshape(3 * F, D), ((1,), (1,)))
        lane = lax.broadcasted_iota(jnp.int32, (T, 128), 1)

        @pl.loop(0, 4)
        def _(q):
            t = pl.ds(pl.multiple_of(q * T, T), T)
            score = jnp.zeros((T, 128), F32)
            for e in range(3):
                cols = slice(e * F, (e + 1) * F)
                val, der = gelu_pair(pre[t, cols])
                low = val.astype(BF).astype(F32)
                back = dyw[t, cols]
                w = wcol[q][:, e : e + 1]
                score = score + jnp.where(lane == e, jnp.sum(low * back, axis=1, keepdims=True), 0.0)
                uw[t, cols] = (low * w).astype(BF)
                dg[t, cols] = (back * w * der).astype(BF)
            psc[base + q] = score.T[0:8, :]

        between(1)
        dxp[level] = mm(dg[...], up_ref[...], ((1,), (1,))).astype(BF).reshape(4, T, D)
        y = mm(uw[...], dn_ref[...].reshape(3 * F, D)).astype(BF)
        wbuf[lev // fold, pl.ds(lev % fold * (4 * per), 4 * per)] = y.reshape(4 * per, WR, D)
        y_copy(lev).start()
        between(2)

    def weight_grads(lev):
        for e in range(3):
            n = LO if e else T
            off = HI if e == 2 else 0
            level = pl.ds(lev * 4, 4)

            def some(a):
                a = a[:, e * F : (e + 1) * F]
                return a.reshape(4, T, F)[:, off : off + n].reshape(4 * n, F)

            hm = hall[level, off : off + n, :].reshape(4 * n, D)
            dyb = dy_all[level, off : off + n, :].reshape(4 * n, D)
            gdn[e] = gdn[e] + mm(some(uw), dyb, ((0,), (0,)))
            gup[e] = gup[e] + mm(some(dg), hm, ((0,), (0,)))

    def far_a(i):
        pl.when(end)(lambda: hg.a(i))

    @pl.loop(0, L)
    def _(k):
        @pl.when(k > 0)
        def _():
            hg.d(k)
            dyg.d(k)

        def between(e):
            @pl.when(k == 0)
            def _():
                for call, i in (((far_a, 3), (hg.b, 1)), ((hg.c, 1), (hg.b, 2)), ())[e]:
                    call(i)

            @pl.when(k == 1)
            def _():
                for call, i in (((hg.c, 2), (hg.b, 3)), ((hg.c, 3),), ())[e]:
                    call(i)

            if e == 1:

                @pl.when(k > 0)
                def _():
                    for g in rgs:
                        g.b(k - 1)

        compute(lev_of(k), between)
        for g in rgs:
            g.a(k)

        @pl.when(k > 0)
        def _():
            for g in rgs:
                g.c(k - 1)

        weight_grads(lev_of(k))

    half = D // 2
    other = pl.multiple_of((1 - core) * half, half)
    mine_d = pl.multiple_of(core * half, half)
    c_up = remote(gup.at[:, :, pl.ds(other, half)], sib_up, one_s.at[0], one_r.at[0], sib)
    c_dn = remote(gdn.at[:, other_f, :], sib_dn, one_s.at[1], one_r.at[1], sib)
    c_up.start()
    c_dn.start()

    @pl.loop(1, S)
    def _(i):
        to = (me + i) % S
        remote(psc.at[to], screcv.at[i], sn_s.at[1, i], sn_r.at[1], (core, to)).start()

    for g in rgs:
        g.b(L - 1)
    c_up.wait_recv()
    for e in range(3):
        tot = gup[e, :, pl.ds(mine_d, half)] + sib_up[e]
        gup_out[e] = tot.T.astype(BF)
        if e == 0:
            for g in rgs:
                g.c(L - 1)
    screcv[0] = psc[me]
    c_dn.wait_recv()
    gdn0_out[...] = gdn[0, mine_f, :] + sib_dn[0]
    for e in range(1, 3):
        gdn12_out[e - 1] = gdn[e, mine_f, :] + sib_dn[e]
    for k in range(1, L):
        for g in rgs:
            g.d(k)
    remote(screcv.at[pl.ds(1, S - 1)], screcv.at[pl.ds(1, S - 1)], sn_s.at[1, 0], sn_r.at[1], (core, xn)).wait_recv()
    sc_out[...] = jnp.sum(screcv[...], axis=0)

    for i in range(L):
        y_copy(i).wait()
    c_up.wait_send()
    c_dn.wait_send()
    hg.finish()
    dyg.finish()
    for g in rgs:
        g.finish()

    @pl.loop(1, S)
    def _(i):
        remote(scall.at[me], scall.at[0], sn_s.at[0, i], sn_r.at[0], (core, xn)).wait_send()
        remote(psc.at[0], screcv.at[0], sn_s.at[1, i], sn_r.at[1], (core, xn)).wait_send()
        remote(smallbuf.at[my], smallbuf.at[my], sm_s.at[0, i], sm_r.at[0], (core, xn)).wait_send()
        for e in range(3):
            for h in range(2):
                up_copy(e, h, i).wait_send()


def front_call(x, dy, docs, es, ss, small, ws, wu, eu, wd, ed, S):
    T, D = x.shape
    WR, FR = ws[0].shape[0], wd.shape[0]
    L, N, F = S // 4, 2 * S, 2 * FR
    vm = pl.BlockSpec(memory_space=pltpu.VMEM)
    hb = pl.BlockSpec(memory_space=pl.ANY)
    V = pltpu.VMEM
    dma = pltpu.SemaphoreType.DMA
    sds = jax.ShapeDtypeStruct
    row = sds((T, D), BF)
    rowf = sds((T, D), F32)
    tokens, blocks, side = V((S, T, D), BF), V((L, T, D), BF), V((S, 8, 128), F32)
    return pl.pallas_call(
        front_kernel,
        out_shape=(
            sds((T, 128), F32), rowf, rowf, rowf, row, row, row, row,
            sds((D // 128, 2 * T, T), F32), row, sds((8, D), F32), sds((8, 128), F32),
            sds((4, N, WR, D), BF), sds((S * T // WR, WR, D), BF), rowf, sds((8, 128), F32), sds((3, D // 2, F), BF),
            sds((FR, D), F32), sds((2, FR, D), F32),
        ),
        in_specs=[vm] * 14,
        out_specs=(vm,) * 12 + (hb, hb) + (vm,) * 5,
        scratch_shapes=[
            V((4, N, WR, D), BF), V((D, 3 * F), BF), V((3, F, D), BF), V((N, 16, 128), F32), V((T, D), BF), V((T, T), F32),
            V((T, D), F32), V((T, D), F32), tokens, tokens, tokens, side, side, side, V((4, T, 128), F32), V((4, T, 128), F32), blocks, blocks, blocks, blocks,
            V((4 * T, 3 * F), F32), V((4 * T, 3 * F), F32), V((4 * T, 3 * F), BF), V((4 * T, 3 * F), BF),
            V((3, F, D), F32), V((3, F, D), F32), V((3, FR, D), F32), V((3, F, D // 2), F32),
            dma((6, 6, L)), dma((6, 6, L)), dma((2, 4, L)), dma((2, 4, L)), dma((2, max(L, 4))), dma((2, max(L, 4))),
            dma((2,)), dma((2,)), dma((2, S)), dma((2,)), dma((2, S)), dma((2,)), dma((L + 1,)),
        ],
        compiler_params=pltpu.CompilerParams(collective_id=1, has_side_effects=True, vmem_limit_bytes=66000000),
        cost_estimate=pl.CostEstimate(flops=17 * 10**9, bytes_accessed=40 * 2**20, transcendentals=2**20),
        name="front",
    )(x, dy, docs, es, ss, small, *ws, wu, eu, wd, ed)


def back_kernel(
    dh_ref, sc_ref, small_ref, stat_ref, u1_ref, u2_ref, x1_ref, dys_ref,
    q_ref, k_ref, v_ref, p_ref, o_ref, e_ref, s_ref, y_hbm, w_hbm, gup_ref,
    lo_out, ig_out, gq_out, gk_out, gv_out, go_out, smalls_out, gup_out,
    wbuf, perm, accs, dx1, dab, do, dq, dk, dv, h1b, dh1, tmpb, keep, send, recv,
    part0, ra0, rbx0, rby0, rd0, rz0, partv, rav, rbxv, rbyv, rdv, rzv, partk, rak, rbxk, rbyk, rdk, rzk,
    partq, raq, rbxq, rbyq, rdq, rzq, ypart, ray, rbxy, rbyy, rdy, rzy, ysum, lsort, smine, ssib, srecv,
    rs_s, rs_r, sib_s, sib_r, sm_s, sm_r, loc,
):
    T, D = dh_ref.shape
    S, WR = part0.shape[0], part0.shape[1]
    L = S // 4
    half = D // 2
    me, core, z, p, xq, yq, dgq = place_of()
    xn = z * 4 + xq
    sib = (1 - core, me)
    lev_of = level_order(z, L)
    far = list(reversed(range(L)))
    fetch = []
    for k in far:
        some = pl.ds(lev_of(k) * 4, 4)
        fetch.append(pltpu.make_async_copy(y_hbm.at[some], ypart.at[some], loc.at[4 + k]))
    for c in fetch:
        c.start()
    greet(S, core)

    dev, levels = (core, z, p, xq, yq, dgq), (lev_of, L)
    g0 = tree_scatter(part0, ra0, rbx0, rby0, rd0, go_out, rs_s.at[0], rs_r.at[0], dev, levels, rz0)
    gv = tree_scatter(partv, rav, rbxv, rbyv, rdv, gv_out, rs_s.at[1], rs_r.at[1], dev, levels, rzv)
    gk = tree_scatter(partk, rak, rbxk, rbyk, rdk, gk_out, rs_s.at[3], rs_r.at[3], dev, levels, rzk)
    gq = tree_scatter(partq, raq, rbxq, rbyq, rdq, gq_out, rs_s.at[4], rs_r.at[4], dev, levels, rzq)
    gy = tree_scatter(ypart, ray, rbxy, rbyy, rdy, ysum, rs_s.at[2], rs_r.at[2], dev, levels, rzy)
    far = list(reversed(range(L)))
    loads = [pltpu.make_async_copy(w_hbm.at[i], wbuf.at[i], loc.at[i]) for i in range(4)]
    for i in (3, 0, 1, 2):
        loads[i].start()

    for k, c in zip(far, fetch):
        c.wait()
        gy.share(k)
        gy.b0(k)
    perm_f, n0 = sort_matrix(e_ref[...], s_ref[...], T)
    perm[...] = perm_f.astype(BF)
    accs[...] = jnp.zeros_like(accs)
    scol = jnp.concatenate([sc_ref[...], jnp.zeros((120, 128), F32)], axis=0).T
    dh1[:, 0:128] = scol

    def acc(i, v):
        accs[i] = accs[i] + jnp.sum(v.reshape(32 // 8, 8, v.shape[1]), axis=0)

    def norm2(r):
        t = pl.ds(r, 32)
        st = stat_ref[t, :]
        c1, c0, gate, r0, r1, inv = (st[:, i : i + 1] for i in (0, 3, 4, 5, 6, 9))
        row = (lax.broadcasted_iota(jnp.int32, (32, 1), 0) + r).astype(F32)
        is0 = row < n0
        s3 = dh1[t, 0:128]
        sm = s3[:, 0:1]
        se = jnp.where(is0, s3[:, 1:2], s3[:, 2:3])
        dc0, dc1 = gate * se, sm
        tot = c0 * dc0 + c1 * dc1
        dcl0, dcl1 = c0 * (dc0 - tot), c1 * (dc1 - tot)
        dgate = c0 * se
        dr0, dr1 = jnp.where(is0, dgate, 0.0), jnp.where(is0, 0.0, dgate)
        tot = r0 * dr0 + r1 * dr1
        drl0, drl1 = r0 * (dr0 - tot), r1 * (dr1 - tot)
        u2 = u2_ref[t, :]
        h2 = u2 * small_ref[2:3, :] + small_ref[3:4, :]
        dh2 = dh_ref[t, :]
        for i, d in enumerate((drl0, drl1, dcl0, dcl1)):
            acc(4 + i, h2 * d)
            dh2 = dh2 + d * small_ref[4 + i : 5 + i, :]
        acc(2, dh2 * u2)
        acc(3, dh2)
        e = dh2 * small_ref[2:3, :]
        inner = e - jnp.mean(e, axis=1, keepdims=True) - u2 * jnp.mean(e * u2, axis=1, keepdims=True)
        g = dys_ref[t, :].astype(F32) + inv * inner
        dx1[t, :] = g
        dab[t, :] = g.astype(BF)
        h1b[t, :] = (u1_ref[t, :] * small_ref[0:1, :] + small_ref[1:2, :]).astype(BF)

    rows_loop(T, 32, norm2)

    other = pl.multiple_of((1 - core) * half, half)
    mine = pl.multiple_of(core * half, half)

    def weight_grad(i, left, right):
        send[i] = mm(left[:, pl.ds(other, half)], right[...], ((0,), (0,))).astype(BF)
        c = remote(send.at[i], recv.at[i], sib_s.at[i], sib_r.at[i], sib)
        c.start()
        keep[i] = mm(left[:, pl.ds(mine, half)], right[...], ((0,), (0,)))
        return c

    def join(i, c, part):
        c.wait_recv()

        @pl.loop(0, S)
        def _(j):
            t = pl.ds(pl.multiple_of(j * WR, WR), WR)
            part[j] = (keep[i, t, :] + recv[i, t, :].astype(F32)).astype(BF)


    def g_copy(i):
        to = (me + i) % S
        src = gup_ref.at[:, pl.ds(pl.multiple_of(to * WR, WR), WR), :]
        return remote(src, gup_out.at[me], sm_s.at[1, i], sm_r.at[1], (core, to))

    @pl.loop(1, S)
    def _(i):
        g_copy(i).start()

    gup_out[me] = gup_ref[:, pl.ds(pl.multiple_of(me * WR, WR), WR), :]
    low = lax.broadcasted_iota(jnp.int32, (T, 128), 1) < 64
    lowb = low.astype(F32).astype(BF)
    highb = (1.0 - low.astype(F32)).astype(BF)

    def heads(j):
        ln = pl.ds(pl.multiple_of(j * 128, 128), 128)
        qp, dop = q_ref[:, ln], do[:, ln]
        q2 = jnp.concatenate([qp * lowb, qp * highb], axis=0)
        do2 = jnp.concatenate([dop * lowb, dop * highb], axis=0)
        pr = p_ref[j]
        dp = mm(do2, v_ref[:, ln], ((1,), (1,)))
        ds = (pr * (dp - jnp.sum(pr * dp, axis=1, keepdims=True))).astype(BF)
        dq2 = mm(ds, k_ref[:, ln])
        dq[:, ln] = jnp.where(low, dq2[0:T], dq2[T:]).astype(BF) * BF(0.125)
        dk[:, ln] = mm(ds, q2, ((0,), (0,))).astype(BF)
        dv[:, ln] = mm(pr.astype(BF), do2, ((0,), (0,))).astype(BF)

    def norm1(r):
        t = pl.ds(r, 32)
        inv = stat_ref[t, :][:, 8:9]
        u = u1_ref[t, :]
        d = dh1[t, :]
        acc(0, d * u)
        acc(1, d)
        e = d * small_ref[0:1, :]
        inner = e - jnp.mean(e, axis=1, keepdims=True) - u * jnp.mean(e * u, axis=1, keepdims=True)
        tmpb[t, :] = (dx1[t, :] + inv * inner).astype(BF)

    def each(*calls):
        for k in far:
            for call in calls:
                call(k)

    def start(i, c, part, g):
        join(i, c, part)
        each(g.share, g.b0)

    c_o = weight_grad(3, o_ref, dab)
    each(gy.a)
    loads[3].wait()
    do[...] = mm(dab[...], wbuf[3], ((1,), (1,))).astype(BF)
    start(3, c_o, part0, g0)
    each(gy.c0)

    @pl.loop(0, D // 256)
    def _(j):
        heads(j)

    each(gy.b1)

    @pl.loop(D // 256, D // 128)
    def _(j):
        heads(j)

    each(g0.a)
    c_v = weight_grad(2, h1b, dv)
    each(g0.c0)
    c_k = weight_grad(1, h1b, dk)
    start(2, c_v, partv, gv)
    c_q = weight_grad(0, h1b, dq)
    start(1, c_k, partk, gk)
    each(g0.b1)
    each(gy.c1)
    for i in range(3):
        loads[i].wait()
    dh1[...] = mm(dq[...], wbuf[0], ((1,), (1,)))
    start(0, c_q, partq, gq)
    each(gv.a)
    dh1[...] = dh1[...] + mm(dk[...], wbuf[1], ((1,), (1,)))
    each(gk.a, gv.c0)
    dh1[...] = dh1[...] + mm(dv[...], wbuf[2], ((1,), (1,)))
    each(gq.a, gv.b1, g0.c1, gk.c0)
    rows_loop(T, 32, norm1)
    each(gk.b1, gq.c0)
    each(gq.b1, gv.c1)
    for k in range(1, L):
        gy.d(k)
    for i in range(8):
        smine[i : i + 1, :] = jnp.sum(accs[i], axis=0, keepdims=True)
    c_s = remote(smine, ssib, sib_s.at[4], sib_r.at[4], sib)
    c_s.start()
    lsort[...] = (x1_ref[...] + ysum[...]).astype(BF)
    lo_out[...] = mm(perm[...], lsort[...], ((0,), (0,))).astype(BF)
    each(gk.c1)
    ig_out[...] = mm(perm[...], tmpb[...], ((0,), (0,))).astype(BF)
    c_s.wait()
    smine[...] = smine[...] + ssib[...]
    group = 128 // WR

    def s_at(i):
        return smine.at[:, pl.ds(pl.multiple_of((core * S + i) // group * 128, 128), 128)]

    def s_copy(i):
        to = (me + i) % S
        return remote(s_at(to), srecv.at[me], sm_s.at[0, i], sm_r.at[0], (core, to))

    @pl.loop(1, S)
    def _(i):
        s_copy(i).start()

    srecv[me] = s_at(me)[...]
    each(gq.c1)
    for g in (g0, gv, gk, gq):
        for k in range(1, L):
            g.d(k)
    allr = srecv.at[pl.ds(0, S - 1)]
    remote(allr, allr, sm_s.at[0, 0], sm_r.at[0], (core, xn)).wait_recv()
    smalls_out[...] = jnp.sum(srecv[...], axis=0)
    for g in (gy, g0, gv, gk, gq):
        g.finish()
    for c in (c_o, c_v, c_k, c_q):
        c.wait_send()

    got = gup_out.at[pl.ds(0, S - 1)]
    remote(got, got, sm_s.at[1, 0], sm_r.at[1], (core, xn)).wait_recv()

    @pl.loop(1, S)
    def _(i):
        s_copy(i).wait_send()
        g_copy(i).wait_send()


def back_call(dh, y, sc, small, stat, u1, u2, x1, dys, q, k, v, p, o, es, ss, wa, gup, S):
    T, D = dh.shape
    WR = D // (2 * S)
    L = S // 4
    vm = pl.BlockSpec(memory_space=pltpu.VMEM)
    hb = pl.BlockSpec(memory_space=pl.ANY)
    V = pltpu.VMEM
    dma = pltpu.SemaphoreType.DMA
    sds = jax.ShapeDtypeStruct
    row = V((T, D), BF)

    def rs_bufs(R):
        return [V((S, R, D), BF)] + [V((L, R, D), BF)] * 4 + [V((L // 2, R, D), BF)]

    return pl.pallas_call(
        back_kernel,
        out_shape=(
            sds((T, D), BF), sds((T, D), BF), sds((WR, D), F32), sds((WR, D), F32), sds((WR, D), F32),
            sds((WR, D), F32), sds((8, 128), F32),
            sds((S, 3, WR, gup.shape[2]), BF),
        ),
        in_specs=[vm] * 15 + [hb, hb, vm],
        out_specs=(vm,) * 8,
        scratch_shapes=[
            V((4, D, D), BF), V((T, T), BF), V((8, 8, D), F32), V((T, D), F32), row, row, row, row, row, row,
            V((T, D), F32), row, V((4, D // 2, D), F32), V((4, D // 2, D), BF), V((4, D // 2, D), BF),
        ]
        + rs_bufs(WR)
        + rs_bufs(WR)
        + rs_bufs(WR)
        + rs_bufs(WR)
        + rs_bufs(T)
        + [
            V((T, D), F32), V((T, D), BF),
            V((8, D), F32), V((8, D), F32), V((S, 8, 128), F32),
            dma((5, 5, L)), dma((5, 5, L)), dma((5,)), dma((5,)), dma((2, S)), dma((2,)), dma((5 + L,)),
        ],
        compiler_params=pltpu.CompilerParams(collective_id=3, has_side_effects=True, vmem_limit_bytes=60000000),
        cost_estimate=pl.CostEstimate(flops=4 * 10**9, bytes_accessed=20 * 2**20, transcendentals=2**20),
        name="back",
    )(dh, sc, small, stat, u1, u2, x1, dys, q, k, v, p, o, es, ss, y, wa, gup)


def finish_kernel(
    lo_hbm, ig_hbm, gq_hbm, gk_hbm, gv_hbm, go_hbm, sm_hbm, gup_hbm, gdn0_hbm, gdn12_hbm, count_ref, load_ref,
    lo_out, ig_out, q_out, k_out, v_out, o_out, up_out, dn_out, eu_out, ed_out, r_out, m_out, n0_out, n1_out, n2_out, n3_out, cnt_out, load_out,
    sm_ref, gup_ref, sems,
):
    pairs = (
        (gup_hbm, gup_ref), (sm_hbm, sm_ref), (lo_hbm, lo_out), (ig_hbm, ig_out), (gq_hbm, q_out), (gk_hbm, k_out),
        (gv_hbm, v_out), (go_hbm, o_out), (gdn0_hbm, dn_out), (gdn12_hbm, ed_out),
    )
    copies = [pltpu.make_async_copy(a, b, sems.at[i]) for i, (a, b) in enumerate(pairs)]
    for c in copies:
        c.start()
    copies[0].wait()
    copies[1].wait()
    S, _, WR, F = gup_ref.shape
    FR = F // 2
    slot = (lax.axis_index("dp") * S + lax.axis_index("shard")) % (128 // WR)
    tokens = lo_out.shape[0] * 2 * S
    zeros = count_ref[0, 0].astype(jnp.int32)
    for i, n in enumerate((zeros, tokens - zeros)):
        cnt_out[i] = n
        load_out[i] = 0.9 * load_ref[i] + 0.1 * n.astype(F32) * 2 / tokens
    for s in range(S):
        for c in range(2):
            cols = slice((c * S + s) * FR, (c * S + s + 1) * FR)
            part = slice(c * FR, (c + 1) * FR)
            up_out[:, cols] = gup_ref[s, 0, :, part].astype(F32)
            for e in range(2):
                eu_out[e, :, cols] = gup_ref[s, 1 + e, :, part].astype(F32)
    mine = sm_ref[:, 0:WR]
    for j in range(1, 128 // WR):
        mine = jnp.where(slot == j, sm_ref[:, j * WR : (j + 1) * WR], mine)
    for i, out in enumerate((n0_out, n1_out, n2_out, n3_out)):
        out[...] = mine[i, :]
    r_out[...] = mine[4:6, :]
    m_out[...] = mine[6:8, :]
    for c in copies[2:]:
        c.wait()


def finish_call(lo, ig, gwq, gwk, gwv, gwo, smalls, gup, gdn0, gdn12, count, load):
    T, D = lo.shape
    S, _, WR, F = gup.shape
    FF = S * F
    sm = pl.BlockSpec(memory_space=pltpu.SMEM)
    vm = pl.BlockSpec(memory_space=pltpu.VMEM)
    sds = jax.ShapeDtypeStruct
    sq = sds((WR, D), F32)
    return pl.pallas_call(
        finish_kernel,
        out_shape=(
            sds((T, D), BF), sds((T, D), BF), sq, sq, sq, sq, sds((WR, FF), F32), sds(gdn0.shape, F32),
            sds((2, WR, FF), F32), sds(gdn12.shape, F32), sds((2, WR), F32), sds((2, WR), F32),
            *[sds((WR,), F32)] * 4, sds((2,), jnp.int32), sds((2,), F32),
        ),
        in_specs=[pl.BlockSpec(memory_space=pl.ANY)] * 10 + [sm, sm],
        out_specs=(vm,) * 16 + (sm, sm),
        scratch_shapes=[
            pltpu.VMEM(smalls.shape, F32), pltpu.VMEM(gup.shape, BF), pltpu.SemaphoreType.DMA((10,)),
        ],
        compiler_params=pltpu.CompilerParams(vmem_limit_bytes=66000000),
        name="finish",
    )(lo, ig, gwq, gwk, gwv, gwo, smalls, gup, gdn0, gdn12, count, load)


def body_plain(
    hidden_in, doc_ids, expert_ids, slot_ids, out_grad, ln1_gain, ln1_bias, w_query, w_key, w_value,
    w_out, ln2_gain, ln2_bias, w_up, w_down, w_router, w_mix, expert_up, expert_down, load_avg,
):
    T, D = hidden_in.shape
    H, HD = HEADS, D // HEADS
    S = lax.axis_size("shard")
    C = lax.axis_size("dp")
    WR = w_query.shape[0]
    FF = w_up.shape[1]
    FR = w_down.shape[0]
    F = FR * C
    E = expert_up.shape[0]
    LO, HI = 80, T - 80

    pos = jnp.where(expert_ids == 0, slot_ids, jnp.sum((expert_ids == 0).astype(jnp.int32)) + slot_ids)
    n0 = jnp.sum((expert_ids == 0).astype(jnp.int32))
    place = lax.iota(jnp.int32, T)
    perm = (pos[None, :] == place[:, None]).astype(BF)
    xs = mm(perm, hidden_in)
    dys = mm(perm, out_grad).astype(BF)
    doc = doc_ids[0]
    allowed = (place[None, :] <= place[:, None]) & (doc[:, None] == doc[None, :])
    allowed = mm(mm(perm, allowed.astype(BF)).astype(BF), perm, ((1,), (1,))) > 0.5
    is0 = (place < n0)[:, None]

    small = jnp.stack(
        [ln1_gain, ln1_bias, ln2_gain, ln2_bias, w_router[:, 0], w_router[:, 1], w_mix[:, 0], w_mix[:, 1]]
    ).astype(F32)
    small = lax.all_gather(small, BOTH, axis=1, tiled=True)
    g1, b1, g2, b2 = small[0], small[1], small[2], small[3]
    wr, wm = small[4:6], small[6:8]

    wa = jnp.stack([w_query, w_key, w_value, w_out])
    wa = lax.all_gather(wa, BOTH, axis=1, tiled=True)
    wq, wk, wv, wo = wa[0], wa[1], wa[2], wa[3]

    ups = jnp.stack([w_up, expert_up[0], expert_up[1]])
    ups = ups.reshape(3, WR, C, S, FR).transpose(3, 0, 1, 2, 4).reshape(S, 3, WR, F)
    ups = lax.all_to_all(ups, "shard", 0, 0)
    ups = lax.all_gather(ups, "dp", axis=0)
    ups = ups.transpose(2, 0, 1, 3, 4).reshape(3, D, F)
    downs = jnp.stack([w_down, expert_down[0], expert_down[1]])
    downs = lax.all_gather(downs, "dp", axis=1, tiled=True)

    dy_all = ag(dys)

    n1, u1, i1 = layer_norm(xs, g1, b1)
    h1b = n1.astype(BF)
    q = (mm(h1b, wq) * 0.125).astype(BF).reshape(T, H, HD)
    k = mm(h1b, wk).astype(BF).reshape(T, H, HD)
    v = mm(h1b, wv).astype(BF).reshape(T, H, HD)
    s = jnp.einsum("ihd,jhd->hij", q, k, preferred_element_type=F32)
    s = jnp.where(allowed[None], s, -1e30)
    ex = jnp.exp(s - jnp.max(s, axis=-1, keepdims=True))
    p = ex / jnp.sum(ex, axis=-1, keepdims=True)
    pb = p.astype(BF)
    o = jnp.einsum("hij,jhd->ihd", pb, v, preferred_element_type=F32).reshape(T, D).astype(BF)
    x1 = xs + mm(o, wo)
    h2, u2, i2 = layer_norm(x1, g2, b2)
    h2b = h2.astype(BF)

    def two(w):
        return jnp.stack([jnp.sum(h2 * w[0], axis=-1), jnp.sum(h2 * w[1], axis=-1)], axis=-1)

    r = jax.nn.softmax(two(wr), axis=-1)
    c = jax.nn.softmax(two(wm), axis=-1)
    gate = jnp.where(is0, r[:, 0:1], r[:, 1:2])
    c0, c1 = c[:, 0:1], c[:, 1:2]
    we = c0 * gate
    scal = jnp.concatenate([c1, jnp.where(is0, we, 0.0), jnp.where(is0, 0.0, we)], axis=1)

    h_all = ag(h2b)
    scal_all = ag(scal)

    def cut(a, e):
        return (a[:, :LO] if e == 1 else a[:, HI:]) if e else a

    partial_y = jnp.zeros((S, T, D), F32)
    partial_dh = jnp.zeros((S, T, D), F32)
    score = []
    gup, gdown = [], []
    for e in range(3):
        he = cut(h_all, e)
        dye = cut(dy_all, e).astype(F32)
        se = cut(scal_all, e)[:, :, e : e + 1]
        n = he.shape[1]
        hf = he.reshape(S * n, D)
        pre = mm(hf, ups[e])
        val, der = gelu_pair(pre)
        ub = val.astype(BF)
        m = mm(ub, downs[e]).reshape(S, n, D)
        dm = (dye * se).astype(BF).reshape(S * n, D)
        dg = (mm(dm, downs[e], ((1,), (1,))) * der).astype(BF)
        gdown.append(mm(ub, dm, ((0,), (0,))))
        gup.append(mm(hf, dg, ((0,), (0,))))
        dx = mm(dg, ups[e], ((1,), (1,))).reshape(S, n, D)
        y = m * se
        sc = jnp.sum(dye * m, axis=-1)
        pad = [(0, 0), (0, T - n) if e < 2 else (T - n, 0)]
        live = is0[None, :, 0]
        partial_y += jnp.pad(y, pad + [(0, 0)])
        partial_dh += jnp.pad(dx, pad + [(0, 0)])
        score.append(jnp.pad(sc, pad))
    yfull = rs(partial_y)
    dh2 = rs(partial_dh)
    sc = lax.psum_scatter(jnp.stack(score, axis=1), "shard", scatter_dimension=0, tiled=False)
    sm = sc[0][:, None]
    se = jnp.where(is0, sc[1][:, None], sc[2][:, None])

    dc0, dc1 = gate * se, sm
    tot = c0 * dc0 + c1 * dc1
    dcl0, dcl1 = c0 * (dc0 - tot), c1 * (dc1 - tot)
    dgate = c0 * se
    dr0, dr1 = jnp.where(is0, dgate, 0.0), jnp.where(is0, 0.0, dgate)
    tot = r[:, 0:1] * dr0 + r[:, 1:2] * dr1
    drl0, drl1 = r[:, 0:1] * (dr0 - tot), r[:, 1:2] * (dr1 - tot)
    layer_out = (x1 + yfull).astype(BF)
    dh2 = dh2 + drl0 * wr[0] + drl1 * wr[1] + dcl0 * wm[0] + dcl1 * wm[1]
    gw = [jnp.sum(h2 * t, axis=0) for t in (drl0, drl1, dcl0, dcl1)]
    dx1, gg2, gb2 = norm_back(dh2, u2, i2, g2)
    dx1 = dx1 + dys.astype(F32)
    dab = dx1.astype(BF)
    gwo = mm(o, dab, ((0,), (0,)))
    do = mm(dab, wo, ((1,), (1,))).astype(BF).reshape(T, H, HD)
    dp = jnp.einsum("ihd,jhd->hij", do, v, preferred_element_type=F32)
    ds = (p * (dp - jnp.sum(p * dp, axis=-1, keepdims=True))).astype(BF)
    dq = jnp.einsum("hij,jhd->ihd", ds, k, preferred_element_type=F32).astype(BF)
    dq = (dq * BF(0.125)).reshape(T, D)
    dk = jnp.einsum("hij,ihd->jhd", ds, q, preferred_element_type=F32).astype(BF).reshape(T, D)
    dv = jnp.einsum("hij,ihd->jhd", pb, do, preferred_element_type=F32).astype(BF).reshape(T, D)
    dh1 = mm(dq, wq, ((1,), (1,))) + mm(dk, wk, ((1,), (1,))) + mm(dv, wv, ((1,), (1,)))
    ga = jnp.stack([mm(h1b, dq, ((0,), (0,))), mm(h1b, dk, ((0,), (0,))), mm(h1b, dv, ((0,), (0,))), gwo])
    dxn, gg1, gb1 = norm_back(dh1, u1, i1, g1)
    input_grad = (dx1 + dxn).astype(BF)

    layer_out = mm(perm, layer_out, ((0,), (0,))).astype(BF)
    input_grad = mm(perm, input_grad, ((0,), (0,))).astype(BF)

    smalls = lax.psum(jnp.stack([gg1, gb1, gg2, gb2] + gw), BOTH)
    mine = lax.dynamic_slice_in_dim(smalls, lax.axis_index(BOTH) * WR, WR, 1)
    ga = ga.reshape(4, C, S, WR, D).transpose(1, 2, 0, 3, 4)
    ga = lax.psum_scatter(ga.astype(BF), "dp", scatter_dimension=0, tiled=False)
    ga = lax.psum_scatter(ga, "shard", scatter_dimension=0, tiled=False).astype(F32)
    gdown = lax.psum_scatter(jnp.stack(gdown), "dp", scatter_dimension=1, tiled=True)
    gup = jnp.stack(gup).reshape(3, C, S, WR, F).transpose(1, 2, 0, 3, 4)
    gup = lax.psum_scatter(gup, "dp", scatter_dimension=0, tiled=False).astype(BF)
    gup = lax.all_to_all(gup, "shard", 0, 0).astype(F32)
    gup = gup.reshape(S, 3, WR, C, FR).transpose(1, 2, 3, 0, 4).reshape(3, WR, FF)

    counts = lax.psum(jnp.stack([n0, T - n0]), BOTH)
    load_new = 0.9 * load_avg + 0.1 * counts.astype(F32) * E / (T * C * S)
    return (
        layer_out, input_grad, mine[0], mine[1], ga[0], ga[1], ga[2], ga[3], mine[2], mine[3],
        gup[0], gdown[0], jnp.stack([mine[4], mine[5]], axis=1), jnp.stack([mine[6], mine[7]], axis=1),
        gup[1:], gdown[1:], counts, load_new,
    )


def body(
    hidden_in, doc_ids, expert_ids, slot_ids, out_grad, ln1_gain, ln1_bias, w_query, w_key, w_value,
    w_out, ln2_gain, ln2_bias, w_up, w_down, w_router, w_mix, expert_up, expert_down, load_avg,
):
    T, D = hidden_in.shape
    H, HD = HEADS, D // HEADS
    S = lax.axis_size("shard")
    C = lax.axis_size("dp")
    WR = w_query.shape[0]
    FF = w_up.shape[1]
    FR = w_down.shape[0]
    F = FR * C
    E = expert_up.shape[0]
    dev = lax.axis_index(BOTH)
    small = jnp.stack(
        [ln1_gain, ln1_bias, ln2_gain, ln2_bias, w_router[:, 0], w_router[:, 1], w_mix[:, 0], w_mix[:, 1]]
    ).astype(F32)
    group = 128 // WR
    slot_of = lax.broadcasted_iota(jnp.int32, (8, 128), 1) // WR
    small = jnp.where(slot_of == dev % group, jnp.tile(small, (1, group)), 0.0)
    (
        stat, u1, u2, x1, dys, q, k, v, p, o, small, count, wa, y_parts, dh2, sc, gup, gdn0, gdn12,
    ) = front_call(
        hidden_in, out_grad, doc_ids, expert_ids.reshape(1, T), slot_ids.reshape(1, T), small,
        (w_query, w_key, w_value, w_out), w_up, expert_up, w_down, expert_down, S,
    )
    y_parts = y_parts.reshape(S, T, D)
    layer_out, input_grad, gwq, gwk, gwv, gwo, smalls, gup = back_call(
        dh2, y_parts, sc, small, stat, u1, u2, x1, dys, q, k, v, p, o,
        expert_ids.reshape(1, T), slot_ids.reshape(1, T), wa.reshape(4, D, D), gup, S,
    )
    lo, ig, gq, gk, gv, go, gu, gd, geu, ged, gr, gm, n0, n1, n2, n3, counts, load_new = finish_call(
        layer_out, input_grad, gwq, gwk, gwv, gwo, smalls, gup, gdn0, gdn12, count, load_avg
    )
    return (
        lo, ig, n0, n1, gq, gk, gv, go, n2, n3, gu, gd, gr.T, gm.T, geu, ged, counts, load_new,
    )


def pick(*args):
    S, C, WR, FR = lax.axis_size("shard"), lax.axis_size("dp"), args[7].shape[0], args[14].shape[0]
    fast = C == 2 and S // 4 == 4 and S % 4 == 0 and WR % 16 == 0 and 128 % WR == 0 and FR % 128 == 0
    return (body if fast else body_plain)(*args)


def solution(mesh):
    row, vec = P(BOTH, None), P(BOTH)
    mid = P(None, BOTH, None)
    return jax.shard_map(
        pick,
        mesh=mesh,
        in_specs=(row, row, vec, vec, row, vec, vec, row, row, row, row, vec, vec, row, row, row, row, mid, mid, P()),
        out_specs=(row, row, vec, vec, row, row, row, row, vec, vec, row, row, row, row, mid, mid, P(), P()),
        check_vma=False,
    )
```
